32 devices in a mesh: dp: 8 (over z, x), tensor: 4 (over y, core).
Axes of the slice: x: 2, y: 2, z: 4, core: 2. Of those that a mesh axis runs over, the one named last changes fastest.
Arguments:
- hidden_in: bfloat16 [16384, 1024], P('dp'), may hold values from -6 to 6
- doc_ids: int32 [8, 2048], P('dp'), may hold values from 0 to 4, never falling along the last dimension, each value on 1 to 800 neighbouring positions
- cotangent: bfloat16 [16384, 1024], P('dp'), may hold values from -6 to 6
- norm_gain: float32 [1024], replicated, may hold values from 0.5 to 1.5
- in_weight: bfloat16 [1024, 4384], P('dp'), may hold values from -0.1875 to 0.1875
- conv_weight: bfloat16 [4, 2304], replicated, may hold values from -3 to 3
- conv_bias: float32 [2304], replicated, may hold values from -1.5 to 1.5
- dt_bias: float32 [32], replicated, may hold values from -6.9 to -2.3
- log_decay: float32 [32], replicated, may hold values from 0 to 2.77
- skip_gain: float32 [32], replicated, may hold values from 0.5 to 1.5
- gate_gain: float32 [2048], replicated, may hold values from 0.5 to 1.5
- out_weight: bfloat16 [1024, 2048], P('dp', 'tensor'), may hold values from -0.125 to 0.125
Outputs:
- layer_out: bfloat16 [16384, 1024], P('dp')
- grad_input: float32 [16384, 1024], P('dp')
- grad_norm_gain: float32 [1024], replicated
- grad_in_weight: float32 [1024, 4384], P('dp')
- grad_conv_weight: float32 [4, 2304], replicated
- grad_conv_bias: float32 [2304], replicated
- grad_dt_bias: float32 [32], replicated
- grad_log_decay: float32 [32], replicated
- grad_skip_gain: float32 [32], replicated
- grad_gate_gain: float32 [2048], replicated
- grad_out_weight: float32 [1024, 2048], P('dp', 'tensor')
The draws below stay inside these ranges and needn't reach their ends.
Inputs may be any that keep to these rules, and one draw needn't show every extreme that they name: `doc_ids`: within each sequence the ids start at 0 and never fall; each document has 1 to 800 tokens, and one has exactly 800.
All inputs are finite; a program needn't handle non-finite values.
Results may differ from the reference program's by a relative error of at most 0.0065.
Values may be sent and summed in bfloat16 or wider, within the bound.
A program may use at most 256 MiB of HBM per device.

```python
import math
import jax
import jax.numpy as jnp
import numpy as np
from jax import lax

D = 1024
HEADS = 32
STATE = 128
KERNEL = 4
SPAN = 256
LEN = 2048
DOCS = 5
DOC_MOST = 800
INNER = 2048
CHANNELS = 2304
COLUMNS = 4384
SEQS = 8
TOKENS = 16384


def block_levels(stream_key, shape, pieces, least, top_value):
    level, own = 1.0, jax.random.fold_in(stream_key, 6)
    for dim, blocks in pieces:
        heights = jnp.exp(jax.random.uniform(jax.random.fold_in(own, dim), (blocks,), jnp.float32, least / len(pieces), top_value / len(pieces)))
        level = level * jnp.repeat(heights, shape[dim] // blocks).reshape([-1 if axis == dim else 1 for axis in range(len(shape))])
    return level


def split_up(number_of, total, limit, lean):
    weights = [(1 << 20) // math.isqrt(standing ** lean) + 1 for standing in range(2, number_of + 1)]
    spare, given = total - limit - (number_of - 1), [1] * (number_of - 1)
    while spare > 0:
        free = [i for i in range(number_of - 1) if given[i] < limit]
        pool, remaining = sum([weights[i] for i in free]), spare
        for i in free:
            extra = min(limit - given[i], max(1, remaining * weights[i] // pool), spare)
            given[i] = given[i] + extra
            spare = spare - extra
    return np.array([limit] + given)


def uneven(key, number_of, total, bound, slope):
    if number_of == 2:
        one = jax.random.randint(key, (), max(1, total - bound), min(bound, total - 1) + 1)
        return jnp.stack([one, total - one])
    sizes = jnp.asarray(split_up(number_of, total, bound, slope), jnp.int32)
    pairs = (number_of - 1) // 2
    giver, receiver = sizes[1:1 + 2 * pairs:2], sizes[2:2 + 2 * pairs:2]
    room = jnp.minimum(giver - 1, bound - receiver)
    moved = jax.random.randint(jax.random.fold_in(key, 1), (pairs,), 0, 1 << 20) % (room + 1)
    sizes = sizes.at[1:1 + 2 * pairs:2].set(giver - moved).at[2:2 + 2 * pairs:2].set(receiver + moved)
    return sizes[jax.random.permutation(jax.random.fold_in(key, 2), number_of)]


def normal_values(stream_key, extent, width, most, split=(), held_as=jnp.bfloat16):
    drawn = width * jax.random.normal(stream_key, extent, jnp.float32)
    if split:
        drawn = drawn * block_levels(stream_key, extent, split, -0.22, 0.18)
    return jnp.clip(drawn, -most, most).astype(held_as)


def setup_inputs(seed: int = 0) -> dict:
    streams_of = jax.random.split(jax.random.key(seed), 13)
    hidden_in = normal_values(streams_of[0], (TOKENS, D), 1.0, 6.0, ((0, 8),))
    doc_ids = jax.vmap(lambda own: jnp.searchsorted(jnp.cumsum(uneven(own, DOCS, LEN, DOC_MOST, 0)), jnp.arange(LEN), side="right"))(jax.random.split(streams_of[1], SEQS)).reshape((SEQS, LEN)).astype(jnp.int32)
    cotangent = normal_values(streams_of[2], (TOKENS, D), 1.0, 6.0, ((0, 8),))
    norm_gain = jnp.clip(1.0 + 0.1 * jax.random.normal(streams_of[3], (D,), jnp.float32), 0.5, 1.5)
    in_weight = normal_values(streams_of[4], (D, COLUMNS), D ** -0.5, 0.1875, ((0, 8),))
    conv_weight = normal_values(streams_of[5], (KERNEL, CHANNELS), KERNEL ** -0.5, 3.0)
    conv_bias = normal_values(streams_of[6], (CHANNELS,), 0.3, 1.5, (), jnp.float32)
    dt_bias = jnp.clip(jax.random.uniform(streams_of[7], (HEADS,), jnp.float32, -6.9, -2.3), -6.9, -2.3)
    log_decay = jnp.clip(jax.random.uniform(streams_of[8], (HEADS,), jnp.float32, 0.0, 2.77), 0.0, 2.77)
    skip_gain = jnp.clip(jax.random.uniform(streams_of[9], (HEADS,), jnp.float32, 0.5, 1.5), 0.5, 1.5)
    gate_gain = jnp.clip(1.0 + 0.1 * jax.random.normal(streams_of[10], (INNER,), jnp.float32), 0.5, 1.5)
    out_weight = normal_values(streams_of[11], (D, INNER), INNER ** -0.5, 0.125, ((0, 8), (1, 4)))
    return dict(hidden_in=hidden_in, doc_ids=doc_ids, cotangent=cotangent, norm_gain=norm_gain, in_weight=in_weight, conv_weight=conv_weight, conv_bias=conv_bias, dt_bias=dt_bias, log_decay=log_decay, skip_gain=skip_gain, gate_gain=gate_gain, out_weight=out_weight)


epsilon = 1e-05
highest = lax.Precision.HIGHEST

@jax.custom_vjp
def low(v):
    return lax.optimization_barrier(v.astype(jnp.bfloat16)).astype(jnp.float32)

@jax.custom_vjp
def low_back(v):
    return v

def low_keep(v):
    return (low(v), None)

def low_pass(kept, grad):
    return (grad,)

def back_keep(v):
    return (v, None)

def back_low(kept, grad):
    return (low(grad),)
low.defvjp(low_keep, low_pass)
low_back.defvjp(back_keep, back_low)

def conv_reset(columns, doc_row, kernel_w, kernel_b):
    seq_len = columns.shape[0]
    tap_count = kernel_w.shape[0]
    result = kernel_b[None, :] + kernel_w[tap_count - 1][None, :] * columns
    for offset in range(1, tap_count):
        shifted = jnp.pad(columns, ((offset, 0), (0, 0)))[:seq_len]
        earlier = jnp.pad(doc_row, (offset, 0), constant_values=-1)[:seq_len]
        keeper = (earlier == doc_row).astype(columns.dtype)
        result = result + kernel_w[tap_count - 1 - offset][None, :] * shifted * keeper[:, None]
    return result

def mixer_seq(mixed_in, step_in, gate_in, doc_row, kernel_w, kernel_b, bias_dt, decay_log, skip_vec):
    seq_len, inner_dim = gate_in.shape
    head_count = step_in.shape[1]
    head_size = inner_dim // head_count
    state_dim = (mixed_in.shape[1] - inner_dim) // 2
    spans = seq_len // SPAN
    activated = jax.nn.silu(conv_reset(mixed_in, doc_row, kernel_w, kernel_b))
    values = activated[:, :inner_dim].reshape(seq_len, head_count, head_size)
    b_rows = activated[:, inner_dim:inner_dim + state_dim].reshape(spans, SPAN, state_dim)
    c_rows = activated[:, inner_dim + state_dim:].reshape(spans, SPAN, state_dim)
    step_dt = jax.nn.softplus(step_in + bias_dt[None, :])
    log_step = step_dt * (-jnp.exp(decay_log))[None, :]
    running = jnp.cumsum(log_step.reshape(spans, SPAN, head_count), axis=1)
    scaled = (values * step_dt[:, :, None]).reshape(spans, SPAN, head_count, head_size)
    doc_blocks = doc_row.reshape(spans, SPAN)
    position = jnp.arange(SPAN)
    causal = position[:, None] >= position[None, :]
    allowed = (doc_blocks[:, :, None] == doc_blocks[:, None, :]) & causal[None]
    running_h = jnp.transpose(running, (0, 2, 1))
    log_gap = running_h[:, :, :, None] - running_h[:, :, None, :]
    decays = jnp.where(allowed[:, None], jnp.exp(jnp.minimum(log_gap, 0.0)), 0.0)
    scores = jnp.einsum('ctn,csn->cts', c_rows, b_rows, precision=highest)
    weights = decays * scores[:, None]
    within = jnp.einsum('chts,cshp->cthp', weights, scaled, precision=highest)
    ending = running[:, -1, :]
    doc_end = doc_blocks[:, -1]
    tail_w = jnp.where((doc_blocks == doc_end[:, None])[:, :, None], jnp.exp(ending[:, None, :] - running), 0.0)
    local_state = jnp.einsum('csn,cshp->chpn', b_rows, scaled * tail_w[:, :, :, None], precision=highest)

    def carry_step(carried, inputs):
        state_now, doc_now = carried
        block_state, total_log, doc_last = inputs
        keep_on = (doc_last == doc_now).astype(block_state.dtype)
        renewed = block_state + jnp.exp(total_log)[:, None, None] * keep_on * state_now
        return ((renewed, doc_last), (state_now, doc_now))
    initial = (jnp.zeros(local_state.shape[1:], local_state.dtype), jnp.array(-1, jnp.int32))
    unused, (entering, doc_enter) = lax.scan(carry_step, initial, (local_state, ending, doc_end))
    reaching = jnp.where((doc_blocks == doc_enter[:, None])[:, :, None], jnp.exp(running), 0.0)
    across = jnp.einsum('ctn,chpn->cthp', c_rows, entering, precision=highest) * reaching[:, :, :, None]
    output = within + across + skip_vec[None, None, :, None] * values.reshape(spans, SPAN, head_count, head_size)
    return output.reshape(seq_len, inner_dim) * jax.nn.silu(gate_in)

def group_forward(hidden, doc_pair, layer_params):
    norm_gain, in_weight, conv_weight, conv_bias, dt_bias, log_decay, skip_gain, gate_gain, out_weight = layer_params
    inv_rms = lax.rsqrt(lax.optimization_barrier(jnp.mean(hidden * hidden, -1, keepdims=True)) + epsilon)
    normed = low(hidden * inv_rms * norm_gain)
    projected = low_back(jnp.dot(normed, in_weight, precision=highest))
    pair_count = doc_pair.shape[0]
    gate_part = projected[:, :INNER].reshape(pair_count, LEN, INNER)
    mixed_part = projected[:, INNER:2 * INNER + 2 * STATE].reshape(pair_count, LEN, CHANNELS)
    step_part = projected[:, 2 * INNER + 2 * STATE:].reshape(pair_count, LEN, HEADS)
    mapped = jax.vmap(mixer_seq, in_axes=(0, 0, 0, 0, None, None, None, None, None))
    gated = mapped(mixed_part, step_part, gate_part, doc_pair, conv_weight, conv_bias, dt_bias, log_decay, skip_gain)
    gated = gated.reshape(pair_count * LEN, INNER)
    inv_gate = lax.rsqrt(lax.optimization_barrier(jnp.mean(gated * gated, -1, keepdims=True)) + epsilon)
    normed_out = low(gated * inv_gate * gate_gain)
    return hidden + jnp.dot(normed_out, out_weight.T, precision=highest)

def reference(hidden_in, doc_ids, cotangent, norm_gain, in_weight, conv_weight, conv_bias, dt_bias, log_decay, skip_gain, gate_gain, out_weight):
    layer_params = (norm_gain.astype(jnp.float32), in_weight.astype(jnp.float32), conv_weight.astype(jnp.float32), conv_bias.astype(jnp.float32), dt_bias.astype(jnp.float32), log_decay.astype(jnp.float32), skip_gain.astype(jnp.float32), gate_gain.astype(jnp.float32), out_weight.astype(jnp.float32))
    hidden = hidden_in.astype(jnp.float32)
    groups = doc_ids.shape[0] // 2

    def whole_layer(hidden_all, param_all):

        def one_group(carried, inputs):
            rows_in, doc_pair = inputs
            return (carried, jax.checkpoint(group_forward)(rows_in, doc_pair, param_all))
        unused, outputs = lax.scan(one_group, jnp.zeros((), jnp.float32), (hidden_all.reshape(groups, 2 * LEN, D), doc_ids.reshape(groups, 2, LEN)))
        return outputs.reshape(hidden_all.shape)
    result, pullback = jax.vjp(whole_layer, hidden, layer_params)
    grad_hidden, grad_params = pullback(cotangent.astype(jnp.float32))
    return (result.astype(jnp.bfloat16), grad_hidden, grad_params[0], grad_params[1], grad_params[2], grad_params[3], grad_params[4], grad_params[5], grad_params[6], grad_params[7], grad_params[8])
```

```python
import jax
import jax.numpy as jnp
from jax import lax
from jax.experimental import pallas as pl
from jax.experimental.pallas import tpu as pltpu
from jax.sharding import PartitionSpec as P

SPAN = 256
LANES = 128
EPS = 1e-05
FAR = -1e30
F32 = jnp.float32
BF16 = jnp.bfloat16


def nn(a, b):
    return lax.dot_general(a, b, (((1,), (0,)), ((), ())), preferred_element_type=F32)


def nt(a, b):
    return lax.dot_general(a, b, (((1,), (1,)), ((), ())), preferred_element_type=F32)


def tn(a, b):
    return lax.dot_general(a, b, (((0,), (0,)), ((), ())), preferred_element_type=F32)


def iota(shape, dim):
    return lax.broadcasted_iota(jnp.int32, shape, dim)


def as_column(row, rows=SPAN):
    return jnp.transpose(jnp.broadcast_to(row, (LANES, rows)))


def as_row(block):
    return jnp.sum(jnp.transpose(block), axis=0, keepdims=True)


def split3(v):
    hi = v.astype(BF16)
    rest = v - hi.astype(F32)
    mid = rest.astype(BF16)
    low = (rest - mid.astype(F32)).astype(BF16)
    return hi, mid, low


def tri_sum(tri, v, heads):
    lane = iota(v.shape, 1)
    v = jnp.where(lane < heads, v, 0.0)
    hi = v.astype(BF16).astype(F32)
    rest = v - hi
    mid = rest.astype(BF16).astype(F32)
    low = rest - mid
    packed = hi + pltpu.roll(mid, heads, 1) + pltpu.roll(low, 2 * heads, 1)
    out = nn(tri, packed.astype(BF16))
    return out + pltpu.roll(out, LANES - heads, 1) + pltpu.roll(out, LANES - 2 * heads, 1)


def pair_lanes(cols, pair, low_half):
    rows = cols.shape[0]
    first = jnp.broadcast_to(cols[:, 2 * pair : 2 * pair + 1], (rows, LANES))
    second = jnp.broadcast_to(cols[:, 2 * pair + 1 : 2 * pair + 2], (rows, LANES))
    return jnp.where(low_half, first, second)


def exact_nt(a, b):
    a_hi, b_hi = a.astype(BF16), b.astype(BF16)
    a_lo = (a - a_hi.astype(F32)).astype(BF16)
    b_lo = (b - b_hi.astype(F32)).astype(BF16)
    return nt(a_hi, b_hi) + (nt(a_hi, b_lo) + nt(a_lo, b_hi))


def softplus(v):
    return jnp.maximum(v, 0.0) + jnp.log1p(jnp.exp(-jnp.abs(v)))


def own_lanes(row, rank, heads):
    total = row.shape[1]
    pick = (iota((total, LANES), 0) == rank * heads + iota((total, LANES), 1)) & (
        iota((total, LANES), 1) < heads
    )
    wide = jnp.broadcast_to(row, (8, total))
    out = lax.dot_general(
        wide, pick.astype(F32), (((1,), (0,)), ((), ())),
        precision=lax.Precision.HIGHEST, preferred_element_type=F32,
    )
    return out[0:1]


def forward_kernel(
    sizes, axis,
    docs_ref, hid_ref, cot_ref, ngain_ref, win_ref, wstep_ref, wout_ref, cw_ref, cb_ref,
    dtb_ref, dec_ref, skip_ref, ggain_ref,
    normed_ref, gate_ref, mixed_ref, pre_ref, ssd_ref, stp_ref, state_ref, dn_ref, sums_ref,
    xbuf, dbuf, state, par, cwb, gain,
):
    inner, heads, model = sizes
    pairs = heads // 2
    chan = inner + 2 * LANES
    i = pl.program_id(0)
    rank = lax.axis_index(axis)
    inner_all = ggain_ref.shape[1]
    off = pl.multiple_of(rank * inner, LANES)

    @pl.when(i == 0)
    def _():
        xbuf[0:8] = jnp.zeros((8, chan), F32)
        dbuf[0:8] = jnp.full((8, LANES), -1.0, F32)
        state[...] = jnp.zeros(state.shape, F32)
        par[0:1] = own_lanes(dtb_ref[...], rank, heads)
        par[1:2] = -jnp.exp(own_lanes(dec_ref[...], rank, heads))
        par[2:3] = own_lanes(skip_ref[...], rank, heads)
        taps = cw_ref.shape[0]
        cwb[0:taps, 0:inner] = cw_ref[:, pl.ds(off, inner)].astype(F32)
        cwb[0:taps, inner:chan] = cw_ref[:, inner_all:].astype(F32)
        cwb[4:5, 0:inner] = cb_ref[:, pl.ds(off, inner)]
        cwb[4:5, inner:chan] = cb_ref[:, inner_all:]
        gain[0:1] = ggain_ref[:, pl.ds(off, inner)]

    hid = hid_ref[...].astype(F32)
    inv = lax.rsqrt(jnp.mean(hid * hid, -1, keepdims=True) + EPS)
    nb = (hid * inv * ngain_ref[...]).astype(BF16)
    normed_ref[...] = nb
    xbuf[8 : 8 + SPAN] = nn(nb, win_ref[:, inner : inner + chan])
    gate_ref[...] = nn(nb, win_ref[:, 0:inner])
    stp = nn(nb, wstep_ref[...])
    stp_ref[...] = stp
    mixed_ref[...] = xbuf[8 : 8 + SPAN]
    dn_ref[...] = nn(cot_ref[...], wout_ref[...])

    drow = docs_ref[pl.ds(i, 1), :].astype(F32)
    dcol = as_column(drow)
    enter = dbuf[7:8]
    dbuf[8 : 8 + SPAN] = dcol
    keeps = [None] + [dbuf[8 - k : 8 - k + SPAN] == dcol for k in range(1, 4)]

    def conv(group):
        lanes = slice(group * LANES, (group + 1) * LANES)
        acc = cwb[4:5, lanes] + cwb[3:4, lanes] * xbuf[8 : 8 + SPAN, lanes]
        for k in range(1, 4):
            acc = acc + cwb[3 - k : 4 - k, lanes] * jnp.where(
                keeps[k], xbuf[8 - k : 8 - k + SPAN, lanes], 0.0
            )
        pre_ref[:, lanes] = acc
        return acc * jax.nn.sigmoid(acc)

    b_act, c_act = conv(pairs), conv(pairs + 1)
    b_rows, c_rows = b_act.astype(BF16), c_act.astype(BF16)

    step = softplus(stp + par[0:1])
    row_i, col_i = iota((SPAN, SPAN), 0), iota((SPAN, SPAN), 1)
    tril = (row_i >= col_i).astype(BF16)
    running = tri_sum(tril, step * par[1:2], heads)
    run_rows = jnp.transpose(running)
    ending = running[SPAN - 1 : SPAN]
    tail = jnp.where(dcol == dcol[SPAN - 1 : SPAN], jnp.exp(ending - running), 0.0)
    reach = jnp.where(dcol == enter, jnp.exp(running), 0.0)
    same = jnp.concatenate([dcol, dcol], 1) == drow
    bias = jnp.where(same & (row_i >= col_i), 0.0, FAR)
    scores = exact_nt(c_act, b_act)
    b_turned = jnp.transpose(b_act).astype(BF16)
    low_half = iota((SPAN, LANES), 1) < LANES // 2
    half = SPAN // 2
    square = jnp.zeros((SPAN, LANES), F32)
    cross = jnp.zeros((SPAN, LANES), F32)
    for pair in range(pairs):
        lanes = slice(pair * LANES, (pair + 1) * LANES)
        act = conv(pair)
        scaled = act * pair_lanes(step, pair, low_half)
        xb = scaled.astype(BF16)
        tail_l = pair_lanes(tail, pair, low_half)
        reach_l = pair_lanes(reach, pair, low_half)
        held = state[:, lanes]
        held_b = held.astype(BF16)
        state_ref[0, :, lanes] = held_b
        state[:, lanes] = nn(b_turned, (scaled * tail_l).astype(BF16)) + reach_l[SPAN - 1 : SPAN] * held
        out = reach_l * nn(c_rows, held_b)
        parts = []
        for sub in range(2):
            head = 2 * pair + sub
            blocks = []
            for blk in range(2):
                rows = slice(blk * half, (blk + 1) * half)
                width = (blk + 1) * half
                gap = running[rows, head : head + 1] - run_rows[head : head + 1, 0:width]
                weight = jnp.exp(gap + bias[rows, 0:width]) * scores[rows, 0:width]
                blocks.append(nn(weight.astype(BF16), xb[0:width]))
            parts.append(jnp.concatenate(blocks, 0))
        out = out + jnp.where(low_half, parts[0], parts[1])
        skip_l = pair_lanes(par[2:3], pair, low_half[0:1])
        ssd = out + skip_l * act
        ssd_ref[:, lanes] = ssd
        gate = gate_ref[:, lanes]
        gated = ssd * (gate * jax.nn.sigmoid(gate))
        square = square + gated * gated
        cross = cross + dn_ref[:, lanes] * gain[0:1, lanes] * gated
    sums_ref[0, pl.ds(i, 1), :] = as_row(square)
    sums_ref[1, pl.ds(i, 1), :] = as_row(cross)
    xbuf[0:8] = xbuf[SPAN : SPAN + 8]
    dbuf[0:8] = dbuf[SPAN : SPAN + 8]


def mixer_forward(
    docs, hidden, cotangent, ngain, w_in, w_step, w_out, conv_w, conv_b, dtb, dec, skip, ggain,
    heads, axis="tensor",
):
    tokens, model = hidden.shape
    inner = w_out.shape[1]
    chan = inner + 2 * LANES
    spans = tokens // SPAN

    def tok(width):
        return pl.BlockSpec((SPAN, width), lambda i: (i, 0))

    def full(arr):
        return pl.BlockSpec(arr.shape, lambda i: (0,) * arr.ndim)

    outs = (
        jax.ShapeDtypeStruct((tokens, model), BF16),
        jax.ShapeDtypeStruct((tokens, inner), F32),
        jax.ShapeDtypeStruct((tokens, chan), F32),
        jax.ShapeDtypeStruct((tokens, chan), F32),
        jax.ShapeDtypeStruct((tokens, inner), F32),
        jax.ShapeDtypeStruct((tokens, LANES), F32),
        jax.ShapeDtypeStruct((spans, LANES, inner), BF16),
        jax.ShapeDtypeStruct((tokens, inner), F32),
        jax.ShapeDtypeStruct((2, spans, SPAN), F32),
    )
    consts = (ngain, w_in, w_step, w_out, conv_w, conv_b, dtb, dec, skip, ggain)
    return pl.pallas_call(
        lambda *refs: forward_kernel((inner, heads, model), axis, *refs),
        out_shape=outs,
        grid=(spans,),
        in_specs=[full(docs), tok(model), tok(model)] + [full(c) for c in consts],
        out_specs=(
            tok(model), tok(inner), tok(chan), tok(chan), tok(inner), tok(LANES),
            pl.BlockSpec((1, LANES, inner), lambda i: (i, 0, 0)),
            tok(inner),
            pl.BlockSpec((2, spans, SPAN), lambda i: (0, 0, 0)),
        ),
        scratch_shapes=[
            pltpu.VMEM((SPAN + 8, chan), F32),
            pltpu.VMEM((SPAN + 8, LANES), F32),
            pltpu.VMEM((LANES, inner), F32),
            pltpu.VMEM((8, LANES), F32),
            pltpu.VMEM((8, chan), F32),
            pltpu.VMEM((8, inner), F32),
        ],
        compiler_params=pltpu.CompilerParams(
            dimension_semantics=("arbitrary",), vmem_limit_bytes=60 * 2**20
        ),
        name="mixer_forward",
    )(docs, hidden, cotangent, *consts)


def backward_kernel(
    sizes, axis,
    docs_ref, gate_ref, mixed_ref, pre_ref, ssd_ref, stp_ref, state_ref, dn_ref, sums_ref,
    cw_ref, dtb_ref, dec_ref, skip_ref, ggain_ref,
    nout_ref, dgate_ref, dmix_ref, dstp_ref, gconv_ref, gchan_ref, ghead_ref,
    pbuf, dbuf, dstate, par, cwb, gain,
):
    inner, heads, inner_all = sizes
    pairs = heads // 2
    chan = inner + 2 * LANES
    spans = docs_ref.shape[0]
    i = pl.program_id(0)
    c = spans - 1 - i
    rank = lax.axis_index(axis)
    off = pl.multiple_of(rank * inner, LANES)

    @pl.when(i == 0)
    def _():
        pbuf[SPAN : SPAN + 8] = jnp.zeros((8, chan), F32)
        dbuf[SPAN : SPAN + 8] = jnp.full((8, LANES), -2.0, F32)
        dstate[...] = jnp.zeros(dstate.shape, F32)
        par[0:1] = own_lanes(dtb_ref[...], rank, heads)
        par[1:2] = -jnp.exp(own_lanes(dec_ref[...], rank, heads))
        par[2:3] = own_lanes(skip_ref[...], rank, heads)
        taps = cw_ref.shape[0]
        cwb[0:taps, 0:inner] = cw_ref[:, pl.ds(off, inner)].astype(F32)
        cwb[0:taps, inner:chan] = cw_ref[:, inner_all:].astype(F32)
        gain[0:1] = ggain_ref[:, pl.ds(off, inner)]
        gconv_ref[...] = jnp.zeros(gconv_ref.shape, F32)
        gchan_ref[...] = jnp.zeros(gchan_ref.shape, F32)
        ghead_ref[...] = jnp.zeros(ghead_ref.shape, F32)

    def fold(v):
        return jnp.sum(v.reshape(SPAN // 8, 8, v.shape[1]), axis=0)

    drow = docs_ref[pl.ds(c, 1), :].astype(F32)
    dcol = as_column(drow)
    before = docs_ref[pl.ds(jnp.maximum(c - 1, 0), 1), :].astype(F32)
    enter = as_column(before)[SPAN - 1 : SPAN]
    enter = jnp.where(c == 0, -1.0, enter)
    dbuf[0:SPAN] = dcol
    keeps = [None] + [dbuf[k : k + SPAN] == dcol for k in range(1, 4)]

    inv = lax.rsqrt(as_column(sums_ref[0, pl.ds(c, 1), :]) * (1.0 / inner_all) + EPS)
    pull = as_column(sums_ref[1, pl.ds(c, 1), :]) * (inv * inv * inv) * (1.0 / inner_all)

    raw = stp_ref[...] + par[0:1]
    step = softplus(raw)
    row_i, col_i = iota((SPAN, SPAN), 0), iota((SPAN, SPAN), 1)
    tril = (row_i >= col_i).astype(BF16)
    log_step = step * par[1:2]
    running = tri_sum(tril, log_step, heads)
    run_rows = jnp.transpose(running)
    ending = running[SPAN - 1 : SPAN]
    tail = jnp.where(dcol == dcol[SPAN - 1 : SPAN], jnp.exp(ending - running), 0.0)
    reach = jnp.where(dcol == enter, jnp.exp(running), 0.0)
    same = jnp.concatenate([dcol, dcol], 1) == drow
    bias = jnp.where(same & (row_i <= col_i), 0.0, FAR)

    def activate(group):
        lanes = slice(group * LANES, (group + 1) * LANES)
        pre = pre_ref[:, lanes]
        sig = jax.nn.sigmoid(pre)
        return pre * sig, sig * (1.0 + pre * (1.0 - sig))

    b_act, b_slope = activate(pairs)
    c_act, c_slope = activate(pairs + 1)
    b_rows, c_rows = b_act.astype(BF16), c_act.astype(BF16)
    c_turned = jnp.transpose(c_act).astype(BF16)
    scores = exact_nt(b_act, c_act)
    low_half = iota((SPAN, LANES), 1) < LANES // 2
    half = SPAN // 2
    d_scores = [jnp.zeros((half, SPAN), F32), jnp.zeros((half, half), F32)]
    d_b = jnp.zeros((SPAN, LANES), F32)
    d_c = jnp.zeros((SPAN, LANES), F32)
    head_up = jnp.zeros((SPAN, LANES), F32)
    head_down = jnp.zeros((SPAN, LANES), F32)
    head_step = jnp.zeros((SPAN, LANES), F32)
    head_hold = jnp.zeros((8, LANES), F32)
    for pair in range(pairs):
        lanes = slice(pair * LANES, (pair + 1) * LANES)
        ones_at = (iota((LANES, LANES), 1) == 2 * pair + iota((LANES, LANES), 0) // (LANES // 2)).astype(BF16)

        def head_sum(v):
            hi = v.astype(BF16)
            low = (v - hi.astype(F32)).astype(BF16)
            return nn(hi, ones_at) + nn(low, ones_at)

        act, slope = activate(pair)
        step_l = pair_lanes(step, pair, low_half)
        tail_l = pair_lanes(tail, pair, low_half)
        reach_l = pair_lanes(reach, pair, low_half)
        skip_l = pair_lanes(par[2:3], pair, low_half[0:1])
        gate = gate_ref[:, lanes]
        sig = jax.nn.sigmoid(gate)
        silu = gate * sig
        ssd = ssd_ref[:, lanes]
        gated = ssd * silu
        dn = dn_ref[:, lanes]
        g_l = gain[0:1, lanes]
        nout = gated * inv
        nout_ref[:, lanes] = (nout * g_l).astype(BF16)
        gchan_ref[0, :, lanes] += fold(dn * nout)
        d_gated = dn * g_l * inv - gated * pull
        d_ssd = d_gated * silu
        dgate_ref[:, lanes] = (d_gated * ssd * (sig * (1.0 + gate * (1.0 - sig)))).astype(BF16)
        gchan_ref[1, :, lanes] += fold(d_ssd * act)
        dyb = d_ssd.astype(BF16)
        scaled = act * step_l
        xb = scaled.astype(BF16)
        held = state_ref[0, :, lanes]
        d_held = dstate[:, lanes]
        d_held_b = d_held.astype(BF16)
        ry = (d_ssd * reach_l).astype(BF16)
        xt = (scaled * tail_l).astype(BF16)
        parts = []
        for sub in range(2):
            head = 2 * pair + sub
            x_own = jnp.where(low_half if sub == 0 else ~low_half, scaled, 0.0).astype(BF16)
            blocks = []
            for blk in range(2):
                rows = slice(blk * half, (blk + 1) * half)
                cols = slice(blk * half, SPAN)
                gap = run_rows[head : head + 1, cols] - running[rows, head : head + 1]
                decay = jnp.exp(gap + bias[rows, cols])
                blocks.append(nn((decay * scores[rows, cols]).astype(BF16), dyb[cols]))
                d_scores[blk] = d_scores[blk] + decay * nt(x_own[rows], dyb[cols])
            parts.append(jnp.concatenate(blocks, 0))
        d_within = jnp.where(low_half, parts[0], parts[1])
        from_state = tail_l * nn(b_rows, d_held_b)
        d_scaled = d_within + from_state
        xf = xb.astype(F32)
        head_up += head_sum(dyb.astype(F32) * (ssd - skip_l * act) - xf * d_within)
        head_down += head_sum(xf * from_state)
        head_step += head_sum(d_scaled * act)
        hold = reach_l[SPAN - 1 : SPAN]
        hold_sum = jnp.sum((d_held * held.astype(F32)).reshape(LANES // 8, 8, LANES), axis=0) * hold
        head_hold += head_sum(hold_sum)
        d_b += nt(xt, d_held_b)
        d_c += nt(ry, held)
        dstate[:, lanes] = hold * d_held + nn(c_turned, ry)
        pbuf[0:SPAN, lanes] = (skip_l * d_ssd + step_l * d_scaled) * slope

    ds_b = jnp.concatenate(
        [
            d_scores[0],
            jnp.concatenate([jnp.zeros((half, half), F32), d_scores[1]], 1),
        ],
        0,
    )
    d_b += nn(ds_b.astype(BF16), c_rows)
    d_c += nn(jnp.transpose(ds_b).astype(BF16), b_rows)
    pbuf[0:SPAN, inner : inner + LANES] = d_b * b_slope
    pbuf[0:SPAN, inner + LANES : chan] = d_c * c_slope

    triu = (row_i <= col_i).astype(BF16)
    below = (row_i > col_i).astype(BF16)
    d_log = (
        tri_sum(triu, head_up, heads)
        + tri_sum(below, head_down, heads)
        + jnp.sum(head_hold, axis=0, keepdims=True)
    )
    d_step = d_log * par[1:2] + head_step
    d_raw = jnp.where(iota((SPAN, LANES), 1) < heads, d_step * jax.nn.sigmoid(raw), 0.0)
    dstp_ref[...] = d_raw.astype(BF16)
    ghead_ref[0] += fold(d_raw)
    ghead_ref[1] += fold(d_log * log_step)

    for group in range(chan // LANES):
        lanes = slice(group * LANES, (group + 1) * LANES)
        mixed = mixed_ref[:, lanes]
        own = pbuf[0:SPAN, lanes]
        acc = cwb[3:4, lanes] * own
        gconv_ref[3, :, lanes] += fold(mixed * own)
        gconv_ref[4, :, lanes] += fold(own)
        for k in range(1, 4):
            later = jnp.where(keeps[k], pbuf[k : k + SPAN, lanes], 0.0)
            acc = acc + cwb[3 - k : 4 - k, lanes] * later
            gconv_ref[3 - k, :, lanes] += fold(mixed * later)
        dmix_ref[:, lanes] = acc.astype(BF16)
    pbuf[SPAN : SPAN + 8] = pbuf[0:8]
    dbuf[SPAN : SPAN + 8] = dbuf[0:8]


def mixer_backward(
    docs, gate, mixed, pre, ssd, stp, states, dn, sums, conv_w, dtb, dec, skip, ggain,
    heads, axis="tensor",
):
    tokens, inner = gate.shape
    chan = inner + 2 * LANES
    spans = tokens // SPAN
    inner_all = ggain.shape[1]

    def tok(width):
        return pl.BlockSpec((SPAN, width), lambda i: (spans - 1 - i, 0))

    def full(shape):
        return pl.BlockSpec(shape, lambda i: (0,) * len(shape))

    outs = (
        jax.ShapeDtypeStruct((tokens, inner), BF16),
        jax.ShapeDtypeStruct((tokens, inner), BF16),
        jax.ShapeDtypeStruct((tokens, chan), BF16),
        jax.ShapeDtypeStruct((tokens, LANES), BF16),
        jax.ShapeDtypeStruct((5, 8, chan), F32),
        jax.ShapeDtypeStruct((2, 8, inner), F32),
        jax.ShapeDtypeStruct((2, 8, LANES), F32),
    )
    consts = (conv_w, dtb, dec, skip, ggain)
    return pl.pallas_call(
        lambda *refs: backward_kernel((inner, heads, inner_all), axis, *refs),
        out_shape=outs,
        grid=(spans,),
        in_specs=[
            full(docs.shape), tok(inner), tok(chan), tok(chan), tok(inner), tok(LANES),
            pl.BlockSpec((1, LANES, inner), lambda i: (spans - 1 - i, 0, 0)),
            tok(inner), full(sums.shape),
        ] + [full(v.shape) for v in consts],
        out_specs=(
            tok(inner), tok(inner), tok(chan), tok(LANES),
            full((5, 8, chan)), full((2, 8, inner)), full((2, 8, LANES)),
        ),
        scratch_shapes=[
            pltpu.VMEM((SPAN + 8, chan), F32),
            pltpu.VMEM((SPAN + 8, LANES), F32),
            pltpu.VMEM((LANES, inner), F32),
            pltpu.VMEM((8, LANES), F32),
            pltpu.VMEM((8, chan), F32),
            pltpu.VMEM((8, inner), F32),
        ],
        compiler_params=pltpu.CompilerParams(
            dimension_semantics=("arbitrary",), vmem_limit_bytes=60 * 2**20
        ),
        name="mixer_backward",
    )(docs, gate, mixed, pre, ssd, stp, states, dn, sums, *consts)


def swap(v, axis, size, to):
    return lax.ppermute(v, axis, [(k, to(k)) for k in range(size)])


def pick(v, index):
    return lax.dynamic_index_in_dim(v, index, 0, keepdims=False)


def body(
    hidden_in, doc_ids, cotangent, norm_gain, in_weight, conv_weight, conv_bias,
    dt_bias, log_decay, skip_gain, gate_gain, out_weight,
):
    tcount, dcount = lax.axis_size("tensor"), lax.axis_size("dp")
    trank, drank = lax.axis_index("tensor"), lax.axis_index("dp")
    lines = dcount // 2
    line, side = drank // 2, drank % 2
    core = trank % 2
    inner_all, head_all = gate_gain.shape[0], dt_bias.shape[0]
    inner, heads = inner_all // tcount, head_all // tcount
    tokens, model = hidden_in.shape
    base_bc = 2 * inner_all
    base_dt = base_bc + 2 * LANES
    depth = in_weight.shape[0]

    own = jnp.concatenate(
        [
            lax.dynamic_slice_in_dim(in_weight, trank * inner, inner, 1),
            lax.dynamic_slice_in_dim(in_weight, inner_all + trank * inner, inner, 1),
            in_weight[:, base_bc:base_dt],
            jnp.pad(
                lax.dynamic_slice_in_dim(in_weight, base_dt + trank * heads, heads, 1),
                ((0, 0), (0, LANES - heads)),
            ),
            out_weight,
        ],
        1,
    )
    width = own.shape[1]

    def line_to(step):
        return lambda k: ((k // 2 + step) % lines) * 2 + k % 2

    def other(k):
        return k ^ 1

    weights = jnp.zeros((dcount, depth, width), BF16)
    for step in range(lines):
        got = own if step == 0 else swap(own, "dp", dcount, line_to(step))
        across = swap(got, "dp", dcount, other)
        source = ((line - step) % lines) * 2
        weights = lax.dynamic_update_slice_in_dim(weights, got[None], source + side, 0)
        weights = lax.dynamic_update_slice_in_dim(weights, across[None], source + 1 - side, 0)
    weights = weights.reshape(model, width)
    cols_in = 2 * inner + 2 * LANES
    w_in, w_step, w_out = weights[:, :cols_in], weights[:, cols_in : cols_in + LANES], weights[:, cols_in + LANES :]

    def row(v):
        return v.reshape(1, -1)

    docs = doc_ids.reshape(tokens // SPAN, SPAN)
    normed, gate, mixed, pre, ssd, stp, states, dn, sums = mixer_forward(
        docs, hidden_in, cotangent, row(norm_gain), w_in, w_step, w_out, conv_weight, row(conv_bias),
        row(dt_bias), row(log_decay), row(skip_gain), row(gate_gain), heads,
    )
    sums = sums + swap(sums, "tensor", tcount, lambda k: k ^ 1)
    sums = sums + swap(sums, "tensor", tcount, lambda k: k ^ 2)
    nout, d_gate, d_mix, d_stp, g_conv, g_chan, g_head = mixer_backward(
        docs, gate, mixed, pre, ssd, stp, states, dn, sums, conv_weight,
        row(dt_bias), row(log_decay), row(skip_gain), row(gate_gain), heads,
    )

    half = tokens // 2

    def tensor_sum(make):
        away = make((1 - core) * half).astype(BF16)
        here = make(core * half)
        got = swap(away, "tensor", tcount, lambda k: k ^ 1)
        mine = (here + got.astype(F32)).astype(BF16)
        theirs = swap(mine, "tensor", tcount, lambda k: k ^ 2)
        return mine.astype(F32) + theirs.astype(F32)

    def both_halves(part):
        got = swap(part, "tensor", tcount, lambda k: k ^ 1)
        low, high = jnp.where(core == 0, part, got), jnp.where(core == 0, got, part)
        return jnp.concatenate([low, high], 0)

    def rows_of(v, start):
        return lax.dynamic_slice_in_dim(v, start, half, 0)

    out_half = tensor_sum(lambda start: nt(rows_of(nout, start), w_out))
    hid_half = rows_of(hidden_in, core * half).astype(F32)
    layer_out = both_halves((hid_half + out_half).astype(BF16))

    d_all = jnp.concatenate([d_gate, d_mix, d_stp], 1)
    w_all = weights[:, : cols_in + LANES]
    d_hidden = tensor_sum(lambda start: nt(rows_of(d_all, start), w_all))
    scaled = d_hidden * norm_gain
    inv_rms = lax.rsqrt(jnp.mean(hid_half * hid_half, -1, keepdims=True) + EPS)
    pull = jnp.mean(scaled * hid_half, -1, keepdims=True)
    delta = inv_rms * scaled - hid_half * inv_rms**3 * pull
    grad_input = cotangent.astype(F32) + both_halves(delta.astype(BF16)).astype(F32)
    g_norm = jnp.sum(d_hidden * hid_half * inv_rms, 0) * (trank < 2).astype(F32)

    def dp_scatter(part):
        part = part.reshape(lines, 2, depth, part.shape[1])
        away = lax.dynamic_index_in_dim(part, 1 - side, 1, keepdims=False).astype(BF16)
        here = lax.dynamic_index_in_dim(part, side, 1, keepdims=False)
        here = here + swap(away, "dp", dcount, other).astype(F32)
        total = pick(here, line)
        low = here.astype(BF16)
        for step in range(1, lines):
            total = total + swap(pick(low, (line + step) % lines), "dp", dcount, line_to(step)).astype(F32)
        return total

    g_out = dp_scatter(tn(cotangent, nout))
    g_in = dp_scatter(tn(normed, d_all))
    g_big = g_in[:, : 2 * inner]
    pair = swap(g_big, "tensor", tcount, lambda k: k ^ 1)
    low, high = jnp.where(core == 0, g_big, pair), jnp.where(core == 0, pair, g_big)
    pairs = jnp.stack([low, high], 0)
    far = swap(pairs, "tensor", tcount, lambda k: k ^ 2)
    first = trank < 2
    quad = jnp.concatenate([jnp.where(first, pairs, far), jnp.where(first, far, pairs)], 0)
    shared = g_in[:, 2 * inner :]
    lane = jnp.arange(LANES) - trank * heads
    step_cols = jnp.where(
        (lane >= 0) & (lane < heads),
        jnp.roll(shared[:, 2 * LANES :], trank * heads, 1), 0.0,
    )
    shared = jnp.concatenate([shared[:, : 2 * LANES], step_cols], 1)
    shared = shared + swap(shared, "tensor", tcount, lambda k: k ^ 1)
    shared = shared + swap(shared, "tensor", tcount, lambda k: k ^ 2)
    grad_in_weight = jnp.concatenate(
        [quad[k, :, :inner] for k in range(tcount)]
        + [quad[k, :, inner:] for k in range(tcount)]
        + [shared[:, : 2 * LANES + head_all]],
        1,
    )

    conv = jnp.sum(g_conv, 1)
    chan = jnp.sum(g_chan, 1)
    head = jnp.sum(g_head, 1)
    skip = jnp.sum(chan[1].reshape(heads, -1), 1)
    spot = trank * inner

    def place(v, total, start):
        return lax.dynamic_update_slice_in_dim(jnp.zeros(v.shape[:-1] + (total,), F32), v, start, v.ndim - 1)

    conv_all = place(conv[:, :inner], inner_all + 2 * LANES, spot).at[:, inner_all:].set(conv[:, inner:])
    heads_all = place(jnp.stack([head[0, :heads], head[1, :heads], skip]), head_all, trank * heads)
    flat = jnp.concatenate(
        [g_norm, conv_all.reshape(-1), heads_all.reshape(-1), place(chan[0], inner_all, spot)]
    )
    flat = jnp.pad(flat, (0, -flat.shape[0] % 1024)).reshape(-1, LANES)
    bit = 1
    while bit < tcount:
        flat = flat + swap(flat, "tensor", tcount, lambda k: k ^ bit)
        bit *= 2
    bit = 1
    while bit < dcount:
        flat = flat + swap(flat, "dp", dcount, lambda k: k ^ bit)
        bit *= 2
    flat = flat.reshape(-1)
    sizes = [model, 5 * conv_all.shape[1], 3 * head_all, inner_all]
    cuts, at = [], 0
    for size in sizes:
        cuts.append(flat[at : at + size])
        at += size
    conv_all = cuts[1].reshape(5, -1)
    heads_all = cuts[2].reshape(3, -1)
    return (
        layer_out, grad_input, cuts[0], grad_in_weight, conv_all[:4], conv_all[4],
        heads_all[0], heads_all[1], heads_all[2], cuts[3], g_out,
    )


def solution(mesh):
    rows, whole = P("dp", None), P()
    return jax.shard_map(
        body,
        mesh=mesh,
        in_specs=(rows, rows, rows, whole, rows, whole, whole, whole, whole, whole, whole, P("dp", "tensor")),
        out_specs=(rows, rows, whole, rows, whole, whole, whole, whole, whole, whole, P("dp", "tensor")),
        check_vma=False,
    )
```

```python
import jax
import jax.numpy as jnp
from jax import lax
from jax.experimental import pallas as pl
from jax.experimental.pallas import tpu as pltpu
from jax.sharding import PartitionSpec as P

SPAN = 256
LANES = 128
EPS = 1e-05
FAR = -1e30
VMEM_MOST = 60 * 2**20
F32 = jnp.float32
BF16 = jnp.bfloat16


def nn(a, b):
    return lax.dot_general(a, b, (((1,), (0,)), ((), ())), preferred_element_type=F32)


def nt(a, b):
    return lax.dot_general(a, b, (((1,), (1,)), ((), ())), preferred_element_type=F32)


def tn(a, b):
    return lax.dot_general(a, b, (((0,), (0,)), ((), ())), preferred_element_type=F32)


def iota(shape, dim):
    return lax.broadcasted_iota(jnp.int32, shape, dim)


def as_column(row, rows=SPAN):
    return jnp.transpose(jnp.broadcast_to(row, (LANES, rows)))


def as_row(block):
    return jnp.sum(jnp.transpose(block), axis=0, keepdims=True)


def split3(v):
    hi = v.astype(BF16)
    rest = v - hi.astype(F32)
    mid = rest.astype(BF16)
    low = (rest - mid.astype(F32)).astype(BF16)
    return hi, mid, low


def tri_sum(tri, v, heads):
    lane = iota(v.shape, 1)
    v = jnp.where(lane < heads, v, 0.0)
    hi = v.astype(BF16).astype(F32)
    rest = v - hi
    mid = rest.astype(BF16).astype(F32)
    low = rest - mid
    packed = hi + pltpu.roll(mid, heads, 1) + pltpu.roll(low, 2 * heads, 1)
    out = nn(tri, packed.astype(BF16))
    return out + pltpu.roll(out, LANES - heads, 1) + pltpu.roll(out, LANES - 2 * heads, 1)


def pair_lanes(cols, pair, low_half):
    rows = cols.shape[0]
    first = jnp.broadcast_to(cols[:, 2 * pair : 2 * pair + 1], (rows, LANES))
    second = jnp.broadcast_to(cols[:, 2 * pair + 1 : 2 * pair + 2], (rows, LANES))
    return jnp.where(low_half, first, second)


def exact_nt(a, b):
    a_hi, b_hi = a.astype(BF16), b.astype(BF16)
    a_lo = (a - a_hi.astype(F32)).astype(BF16)
    b_lo = (b - b_hi.astype(F32)).astype(BF16)
    return nt(a_hi, b_hi) + (nt(a_hi, b_lo) + nt(a_lo, b_hi))


def softplus(v):
    return jnp.maximum(v, 0.0) + jnp.log1p(jnp.exp(-jnp.abs(v)))


def own_lanes(row, rank, heads):
    total = row.shape[1]
    pick = (iota((total, LANES), 0) == rank * heads + iota((total, LANES), 1)) & (
        iota((total, LANES), 1) < heads
    )
    wide = jnp.broadcast_to(row, (8, total))
    out = lax.dot_general(
        wide, pick.astype(F32), (((1,), (0,)), ((), ())),
        precision=lax.Precision.HIGHEST, preferred_element_type=F32,
    )
    return out[0:1]


def fold(v):
    return jnp.sum(v.reshape(SPAN // 8, 8, v.shape[1]), axis=0)


def own_params(rank, heads, inner, inner_all, dtb_ref, dec_ref, skip_ref, cw_ref, cb_ref, par, cwb):
    chan = inner + 2 * LANES
    off = pl.multiple_of(rank * inner, LANES)
    taps = cw_ref.shape[0]
    par[0:1] = own_lanes(dtb_ref[...], rank, heads)
    par[1:2] = -jnp.exp(own_lanes(dec_ref[...], rank, heads))
    par[2:3] = own_lanes(skip_ref[...], rank, heads)
    cwb[0:taps, 0:inner] = cw_ref[:, pl.ds(off, inner)].astype(F32)
    cwb[0:taps, inner:chan] = cw_ref[:, inner_all:].astype(F32)
    cwb[taps : taps + 1, 0:inner] = cb_ref[:, pl.ds(off, inner)]
    cwb[taps : taps + 1, inner:chan] = cb_ref[:, inner_all:]


def forward_kernel(
    dims, axis, base, kept,
    docs_ref, normed_ref, cot_ref, win_ref, wout_ref, cw_ref, cb_ref,
    dtb_ref, dec_ref, skip_ref, ggain_ref, xin_ref, din_ref, sin_ref, *refs,
):
    (
        gate_ref, mixed_ref, pre_ref, ssd_ref, stp_ref, state_ref, dn_ref,
        gg_ref, sums_ref, xout_ref, dout_ref, sout_ref,
        xbuf, dbuf, state, par, cwb, gain,
    ) = refs[kept:]
    inner, heads = dims
    pairs = heads // 2
    chan = inner + 2 * LANES
    step_i = pl.program_id(0)
    i = base + step_i
    rank = lax.axis_index(axis)
    inner_all = ggain_ref.shape[1]

    @pl.when(step_i == 0)
    def _():
        xbuf[0:8] = xin_ref[...]
        dbuf[0:8] = din_ref[...]
        state[...] = sin_ref[...]
        own_params(rank, heads, inner, inner_all, dtb_ref, dec_ref, skip_ref, cw_ref, cb_ref, par, cwb)
        gain[0:1] = ggain_ref[:, pl.ds(pl.multiple_of(rank * inner, LANES), inner)]

    nb = normed_ref[...]
    xbuf[8 : 8 + SPAN] = nn(nb, win_ref[:, inner : inner + chan])
    gate_ref[...] = nn(nb, win_ref[:, 0:inner])
    stp = nn(nb, win_ref[:, inner + chan : inner + chan + LANES])
    stp_ref[...] = stp
    mixed_ref[...] = xbuf[8 : 8 + SPAN]
    dn_ref[...] = nn(cot_ref[...], wout_ref[...])

    drow = docs_ref[pl.ds(i, 1), :].astype(F32)
    dcol = as_column(drow)
    enter = dbuf[7:8]
    dbuf[8 : 8 + SPAN] = dcol
    keeps = [None] + [dbuf[8 - k : 8 - k + SPAN] == dcol for k in range(1, 4)]

    def conv(group):
        lanes = slice(group * LANES, (group + 1) * LANES)
        acc = cwb[4:5, lanes] + cwb[3:4, lanes] * xbuf[8 : 8 + SPAN, lanes]
        for k in range(1, 4):
            acc = acc + cwb[3 - k : 4 - k, lanes] * jnp.where(
                keeps[k], xbuf[8 - k : 8 - k + SPAN, lanes], 0.0
            )
        pre_ref[:, lanes] = acc
        return acc * jax.nn.sigmoid(acc)

    b_act, c_act = conv(pairs), conv(pairs + 1)
    b_rows, c_rows = b_act.astype(BF16), c_act.astype(BF16)

    step = softplus(stp + par[0:1])
    row_i, col_i = iota((SPAN, SPAN), 0), iota((SPAN, SPAN), 1)
    tril = (row_i >= col_i).astype(BF16)
    running = tri_sum(tril, step * par[1:2], heads)
    run_rows = jnp.transpose(running)
    ending = running[SPAN - 1 : SPAN]
    tail = jnp.where(dcol == dcol[SPAN - 1 : SPAN], jnp.exp(ending - running), 0.0)
    reach = jnp.where(dcol == enter, jnp.exp(running), 0.0)
    same = jnp.concatenate([dcol, dcol], 1) == drow
    bias = jnp.where(same & (row_i >= col_i), 0.0, FAR)
    scores = exact_nt(c_act, b_act)
    b_turned = jnp.transpose(b_act).astype(BF16)
    low_half = iota((SPAN, LANES), 1) < LANES // 2
    half = SPAN // 2
    square = jnp.zeros((SPAN, LANES), F32)
    cross = jnp.zeros((SPAN, LANES), F32)
    for pair in range(pairs):
        lanes = slice(pair * LANES, (pair + 1) * LANES)
        act = conv(pair)
        scaled = act * pair_lanes(step, pair, low_half)
        xb = scaled.astype(BF16)
        tail_l = pair_lanes(tail, pair, low_half)
        reach_l = pair_lanes(reach, pair, low_half)
        held = state[:, lanes]
        held_b = held.astype(BF16)
        state_ref[0, :, lanes] = held_b
        state[:, lanes] = nn(b_turned, (scaled * tail_l).astype(BF16)) + reach_l[SPAN - 1 : SPAN] * held
        out = reach_l * nn(c_rows, held_b)
        parts = []
        for sub in range(2):
            head = 2 * pair + sub
            blocks = []
            for blk in range(2):
                rows = slice(blk * half, (blk + 1) * half)
                width = (blk + 1) * half
                gap = running[rows, head : head + 1] - run_rows[head : head + 1, 0:width]
                weight = jnp.exp(gap + bias[rows, 0:width]) * scores[rows, 0:width]
                blocks.append(nn(weight.astype(BF16), xb[0:width]))
            parts.append(jnp.concatenate(blocks, 0))
        out = out + jnp.where(low_half, parts[0], parts[1])
        skip_l = pair_lanes(par[2:3], pair, low_half[0:1])
        ssd = out + skip_l * act
        ssd_ref[:, lanes] = ssd
        gate = gate_ref[:, lanes]
        gated = ssd * (gate * jax.nn.sigmoid(gate))
        square = square + gated * gated
        gained = gain[0:1, lanes] * gated
        gg_ref[:, lanes] = gained.astype(BF16)
        cross = cross + dn_ref[:, lanes] * gained
    sums_ref[0, pl.ds(step_i, 1), :] = as_row(square)
    sums_ref[1, pl.ds(step_i, 1), :] = as_row(cross)
    xbuf[0:8] = xbuf[SPAN : SPAN + 8]
    dbuf[0:8] = dbuf[SPAN : SPAN + 8]
    xout_ref[...] = xbuf[0:8]
    dout_ref[...] = dbuf[0:8]
    sout_ref[...] = state[...]


def mixer_forward(docs, normed, cotangent, w_in, w_out, params, ggain, carry, held, base, count, heads):
    tokens, model = normed.shape
    inner = w_out.shape[1]
    chan = inner + 2 * LANES
    spans = tokens // SPAN

    def tok(width):
        return pl.BlockSpec((SPAN, width), lambda i: (i + base, 0))

    def part(width):
        return pl.BlockSpec((SPAN, width), lambda i: (i, 0))

    def full(arr):
        return pl.BlockSpec(arr.shape, lambda i: (0,) * arr.ndim)

    whole = (
        jax.ShapeDtypeStruct((tokens, inner), F32),
        jax.ShapeDtypeStruct((tokens, chan), F32),
        jax.ShapeDtypeStruct((tokens, chan), F32),
        jax.ShapeDtypeStruct((tokens, inner), F32),
        jax.ShapeDtypeStruct((tokens, LANES), F32),
        jax.ShapeDtypeStruct((spans, LANES, inner), BF16),
        jax.ShapeDtypeStruct((tokens, inner), F32),
    )
    whole_specs = (
        tok(inner), tok(chan), tok(chan), tok(inner), tok(LANES),
        pl.BlockSpec((1, LANES, inner), lambda i: (i + base, 0, 0)),
        tok(inner),
    )
    own = (
        jax.ShapeDtypeStruct((count * SPAN, inner), BF16),
        jax.ShapeDtypeStruct((2, count, SPAN), F32),
        jax.ShapeDtypeStruct((8, chan), F32),
        jax.ShapeDtypeStruct((8, LANES), F32),
        jax.ShapeDtypeStruct((LANES, inner), F32),
    )
    own_specs = (part(inner),) + tuple(full(v) for v in own[1:])
    consts = (w_in, w_out) + params + (ggain,) + carry
    first = 3 + len(consts)
    return pl.pallas_call(
        lambda *refs: forward_kernel((inner, heads), "tensor", base, len(held), *refs),
        out_shape=whole + own,
        grid=(count,),
        in_specs=[full(docs), tok(model), tok(model)]
        + [full(v) for v in consts]
        + [pl.BlockSpec(memory_space=pl.ANY)] * len(held),
        out_specs=whole_specs + own_specs,
        input_output_aliases={first + k: k for k in range(len(held))},
        scratch_shapes=[
            pltpu.VMEM((SPAN + 8, chan), F32),
            pltpu.VMEM((SPAN + 8, LANES), F32),
            pltpu.VMEM((LANES, inner), F32),
            pltpu.VMEM((8, LANES), F32),
            pltpu.VMEM((8, chan), F32),
            pltpu.VMEM((8, inner), F32),
        ],
        compiler_params=pltpu.CompilerParams(
            dimension_semantics=("arbitrary",), vmem_limit_bytes=VMEM_MOST
        ),
        name="mixer_forward",
    )(docs, normed, cotangent, *consts, *held)


def gating_kernel(
    inner_all, axis, gate_ref, ssd_ref, dn_ref, sums_ref, ggain_ref,
    nout_ref, dgate_ref, dssd_ref, ggrad_ref,
):
    c = pl.program_id(0)
    inner = gate_ref.shape[1]
    gain = ggain_ref[:, pl.ds(pl.multiple_of(lax.axis_index(axis) * inner, LANES), inner)]

    @pl.when(c == 0)
    def _():
        ggrad_ref[...] = jnp.zeros(ggrad_ref.shape, F32)

    inv = lax.rsqrt(as_column(sums_ref[0, pl.ds(c, 1), :]) * (1.0 / inner_all) + EPS)
    pull = as_column(sums_ref[1, pl.ds(c, 1), :]) * (inv * inv * inv) * (1.0 / inner_all)
    for group in range(inner // LANES):
        lanes = slice(group * LANES, (group + 1) * LANES)
        gate = gate_ref[:, lanes]
        sig = jax.nn.sigmoid(gate)
        silu = gate * sig
        ssd = ssd_ref[:, lanes]
        gated = ssd * silu
        dn = dn_ref[:, lanes]
        g_l = gain[:, lanes]
        nout = gated * inv
        nout_ref[:, lanes] = (nout * g_l).astype(BF16)
        ggrad_ref[:, lanes] += fold(dn * nout)
        d_gated = dn * g_l * inv - gated * pull
        dssd_ref[:, lanes] = d_gated * silu
        dgate_ref[:, lanes] = (d_gated * ssd * (sig * (1.0 + gate * (1.0 - sig)))).astype(BF16)


def gating(gate, ssd, dn, sums, ggain):
    tokens, inner = gate.shape

    def full(shape):
        return pl.BlockSpec(shape, lambda i: (0,) * len(shape))

    tok = pl.BlockSpec((SPAN, inner), lambda i: (i, 0))
    return pl.pallas_call(
        lambda *refs: gating_kernel(ggain.shape[1], "tensor", *refs),
        out_shape=(
            jax.ShapeDtypeStruct((tokens, inner), BF16),
            jax.ShapeDtypeStruct((tokens, inner), BF16),
            jax.ShapeDtypeStruct((tokens, inner), F32),
            jax.ShapeDtypeStruct((8, inner), F32),
        ),
        grid=(tokens // SPAN,),
        in_specs=[tok, tok, tok, full(sums.shape), full(ggain.shape)],
        out_specs=(tok, tok, tok, full((8, inner))),
        compiler_params=pltpu.CompilerParams(dimension_semantics=("arbitrary",)),
        name="gating",
    )(gate, ssd, dn, sums, ggain)


def backward_kernel(
    dims, axis, base, count,
    docs_ref, mixed_ref, pre_ref, ssd_ref, stp_ref, state_ref, dssd_ref, dgate_ref,
    cw_ref, cb_ref, dtb_ref, dec_ref, skip_ref, pin_ref, din_ref, sin_ref,
    dall_ref, gconv_ref, gskip_ref, ghead_ref, pout_ref, dout_ref, sout_ref,
    pbuf, dbuf, dstate, par, cwb,
):
    inner, heads, inner_all = dims
    pairs = heads // 2
    chan = inner + 2 * LANES
    i = pl.program_id(0)
    c = base + count - 1 - i
    rank = lax.axis_index(axis)

    @pl.when(i == 0)
    def _():
        pbuf[SPAN : SPAN + 8] = pin_ref[...]
        dbuf[SPAN : SPAN + 8] = din_ref[...]
        dstate[...] = sin_ref[...]
        own_params(rank, heads, inner, inner_all, dtb_ref, dec_ref, skip_ref, cw_ref, cb_ref, par, cwb)
        gconv_ref[...] = jnp.zeros(gconv_ref.shape, F32)
        gskip_ref[...] = jnp.zeros(gskip_ref.shape, F32)
        ghead_ref[...] = jnp.zeros(ghead_ref.shape, F32)

    dall_ref[:, 0:inner] = dgate_ref[...]
    drow = docs_ref[pl.ds(c, 1), :].astype(F32)
    dcol = as_column(drow)
    before = docs_ref[pl.ds(jnp.maximum(c - 1, 0), 1), :].astype(F32)
    enter = as_column(before)[SPAN - 1 : SPAN]
    enter = jnp.where(c == 0, -1.0, enter)
    dbuf[0:SPAN] = dcol
    keeps = [None] + [dbuf[k : k + SPAN] == dcol for k in range(1, 4)]

    raw = stp_ref[...] + par[0:1]
    step = softplus(raw)
    row_i, col_i = iota((SPAN, SPAN), 0), iota((SPAN, SPAN), 1)
    tril = (row_i >= col_i).astype(BF16)
    log_step = step * par[1:2]
    running = tri_sum(tril, log_step, heads)
    run_rows = jnp.transpose(running)
    ending = running[SPAN - 1 : SPAN]
    tail = jnp.where(dcol == dcol[SPAN - 1 : SPAN], jnp.exp(ending - running), 0.0)
    reach = jnp.where(dcol == enter, jnp.exp(running), 0.0)
    same = jnp.concatenate([dcol, dcol], 1) == drow
    bias = jnp.where(same & (row_i <= col_i), 0.0, FAR)

    def activate(group):
        lanes = slice(group * LANES, (group + 1) * LANES)
        pre = pre_ref[:, lanes]
        sig = jax.nn.sigmoid(pre)
        return pre * sig, sig * (1.0 + pre * (1.0 - sig))

    b_act, b_slope = activate(pairs)
    c_act, c_slope = activate(pairs + 1)
    b_rows, c_rows = b_act.astype(BF16), c_act.astype(BF16)
    c_turned = jnp.transpose(c_act).astype(BF16)
    scores = exact_nt(b_act, c_act)
    low_half = iota((SPAN, LANES), 1) < LANES // 2
    half = SPAN // 2
    d_scores = [jnp.zeros((half, SPAN), F32), jnp.zeros((half, half), F32)]
    d_b = jnp.zeros((SPAN, LANES), F32)
    d_c = jnp.zeros((SPAN, LANES), F32)
    head_up = jnp.zeros((SPAN, LANES), F32)
    head_down = jnp.zeros((SPAN, LANES), F32)
    head_step = jnp.zeros((SPAN, LANES), F32)
    head_hold = jnp.zeros((8, LANES), F32)
    for pair in range(pairs):
        lanes = slice(pair * LANES, (pair + 1) * LANES)
        ones_at = (iota((LANES, LANES), 1) == 2 * pair + iota((LANES, LANES), 0) // (LANES // 2)).astype(BF16)

        def head_sum(v):
            hi = v.astype(BF16)
            low = (v - hi.astype(F32)).astype(BF16)
            return nn(hi, ones_at) + nn(low, ones_at)

        act, slope = activate(pair)
        step_l = pair_lanes(step, pair, low_half)
        tail_l = pair_lanes(tail, pair, low_half)
        reach_l = pair_lanes(reach, pair, low_half)
        skip_l = pair_lanes(par[2:3], pair, low_half[0:1])
        ssd = ssd_ref[:, lanes]
        d_ssd = dssd_ref[:, lanes]
        gskip_ref[:, lanes] += fold(d_ssd * act)
        dyb = d_ssd.astype(BF16)
        scaled = act * step_l
        xb = scaled.astype(BF16)
        held = state_ref[0, :, lanes]
        d_held = dstate[:, lanes]
        d_held_b = d_held.astype(BF16)
        ry = (d_ssd * reach_l).astype(BF16)
        xt = (scaled * tail_l).astype(BF16)
        parts = []
        for sub in range(2):
            head = 2 * pair + sub
            x_own = jnp.where(low_half if sub == 0 else ~low_half, scaled, 0.0).astype(BF16)
            blocks = []
            for blk in range(2):
                rows = slice(blk * half, (blk + 1) * half)
                cols = slice(blk * half, SPAN)
                gap = run_rows[head : head + 1, cols] - running[rows, head : head + 1]
                decay = jnp.exp(gap + bias[rows, cols])
                blocks.append(nn((decay * scores[rows, cols]).astype(BF16), dyb[cols]))
                d_scores[blk] = d_scores[blk] + decay * nt(x_own[rows], dyb[cols])
            parts.append(jnp.concatenate(blocks, 0))
        d_within = jnp.where(low_half, parts[0], parts[1])
        from_state = tail_l * nn(b_rows, d_held_b)
        d_scaled = d_within + from_state
        xf = xb.astype(F32)
        head_up += head_sum(dyb.astype(F32) * (ssd - skip_l * act) - xf * d_within)
        head_down += head_sum(xf * from_state)
        head_step += head_sum(d_scaled * act)
        hold = reach_l[SPAN - 1 : SPAN]
        hold_sum = jnp.sum((d_held * held.astype(F32)).reshape(LANES // 8, 8, LANES), axis=0) * hold
        head_hold += head_sum(hold_sum)
        d_b += nt(xt, d_held_b)
        d_c += nt(ry, held)
        dstate[:, lanes] = hold * d_held + nn(c_turned, ry)
        pbuf[0:SPAN, lanes] = (skip_l * d_ssd + step_l * d_scaled) * slope

    ds_b = jnp.concatenate(
        [
            d_scores[0],
            jnp.concatenate([jnp.zeros((half, half), F32), d_scores[1]], 1),
        ],
        0,
    )
    d_b += nn(ds_b.astype(BF16), c_rows)
    d_c += nn(jnp.transpose(ds_b).astype(BF16), b_rows)
    pbuf[0:SPAN, inner : inner + LANES] = d_b * b_slope
    pbuf[0:SPAN, inner + LANES : chan] = d_c * c_slope

    triu = (row_i <= col_i).astype(BF16)
    below = (row_i > col_i).astype(BF16)
    d_log = (
        tri_sum(triu, head_up, heads)
        + tri_sum(below, head_down, heads)
        + jnp.sum(head_hold, axis=0, keepdims=True)
    )
    d_step = d_log * par[1:2] + head_step
    d_raw = jnp.where(iota((SPAN, LANES), 1) < heads, d_step * jax.nn.sigmoid(raw), 0.0)
    dall_ref[:, inner + chan :] = d_raw.astype(BF16)
    ghead_ref[0] += fold(d_raw)
    ghead_ref[1] += fold(d_log * log_step)

    for group in range(chan // LANES):
        lanes = slice(group * LANES, (group + 1) * LANES)
        mixed = mixed_ref[:, lanes]
        own = pbuf[0:SPAN, lanes]
        acc = cwb[3:4, lanes] * own
        gconv_ref[3, :, lanes] += fold(mixed * own)
        gconv_ref[4, :, lanes] += fold(own)
        for k in range(1, 4):
            later = jnp.where(keeps[k], pbuf[k : k + SPAN, lanes], 0.0)
            acc = acc + cwb[3 - k : 4 - k, lanes] * later
            gconv_ref[3 - k, :, lanes] += fold(mixed * later)
        dall_ref[:, inner + group * LANES : inner + (group + 1) * LANES] = acc.astype(BF16)
    pbuf[SPAN : SPAN + 8] = pbuf[0:8]
    dbuf[SPAN : SPAN + 8] = dbuf[0:8]
    pout_ref[...] = pbuf[0:8]
    dout_ref[...] = dbuf[0:8]
    sout_ref[...] = dstate[...]


def mixer_backward(docs, arrays, params, carry, base, count, heads, inner_all):
    mixed, pre, ssd, stp, states, dssd, dgate = arrays
    tokens, inner = ssd.shape
    chan = inner + 2 * LANES
    width = inner + chan + LANES

    def tok(wide):
        return pl.BlockSpec((SPAN, wide), lambda i: (base + count - 1 - i, 0))

    def full(shape):
        return pl.BlockSpec(shape, lambda i: (0,) * len(shape))

    outs = (
        jax.ShapeDtypeStruct((count * SPAN, width), BF16),
        jax.ShapeDtypeStruct((5, 8, chan), F32),
        jax.ShapeDtypeStruct((8, inner), F32),
        jax.ShapeDtypeStruct((2, 8, LANES), F32),
        jax.ShapeDtypeStruct((8, chan), F32),
        jax.ShapeDtypeStruct((8, LANES), F32),
        jax.ShapeDtypeStruct((LANES, inner), F32),
    )
    consts = params + carry
    return pl.pallas_call(
        lambda *refs: backward_kernel((inner, heads, inner_all), "tensor", base, count, *refs),
        out_shape=outs,
        grid=(count,),
        in_specs=[
            full(docs.shape), tok(chan), tok(chan), tok(inner), tok(LANES),
            pl.BlockSpec((1, LANES, inner), lambda i: (base + count - 1 - i, 0, 0)),
            tok(inner), tok(inner),
        ]
        + [full(v.shape) for v in consts],
        out_specs=(pl.BlockSpec((SPAN, width), lambda i: (count - 1 - i, 0)),)
        + tuple(full(v.shape) for v in outs[1:]),
        scratch_shapes=[
            pltpu.VMEM((SPAN + 8, chan), F32),
            pltpu.VMEM((SPAN + 8, LANES), F32),
            pltpu.VMEM((LANES, inner), F32),
            pltpu.VMEM((8, LANES), F32),
            pltpu.VMEM((8, chan), F32),
        ],
        compiler_params=pltpu.CompilerParams(
            dimension_semantics=("arbitrary",), vmem_limit_bytes=VMEM_MOST
        ),
        name="mixer_backward",
    )(docs, mixed, pre, ssd, stp, states, dssd, dgate, *consts)


def swap(v, axis, to):
    return lax.ppermute(v, axis, [(k, to(k)) for k in range(lax.axis_size(axis))])


def flip(bits):
    return lambda k: k ^ bits


def body(
    hidden_in, doc_ids, cotangent, norm_gain, in_weight, conv_weight, conv_bias,
    dt_bias, log_decay, skip_gain, gate_gain, out_weight,
):
    tcount, dcount = lax.axis_size("tensor"), lax.axis_size("dp")
    trank, drank = lax.axis_index("tensor"), lax.axis_index("dp")
    lines = dcount // 2
    line, side = drank // 2, drank % 2
    core = trank % 2
    inner_all, head_all = gate_gain.shape[0], dt_bias.shape[0]
    inner, heads = inner_all // tcount, head_all // tcount
    tokens, model = hidden_in.shape
    base_bc = 2 * inner_all
    base_dt = base_bc + 2 * LANES
    depth = in_weight.shape[0]
    chan = inner + 2 * LANES

    def line_to(step):
        return lambda k: ((k // 2 + step) % lines) * 2 + k % 2

    def gather(own):
        width = own.shape[1]
        held = jnp.zeros((dcount, depth, width), BF16)
        for step in range(lines):
            got = own if step == 0 else swap(own, "dp", line_to(step))
            across = swap(got, "dp", flip(1))
            source = ((line - step) % lines) * 2
            held = lax.dynamic_update_slice_in_dim(held, got[None], source + side, 0)
            held = lax.dynamic_update_slice_in_dim(held, across[None], source + 1 - side, 0)
        return held.reshape(model, width)

    w_in = gather(
        jnp.concatenate(
            [
                lax.dynamic_slice_in_dim(in_weight, trank * inner, inner, 1),
                lax.dynamic_slice_in_dim(in_weight, inner_all + trank * inner, inner, 1),
                in_weight[:, base_bc:base_dt],
                jnp.pad(
                    lax.dynamic_slice_in_dim(in_weight, base_dt + trank * heads, heads, 1),
                    ((0, 0), (0, LANES - heads)),
                ),
            ],
            1,
        )
    )
    w_out = gather(out_weight)

    hidden = hidden_in.astype(F32)
    inv_rms = lax.rsqrt(jnp.mean(hidden * hidden, -1, keepdims=True) + EPS)
    normed = (hidden * inv_rms * norm_gain).astype(BF16)

    def features(v, which):
        return jnp.concatenate(
            [
                lax.dynamic_slice_in_dim(v, (((line + j) % lines) * 2 + which) * depth, depth, 1)
                for j in range(lines)
            ],
            1,
        )

    n_away, n_here = features(normed, 1 - side), features(normed, side)
    c_away, c_here = features(cotangent, 1 - side), features(cotangent, side)

    def row(v):
        return v.reshape(1, -1)

    docs = doc_ids.reshape(tokens // SPAN, SPAN)
    spans = tokens // SPAN
    count = spans // 2
    span_rows = count * SPAN
    part = span_rows // 2
    params = (conv_weight, row(conv_bias), row(dt_bias), row(log_decay), row(skip_gain))

    def tensor_sum(left, right):
        def make(start):
            return nt(lax.dynamic_slice_in_dim(left, start, part, 0), right)

        away = make((1 - core) * part).astype(BF16)
        got = swap(away, "tensor", flip(1))
        mine = (make(core * part) + got.astype(F32)).astype(BF16)
        theirs = swap(mine, "tensor", flip(2))
        return mine.astype(F32) + theirs.astype(F32)

    def both(own):
        got = swap(own, "tensor", flip(1))
        return [jnp.where(core == 0, own, got), jnp.where(core == 0, got, own)]

    def my_rows(v, h):
        return lax.dynamic_slice_in_dim(v, h * span_rows + core * part, part, 0)

    carry = (
        jnp.zeros((8, chan), F32), jnp.full((8, LANES), -1.0, F32), jnp.zeros((LANES, inner), F32),
    )
    held, sums, outs = (), [], []
    for h in range(2):
        made = mixer_forward(
            docs, normed, cotangent, w_in, w_out, params, row(gate_gain), carry, held,
            h * count, count, heads,
        )
        held, carry = made[:7], made[9:]
        outs.append(tensor_sum(made[7], w_out))
        sums.append(made[8])
    sums = jnp.concatenate(sums, 1)
    sums = sums + swap(sums, "tensor", flip(1))
    sums = sums + swap(sums, "tensor", flip(2))
    gate, mixed, pre, ssd, stp, states, dn = held
    nout, d_gate, d_ssd, g_gain = gating(gate, ssd, dn, sums, row(gate_gain))

    inv_gate = lax.rsqrt(sums[0].reshape(tokens, 1) * (1.0 / inner_all) + EPS)
    layer_out = []
    for h in range(2):
        layer_out += both((my_rows(hidden, h) + outs[h] * my_rows(inv_gate, h)).astype(BF16))
    layer_out = jnp.concatenate(layer_out, 0)

    def dp_scatter(away, here):
        here = here + swap(away.astype(BF16), "dp", flip(1)).astype(F32)
        total = here[:depth]
        for j in range(1, lines):
            total = total + swap(
                here[j * depth : (j + 1) * depth].astype(BF16), "dp", line_to(j)
            ).astype(F32)
        return total

    g_out = dp_scatter(tn(c_away, nout), tn(c_here, nout))
    g_gate = dp_scatter(tn(n_away, d_gate), tn(n_here, d_gate))

    carry = (
        jnp.zeros((8, chan), F32), jnp.full((8, LANES), -2.0, F32), jnp.zeros((LANES, inner), F32),
    )
    g_conv = g_skip = g_head = 0.0
    away = here = 0.0
    g_norm = 0.0
    halves = [None, None]
    for h in (1, 0):
        d_all, conv_h, skip_h, head_h, *carry = mixer_backward(
            docs, (mixed, pre, ssd, stp, states, d_ssd, d_gate), params, tuple(carry),
            h * count, count, heads, inner_all,
        )
        g_conv, g_skip, g_head = g_conv + conv_h, g_skip + skip_h, g_head + head_h
        d_hidden = tensor_sum(d_all, w_in)
        hid, inv = my_rows(hidden, h), my_rows(inv_rms, h)
        scaled = d_hidden * norm_gain
        pull = jnp.mean(scaled * hid, -1, keepdims=True)
        halves[h] = both((inv * scaled - hid * inv**3 * pull).astype(BF16))
        g_norm = g_norm + jnp.sum(d_hidden * hid * inv, 0)
        rows = slice(h * span_rows, (h + 1) * span_rows)
        away = away + tn(n_away[rows], d_all[:, inner:])
        here = here + tn(n_here[rows], d_all[:, inner:])
    grad_input = cotangent.astype(F32) + jnp.concatenate(halves[0] + halves[1], 0).astype(F32)
    g_norm = g_norm * (trank < 2).astype(F32)

    g_value = dp_scatter(away[:, :inner], here[:, :inner])
    shared = dp_scatter(away[:, inner:], here[:, inner:])

    def all_heads(v):
        pair = swap(v, "tensor", flip(1))
        low, high = jnp.where(core == 0, v, pair), jnp.where(core == 0, pair, v)
        pairs = jnp.concatenate([low, high], 1)
        far = swap(pairs, "tensor", flip(2))
        first = trank < 2
        return [jnp.where(first, pairs, far), jnp.where(first, far, pairs)]

    lane = jnp.arange(LANES) - trank * heads
    shared = jnp.concatenate(
        [
            shared[:, : 2 * LANES],
            jnp.where(
                (lane >= 0) & (lane < heads), jnp.roll(shared[:, 2 * LANES :], trank * heads, 1), 0.0
            ),
        ],
        1,
    )
    shared = shared + swap(shared, "tensor", flip(1))
    shared = shared + swap(shared, "tensor", flip(2))
    grad_in_weight = jnp.concatenate(
        all_heads(g_gate) + all_heads(g_value) + [shared[:, : 2 * LANES + head_all]], 1
    )

    conv = jnp.sum(g_conv, 1)
    head = jnp.sum(g_head, 1)
    skip = jnp.sum(jnp.sum(g_skip, 0).reshape(heads, -1), 1)
    spot = trank * inner

    def place(v, total, start):
        return lax.dynamic_update_slice_in_dim(
            jnp.zeros(v.shape[:-1] + (total,), F32), v, start, v.ndim - 1
        )

    conv_all = place(conv[:, :inner], inner_all + 2 * LANES, spot).at[:, inner_all:].set(conv[:, inner:])
    heads_all = place(jnp.stack([head[0, :heads], head[1, :heads], skip]), head_all, trank * heads)
    flat = jnp.concatenate(
        [g_norm, conv_all.reshape(-1), heads_all.reshape(-1), place(jnp.sum(g_gain, 0), inner_all, spot)]
    )
    flat = jnp.pad(flat, (0, -flat.shape[0] % 1024)).reshape(-1, LANES)
    for axis, size in (("tensor", tcount), ("dp", dcount)):
        bit = 1
        while bit < size:
            flat = flat + swap(flat, axis, flip(bit))
            bit *= 2
    flat = flat.reshape(-1)
    cuts, at = [], 0
    for size in (model, 5 * conv_all.shape[1], 3 * head_all, inner_all):
        cuts.append(flat[at : at + size])
        at += size
    conv_all = cuts[1].reshape(5, -1)
    heads_all = cuts[2].reshape(3, -1)
    return (
        layer_out, grad_input, cuts[0], grad_in_weight, conv_all[:4], conv_all[4],
        heads_all[0], heads_all[1], heads_all[2], cuts[3], g_out,
    )


def solution(mesh):
    rows, whole = P("dp", None), P()
    return jax.shard_map(
        body,
        mesh=mesh,
        in_specs=(rows, rows, rows, whole, rows, whole, whole, whole, whole, whole, whole, P("dp", "tensor")),
        out_specs=(rows, rows, whole, rows, whole, whole, whole, whole, whole, whole, P("dp", "tensor")),
        check_vma=False,
    )
```

```python
import jax
import jax.numpy as jnp
from jax import lax
from jax.experimental import pallas as pl
from jax.experimental.pallas import tpu as pltpu
from jax.sharding import PartitionSpec as P

SPAN = 256
LANES = 128
EPS = 1e-05
FAR = -1e30
VMEM_MOST = 60 * 2**20
F32 = jnp.float32
BF16 = jnp.bfloat16


def cost(micros):
    return pl.CostEstimate(flops=int(micros * 1.15e9), bytes_accessed=1 << 20, transcendentals=0)


def nn(a, b):
    return lax.dot_general(a, b, (((1,), (0,)), ((), ())), preferred_element_type=F32)


def nt(a, b):
    return lax.dot_general(a, b, (((1,), (1,)), ((), ())), preferred_element_type=F32)


def tn(a, b):
    return lax.dot_general(a, b, (((0,), (0,)), ((), ())), preferred_element_type=F32)


def iota(shape, dim):
    return lax.broadcasted_iota(jnp.int32, shape, dim)


def as_column(row, rows=SPAN):
    return jnp.transpose(jnp.broadcast_to(row, (LANES, rows)))


def as_row(block):
    return jnp.sum(jnp.transpose(block), axis=0, keepdims=True)


def split3(v):
    hi = v.astype(BF16)
    rest = v - hi.astype(F32)
    mid = rest.astype(BF16)
    low = (rest - mid.astype(F32)).astype(BF16)
    return hi, mid, low


def tri_sum(tri, v, heads):
    lane = iota(v.shape, 1)
    v = jnp.where(lane < heads, v, 0.0)
    hi = v.astype(BF16).astype(F32)
    rest = v - hi
    mid = rest.astype(BF16).astype(F32)
    low = rest - mid
    packed = hi + pltpu.roll(mid, heads, 1) + pltpu.roll(low, 2 * heads, 1)
    out = nn(tri, packed.astype(BF16))
    return out + pltpu.roll(out, LANES - heads, 1) + pltpu.roll(out, LANES - 2 * heads, 1)


def pair_lanes(cols, pair, low_half):
    rows = cols.shape[0]
    first = jnp.broadcast_to(cols[:, 2 * pair : 2 * pair + 1], (rows, LANES))
    second = jnp.broadcast_to(cols[:, 2 * pair + 1 : 2 * pair + 2], (rows, LANES))
    return jnp.where(low_half, first, second)


def exact_nt(a, b):
    a_hi, b_hi = a.astype(BF16), b.astype(BF16)
    a_lo = (a - a_hi.astype(F32)).astype(BF16)
    b_lo = (b - b_hi.astype(F32)).astype(BF16)
    return nt(a_hi, b_hi) + (nt(a_hi, b_lo) + nt(a_lo, b_hi))


def softplus(v):
    return jnp.maximum(v, 0.0) + jnp.log1p(jnp.exp(-jnp.abs(v)))


def own_lanes(row, rank, heads):
    total = row.shape[1]
    pick = (iota((total, LANES), 0) == rank * heads + iota((total, LANES), 1)) & (
        iota((total, LANES), 1) < heads
    )
    wide = jnp.broadcast_to(row, (8, total))
    out = lax.dot_general(
        wide, pick.astype(F32), (((1,), (0,)), ((), ())),
        precision=lax.Precision.HIGHEST, preferred_element_type=F32,
    )
    return out[0:1]


def fold(v):
    return jnp.sum(v.reshape(SPAN // 8, 8, v.shape[1]), axis=0)


def own_params(rank, heads, inner, inner_all, dtb_ref, dec_ref, skip_ref, cw_ref, cb_ref, par, cwb):
    chan = inner + 2 * LANES
    off = pl.multiple_of(rank * inner, LANES)
    taps = cw_ref.shape[0]
    par[0:1] = own_lanes(dtb_ref[...], rank, heads)
    par[1:2] = -jnp.exp(own_lanes(dec_ref[...], rank, heads))
    par[2:3] = own_lanes(skip_ref[...], rank, heads)
    cwb[0:taps, 0:inner] = cw_ref[:, pl.ds(off, inner)].astype(F32)
    cwb[0:taps, inner:chan] = cw_ref[:, inner_all:].astype(F32)
    cwb[taps : taps + 1, 0:inner] = cb_ref[:, pl.ds(off, inner)]
    cwb[taps : taps + 1, inner:chan] = cb_ref[:, inner_all:]


def forward_kernel(
    dims, axis, base, kept,
    docs_ref, normed_ref, cot_ref, win_ref, wout_ref, cw_ref, cb_ref,
    dtb_ref, dec_ref, skip_ref, ggain_ref, xin_ref, din_ref, sin_ref, *refs,
):
    (
        gate_ref, mixed_ref, pre_ref, ssd_ref, stp_ref, state_ref, dn_ref,
        gg_ref, sums_ref, xout_ref, dout_ref, sout_ref,
        xbuf, dbuf, state, par, cwb, gain,
    ) = refs[kept:]
    inner, heads = dims
    pairs = heads // 2
    chan = inner + 2 * LANES
    step_i = pl.program_id(0)
    i = base + step_i
    rank = lax.axis_index(axis)
    inner_all = ggain_ref.shape[1]

    @pl.when(step_i == 0)
    def _():
        xbuf[0:8] = xin_ref[...]
        dbuf[0:8] = din_ref[...]
        state[...] = sin_ref[...]
        own_params(rank, heads, inner, inner_all, dtb_ref, dec_ref, skip_ref, cw_ref, cb_ref, par, cwb)
        gain[0:1] = ggain_ref[:, pl.ds(pl.multiple_of(rank * inner, LANES), inner)]

    nb = normed_ref[...]
    xbuf[8 : 8 + SPAN] = nn(nb, win_ref[:, inner : inner + chan])
    gate_ref[...] = nn(nb, win_ref[:, 0:inner])
    stp = nn(nb, win_ref[:, inner + chan : inner + chan + LANES])
    stp_ref[...] = stp
    mixed_ref[...] = xbuf[8 : 8 + SPAN]
    dn_ref[...] = nn(cot_ref[...], wout_ref[...])

    drow = docs_ref[pl.ds(i, 1), :].astype(F32)
    dcol = as_column(drow)
    enter = dbuf[7:8]
    dbuf[8 : 8 + SPAN] = dcol
    keeps = [None] + [dbuf[8 - k : 8 - k + SPAN] == dcol for k in range(1, 4)]

    def conv(group):
        lanes = slice(group * LANES, (group + 1) * LANES)
        acc = cwb[4:5, lanes] + cwb[3:4, lanes] * xbuf[8 : 8 + SPAN, lanes]
        for k in range(1, 4):
            acc = acc + cwb[3 - k : 4 - k, lanes] * jnp.where(
                keeps[k], xbuf[8 - k : 8 - k + SPAN, lanes], 0.0
            )
        pre_ref[:, lanes] = acc
        return acc * jax.nn.sigmoid(acc)

    b_act, c_act = conv(pairs), conv(pairs + 1)
    b_rows, c_rows = b_act.astype(BF16), c_act.astype(BF16)

    step = softplus(stp + par[0:1])
    row_i, col_i = iota((SPAN, SPAN), 0), iota((SPAN, SPAN), 1)
    tril = (row_i >= col_i).astype(BF16)
    running = tri_sum(tril, step * par[1:2], heads)
    run_rows = jnp.transpose(running)
    ending = running[SPAN - 1 : SPAN]
    tail = jnp.where(dcol == dcol[SPAN - 1 : SPAN], jnp.exp(ending - running), 0.0)
    reach = jnp.where(dcol == enter, jnp.exp(running), 0.0)
    same = jnp.concatenate([dcol, dcol], 1) == drow
    bias = jnp.where(same & (row_i >= col_i), 0.0, FAR)
    scores = exact_nt(c_act, b_act)
    b_turned = jnp.transpose(b_act).astype(BF16)
    low_half = iota((SPAN, LANES), 1) < LANES // 2
    half = SPAN // 2
    square = jnp.zeros((SPAN, LANES), F32)
    cross = jnp.zeros((SPAN, LANES), F32)
    for pair in range(pairs):
        lanes = slice(pair * LANES, (pair + 1) * LANES)
        act = conv(pair)
        scaled = act * pair_lanes(step, pair, low_half)
        xb = scaled.astype(BF16)
        tail_l = pair_lanes(tail, pair, low_half)
        reach_l = pair_lanes(reach, pair, low_half)
        held = state[:, lanes]
        held_b = held.astype(BF16)
        state_ref[0, :, lanes] = held_b
        state[:, lanes] = nn(b_turned, (scaled * tail_l).astype(BF16)) + reach_l[SPAN - 1 : SPAN] * held
        out = reach_l * nn(c_rows, held_b)
        parts = []
        for sub in range(2):
            head = 2 * pair + sub
            blocks = []
            for blk in range(2):
                rows = slice(blk * half, (blk + 1) * half)
                width = (blk + 1) * half
                gap = running[rows, head : head + 1] - run_rows[head : head + 1, 0:width]
                weight = jnp.exp(gap + bias[rows, 0:width]) * scores[rows, 0:width]
                blocks.append(nn(weight.astype(BF16), xb[0:width]))
            parts.append(jnp.concatenate(blocks, 0))
        out = out + jnp.where(low_half, parts[0], parts[1])
        skip_l = pair_lanes(par[2:3], pair, low_half[0:1])
        ssd = out + skip_l * act
        ssd_ref[:, lanes] = ssd
        gate = gate_ref[:, lanes]
        gated = ssd * (gate * jax.nn.sigmoid(gate))
        square = square + gated * gated
        gained = gain[0:1, lanes] * gated
        gg_ref[:, lanes] = gained.astype(BF16)
        cross = cross + dn_ref[:, lanes] * gained
    sums_ref[0, pl.ds(step_i, 1), :] = as_row(square)
    sums_ref[1, pl.ds(step_i, 1), :] = as_row(cross)
    xbuf[0:8] = xbuf[SPAN : SPAN + 8]
    dbuf[0:8] = dbuf[SPAN : SPAN + 8]
    xout_ref[...] = xbuf[0:8]
    dout_ref[...] = dbuf[0:8]
    sout_ref[...] = state[...]


def mixer_forward(docs, normed, cotangent, w_in, w_out, params, ggain, carry, held, base, count, heads):
    tokens, model = normed.shape
    inner = w_out.shape[1]
    chan = inner + 2 * LANES
    spans = tokens // SPAN

    def tok(width):
        return pl.BlockSpec((SPAN, width), lambda i: (i + base, 0))

    def part(width):
        return pl.BlockSpec((SPAN, width), lambda i: (i, 0))

    def full(arr):
        return pl.BlockSpec(arr.shape, lambda i: (0,) * arr.ndim)

    whole = (
        jax.ShapeDtypeStruct((tokens, inner), F32),
        jax.ShapeDtypeStruct((tokens, chan), F32),
        jax.ShapeDtypeStruct((tokens, chan), F32),
        jax.ShapeDtypeStruct((tokens, inner), F32),
        jax.ShapeDtypeStruct((tokens, LANES), F32),
        jax.ShapeDtypeStruct((spans, LANES, inner), BF16),
        jax.ShapeDtypeStruct((tokens, inner), F32),
    )
    whole_specs = (
        tok(inner), tok(chan), tok(chan), tok(inner), tok(LANES),
        pl.BlockSpec((1, LANES, inner), lambda i: (i + base, 0, 0)),
        tok(inner),
    )
    own = (
        jax.ShapeDtypeStruct((count * SPAN, inner), BF16),
        jax.ShapeDtypeStruct((2, count, SPAN), F32),
        jax.ShapeDtypeStruct((8, chan), F32),
        jax.ShapeDtypeStruct((8, LANES), F32),
        jax.ShapeDtypeStruct((LANES, inner), F32),
    )
    own_specs = (part(inner),) + tuple(full(v) for v in own[1:])
    consts = (w_in, w_out) + params + (ggain,) + carry
    first = 3 + len(consts)
    return pl.pallas_call(
        lambda *refs: forward_kernel((inner, heads), "tensor", base, len(held), *refs),
        out_shape=whole + own,
        grid=(count,),
        in_specs=[full(docs), tok(model), tok(model)]
        + [full(v) for v in consts]
        + [pl.BlockSpec(memory_space=pl.ANY)] * len(held),
        out_specs=whole_specs + own_specs,
        input_output_aliases={first + k: k for k in range(len(held))},
        scratch_shapes=[
            pltpu.VMEM((SPAN + 8, chan), F32),
            pltpu.VMEM((SPAN + 8, LANES), F32),
            pltpu.VMEM((LANES, inner), F32),
            pltpu.VMEM((8, LANES), F32),
            pltpu.VMEM((8, chan), F32),
            pltpu.VMEM((8, inner), F32),
        ],
        compiler_params=pltpu.CompilerParams(
            dimension_semantics=("arbitrary",), vmem_limit_bytes=VMEM_MOST
        ),
        cost_estimate=cost(18.0),
        name="mixer_forward",
    )(docs, normed, cotangent, *consts, *held)


def gating_kernel(
    inner_all, axis, gate_ref, ssd_ref, dn_ref, sums_ref, ggain_ref,
    nout_ref, dgate_ref, dssd_ref, ggrad_ref,
):
    c = pl.program_id(0)
    inner = gate_ref.shape[1]
    gain = ggain_ref[:, pl.ds(pl.multiple_of(lax.axis_index(axis) * inner, LANES), inner)]

    @pl.when(c == 0)
    def _():
        ggrad_ref[...] = jnp.zeros(ggrad_ref.shape, F32)

    inv = lax.rsqrt(as_column(sums_ref[0, pl.ds(c, 1), :]) * (1.0 / inner_all) + EPS)
    pull = as_column(sums_ref[1, pl.ds(c, 1), :]) * (inv * inv * inv) * (1.0 / inner_all)
    for group in range(inner // LANES):
        lanes = slice(group * LANES, (group + 1) * LANES)
        gate = gate_ref[:, lanes]
        sig = jax.nn.sigmoid(gate)
        silu = gate * sig
        ssd = ssd_ref[:, lanes]
        gated = ssd * silu
        dn = dn_ref[:, lanes]
        g_l = gain[:, lanes]
        nout = gated * inv
        nout_ref[:, lanes] = (nout * g_l).astype(BF16)
        ggrad_ref[:, lanes] += fold(dn * nout)
        d_gated = dn * g_l * inv - gated * pull
        dssd_ref[:, lanes] = d_gated * silu
        dgate_ref[:, lanes] = (d_gated * ssd * (sig * (1.0 + gate * (1.0 - sig)))).astype(BF16)


def gating(gate, ssd, dn, sums, ggain):
    tokens, inner = gate.shape

    def full(shape):
        return pl.BlockSpec(shape, lambda i: (0,) * len(shape))

    tok = pl.BlockSpec((SPAN, inner), lambda i: (i, 0))
    return pl.pallas_call(
        lambda *refs: gating_kernel(ggain.shape[1], "tensor", *refs),
        out_shape=(
            jax.ShapeDtypeStruct((tokens, inner), BF16),
            jax.ShapeDtypeStruct((tokens, inner), BF16),
            jax.ShapeDtypeStruct((tokens, inner), F32),
            jax.ShapeDtypeStruct((8, inner), F32),
        ),
        grid=(tokens // SPAN,),
        in_specs=[tok, tok, tok, full(sums.shape), full(ggain.shape)],
        out_specs=(tok, tok, tok, full((8, inner))),
        compiler_params=pltpu.CompilerParams(dimension_semantics=("arbitrary",)),
        cost_estimate=cost(10.0),
        name="gating",
    )(gate, ssd, dn, sums, ggain)


def backward_kernel(
    dims, axis, base, count,
    docs_ref, mixed_ref, pre_ref, ssd_ref, stp_ref, state_ref, dssd_ref, dgate_ref,
    cw_ref, cb_ref, dtb_ref, dec_ref, skip_ref, pin_ref, din_ref, sin_ref,
    dall_ref, gconv_ref, gskip_ref, ghead_ref, pout_ref, dout_ref, sout_ref,
    pbuf, dbuf, dstate, par, cwb,
):
    inner, heads, inner_all = dims
    pairs = heads // 2
    chan = inner + 2 * LANES
    i = pl.program_id(0)
    c = base + count - 1 - i
    rank = lax.axis_index(axis)

    @pl.when(i == 0)
    def _():
        pbuf[SPAN : SPAN + 8] = pin_ref[...]
        dbuf[SPAN : SPAN + 8] = din_ref[...]
        dstate[...] = sin_ref[...]
        own_params(rank, heads, inner, inner_all, dtb_ref, dec_ref, skip_ref, cw_ref, cb_ref, par, cwb)
        gconv_ref[...] = jnp.zeros(gconv_ref.shape, F32)
        gskip_ref[...] = jnp.zeros(gskip_ref.shape, F32)
        ghead_ref[...] = jnp.zeros(ghead_ref.shape, F32)

    dall_ref[:, 0:inner] = dgate_ref[...]
    drow = docs_ref[pl.ds(c, 1), :].astype(F32)
    dcol = as_column(drow)
    before = docs_ref[pl.ds(jnp.maximum(c - 1, 0), 1), :].astype(F32)
    enter = as_column(before)[SPAN - 1 : SPAN]
    enter = jnp.where(c == 0, -1.0, enter)
    dbuf[0:SPAN] = dcol
    keeps = [None] + [dbuf[k : k + SPAN] == dcol for k in range(1, 4)]

    raw = stp_ref[...] + par[0:1]
    step = softplus(raw)
    row_i, col_i = iota((SPAN, SPAN), 0), iota((SPAN, SPAN), 1)
    tril = (row_i >= col_i).astype(BF16)
    log_step = step * par[1:2]
    running = tri_sum(tril, log_step, heads)
    run_rows = jnp.transpose(running)
    ending = running[SPAN - 1 : SPAN]
    tail = jnp.where(dcol == dcol[SPAN - 1 : SPAN], jnp.exp(ending - running), 0.0)
    reach = jnp.where(dcol == enter, jnp.exp(running), 0.0)
    same = jnp.concatenate([dcol, dcol], 1) == drow
    bias = jnp.where(same & (row_i <= col_i), 0.0, FAR)

    def activate(group):
        lanes = slice(group * LANES, (group + 1) * LANES)
        pre = pre_ref[:, lanes]
        sig = jax.nn.sigmoid(pre)
        return pre * sig, sig * (1.0 + pre * (1.0 - sig))

    b_act, b_slope = activate(pairs)
    c_act, c_slope = activate(pairs + 1)
    b_rows, c_rows = b_act.astype(BF16), c_act.astype(BF16)
    c_turned = jnp.transpose(c_act).astype(BF16)
    scores = exact_nt(b_act, c_act)
    low_half = iota((SPAN, LANES), 1) < LANES // 2
    half = SPAN // 2
    d_scores = [jnp.zeros((half, SPAN), F32), jnp.zeros((half, half), F32)]
    d_b = jnp.zeros((SPAN, LANES), F32)
    d_c = jnp.zeros((SPAN, LANES), F32)
    head_up = jnp.zeros((SPAN, LANES), F32)
    head_down = jnp.zeros((SPAN, LANES), F32)
    head_step = jnp.zeros((SPAN, LANES), F32)
    head_hold = jnp.zeros((8, LANES), F32)
    for pair in range(pairs):
        lanes = slice(pair * LANES, (pair + 1) * LANES)
        ones_at = (iota((LANES, LANES), 1) == 2 * pair + iota((LANES, LANES), 0) // (LANES // 2)).astype(BF16)

        def head_sum(v):
            hi = v.astype(BF16)
            low = (v - hi.astype(F32)).astype(BF16)
            return nn(hi, ones_at) + nn(low, ones_at)

        act, slope = activate(pair)
        step_l = pair_lanes(step, pair, low_half)
        tail_l = pair_lanes(tail, pair, low_half)
        reach_l = pair_lanes(reach, pair, low_half)
        skip_l = pair_lanes(par[2:3], pair, low_half[0:1])
        ssd = ssd_ref[:, lanes]
        d_ssd = dssd_ref[:, lanes]
        gskip_ref[:, lanes] += fold(d_ssd * act)
        dyb = d_ssd.astype(BF16)
        scaled = act * step_l
        xb = scaled.astype(BF16)
        held = state_ref[0, :, lanes]
        d_held = dstate[:, lanes]
        d_held_b = d_held.astype(BF16)
        ry = (d_ssd * reach_l).astype(BF16)
        xt = (scaled * tail_l).astype(BF16)
        parts = []
        for sub in range(2):
            head = 2 * pair + sub
            x_own = jnp.where(low_half if sub == 0 else ~low_half, scaled, 0.0).astype(BF16)
            blocks = []
            for blk in range(2):
                rows = slice(blk * half, (blk + 1) * half)
                cols = slice(blk * half, SPAN)
                gap = run_rows[head : head + 1, cols] - running[rows, head : head + 1]
                decay = jnp.exp(gap + bias[rows, cols])
                blocks.append(nn((decay * scores[rows, cols]).astype(BF16), dyb[cols]))
                d_scores[blk] = d_scores[blk] + decay * nt(x_own[rows], dyb[cols])
            parts.append(jnp.concatenate(blocks, 0))
        d_within = jnp.where(low_half, parts[0], parts[1])
        from_state = tail_l * nn(b_rows, d_held_b)
        d_scaled = d_within + from_state
        xf = xb.astype(F32)
        head_up += head_sum(dyb.astype(F32) * (ssd - skip_l * act) - xf * d_within)
        head_down += head_sum(xf * from_state)
        head_step += head_sum(d_scaled * act)
        hold = reach_l[SPAN - 1 : SPAN]
        hold_sum = jnp.sum((d_held * held.astype(F32)).reshape(LANES // 8, 8, LANES), axis=0) * hold
        head_hold += head_sum(hold_sum)
        d_b += nt(xt, d_held_b)
        d_c += nt(ry, held)
        dstate[:, lanes] = hold * d_held + nn(c_turned, ry)
        pbuf[0:SPAN, lanes] = (skip_l * d_ssd + step_l * d_scaled) * slope

    ds_b = jnp.concatenate(
        [
            d_scores[0],
            jnp.concatenate([jnp.zeros((half, half), F32), d_scores[1]], 1),
        ],
        0,
    )
    d_b += nn(ds_b.astype(BF16), c_rows)
    d_c += nn(jnp.transpose(ds_b).astype(BF16), b_rows)
    pbuf[0:SPAN, inner : inner + LANES] = d_b * b_slope
    pbuf[0:SPAN, inner + LANES : chan] = d_c * c_slope

    triu = (row_i <= col_i).astype(BF16)
    below = (row_i > col_i).astype(BF16)
    d_log = (
        tri_sum(triu, head_up, heads)
        + tri_sum(below, head_down, heads)
        + jnp.sum(head_hold, axis=0, keepdims=True)
    )
    d_step = d_log * par[1:2] + head_step
    d_raw = jnp.where(iota((SPAN, LANES), 1) < heads, d_step * jax.nn.sigmoid(raw), 0.0)
    dall_ref[:, inner + chan :] = d_raw.astype(BF16)
    ghead_ref[0] += fold(d_raw)
    ghead_ref[1] += fold(d_log * log_step)

    for group in range(chan // LANES):
        lanes = slice(group * LANES, (group + 1) * LANES)
        mixed = mixed_ref[:, lanes]
        own = pbuf[0:SPAN, lanes]
        acc = cwb[3:4, lanes] * own
        gconv_ref[3, :, lanes] += fold(mixed * own)
        gconv_ref[4, :, lanes] += fold(own)
        for k in range(1, 4):
            later = jnp.where(keeps[k], pbuf[k : k + SPAN, lanes], 0.0)
            acc = acc + cwb[3 - k : 4 - k, lanes] * later
            gconv_ref[3 - k, :, lanes] += fold(mixed * later)
        dall_ref[:, inner + group * LANES : inner + (group + 1) * LANES] = acc.astype(BF16)
    pbuf[SPAN : SPAN + 8] = pbuf[0:8]
    dbuf[SPAN : SPAN + 8] = dbuf[0:8]
    pout_ref[...] = pbuf[0:8]
    dout_ref[...] = dbuf[0:8]
    sout_ref[...] = dstate[...]


def mixer_backward(docs, arrays, params, carry, base, count, heads, inner_all):
    mixed, pre, ssd, stp, states, dssd, dgate = arrays
    tokens, inner = ssd.shape
    chan = inner + 2 * LANES
    width = inner + chan + LANES

    def tok(wide):
        return pl.BlockSpec((SPAN, wide), lambda i: (base + count - 1 - i, 0))

    def full(shape):
        return pl.BlockSpec(shape, lambda i: (0,) * len(shape))

    outs = (
        jax.ShapeDtypeStruct((count * SPAN, width), BF16),
        jax.ShapeDtypeStruct((5, 8, chan), F32),
        jax.ShapeDtypeStruct((8, inner), F32),
        jax.ShapeDtypeStruct((2, 8, LANES), F32),
        jax.ShapeDtypeStruct((8, chan), F32),
        jax.ShapeDtypeStruct((8, LANES), F32),
        jax.ShapeDtypeStruct((LANES, inner), F32),
    )
    consts = params + carry
    return pl.pallas_call(
        lambda *refs: backward_kernel((inner, heads, inner_all), "tensor", base, count, *refs),
        out_shape=outs,
        grid=(count,),
        in_specs=[
            full(docs.shape), tok(chan), tok(chan), tok(inner), tok(LANES),
            pl.BlockSpec((1, LANES, inner), lambda i: (base + count - 1 - i, 0, 0)),
            tok(inner), tok(inner),
        ]
        + [full(v.shape) for v in consts],
        out_specs=(pl.BlockSpec((SPAN, width), lambda i: (count - 1 - i, 0)),)
        + tuple(full(v.shape) for v in outs[1:]),
        scratch_shapes=[
            pltpu.VMEM((SPAN + 8, chan), F32),
            pltpu.VMEM((SPAN + 8, LANES), F32),
            pltpu.VMEM((LANES, inner), F32),
            pltpu.VMEM((8, LANES), F32),
            pltpu.VMEM((8, chan), F32),
        ],
        compiler_params=pltpu.CompilerParams(
            dimension_semantics=("arbitrary",), vmem_limit_bytes=VMEM_MOST
        ),
        cost_estimate=cost(20.0),
        name="mixer_backward",
    )(docs, mixed, pre, ssd, stp, states, dssd, dgate, *consts)


MESH_IDS = pl.DeviceIdType.MESH


def gather_kernel(
    dims, hid_ref, cot_ref, ngain_ref, w_ref, step_ref, wo_ref,
    win_ref, wout_ref, normed_ref, *refs,
):
    lines, depth, inner, inner_all, aligned = dims
    outs = refs[:4] if aligned else ()
    mine, zsend, zrecv, xsend, xrecv, takes, puts = refs[len(outs):]
    trank, drank = lax.axis_index("tensor"), lax.axis_index("dp")
    line, side = drank // 2, drank % 2
    model = hid_ref.shape[1]
    off = pl.multiple_of(trank * inner, LANES)
    pieces = (
        (w_ref, inner_all + off, win_ref, inner, inner),
        (w_ref, 2 * inner_all, win_ref, 2 * inner, 2 * LANES),
        (step_ref, 0, win_ref, 2 * inner + 2 * LANES, LANES),
        (w_ref, off, win_ref, 0, inner),
        (wo_ref, 0, wout_ref, 0, inner),
    )

    def peer(step):
        return {"dp": lax.rem(line + step, lines) * 2 + side}

    partner = {"dp": line * 2 + 1 - side}
    barrier = pltpu.get_barrier_semaphore()
    for step in range(1, lines):
        pl.semaphore_signal(barrier, inc=1, device_id=peer(step), device_id_type=MESH_IDS)
    pl.semaphore_signal(barrier, inc=1, device_id=partner, device_id_type=MESH_IDS)
    pl.semaphore_wait(barrier, lines)

    def rows(index):
        return pl.ds(pl.multiple_of(index * depth, depth), depth)

    def block(p, index):
        _, _, dst, at, width = pieces[p]
        return dst.at[rows(index), pl.ds(at, width)]

    def own(p):
        src, at, _, _, width = pieces[p]
        return src.at[:, pl.ds(at, width)]

    def z_copy(p, step, src, index):
        return pltpu.make_async_remote_copy(
            src_ref=src, dst_ref=block(p, index), send_sem=zsend.at[p, step - 1],
            recv_sem=zrecv.at[p, step - 1], device_id=peer(step), device_id_type=MESH_IDS,
        )

    def x_copy(p, step, src, index):
        return pltpu.make_async_remote_copy(
            src_ref=src, dst_ref=block(p, index), send_sem=xsend.at[p, step],
            recv_sem=xrecv.at[p, step], device_id=partner, device_id_type=MESH_IDS,
        )

    count = len(pieces)
    for p in range(count):
        for step in range(1, lines):
            z_copy(p, step, own(p), drank).start()
        x_copy(p, 0, own(p), drank).start()
    spots, at = [], 0
    for p in range(count):
        spots.append(mine.at[:, pl.ds(at, pieces[p][4])])
        at += pieces[p][4]
    fetched = [pltpu.make_async_copy(own(p), spots[p], takes.at[p]) for p in range(count)]
    for copy in fetched:
        copy.start()

    gain = ngain_ref[...]

    def normalize(hid, cot, normed, *sorted_refs):
        value = hid[...].astype(F32)
        inv = lax.rsqrt(jnp.mean(value * value, -1, keepdims=True) + EPS)
        normed[...] = (value * inv * gain).astype(BF16)
        if aligned:
            for src, away, here in (
                (normed, sorted_refs[0], sorted_refs[1]), (cot, sorted_refs[2], sorted_refs[3]),
            ):
                for j in range(lines):
                    first = lax.rem(line + j, lines) * 2
                    lanes = slice(j * depth, (j + 1) * depth)
                    away[:, lanes] = src[:, pl.ds(pl.multiple_of((first + 1 - side) * depth, depth), depth)]
                    here[:, lanes] = src[:, pl.ds(pl.multiple_of((first + side) * depth, depth), depth)]

    full = pl.BlockSpec((SPAN, model), lambda i: (i, 0))
    half = pl.BlockSpec((SPAN, lines * depth), lambda i: (i, 0))
    pltpu.emit_pipeline(
        normalize, grid=(hid_ref.shape[0] // SPAN,), in_specs=[full, full],
        out_specs=[full] + [half] * len(outs),
    )(hid_ref, cot_ref, normed_ref, *outs)

    stored = [pltpu.make_async_copy(spots[p], block(p, drank), puts.at[p]) for p in range(count)]
    for p in range(count):
        fetched[p].wait()
        stored[p].start()
    for p in range(count):
        for step in range(1, lines):
            source = lax.rem(line - step + lines, lines) * 2 + side
            got = block(p, source)
            z_copy(p, step, got, source).wait_recv()
            x_copy(p, step, got, source).start()
    for p in range(count):
        for step in range(lines):
            source = lax.rem(line - step + lines, lines) * 2 + 1 - side
            x_copy(p, step, block(p, source), source).wait_recv()
    for p in range(count):
        for step in range(1, lines):
            z_copy(p, step, own(p), drank).wait_send()
        for step in range(lines):
            x_copy(p, step, own(p), drank).wait_send()
        stored[p].wait()


def gather_weights(hidden, cotangent, norm_gain, in_weight, own_step, out_weight, lines, inner_all):
    tokens, model = hidden.shape
    depth, inner = out_weight.shape
    aligned = depth % LANES == 0
    width = 2 * inner + 3 * LANES
    half = jax.ShapeDtypeStruct((tokens, lines * depth), BF16)
    anywhere = pl.BlockSpec(memory_space=pl.ANY)
    outs = (
        jax.ShapeDtypeStruct((model, width), BF16),
        jax.ShapeDtypeStruct((model, inner), BF16),
        jax.ShapeDtypeStruct((tokens, model), BF16),
    ) + (half,) * (4 if aligned else 0)
    dma = pltpu.SemaphoreType.DMA
    return pl.pallas_call(
        lambda *refs: gather_kernel((lines, depth, inner, inner_all, aligned), *refs),
        out_shape=outs,
        in_specs=[anywhere, anywhere, pl.BlockSpec(memory_space=pltpu.VMEM)] + [anywhere] * 3,
        out_specs=(anywhere,) * len(outs),
        scratch_shapes=[
            pltpu.VMEM((depth, width + inner), BF16),
            dma((5, max(1, lines - 1))), dma((5, max(1, lines - 1))), dma((5, lines)), dma((5, lines)),
            dma((5,)), dma((5,)),
        ],
        compiler_params=pltpu.CompilerParams(collective_id=0, has_side_effects=True),
        cost_estimate=cost(45.0),
        name="gather_weights",
    )(hidden, cotangent, norm_gain, in_weight, own_step, out_weight)


def swap(v, axis, to):
    return lax.ppermute(v, axis, [(k, to(k)) for k in range(lax.axis_size(axis))])


def tie(*items):
    return lax.optimization_barrier(items)


def flip(bits):
    return lambda k: k ^ bits


def body(
    hidden_in, doc_ids, cotangent, norm_gain, in_weight, conv_weight, conv_bias,
    dt_bias, log_decay, skip_gain, gate_gain, out_weight,
):
    tcount, dcount = lax.axis_size("tensor"), lax.axis_size("dp")
    trank, drank = lax.axis_index("tensor"), lax.axis_index("dp")
    lines = dcount // 2
    line, side = drank // 2, drank % 2
    core = trank % 2
    inner_all, head_all = gate_gain.shape[0], dt_bias.shape[0]
    inner, heads = inner_all // tcount, head_all // tcount
    tokens, model = hidden_in.shape
    base_bc = 2 * inner_all
    base_dt = base_bc + 2 * LANES
    depth = in_weight.shape[0]
    chan = inner + 2 * LANES

    def line_to(step):
        return lambda k: ((k // 2 + step) % lines) * 2 + k % 2

    own_step = jnp.pad(
        lax.dynamic_slice_in_dim(in_weight, base_dt + trank * heads, heads, 1),
        ((0, 0), (0, LANES - heads)),
    )
    w_in, w_out, normed, *sorted_parts = gather_weights(
        hidden_in, cotangent, norm_gain.reshape(1, -1), in_weight, own_step, out_weight,
        lines, inner_all,
    )
    if not sorted_parts:

        def features(v, which):
            return jnp.concatenate(
                [
                    lax.dynamic_slice_in_dim(v, (((line + j) % lines) * 2 + which) * depth, depth, 1)
                    for j in range(lines)
                ],
                1,
            )

        sorted_parts = [features(v, which) for v in (normed, cotangent) for which in (1 - side, side)]
    n_away, n_here, c_away, c_here = sorted_parts

    def row(v):
        return v.reshape(1, -1)

    docs = doc_ids.reshape(tokens // SPAN, SPAN)
    spans = tokens // SPAN
    count = spans // 2
    span_rows = count * SPAN
    part = span_rows // 2
    params = (conv_weight, row(conv_bias), row(dt_bias), row(log_decay), row(skip_gain))

    def own_share(left, right):
        def make(start):
            return nt(lax.dynamic_slice_in_dim(left, start, part, 0), right)

        got = swap(make((1 - core) * part).astype(BF16), "tensor", flip(1))
        return (make(core * part) + got.astype(F32)).astype(BF16)

    def chips_sum(mine, theirs):
        return mine.astype(F32) + theirs.astype(F32)

    def both(own):
        got = swap(own, "tensor", flip(1))
        return [jnp.where(core == 0, own, got), jnp.where(core == 0, got, own)]

    def my_rows(v, h):
        return lax.dynamic_slice_in_dim(v, h * span_rows + core * part, part, 0)

    carry = (
        jnp.zeros((8, chan), F32), jnp.full((8, LANES), -1.0, F32), jnp.zeros((LANES, inner), F32),
    )
    def forward(h, carry, held):
        return mixer_forward(
            docs, normed, cotangent, w_in, w_out, params, row(gate_gain), carry, held,
            h * count, count, heads,
        )

    made = forward(0, carry, ())
    held, gg, sums_a, carry = made[:7], made[7], made[8], made[9:]
    out_a = own_share(gg, w_out)
    out_a, carry = tie(out_a, carry)
    far_a = swap(out_a, "tensor", flip(2))
    made = forward(1, carry, held)
    held, gg, sums_b = made[:7], made[7], made[8]
    sums = jnp.concatenate([sums_a, sums_b], 1)
    sums = sums + swap(sums, "tensor", flip(1))
    sums = sums + swap(sums, "tensor", flip(2))
    out_b = own_share(gg, w_out)
    out_b, sums, far_a = tie(out_b, sums, far_a)
    far_b = swap(out_b, "tensor", flip(2))
    gate, mixed, pre, ssd, stp, states, dn = held
    nout, d_gate, d_ssd, g_gain = gating(gate, ssd, dn, sums, row(gate_gain))
    inv_gate = lax.rsqrt(sums[0].reshape(tokens, 1) * (1.0 / inner_all) + EPS)

    def to_side(away):
        return swap(away, "dp", flip(1))

    def to_lines(here, got):
        here = here + got.astype(F32)
        return here, [here[j * depth : (j + 1) * depth].astype(BF16) for j in range(1, lines)]

    def lines_sum(here, low):
        total = here[:depth]
        for j in range(1, lines):
            total = total + swap(low[j - 1], "dp", line_to(j)).astype(F32)
        return total

    o_away, g_away = tn(c_away, nout).astype(BF16), tn(n_away, d_gate).astype(BF16)
    o_here, g_here = tn(c_here, nout), tn(n_here, d_gate)
    o_away, g_away, o_here, g_here, d_ssd = tie(o_away, g_away, o_here, g_here, d_ssd)
    o_got, g_got = to_side(o_away), to_side(g_away)

    def backward(h, carry, d_ssd):
        return mixer_backward(
            docs, (mixed, pre, ssd, stp, states, d_ssd, d_gate), params, carry,
            h * count, count, heads, inner_all,
        )

    carry = (
        jnp.zeros((8, chan), F32), jnp.full((8, LANES), -2.0, F32), jnp.zeros((LANES, inner), F32),
    )
    d_b, conv_b, skip_b, head_b, *carry = backward(1, carry, d_ssd)
    d_b, o_got, g_got, far_b = tie(d_b, o_got, g_got, far_b)
    o_here, o_low = to_lines(o_here, o_got)
    g_here, g_low = to_lines(g_here, g_got)
    hid_b = own_share(d_b, w_in)
    low_rows, high_rows = slice(0, span_rows), slice(span_rows, tokens)
    away_b, here_b = tn(n_away[high_rows], d_b[:, inner:]), tn(n_here[high_rows], d_b[:, inner:])
    o_low, g_low, hid_b, carry, away_b, here_b = tie(o_low, g_low, hid_b, tuple(carry), away_b, here_b)
    hid_far_b = swap(hid_b, "tensor", flip(2))
    g_out, g_gate = lines_sum(o_here, o_low), lines_sum(g_here, g_low)
    d_a, conv_a, skip_a, head_a, *_ = backward(0, carry, d_ssd)
    d_a, g_out, g_gate, hid_far_b = tie(d_a, g_out, g_gate, hid_far_b)
    g_conv, g_skip, g_head = conv_a + conv_b, skip_a + skip_b, head_a + head_b

    away = (away_b + tn(n_away[low_rows], d_a[:, inner:])).astype(BF16)
    v_got, s_got = to_side(away[:, :inner]), to_side(away[:, inner:])
    hid_a = own_share(d_a, w_in)
    hid_far_a = swap(hid_a, "tensor", flip(2))
    here = here_b + tn(n_here[low_rows], d_a[:, inner:])
    g_value = lines_sum(*to_lines(here[:, :inner], v_got))
    shared = lines_sum(*to_lines(here[:, inner:], s_got))

    layer_out, halves, g_norm = [], [], 0.0
    for h, out, d_hidden in (
        (0, chips_sum(out_a, far_a), chips_sum(hid_a, hid_far_a)),
        (1, chips_sum(out_b, far_b), chips_sum(hid_b, hid_far_b)),
    ):
        hid = my_rows(hidden_in, h).astype(F32)
        inv = lax.rsqrt(jnp.mean(hid * hid, -1, keepdims=True) + EPS)
        layer_out += both((hid + out * my_rows(inv_gate, h)).astype(BF16))
        scaled = d_hidden * norm_gain
        pull = jnp.mean(scaled * hid, -1, keepdims=True)
        halves += both((inv * scaled - hid * inv**3 * pull).astype(BF16))
        g_norm = g_norm + jnp.sum(d_hidden * hid * inv, 0)
    layer_out = jnp.concatenate(layer_out, 0)
    grad_input = cotangent.astype(F32) + jnp.concatenate(halves, 0).astype(F32)
    g_norm = g_norm * (trank < 2).astype(F32)

    def all_heads(v):
        pair = swap(v, "tensor", flip(1))
        low, high = jnp.where(core == 0, v, pair), jnp.where(core == 0, pair, v)
        pairs = jnp.concatenate([low, high], 1)
        far = swap(pairs, "tensor", flip(2))
        first = trank < 2
        return [jnp.where(first, pairs, far), jnp.where(first, far, pairs)]

    lane = jnp.arange(LANES) - trank * heads
    shared = jnp.concatenate(
        [
            shared[:, : 2 * LANES],
            jnp.where(
                (lane >= 0) & (lane < heads), jnp.roll(shared[:, 2 * LANES :], trank * heads, 1), 0.0
            ),
        ],
        1,
    )
    shared = shared + swap(shared, "tensor", flip(1))
    shared = shared + swap(shared, "tensor", flip(2))
    grad_in_weight = jnp.concatenate(
        all_heads(g_gate) + all_heads(g_value) + [shared[:, : 2 * LANES + head_all]], 1
    )

    conv = jnp.sum(g_conv, 1)
    head = jnp.sum(g_head, 1)
    skip = jnp.sum(jnp.sum(g_skip, 0).reshape(heads, -1), 1)
    spot = trank * inner

    def place(v, total, start):
        return lax.dynamic_update_slice_in_dim(
            jnp.zeros(v.shape[:-1] + (total,), F32), v, start, v.ndim - 1
        )

    conv_all = place(conv[:, :inner], inner_all + 2 * LANES, spot).at[:, inner_all:].set(conv[:, inner:])
    heads_all = place(jnp.stack([head[0, :heads], head[1, :heads], skip]), head_all, trank * heads)
    flat = jnp.concatenate(
        [g_norm, conv_all.reshape(-1), heads_all.reshape(-1), place(jnp.sum(g_gain, 0), inner_all, spot)]
    )
    flat = jnp.pad(flat, (0, -flat.shape[0] % 1024)).reshape(-1, LANES)
    for axis, size in (("tensor", tcount), ("dp", dcount)):
        bit = 1
        while bit < size:
            flat = flat + swap(flat, axis, flip(bit))
            bit *= 2
    flat = flat.reshape(-1)
    cuts, at = [], 0
    for size in (model, 5 * conv_all.shape[1], 3 * head_all, inner_all):
        cuts.append(flat[at : at + size])
        at += size
    conv_all = cuts[1].reshape(5, -1)
    heads_all = cuts[2].reshape(3, -1)
    return (
        layer_out, grad_input, cuts[0], grad_in_weight, conv_all[:4], conv_all[4],
        heads_all[0], heads_all[1], heads_all[2], cuts[3], g_out,
    )


def solution(mesh):
    rows, whole = P("dp", None), P()
    return jax.shard_map(
        body,
        mesh=mesh,
        in_specs=(rows, rows, rows, whole, rows, whole, whole, whole, whole, whole, whole, P("dp", "tensor")),
        out_specs=(rows, rows, whole, rows, whole, whole, whole, whole, whole, whole, P("dp", "tensor")),
        check_vma=False,
    )
```

```python
import jax
import jax.numpy as jnp
from jax import lax
from jax.experimental import pallas as pl
from jax.experimental.pallas import tpu as pltpu
from jax.sharding import PartitionSpec as P

SPAN = 256
LANES = 128
EPS = 1e-05
FAR = -1e30
VMEM_MOST = 60 * 2**20
F32 = jnp.float32
BF16 = jnp.bfloat16


def cost(micros):
    return pl.CostEstimate(flops=int(micros * 1.15e9), bytes_accessed=1 << 20, transcendentals=0)


def nn(a, b):
    return lax.dot_general(a, b, (((1,), (0,)), ((), ())), preferred_element_type=F32)


def nt(a, b):
    return lax.dot_general(a, b, (((1,), (1,)), ((), ())), preferred_element_type=F32)


def tn(a, b):
    return lax.dot_general(a, b, (((0,), (0,)), ((), ())), preferred_element_type=F32)


def iota(shape, dim):
    return lax.broadcasted_iota(jnp.int32, shape, dim)


def as_column(row, rows=SPAN):
    return jnp.transpose(jnp.broadcast_to(row, (LANES, rows)))


def as_row(block):
    return jnp.sum(jnp.transpose(block), axis=0, keepdims=True)


def split3(v):
    hi = v.astype(BF16)
    rest = v - hi.astype(F32)
    mid = rest.astype(BF16)
    low = (rest - mid.astype(F32)).astype(BF16)
    return hi, mid, low


def tri_sum(tri, v, heads):
    lane = iota(v.shape, 1)
    v = jnp.where(lane < heads, v, 0.0)
    hi = v.astype(BF16).astype(F32)
    rest = v - hi
    mid = rest.astype(BF16).astype(F32)
    low = rest - mid
    packed = hi + pltpu.roll(mid, heads, 1) + pltpu.roll(low, 2 * heads, 1)
    out = nn(tri, packed.astype(BF16))
    return out + pltpu.roll(out, LANES - heads, 1) + pltpu.roll(out, LANES - 2 * heads, 1)


def pair_lanes(cols, pair, low_half):
    rows = cols.shape[0]
    first = jnp.broadcast_to(cols[:, 2 * pair : 2 * pair + 1], (rows, LANES))
    second = jnp.broadcast_to(cols[:, 2 * pair + 1 : 2 * pair + 2], (rows, LANES))
    return jnp.where(low_half, first, second)


def exact_nt(a, b):
    a_hi, b_hi = a.astype(BF16), b.astype(BF16)
    a_lo = (a - a_hi.astype(F32)).astype(BF16)
    b_lo = (b - b_hi.astype(F32)).astype(BF16)
    return nt(a_hi, b_hi) + (nt(a_hi, b_lo) + nt(a_lo, b_hi))


def softplus(v):
    return jnp.maximum(v, 0.0) + jnp.log1p(jnp.exp(-jnp.abs(v)))


def own_lanes(row, rank, heads):
    total = row.shape[1]
    pick = (iota((total, LANES), 0) == rank * heads + iota((total, LANES), 1)) & (
        iota((total, LANES), 1) < heads
    )
    wide = jnp.broadcast_to(row, (8, total))
    out = lax.dot_general(
        wide, pick.astype(F32), (((1,), (0,)), ((), ())),
        precision=lax.Precision.HIGHEST, preferred_element_type=F32,
    )
    return out[0:1]


def fold(v):
    return jnp.sum(v.reshape(SPAN // 8, 8, v.shape[1]), axis=0)


def own_params(rank, heads, inner, inner_all, dtb_ref, dec_ref, skip_ref, cw_ref, cb_ref, par, cwb):
    chan = inner + 2 * LANES
    off = pl.multiple_of(rank * inner, LANES)
    taps = cw_ref.shape[0]
    par[0:1] = own_lanes(dtb_ref[...], rank, heads)
    par[1:2] = -jnp.exp(own_lanes(dec_ref[...], rank, heads))
    par[2:3] = own_lanes(skip_ref[...], rank, heads)
    cwb[0:taps, 0:inner] = cw_ref[:, pl.ds(off, inner)].astype(F32)
    cwb[0:taps, inner:chan] = cw_ref[:, inner_all:].astype(F32)
    cwb[taps : taps + 1, 0:inner] = cb_ref[:, pl.ds(off, inner)]
    cwb[taps : taps + 1, inner:chan] = cb_ref[:, inner_all:]


def forward_kernel(
    dims, axis, base, kept,
    docs_ref, normed_ref, cot_ref, win_ref, wout_ref, cw_ref, cb_ref,
    dtb_ref, dec_ref, skip_ref, ggain_ref, xin_ref, din_ref, sin_ref, *refs,
):
    (
        gate_ref, mixed_ref, pre_ref, ssd_ref, stp_ref, state_ref, dn_ref,
        gg_ref, sums_ref, xout_ref, dout_ref, sout_ref,
        xbuf, dbuf, state, par, cwb, gain,
    ) = refs[kept:]
    inner, heads = dims
    pairs = heads // 2
    chan = inner + 2 * LANES
    step_i = pl.program_id(0)
    i = base + step_i
    rank = lax.axis_index(axis)
    inner_all = ggain_ref.shape[1]

    @pl.when(step_i == 0)
    def _():
        xbuf[0:8] = xin_ref[...]
        dbuf[0:8] = din_ref[...]
        state[...] = sin_ref[...]
        own_params(rank, heads, inner, inner_all, dtb_ref, dec_ref, skip_ref, cw_ref, cb_ref, par, cwb)
        gain[0:1] = ggain_ref[:, pl.ds(pl.multiple_of(rank * inner, LANES), inner)]

    nb = normed_ref[...]
    xbuf[8 : 8 + SPAN] = nn(nb, win_ref[:, inner : inner + chan])
    gate_ref[...] = nn(nb, win_ref[:, 0:inner])
    stp = nn(nb, win_ref[:, inner + chan : inner + chan + LANES])
    stp_ref[...] = stp
    mixed_ref[...] = xbuf[8 : 8 + SPAN]
    dn_ref[...] = nn(cot_ref[...], wout_ref[...])

    drow = docs_ref[pl.ds(i, 1), :].astype(F32)
    dcol = as_column(drow)
    enter = dbuf[7:8]
    dbuf[8 : 8 + SPAN] = dcol
    keeps = [None] + [dbuf[8 - k : 8 - k + SPAN] == dcol for k in range(1, 4)]

    def conv(group):
        lanes = slice(group * LANES, (group + 1) * LANES)
        acc = cwb[4:5, lanes] + cwb[3:4, lanes] * xbuf[8 : 8 + SPAN, lanes]
        for k in range(1, 4):
            acc = acc + cwb[3 - k : 4 - k, lanes] * jnp.where(
                keeps[k], xbuf[8 - k : 8 - k + SPAN, lanes], 0.0
            )
        pre_ref[:, lanes] = acc
        return acc * jax.nn.sigmoid(acc)

    b_act, c_act = conv(pairs), conv(pairs + 1)
    b_rows, c_rows = b_act.astype(BF16), c_act.astype(BF16)

    step = softplus(stp + par[0:1])
    row_i, col_i = iota((SPAN, SPAN), 0), iota((SPAN, SPAN), 1)
    tril = (row_i >= col_i).astype(BF16)
    running = tri_sum(tril, step * par[1:2], heads)
    run_rows = jnp.transpose(running)
    ending = running[SPAN - 1 : SPAN]
    tail = jnp.where(dcol == dcol[SPAN - 1 : SPAN], jnp.exp(ending - running), 0.0)
    reach = jnp.where(dcol == enter, jnp.exp(running), 0.0)
    same = jnp.concatenate([dcol, dcol], 1) == drow
    bias = jnp.where(same & (row_i >= col_i), 0.0, FAR)
    scores = exact_nt(c_act, b_act)
    b_turned = jnp.transpose(b_act).astype(BF16)
    low_half = iota((SPAN, LANES), 1) < LANES // 2
    half = SPAN // 2
    square = jnp.zeros((SPAN, LANES), F32)
    cross = jnp.zeros((SPAN, LANES), F32)
    for pair in range(pairs):
        lanes = slice(pair * LANES, (pair + 1) * LANES)
        act = conv(pair)
        scaled = act * pair_lanes(step, pair, low_half)
        xb = scaled.astype(BF16)
        tail_l = pair_lanes(tail, pair, low_half)
        reach_l = pair_lanes(reach, pair, low_half)
        held = state[:, lanes]
        held_b = held.astype(BF16)
        state_ref[0, :, lanes] = held_b
        state[:, lanes] = nn(b_turned, (scaled * tail_l).astype(BF16)) + reach_l[SPAN - 1 : SPAN] * held
        out = reach_l * nn(c_rows, held_b)
        parts = []
        for sub in range(2):
            head = 2 * pair + sub
            blocks = []
            for blk in range(2):
                rows = slice(blk * half, (blk + 1) * half)
                width = (blk + 1) * half
                gap = running[rows, head : head + 1] - run_rows[head : head + 1, 0:width]
                weight = jnp.exp(gap + bias[rows, 0:width]) * scores[rows, 0:width]
                blocks.append(nn(weight.astype(BF16), xb[0:width]))
            parts.append(jnp.concatenate(blocks, 0))
        out = out + jnp.where(low_half, parts[0], parts[1])
        skip_l = pair_lanes(par[2:3], pair, low_half[0:1])
        ssd = out + skip_l * act
        ssd_ref[:, lanes] = ssd
        gate = gate_ref[:, lanes]
        gated = ssd * (gate * jax.nn.sigmoid(gate))
        square = square + gated * gated
        gained = gain[0:1, lanes] * gated
        gg_ref[:, lanes] = gained.astype(BF16)
        cross = cross + dn_ref[:, lanes] * gained
    sums_ref[0, pl.ds(step_i, 1), :] = as_row(square)
    sums_ref[1, pl.ds(step_i, 1), :] = as_row(cross)
    xbuf[0:8] = xbuf[SPAN : SPAN + 8]
    dbuf[0:8] = dbuf[SPAN : SPAN + 8]
    xout_ref[...] = xbuf[0:8]
    dout_ref[...] = dbuf[0:8]
    sout_ref[...] = state[...]


def mixer_forward(docs, normed, cotangent, w_in, w_out, params, ggain, carry, held, base, count, heads):
    tokens, model = normed.shape
    inner = w_out.shape[1]
    chan = inner + 2 * LANES
    spans = tokens // SPAN

    def tok(width):
        return pl.BlockSpec((SPAN, width), lambda i: (i + base, 0))

    def part(width):
        return pl.BlockSpec((SPAN, width), lambda i: (i, 0))

    def full(arr):
        return pl.BlockSpec(arr.shape, lambda i: (0,) * arr.ndim)

    whole = (
        jax.ShapeDtypeStruct((tokens, inner), F32),
        jax.ShapeDtypeStruct((tokens, chan), F32),
        jax.ShapeDtypeStruct((tokens, chan), F32),
        jax.ShapeDtypeStruct((tokens, inner), F32),
        jax.ShapeDtypeStruct((tokens, LANES), F32),
        jax.ShapeDtypeStruct((spans, LANES, inner), BF16),
        jax.ShapeDtypeStruct((tokens, inner), F32),
    )
    whole_specs = (
        tok(inner), tok(chan), tok(chan), tok(inner), tok(LANES),
        pl.BlockSpec((1, LANES, inner), lambda i: (i + base, 0, 0)),
        tok(inner),
    )
    own = (
        jax.ShapeDtypeStruct((count * SPAN, inner), BF16),
        jax.ShapeDtypeStruct((2, count, SPAN), F32),
        jax.ShapeDtypeStruct((8, chan), F32),
        jax.ShapeDtypeStruct((8, LANES), F32),
        jax.ShapeDtypeStruct((LANES, inner), F32),
    )
    own_specs = (part(inner),) + tuple(full(v) for v in own[1:])
    consts = (w_in, w_out) + params + (ggain,) + carry
    first = 3 + len(consts)
    return pl.pallas_call(
        lambda *refs: forward_kernel((inner, heads), "tensor", base, len(held), *refs),
        out_shape=whole + own,
        grid=(count,),
        in_specs=[full(docs), tok(model), tok(model)]
        + [full(v) for v in consts]
        + [pl.BlockSpec(memory_space=pl.ANY)] * len(held),
        out_specs=whole_specs + own_specs,
        input_output_aliases={first + k: k for k in range(len(held))},
        scratch_shapes=[
            pltpu.VMEM((SPAN + 8, chan), F32),
            pltpu.VMEM((SPAN + 8, LANES), F32),
            pltpu.VMEM((LANES, inner), F32),
            pltpu.VMEM((8, LANES), F32),
            pltpu.VMEM((8, chan), F32),
            pltpu.VMEM((8, inner), F32),
        ],
        compiler_params=pltpu.CompilerParams(
            dimension_semantics=("arbitrary",), vmem_limit_bytes=VMEM_MOST
        ),
        cost_estimate=cost(18.0),
        name="mixer_forward",
    )(docs, normed, cotangent, *consts, *held)


def gating_kernel(
    inner_all, axis, gate_ref, ssd_ref, dn_ref, sums_ref, ggain_ref,
    nout_ref, dgate_ref, dssd_ref, ggrad_ref,
):
    c = pl.program_id(0)
    inner = gate_ref.shape[1]
    gain = ggain_ref[:, pl.ds(pl.multiple_of(lax.axis_index(axis) * inner, LANES), inner)]

    @pl.when(c == 0)
    def _():
        ggrad_ref[...] = jnp.zeros(ggrad_ref.shape, F32)

    inv = lax.rsqrt(as_column(sums_ref[0, pl.ds(c, 1), :]) * (1.0 / inner_all) + EPS)
    pull = as_column(sums_ref[1, pl.ds(c, 1), :]) * (inv * inv * inv) * (1.0 / inner_all)
    for group in range(inner // LANES):
        lanes = slice(group * LANES, (group + 1) * LANES)
        gate = gate_ref[:, lanes]
        sig = jax.nn.sigmoid(gate)
        silu = gate * sig
        ssd = ssd_ref[:, lanes]
        gated = ssd * silu
        dn = dn_ref[:, lanes]
        g_l = gain[:, lanes]
        nout = gated * inv
        nout_ref[:, lanes] = (nout * g_l).astype(BF16)
        ggrad_ref[:, lanes] += fold(dn * nout)
        d_gated = dn * g_l * inv - gated * pull
        dssd_ref[:, lanes] = d_gated * silu
        dgate_ref[:, lanes] = (d_gated * ssd * (sig * (1.0 + gate * (1.0 - sig)))).astype(BF16)


def gating(gate, ssd, dn, sums, ggain):
    tokens, inner = gate.shape

    def full(shape):
        return pl.BlockSpec(shape, lambda i: (0,) * len(shape))

    tok = pl.BlockSpec((SPAN, inner), lambda i: (i, 0))
    return pl.pallas_call(
        lambda *refs: gating_kernel(ggain.shape[1], "tensor", *refs),
        out_shape=(
            jax.ShapeDtypeStruct((tokens, inner), BF16),
            jax.ShapeDtypeStruct((tokens, inner), BF16),
            jax.ShapeDtypeStruct((tokens, inner), F32),
            jax.ShapeDtypeStruct((8, inner), F32),
        ),
        grid=(tokens // SPAN,),
        in_specs=[tok, tok, tok, full(sums.shape), full(ggain.shape)],
        out_specs=(tok, tok, tok, full((8, inner))),
        compiler_params=pltpu.CompilerParams(dimension_semantics=("arbitrary",)),
        cost_estimate=cost(10.0),
        name="gating",
    )(gate, ssd, dn, sums, ggain)


def backward_kernel(
    dims, axis, base, count,
    docs_ref, mixed_ref, pre_ref, ssd_ref, stp_ref, state_ref, dssd_ref, dgate_ref,
    cw_ref, cb_ref, dtb_ref, dec_ref, skip_ref, pin_ref, din_ref, sin_ref,
    dall_ref, gconv_ref, gskip_ref, ghead_ref, pout_ref, dout_ref, sout_ref,
    pbuf, dbuf, dstate, par, cwb,
):
    inner, heads, inner_all = dims
    pairs = heads // 2
    chan = inner + 2 * LANES
    i = pl.program_id(0)
    c = base + count - 1 - i
    rank = lax.axis_index(axis)

    @pl.when(i == 0)
    def _():
        pbuf[SPAN : SPAN + 8] = pin_ref[...]
        dbuf[SPAN : SPAN + 8] = din_ref[...]
        dstate[...] = sin_ref[...]
        own_params(rank, heads, inner, inner_all, dtb_ref, dec_ref, skip_ref, cw_ref, cb_ref, par, cwb)
        gconv_ref[...] = jnp.zeros(gconv_ref.shape, F32)
        gskip_ref[...] = jnp.zeros(gskip_ref.shape, F32)
        ghead_ref[...] = jnp.zeros(ghead_ref.shape, F32)

    dall_ref[:, 0:inner] = dgate_ref[...]
    drow = docs_ref[pl.ds(c, 1), :].astype(F32)
    dcol = as_column(drow)
    before = docs_ref[pl.ds(jnp.maximum(c - 1, 0), 1), :].astype(F32)
    enter = as_column(before)[SPAN - 1 : SPAN]
    enter = jnp.where(c == 0, -1.0, enter)
    dbuf[0:SPAN] = dcol
    keeps = [None] + [dbuf[k : k + SPAN] == dcol for k in range(1, 4)]

    raw = stp_ref[...] + par[0:1]
    step = softplus(raw)
    row_i, col_i = iota((SPAN, SPAN), 0), iota((SPAN, SPAN), 1)
    tril = (row_i >= col_i).astype(BF16)
    log_step = step * par[1:2]
    running = tri_sum(tril, log_step, heads)
    run_rows = jnp.transpose(running)
    ending = running[SPAN - 1 : SPAN]
    tail = jnp.where(dcol == dcol[SPAN - 1 : SPAN], jnp.exp(ending - running), 0.0)
    reach = jnp.where(dcol == enter, jnp.exp(running), 0.0)
    same = jnp.concatenate([dcol, dcol], 1) == drow
    bias = jnp.where(same & (row_i <= col_i), 0.0, FAR)

    def activate(group):
        lanes = slice(group * LANES, (group + 1) * LANES)
        pre = pre_ref[:, lanes]
        sig = jax.nn.sigmoid(pre)
        return pre * sig, sig * (1.0 + pre * (1.0 - sig))

    b_act, b_slope = activate(pairs)
    c_act, c_slope = activate(pairs + 1)
    b_rows, c_rows = b_act.astype(BF16), c_act.astype(BF16)
    c_turned = jnp.transpose(c_act).astype(BF16)
    scores = exact_nt(b_act, c_act)
    low_half = iota((SPAN, LANES), 1) < LANES // 2
    half = SPAN // 2
    d_scores = [jnp.zeros((half, SPAN), F32), jnp.zeros((half, half), F32)]
    d_b = jnp.zeros((SPAN, LANES), F32)
    d_c = jnp.zeros((SPAN, LANES), F32)
    head_up = jnp.zeros((SPAN, LANES), F32)
    head_down = jnp.zeros((SPAN, LANES), F32)
    head_step = jnp.zeros((SPAN, LANES), F32)
    head_hold = jnp.zeros((8, LANES), F32)
    for pair in range(pairs):
        lanes = slice(pair * LANES, (pair + 1) * LANES)
        ones_at = (iota((LANES, LANES), 1) == 2 * pair + iota((LANES, LANES), 0) // (LANES // 2)).astype(BF16)

        def head_sum(v):
            hi = v.astype(BF16)
            low = (v - hi.astype(F32)).astype(BF16)
            return nn(hi, ones_at) + nn(low, ones_at)

        act, slope = activate(pair)
        step_l = pair_lanes(step, pair, low_half)
        tail_l = pair_lanes(tail, pair, low_half)
        reach_l = pair_lanes(reach, pair, low_half)
        skip_l = pair_lanes(par[2:3], pair, low_half[0:1])
        ssd = ssd_ref[:, lanes]
        d_ssd = dssd_ref[:, lanes]
        gskip_ref[:, lanes] += fold(d_ssd * act)
        dyb = d_ssd.astype(BF16)
        scaled = act * step_l
        xb = scaled.astype(BF16)
        held = state_ref[0, :, lanes]
        d_held = dstate[:, lanes]
        d_held_b = d_held.astype(BF16)
        ry = (d_ssd * reach_l).astype(BF16)
        xt = (scaled * tail_l).astype(BF16)
        parts = []
        for sub in range(2):
            head = 2 * pair + sub
            x_own = jnp.where(low_half if sub == 0 else ~low_half, scaled, 0.0).astype(BF16)
            blocks = []
            for blk in range(2):
                rows = slice(blk * half, (blk + 1) * half)
                cols = slice(blk * half, SPAN)
                gap = run_rows[head : head + 1, cols] - running[rows, head : head + 1]
                decay = jnp.exp(gap + bias[rows, cols])
                blocks.append(nn((decay * scores[rows, cols]).astype(BF16), dyb[cols]))
                d_scores[blk] = d_scores[blk] + decay * nt(x_own[rows], dyb[cols])
            parts.append(jnp.concatenate(blocks, 0))
        d_within = jnp.where(low_half, parts[0], parts[1])
        from_state = tail_l * nn(b_rows, d_held_b)
        d_scaled = d_within + from_state
        xf = xb.astype(F32)
        head_up += head_sum(dyb.astype(F32) * (ssd - skip_l * act) - xf * d_within)
        head_down += head_sum(xf * from_state)
        head_step += head_sum(d_scaled * act)
        hold = reach_l[SPAN - 1 : SPAN]
        hold_sum = jnp.sum((d_held * held.astype(F32)).reshape(LANES // 8, 8, LANES), axis=0) * hold
        head_hold += head_sum(hold_sum)
        d_b += nt(xt, d_held_b)
        d_c += nt(ry, held)
        dstate[:, lanes] = hold * d_held + nn(c_turned, ry)
        pbuf[0:SPAN, lanes] = (skip_l * d_ssd + step_l * d_scaled) * slope

    ds_b = jnp.concatenate(
        [
            d_scores[0],
            jnp.concatenate([jnp.zeros((half, half), F32), d_scores[1]], 1),
        ],
        0,
    )
    d_b += nn(ds_b.astype(BF16), c_rows)
    d_c += nn(jnp.transpose(ds_b).astype(BF16), b_rows)
    pbuf[0:SPAN, inner : inner + LANES] = d_b * b_slope
    pbuf[0:SPAN, inner + LANES : chan] = d_c * c_slope

    triu = (row_i <= col_i).astype(BF16)
    below = (row_i > col_i).astype(BF16)
    d_log = (
        tri_sum(triu, head_up, heads)
        + tri_sum(below, head_down, heads)
        + jnp.sum(head_hold, axis=0, keepdims=True)
    )
    d_step = d_log * par[1:2] + head_step
    d_raw = jnp.where(iota((SPAN, LANES), 1) < heads, d_step * jax.nn.sigmoid(raw), 0.0)
    dall_ref[:, inner + chan :] = d_raw.astype(BF16)
    ghead_ref[0] += fold(d_raw)
    ghead_ref[1] += fold(d_log * log_step)

    for group in range(chan // LANES):
        lanes = slice(group * LANES, (group + 1) * LANES)
        mixed = mixed_ref[:, lanes]
        own = pbuf[0:SPAN, lanes]
        acc = cwb[3:4, lanes] * own
        gconv_ref[3, :, lanes] += fold(mixed * own)
        gconv_ref[4, :, lanes] += fold(own)
        for k in range(1, 4):
            later = jnp.where(keeps[k], pbuf[k : k + SPAN, lanes], 0.0)
            acc = acc + cwb[3 - k : 4 - k, lanes] * later
            gconv_ref[3 - k, :, lanes] += fold(mixed * later)
        dall_ref[:, inner + group * LANES : inner + (group + 1) * LANES] = acc.astype(BF16)
    pbuf[SPAN : SPAN + 8] = pbuf[0:8]
    dbuf[SPAN : SPAN + 8] = dbuf[0:8]
    pout_ref[...] = pbuf[0:8]
    dout_ref[...] = dbuf[0:8]
    sout_ref[...] = dstate[...]


def mixer_backward(docs, arrays, params, carry, base, count, heads, inner_all):
    mixed, pre, ssd, stp, states, dssd, dgate = arrays
    tokens, inner = ssd.shape
    chan = inner + 2 * LANES
    width = inner + chan + LANES

    def tok(wide):
        return pl.BlockSpec((SPAN, wide), lambda i: (base + count - 1 - i, 0))

    def full(shape):
        return pl.BlockSpec(shape, lambda i: (0,) * len(shape))

    outs = (
        jax.ShapeDtypeStruct((count * SPAN, width), BF16),
        jax.ShapeDtypeStruct((5, 8, chan), F32),
        jax.ShapeDtypeStruct((8, inner), F32),
        jax.ShapeDtypeStruct((2, 8, LANES), F32),
        jax.ShapeDtypeStruct((8, chan), F32),
        jax.ShapeDtypeStruct((8, LANES), F32),
        jax.ShapeDtypeStruct((LANES, inner), F32),
    )
    consts = params + carry
    return pl.pallas_call(
        lambda *refs: backward_kernel((inner, heads, inner_all), "tensor", base, count, *refs),
        out_shape=outs,
        grid=(count,),
        in_specs=[
            full(docs.shape), tok(chan), tok(chan), tok(inner), tok(LANES),
            pl.BlockSpec((1, LANES, inner), lambda i: (base + count - 1 - i, 0, 0)),
            tok(inner), tok(inner),
        ]
        + [full(v.shape) for v in consts],
        out_specs=(pl.BlockSpec((SPAN, width), lambda i: (count - 1 - i, 0)),)
        + tuple(full(v.shape) for v in outs[1:]),
        scratch_shapes=[
            pltpu.VMEM((SPAN + 8, chan), F32),
            pltpu.VMEM((SPAN + 8, LANES), F32),
            pltpu.VMEM((LANES, inner), F32),
            pltpu.VMEM((8, LANES), F32),
            pltpu.VMEM((8, chan), F32),
        ],
        compiler_params=pltpu.CompilerParams(
            dimension_semantics=("arbitrary",), vmem_limit_bytes=VMEM_MOST
        ),
        cost_estimate=cost(20.0),
        name="mixer_backward",
    )(docs, mixed, pre, ssd, stp, states, dssd, dgate, *consts)


MESH_IDS = pl.DeviceIdType.MESH


def gather_kernel(
    dims, hid_ref, cot_ref, ngain_ref, w_ref, step_ref, wo_ref,
    win_ref, wout_ref, normed_ref, *refs,
):
    lines, depth, inner, inner_all, aligned = dims
    outs = refs[:4] if aligned else ()
    mine, zsend, zrecv, xsend, xrecv, takes, puts = refs[len(outs):]
    trank, drank = lax.axis_index("tensor"), lax.axis_index("dp")
    line, side = drank // 2, drank % 2
    model = hid_ref.shape[1]
    off = pl.multiple_of(trank * inner, LANES)
    pieces = (
        (w_ref, inner_all + off, win_ref, inner, inner),
        (w_ref, 2 * inner_all, win_ref, 2 * inner, 2 * LANES),
        (step_ref, 0, win_ref, 2 * inner + 2 * LANES, LANES),
        (w_ref, off, win_ref, 0, inner),
        (wo_ref, 0, wout_ref, 0, inner),
    )

    def peer(step):
        return {"dp": lax.rem(line + step, lines) * 2 + side}

    partner = {"dp": line * 2 + 1 - side}
    barrier = pltpu.get_barrier_semaphore()
    for step in range(1, lines):
        pl.semaphore_signal(barrier, inc=1, device_id=peer(step), device_id_type=MESH_IDS)
    pl.semaphore_signal(barrier, inc=1, device_id=partner, device_id_type=MESH_IDS)
    pl.semaphore_wait(barrier, lines)

    def rows(index):
        return pl.ds(pl.multiple_of(index * depth, depth), depth)

    def block(p, index):
        _, _, dst, at, width = pieces[p]
        return dst.at[rows(index), pl.ds(at, width)]

    def own(p):
        src, at, _, _, width = pieces[p]
        return src.at[:, pl.ds(at, width)]

    def z_copy(p, step, src, index):
        return pltpu.make_async_remote_copy(
            src_ref=src, dst_ref=block(p, index), send_sem=zsend.at[p, step - 1],
            recv_sem=zrecv.at[p, step - 1], device_id=peer(step), device_id_type=MESH_IDS,
        )

    def x_copy(p, step, src, index):
        return pltpu.make_async_remote_copy(
            src_ref=src, dst_ref=block(p, index), send_sem=xsend.at[p, step],
            recv_sem=xrecv.at[p, step], device_id=partner, device_id_type=MESH_IDS,
        )

    count = len(pieces)
    for p in range(count):
        for step in range(1, lines):
            z_copy(p, step, own(p), drank).start()
        x_copy(p, 0, own(p), drank).start()
    spots, at = [], 0
    for p in range(count):
        spots.append(mine.at[:, pl.ds(at, pieces[p][4])])
        at += pieces[p][4]
    fetched = [pltpu.make_async_copy(own(p), spots[p], takes.at[p]) for p in range(count)]
    for copy in fetched:
        copy.start()

    gain = ngain_ref[...]

    def normalize(hid, cot, normed, *sorted_refs):
        value = hid[...].astype(F32)
        inv = lax.rsqrt(jnp.mean(value * value, -1, keepdims=True) + EPS)
        normed[...] = (value * inv * gain).astype(BF16)
        if aligned:
            for src, away, here in (
                (normed, sorted_refs[0], sorted_refs[1]), (cot, sorted_refs[2], sorted_refs[3]),
            ):
                for j in range(lines):
                    first = lax.rem(line + j, lines) * 2
                    lanes = slice(j * depth, (j + 1) * depth)
                    away[:, lanes] = src[:, pl.ds(pl.multiple_of((first + 1 - side) * depth, depth), depth)]
                    here[:, lanes] = src[:, pl.ds(pl.multiple_of((first + side) * depth, depth), depth)]

    full = pl.BlockSpec((SPAN, model), lambda i: (i, 0))
    half = pl.BlockSpec((SPAN, lines * depth), lambda i: (i, 0))
    pltpu.emit_pipeline(
        normalize, grid=(hid_ref.shape[0] // SPAN,), in_specs=[full, full],
        out_specs=[full] + [half] * len(outs),
    )(hid_ref, cot_ref, normed_ref, *outs)

    stored = [pltpu.make_async_copy(spots[p], block(p, drank), puts.at[p]) for p in range(count)]
    for p in range(count):
        fetched[p].wait()
        stored[p].start()
    for p in range(count):
        for step in range(1, lines):
            source = lax.rem(line - step + lines, lines) * 2 + side
            got = block(p, source)
            z_copy(p, step, got, source).wait_recv()
            x_copy(p, step, got, source).start()
    for p in range(count):
        for step in range(lines):
            source = lax.rem(line - step + lines, lines) * 2 + 1 - side
            x_copy(p, step, block(p, source), source).wait_recv()
    for p in range(count):
        for step in range(1, lines):
            z_copy(p, step, own(p), drank).wait_send()
        for step in range(lines):
            x_copy(p, step, own(p), drank).wait_send()
        stored[p].wait()


def gather_weights(hidden, cotangent, norm_gain, in_weight, own_step, out_weight, lines, inner_all):
    tokens, model = hidden.shape
    depth, inner = out_weight.shape
    aligned = depth % LANES == 0
    width = 2 * inner + 3 * LANES
    half = jax.ShapeDtypeStruct((tokens, lines * depth), BF16)
    anywhere = pl.BlockSpec(memory_space=pl.ANY)
    outs = (
        jax.ShapeDtypeStruct((model, width), BF16),
        jax.ShapeDtypeStruct((model, inner), BF16),
        jax.ShapeDtypeStruct((tokens, model), BF16),
    ) + (half,) * (4 if aligned else 0)
    dma = pltpu.SemaphoreType.DMA
    return pl.pallas_call(
        lambda *refs: gather_kernel((lines, depth, inner, inner_all, aligned), *refs),
        out_shape=outs,
        in_specs=[anywhere, anywhere, pl.BlockSpec(memory_space=pltpu.VMEM)] + [anywhere] * 3,
        out_specs=(anywhere,) * len(outs),
        scratch_shapes=[
            pltpu.VMEM((depth, width + inner), BF16),
            dma((5, max(1, lines - 1))), dma((5, max(1, lines - 1))), dma((5, lines)), dma((5, lines)),
            dma((5,)), dma((5,)),
        ],
        compiler_params=pltpu.CompilerParams(collective_id=0, has_side_effects=True),
        cost_estimate=cost(45.0),
        name="gather_weights",
    )(hidden, cotangent, norm_gain, in_weight, own_step, out_weight)


def tail_kernel(
    dims, da_ref, db_ref, naway_ref, nhere_ref, w_ref, hid_ref, ngain_ref, ggate_ref, flat_ref,
    delta_ref, gin_ref, flatout_ref,
    da, db, naway, nhere, w, hid, loads,
    x_out, x_in, x_sem, here, low, z_in, z_sem, total,
    h_out, h_in, h_sem, mine, y_in, y_sem, done, d_sem, delta_sem,
    gates, g_sem, values, v_sem, shared, s_sem, put_sem,
    flat, flat_in, f_sem,
):
    lines, depth, inner, heads, inner_all = dims
    trank, drank = lax.axis_index("tensor"), lax.axis_index("dp")
    line, side = drank // 2, drank % 2
    core = trank % 2
    across = {"tensor": trank + 1 - 2 * core}
    beyond = {"tensor": (trank + 2) % 4}
    partner = {"dp": line * 2 + 1 - side}
    half = da_ref.shape[0]
    part = half // 2
    wide = inner + 3 * LANES
    blocks = lines * depth // LANES
    pieces = part // LANES

    def peer(step):
        return {"dp": lax.rem(line + step, lines) * 2 + side}

    barrier = pltpu.get_barrier_semaphore()
    for device in [across, beyond, partner] + [peer(step) for step in range(1, lines)]:
        pl.semaphore_signal(barrier, inc=1, device_id=device, device_id_type=MESH_IDS)
    pl.semaphore_wait(barrier, lines + 2)

    def remote(src, dst, sems, index, device):
        return pltpu.make_async_remote_copy(
            src_ref=src, dst_ref=dst, send_sem=sems.at[0, index], recv_sem=sems.at[1, index],
            device_id=device, device_id_type=MESH_IDS,
        )

    gate_near = remote(ggate_ref, gates.at[1], g_sem, 0, across)
    gate_far = remote(ggate_ref, gates.at[2], g_sem, 1, beyond)
    gate_pass = remote(gates.at[2], gates.at[3], g_sem, 2, across)
    gate_near.start()
    gate_far.start()

    fetch = [
        pltpu.make_async_copy(src, dst, loads.at[k])
        for k, (src, dst) in enumerate(
            (
                (naway_ref, naway), (da_ref, da), (db_ref, db), (w_ref, w), (hid_ref, hid),
                (nhere_ref, nhere), (ggate_ref, gates.at[0]), (flat_ref, flat),
            )
        )
    ]
    for copy in fetch:
        copy.start()

    def block_rows(k):
        return pl.ds(pl.multiple_of(k * LANES, LANES), LANES)

    def weight_grad(source, k):
        cols = block_rows(k)
        return tn(source[0:half, cols], da[:, inner:]) + tn(source[half : 2 * half, cols], db[:, inner:])

    def x_copy(k):
        rows = block_rows(k)
        return remote(x_out.at[rows], x_in.at[rows], x_sem, k, partner)

    for copy in fetch[:3]:
        copy.wait()

    def send_block(k, carry):
        x_out[block_rows(k)] = weight_grad(naway, k).astype(BF16)
        x_copy(k).start()
        return carry

    lax.fori_loop(0, blocks, send_block, 0)

    for copy in fetch[3:5]:
        copy.wait()

    def share(start, k):
        rows = pl.ds(pl.multiple_of(start + k * LANES, LANES), LANES)
        made = nt(da[rows], w[...])
        value = hid[rows].astype(F32)
        inv = lax.rsqrt(jnp.mean(value * value, -1, keepdims=True) + EPS)
        return made, jnp.sum(made * (value * inv), axis=0, keepdims=True)

    def h_copy(k):
        rows = block_rows(k)
        return remote(h_out.at[rows], h_in.at[rows], h_sem, k, across)

    def send_share(k, norm):
        made, part_sum = share((1 - core) * part, k)
        h_out[block_rows(k)] = made.astype(BF16)
        h_copy(k).start()
        return norm + part_sum

    norm = lax.fori_loop(0, pieces, send_share, jnp.zeros((1, w.shape[0]), F32))

    def y_copy(k):
        rows = block_rows(k)
        return remote(mine.at[rows], y_in.at[rows], y_sem, k, beyond)

    def join_share(k, norm):
        made, part_sum = share(core * part, k)
        h_copy(k).wait_recv()
        mine[block_rows(k)] = (made + h_in[block_rows(k)].astype(F32)).astype(BF16)
        y_copy(k).start()
        return norm + part_sum

    norm = lax.fori_loop(0, pieces, join_share, norm)
    gate_far.wait_recv()
    gate_pass.start()

    fetch[7].wait()
    for k in range(w.shape[0] // LANES):
        flat[k : k + 1] = flat[k : k + 1] + norm[:, k * LANES : (k + 1) * LANES]
    hops = [across, beyond, partner]
    bit = 1
    while bit < lines:
        hops.append({"dp": (line + bit * (1 - 2 * ((line // bit) % 2))) * 2 + side})
        bit *= 2

    def flat_copy(k):
        return remote(flat.at[...] if k == 0 else flat_in.at[len(hops) + k], flat_in.at[k], f_sem, k, hops[k])

    flat_copy(0).start()
    fetch[5].wait()

    def keep_block(k, carry):
        here[block_rows(k)] = weight_grad(nhere, k)
        return carry

    lax.fori_loop(0, blocks, keep_block, 0)

    def flat_step(k):
        flat_copy(k).wait_recv()
        held = flat[...] if k == 0 else flat_in[len(hops) + k]
        held = held + flat_in[k]
        if k + 1 < len(hops):
            flat_in[len(hops) + k + 1] = held
            flat_copy(k + 1).start()
        return held

    flat_step(0)

    def z_copy(step):
        rows = pl.ds(step * depth, depth)
        return remote(low.at[rows], z_in.at[step - 1], z_sem, step - 1, peer(step))

    per = LANES // depth
    for k in range(blocks):
        x_copy(k).wait_recv()
        rows = slice(k * LANES, (k + 1) * LANES)
        joined = here[rows] + x_in[rows].astype(F32)
        low[rows] = joined.astype(BF16)
        if k == 0:
            total[...] = joined[0:depth]
        for step in range(max(1, k * per), (k + 1) * per):
            z_copy(step).start()
        if k == 0:
            flat_step(1)

    gain = ngain_ref[...]

    def done_copy(k):
        rows = block_rows(k)
        return remote(done.at[0, rows], done.at[1, rows], d_sem, k, across)

    def own_rows(k):
        return pl.ds(pl.multiple_of(core * part + k * LANES, LANES), LANES)

    def own_put(k):
        return pltpu.make_async_copy(done.at[0, block_rows(k)], delta_ref.at[own_rows(k)], delta_sem.at[0, k])

    def finish(k, carry):
        y_copy(k).wait_recv()
        rows = block_rows(k)
        d_hidden = mine[rows].astype(F32) + y_in[rows].astype(F32)
        value = hid[own_rows(k)].astype(F32)
        inv = lax.rsqrt(jnp.mean(value * value, -1, keepdims=True) + EPS)
        scaled = d_hidden * gain
        pull = jnp.mean(scaled * value, -1, keepdims=True)
        done[0, rows] = (inv * scaled - value * (inv * inv * inv) * pull).astype(BF16)
        done_copy(k).start()
        own_put(k).start()
        return carry

    lax.fori_loop(0, pieces, finish, 0)
    flat_step(2)

    for step in range(1, lines):
        z_copy(step).wait_recv()
        total[...] += z_in[step - 1].astype(F32)
    values[0] = total[:, 0:inner]
    shared[0, :, 0 : 2 * LANES] = total[:, inner : inner + 2 * LANES]
    steps = pltpu.roll(total[:, inner + 2 * LANES :], trank * heads, 1)
    lane = iota(steps.shape, 1) - trank * heads
    shared[0, :, 2 * LANES :] = jnp.where((lane >= 0) & (lane < heads), steps, 0.0)
    shared_near = remote(shared.at[0], shared.at[1], s_sem, 0, across)
    shared_far = remote(shared.at[2], shared.at[3], s_sem, 1, beyond)
    value_near = remote(values.at[0], values.at[1], v_sem, 0, across)
    value_far = remote(values.at[0], values.at[2], v_sem, 1, beyond)
    value_pass = remote(values.at[2], values.at[3], v_sem, 2, across)
    shared_near.start()
    value_far.start()
    value_near.start()

    last = flat_in.shape[0] - 1
    for k in range(3, len(hops)):
        held = flat_step(k)
    flat_in[last] = held
    flat_put = pltpu.make_async_copy(flat_in.at[last], flatout_ref, put_sem.at[9])
    flat_put.start()

    shared_near.wait_recv()
    shared[2] = shared[0] + shared[1]
    shared_far.start()

    def put(source, k, first, column_of, index):
        column = pl.multiple_of(first + column_of * inner, LANES)
        return pltpu.make_async_copy(source.at[k], gin_ref.at[:, pl.ds(column, inner)], put_sem.at[index])

    owners = (trank, trank + 1 - 2 * core, (trank + 2) % 4, (trank + 1 - 2 * core + 2) % 4)
    fetch[6].wait()
    puts = [put(gates, 0, 0, owners[0], 0), put(values, 0, inner_all, owners[0], 4)]
    puts[0].start()
    puts[1].start()

    def other_put(k):
        rows = block_rows(k)
        dst = pl.ds(pl.multiple_of((1 - core) * part + k * LANES, LANES), LANES)
        return pltpu.make_async_copy(done.at[1, rows], delta_ref.at[dst], delta_sem.at[1, k])

    def other_rows(k, carry):
        done_copy(k).wait_recv()
        other_put(k).start()
        return carry

    lax.fori_loop(0, pieces, other_rows, 0)
    for k, (near, far, passed, source, first, at) in enumerate(
        (
            (gate_near, gate_far, gate_pass, gates, 0, 0),
            (value_near, value_far, value_pass, values, inner_all, 4),
        )
    ):
        near.wait_recv()
        if k == 1:
            far.wait_recv()
            passed.start()
        puts += [put(source, 1, first, owners[1], at + 1), put(source, 2, first, owners[2], at + 2)]
        puts[-2].start()
        puts[-1].start()
    shared_far.wait_recv()
    shared[1] = shared[2] + shared[3]
    shared_put = pltpu.make_async_copy(
        shared.at[1], gin_ref.at[:, pl.ds(2 * inner_all, 3 * LANES)], put_sem.at[8]
    )
    shared_put.start()
    for passed, source, first, at in ((gate_pass, gates, 0, 3), (value_pass, values, inner_all, 7)):
        passed.wait_recv()
        puts.append(put(source, 3, first, owners[3], at))
        puts[-1].start()

    def drain(k, carry):
        h_copy(k).wait_send()
        y_copy(k).wait_send()
        done_copy(k).wait_send()
        own_put(k).wait()
        other_put(k).wait()
        return carry

    lax.fori_loop(0, pieces, drain, 0)
    for k in range(blocks):
        x_copy(k).wait_send()
    for step in range(1, lines):
        z_copy(step).wait_send()
    for copy in (
        gate_near, gate_far, gate_pass, value_near, value_far, value_pass, shared_near, shared_far,
    ):
        copy.wait_send()
    for k in range(len(hops)):
        flat_copy(k).wait_send()
    for copy in puts + [shared_put, flat_put]:
        copy.wait()


def tail(da, db, naway, nhere, w, hid, norm_gain, ggate, flat, lines, depth, heads, inner_all):
    half, width = da.shape
    model = w.shape[0]
    inner = ggate.shape[1]
    wide = width - inner
    part = half // 2
    blocks, pieces = lines * depth // LANES, part // LANES
    hops = 3 + (lines - 1).bit_length()
    dma = pltpu.SemaphoreType.DMA
    vmem = pltpu.VMEM
    anywhere = pl.BlockSpec(memory_space=pl.ANY)
    fars = max(1, lines - 1)
    return pl.pallas_call(
        lambda *refs: tail_kernel((lines, depth, inner, heads, inner_all), *refs),
        out_shape=(
            jax.ShapeDtypeStruct((half, model), BF16),
            jax.ShapeDtypeStruct((depth, 2 * inner_all + 3 * LANES), F32),
            jax.ShapeDtypeStruct(flat.shape, F32),
        ),
        in_specs=[anywhere] * 6 + [pl.BlockSpec(memory_space=vmem)] + [anywhere] * 2,
        out_specs=(anywhere,) * 3,
        scratch_shapes=[
            vmem(da.shape, BF16), vmem(db.shape, BF16), vmem(naway.shape, BF16), vmem(nhere.shape, BF16),
            vmem(w.shape, BF16), vmem(hid.shape, BF16), dma((8,)),
            vmem((lines * depth, wide), BF16), vmem((lines * depth, wide), BF16), dma((2, blocks)),
            vmem((lines * depth, wide), F32), vmem((lines * depth, wide), BF16),
            vmem((fars, depth, wide), BF16), dma((2, fars)), vmem((depth, wide), F32),
            vmem((part, model), BF16), vmem((part, model), BF16), dma((2, pieces)),
            vmem((part, model), BF16), vmem((part, model), BF16), dma((2, pieces)),
            vmem((2, part, model), BF16), dma((2, pieces)), dma((2, pieces)),
            vmem((4, depth, inner), F32), dma((2, 3)),
            vmem((4, depth, inner), F32), dma((2, 3)),
            vmem((4, depth, 3 * LANES), F32), dma((2, 2)), dma((10,)),
            vmem(flat.shape, F32), vmem((2 * hops + 1,) + flat.shape, F32), dma((2, hops)),
        ],
        compiler_params=pltpu.CompilerParams(
            collective_id=1, has_side_effects=True, vmem_limit_bytes=VMEM_MOST
        ),
        cost_estimate=cost(45.0),
        name="tail",
    )(da, db, naway, nhere, w, hid, norm_gain, ggate, flat)


def swap(v, axis, to):
    return lax.ppermute(v, axis, [(k, to(k)) for k in range(lax.axis_size(axis))])


def tie(*items):
    return lax.optimization_barrier(items)


def flip(bits):
    return lambda k: k ^ bits


def body(
    hidden_in, doc_ids, cotangent, norm_gain, in_weight, conv_weight, conv_bias,
    dt_bias, log_decay, skip_gain, gate_gain, out_weight,
):
    tcount, dcount = lax.axis_size("tensor"), lax.axis_size("dp")
    trank, drank = lax.axis_index("tensor"), lax.axis_index("dp")
    lines = dcount // 2
    line, side = drank // 2, drank % 2
    core = trank % 2
    inner_all, head_all = gate_gain.shape[0], dt_bias.shape[0]
    inner, heads = inner_all // tcount, head_all // tcount
    tokens, model = hidden_in.shape
    base_bc = 2 * inner_all
    base_dt = base_bc + 2 * LANES
    depth = in_weight.shape[0]
    chan = inner + 2 * LANES

    def line_to(step):
        return lambda k: ((k // 2 + step) % lines) * 2 + k % 2

    own_step = jnp.pad(
        lax.dynamic_slice_in_dim(in_weight, base_dt + trank * heads, heads, 1),
        ((0, 0), (0, LANES - heads)),
    )
    w_in, w_out, normed, *sorted_parts = gather_weights(
        hidden_in, cotangent, norm_gain.reshape(1, -1), in_weight, own_step, out_weight,
        lines, inner_all,
    )
    if not sorted_parts:

        def features(v, which):
            return jnp.concatenate(
                [
                    lax.dynamic_slice_in_dim(v, (((line + j) % lines) * 2 + which) * depth, depth, 1)
                    for j in range(lines)
                ],
                1,
            )

        sorted_parts = [features(v, which) for v in (normed, cotangent) for which in (1 - side, side)]
    n_away, n_here, c_away, c_here = sorted_parts

    def row(v):
        return v.reshape(1, -1)

    docs = doc_ids.reshape(tokens // SPAN, SPAN)
    spans = tokens // SPAN
    count = spans // 2
    span_rows = count * SPAN
    part = span_rows // 2
    params = (conv_weight, row(conv_bias), row(dt_bias), row(log_decay), row(skip_gain))

    def own_share(left, right):
        def make(start):
            return nt(lax.dynamic_slice_in_dim(left, start, part, 0), right)

        got = swap(make((1 - core) * part).astype(BF16), "tensor", flip(1))
        return (make(core * part) + got.astype(F32)).astype(BF16)

    def chips_sum(mine, theirs):
        return mine.astype(F32) + theirs.astype(F32)

    def both(own):
        got = swap(own, "tensor", flip(1))
        return [jnp.where(core == 0, own, got), jnp.where(core == 0, got, own)]

    def my_rows(v, h):
        return lax.dynamic_slice_in_dim(v, h * span_rows + core * part, part, 0)

    carry = (
        jnp.zeros((8, chan), F32), jnp.full((8, LANES), -1.0, F32), jnp.zeros((LANES, inner), F32),
    )
    def forward(h, carry, held):
        return mixer_forward(
            docs, normed, cotangent, w_in, w_out, params, row(gate_gain), carry, held,
            h * count, count, heads,
        )

    made = forward(0, carry, ())
    held, gg, sums_a, carry = made[:7], made[7], made[8], made[9:]
    out_a = own_share(gg, w_out)
    out_a, carry = tie(out_a, carry)
    far_a = swap(out_a, "tensor", flip(2))
    made = forward(1, carry, held)
    held, gg, sums_b = made[:7], made[7], made[8]
    sums = jnp.concatenate([sums_a, sums_b], 1)
    sums = sums + swap(sums, "tensor", flip(1))
    sums = sums + swap(sums, "tensor", flip(2))
    out_b = own_share(gg, w_out)
    out_b, sums, far_a = tie(out_b, sums, far_a)
    far_b = swap(out_b, "tensor", flip(2))
    gate, mixed, pre, ssd, stp, states, dn = held
    nout, d_gate, d_ssd, g_gain = gating(gate, ssd, dn, sums, row(gate_gain))
    inv_gate = lax.rsqrt(sums[0].reshape(tokens, 1) * (1.0 / inner_all) + EPS)

    def to_side(away):
        return swap(away, "dp", flip(1))

    def to_lines(here, got):
        here = here + got.astype(F32)
        return here, [here[j * depth : (j + 1) * depth].astype(BF16) for j in range(1, lines)]

    def lines_sum(here, low):
        total = here[:depth]
        for j in range(1, lines):
            total = total + swap(low[j - 1], "dp", line_to(j)).astype(F32)
        return total

    o_away, g_away = tn(c_away, nout).astype(BF16), tn(n_away, d_gate).astype(BF16)
    o_here, g_here = tn(c_here, nout), tn(n_here, d_gate)
    o_away, g_away, o_here, g_here, d_ssd = tie(o_away, g_away, o_here, g_here, d_ssd)
    o_got, g_got = to_side(o_away), to_side(g_away)

    def backward(h, carry, d_ssd):
        return mixer_backward(
            docs, (mixed, pre, ssd, stp, states, d_ssd, d_gate), params, carry,
            h * count, count, heads, inner_all,
        )

    carry = (
        jnp.zeros((8, chan), F32), jnp.full((8, LANES), -2.0, F32), jnp.zeros((LANES, inner), F32),
    )
    d_b, conv_b, skip_b, head_b, *carry = backward(1, carry, d_ssd)
    d_b, o_got, g_got, far_b = tie(d_b, o_got, g_got, far_b)
    o_here, o_low = to_lines(o_here, o_got)
    g_here, g_low = to_lines(g_here, g_got)
    hid_b = own_share(d_b, w_in)
    o_low, g_low, hid_b, carry = tie(o_low, g_low, hid_b, tuple(carry))
    hid_far_b = swap(hid_b, "tensor", flip(2))
    g_out, g_gate = lines_sum(o_here, o_low), lines_sum(g_here, g_low)
    d_a, conv_a, skip_a, head_a, *_ = backward(0, carry, d_ssd)
    d_a, g_out, g_gate, hid_far_b = tie(d_a, g_out, g_gate, hid_far_b)
    g_conv, g_skip, g_head = conv_a + conv_b, skip_a + skip_b, head_a + head_b

    def input_grad(h, d_hidden):
        hid = my_rows(hidden_in, h).astype(F32)
        inv = lax.rsqrt(jnp.mean(hid * hid, -1, keepdims=True) + EPS)
        scaled = d_hidden * norm_gain
        pull = jnp.mean(scaled * hid, -1, keepdims=True)
        norm = jnp.sum(d_hidden * hid * inv, 0) * (trank < 2).astype(F32)
        return (inv * scaled - hid * inv**3 * pull).astype(BF16), norm

    layer_out = []
    for h, out in ((0, chips_sum(out_a, far_a)), (1, chips_sum(out_b, far_b))):
        hid = my_rows(hidden_in, h).astype(F32)
        layer_out += both((hid + out * my_rows(inv_gate, h)).astype(BF16))
    layer_out = jnp.concatenate(layer_out, 0)
    delta_b, norm_b = input_grad(1, chips_sum(hid_b, hid_far_b))
    delta_b = both(delta_b)

    conv = jnp.sum(g_conv, 1)
    head = jnp.sum(g_head, 1)
    skip = jnp.sum(jnp.sum(g_skip, 0).reshape(heads, -1), 1)
    spot = trank * inner

    def place(v, total, start):
        return lax.dynamic_update_slice_in_dim(
            jnp.zeros(v.shape[:-1] + (total,), F32), v, start, v.ndim - 1
        )

    conv_all = place(conv[:, :inner], inner_all + 2 * LANES, spot).at[:, inner_all:].set(conv[:, inner:])
    heads_all = place(jnp.stack([head[0, :heads], head[1, :heads], skip]), head_all, trank * heads)
    flat = jnp.concatenate(
        [norm_b, conv_all.reshape(-1), heads_all.reshape(-1), place(jnp.sum(g_gain, 0), inner_all, spot)]
    )
    flat = jnp.pad(flat, (0, -flat.shape[0] % 1024)).reshape(-1, LANES)

    delta_a, grad_in, flat = tail(
        d_a, d_b, n_away, n_here, w_in, hidden_in[:span_rows], row(norm_gain), g_gate, flat,
        lines, depth, heads, inner_all,
    )
    grad_input = cotangent.astype(F32) + jnp.concatenate([delta_a] + delta_b, 0).astype(F32)
    grad_in_weight = grad_in[:, : in_weight.shape[1]]

    flat = flat.reshape(-1)
    cuts, at = [], 0
    for size in (model, 5 * conv_all.shape[1], 3 * head_all, inner_all):
        cuts.append(flat[at : at + size])
        at += size
    conv_all = cuts[1].reshape(5, -1)
    heads_all = cuts[2].reshape(3, -1)
    return (
        layer_out, grad_input, cuts[0], grad_in_weight, conv_all[:4], conv_all[4],
        heads_all[0], heads_all[1], heads_all[2], cuts[3], g_out,
    )


def solution(mesh):
    rows, whole = P("dp", None), P()
    return jax.shard_map(
        body,
        mesh=mesh,
        in_specs=(rows, rows, rows, whole, rows, whole, whole, whole, whole, whole, whole, P("dp", "tensor")),
        out_specs=(rows, rows, whole, rows, whole, whole, whole, whole, whole, whole, P("dp", "tensor")),
        check_vma=False,
    )
```

```python
import jax
import jax.numpy as jnp
from jax import lax
from jax.experimental import pallas as pl
from jax.experimental.pallas import tpu as pltpu
from jax.sharding import PartitionSpec as P

SPAN = 256
LANES = 128
EPS = 1e-05
FAR = -1e30
VMEM_MOST = 60 * 2**20
F32 = jnp.float32
BF16 = jnp.bfloat16


def cost(micros):
    return pl.CostEstimate(flops=int(micros * 1.15e9), bytes_accessed=1 << 20, transcendentals=0)


def nn(a, b):
    return lax.dot_general(a, b, (((1,), (0,)), ((), ())), preferred_element_type=F32)


def nt(a, b):
    return lax.dot_general(a, b, (((1,), (1,)), ((), ())), preferred_element_type=F32)


def tn(a, b):
    return lax.dot_general(a, b, (((0,), (0,)), ((), ())), preferred_element_type=F32)


def iota(shape, dim):
    return lax.broadcasted_iota(jnp.int32, shape, dim)


def as_column(row, rows=SPAN):
    return jnp.transpose(jnp.broadcast_to(row, (LANES, rows)))


def as_row(block):
    return jnp.sum(jnp.transpose(block), axis=0, keepdims=True)


def split3(v):
    hi = v.astype(BF16)
    rest = v - hi.astype(F32)
    mid = rest.astype(BF16)
    low = (rest - mid.astype(F32)).astype(BF16)
    return hi, mid, low


def tri_sum(tri, v, heads):
    lane = iota(v.shape, 1)
    v = jnp.where(lane < heads, v, 0.0)
    hi = v.astype(BF16).astype(F32)
    rest = v - hi
    mid = rest.astype(BF16).astype(F32)
    low = rest - mid
    packed = hi + pltpu.roll(mid, heads, 1) + pltpu.roll(low, 2 * heads, 1)
    out = nn(tri, packed.astype(BF16))
    return out + pltpu.roll(out, LANES - heads, 1) + pltpu.roll(out, LANES - 2 * heads, 1)


def pair_lanes(cols, pair, low_half):
    rows = cols.shape[0]
    first = jnp.broadcast_to(cols[:, 2 * pair : 2 * pair + 1], (rows, LANES))
    second = jnp.broadcast_to(cols[:, 2 * pair + 1 : 2 * pair + 2], (rows, LANES))
    return jnp.where(low_half, first, second)


def exact_nt(a, b):
    a_hi, b_hi = a.astype(BF16), b.astype(BF16)
    a_lo = (a - a_hi.astype(F32)).astype(BF16)
    b_lo = (b - b_hi.astype(F32)).astype(BF16)
    return nt(a_hi, b_hi) + (nt(a_hi, b_lo) + nt(a_lo, b_hi))


def softplus(v):
    return jnp.maximum(v, 0.0) + jnp.log1p(jnp.exp(-jnp.abs(v)))


def own_lanes(row, rank, heads):
    total = row.shape[1]
    pick = (iota((total, LANES), 0) == rank * heads + iota((total, LANES), 1)) & (
        iota((total, LANES), 1) < heads
    )
    wide = jnp.broadcast_to(row, (8, total))
    out = lax.dot_general(
        wide, pick.astype(F32), (((1,), (0,)), ((), ())),
        precision=lax.Precision.HIGHEST, preferred_element_type=F32,
    )
    return out[0:1]


def fold(v):
    return jnp.sum(v.reshape(SPAN // 8, 8, v.shape[1]), axis=0)


def own_params(rank, heads, inner, inner_all, dtb_ref, dec_ref, skip_ref, cw_ref, cb_ref, par, cwb):
    chan = inner + 2 * LANES
    off = pl.multiple_of(rank * inner, LANES)
    taps = cw_ref.shape[0]
    par[0:1] = own_lanes(dtb_ref[...], rank, heads)
    par[1:2] = -jnp.exp(own_lanes(dec_ref[...], rank, heads))
    par[2:3] = own_lanes(skip_ref[...], rank, heads)
    cwb[0:taps, 0:inner] = cw_ref[:, pl.ds(off, inner)].astype(F32)
    cwb[0:taps, inner:chan] = cw_ref[:, inner_all:].astype(F32)
    cwb[taps : taps + 1, 0:inner] = cb_ref[:, pl.ds(off, inner)]
    cwb[taps : taps + 1, inner:chan] = cb_ref[:, inner_all:]


MESH_IDS = pl.DeviceIdType.MESH


def forward_kernel(
    dims, docs_ref, normed_ref, cot_ref, win_ref, wout_ref, cw_ref, cb_ref,
    dtb_ref, dec_ref, skip_ref, ggain_ref,
    gate_ref, mixed_ref, pre_ref, ssd_ref, stp_ref, state_ref, dn_ref,
    sums_ref, mine_ref, far_ref,
    xbuf, dbuf, state, par, cwb, gain, gg_ref,
    own_sums, h_out, h_in, kept, mine, far, h_sem, y_sem, s_in, s_sem, put_sem,
):
    inner, heads, early = dims
    pairs = heads // 2
    chan = inner + 2 * LANES
    i = pl.program_id(0)
    spans = pl.num_programs(0)
    rank = lax.axis_index("tensor")
    core = rank % 2
    inner_all = ggain_ref.shape[1]
    half = SPAN // 2
    across = {"tensor": rank + 1 - 2 * core}
    beyond = {"tensor": (rank + 2) % 4}
    crossed = {"tensor": (rank + 3 - 2 * core) % 4}

    @pl.when(i == 0)
    def _():
        barrier = pltpu.get_barrier_semaphore()
        for device in (across, beyond, crossed):
            pl.semaphore_signal(barrier, inc=1, device_id=device, device_id_type=MESH_IDS)
        pl.semaphore_wait(barrier, 3)
        xbuf[0:8] = jnp.zeros((8, chan), F32)
        dbuf[0:8] = jnp.full((8, LANES), -1.0, F32)
        state[...] = jnp.zeros(state.shape, F32)
        own_params(rank, heads, inner, inner_all, dtb_ref, dec_ref, skip_ref, cw_ref, cb_ref, par, cwb)
        gain[0:1] = ggain_ref[:, pl.ds(pl.multiple_of(rank * inner, LANES), inner)]

    def slot(k):
        return pl.ds(pl.multiple_of(k * half, half), half)

    def h_copy(k):
        return pltpu.make_async_remote_copy(
            src_ref=h_out.at[slot(k)], dst_ref=h_in.at[slot(k)], send_sem=h_sem.at[0, k],
            recv_sem=h_sem.at[1, k], device_id=across, device_id_type=MESH_IDS,
        )

    def y_copy(k):
        return pltpu.make_async_remote_copy(
            src_ref=mine.at[slot(k)], dst_ref=far.at[slot(k)], send_sem=y_sem.at[0, k],
            recv_sem=y_sem.at[1, k], device_id=beyond, device_id_type=MESH_IDS,
        )

    def join(k):
        h_copy(k).wait_recv()
        mine[slot(k)] = (kept[...] + h_in[slot(k)].astype(F32)).astype(BF16)

    @pl.when(i > 0)
    def _():
        join(i - 1)

        @pl.when(i - 1 < early)
        def _():
            y_copy(i - 1).start()

    nb = normed_ref[...]
    xbuf[8 : 8 + SPAN] = nn(nb, win_ref[:, inner : inner + chan])
    gate_ref[...] = nn(nb, win_ref[:, 0:inner])
    stp = nn(nb, win_ref[:, inner + chan : inner + chan + LANES])
    stp_ref[...] = stp
    mixed_ref[...] = xbuf[8 : 8 + SPAN]
    dn_ref[...] = nn(cot_ref[...], wout_ref[...])

    drow = docs_ref[:, pl.ds(pl.multiple_of(i * SPAN, SPAN), SPAN)].astype(F32)
    dcol = as_column(drow)
    enter = dbuf[7:8]
    dbuf[8 : 8 + SPAN] = dcol
    keeps = [None] + [dbuf[8 - k : 8 - k + SPAN] == dcol for k in range(1, 4)]

    def conv(group):
        lanes = slice(group * LANES, (group + 1) * LANES)
        acc = cwb[4:5, lanes] + cwb[3:4, lanes] * xbuf[8 : 8 + SPAN, lanes]
        for k in range(1, 4):
            acc = acc + cwb[3 - k : 4 - k, lanes] * jnp.where(
                keeps[k], xbuf[8 - k : 8 - k + SPAN, lanes], 0.0
            )
        pre_ref[:, lanes] = acc
        return acc * jax.nn.sigmoid(acc)

    b_act, c_act = conv(pairs), conv(pairs + 1)
    b_rows, c_rows = b_act.astype(BF16), c_act.astype(BF16)

    step = softplus(stp + par[0:1])
    row_i, col_i = iota((SPAN, SPAN), 0), iota((SPAN, SPAN), 1)
    tril = (row_i >= col_i).astype(BF16)
    running = tri_sum(tril, step * par[1:2], heads)
    run_rows = jnp.transpose(running)
    ending = running[SPAN - 1 : SPAN]
    tail = jnp.where(dcol == dcol[SPAN - 1 : SPAN], jnp.exp(ending - running), 0.0)
    reach = jnp.where(dcol == enter, jnp.exp(running), 0.0)
    same = jnp.concatenate([dcol, dcol], 1) == drow
    bias = jnp.where(same & (row_i >= col_i), 0.0, FAR)
    scores = exact_nt(c_act, b_act)
    b_turned = jnp.transpose(b_act).astype(BF16)
    low_half = iota((SPAN, LANES), 1) < LANES // 2
    square = jnp.zeros((SPAN, LANES), F32)
    cross = jnp.zeros((SPAN, LANES), F32)
    for pair in range(pairs):
        lanes = slice(pair * LANES, (pair + 1) * LANES)
        act = conv(pair)
        scaled = act * pair_lanes(step, pair, low_half)
        xb = scaled.astype(BF16)
        tail_l = pair_lanes(tail, pair, low_half)
        reach_l = pair_lanes(reach, pair, low_half)
        held = state[:, lanes]
        held_b = held.astype(BF16)
        state_ref[0, :, lanes] = held_b
        state[:, lanes] = nn(b_turned, (scaled * tail_l).astype(BF16)) + reach_l[SPAN - 1 : SPAN] * held
        out = reach_l * nn(c_rows, held_b)
        parts = []
        for sub in range(2):
            head = 2 * pair + sub
            blocks = []
            for blk in range(2):
                rows = slice(blk * half, (blk + 1) * half)
                width = (blk + 1) * half
                gap = running[rows, head : head + 1] - run_rows[head : head + 1, 0:width]
                weight = jnp.exp(gap + bias[rows, 0:width]) * scores[rows, 0:width]
                blocks.append(nn(weight.astype(BF16), xb[0:width]))
            parts.append(jnp.concatenate(blocks, 0))
        out = out + jnp.where(low_half, parts[0], parts[1])
        skip_l = pair_lanes(par[2:3], pair, low_half[0:1])
        ssd = out + skip_l * act
        ssd_ref[:, lanes] = ssd
        gate = gate_ref[:, lanes]
        gated = ssd * (gate * jax.nn.sigmoid(gate))
        square = square + gated * gated
        gained = gain[0:1, lanes] * gated
        gg_ref[:, lanes] = gained.astype(BF16)
        cross = cross + dn_ref[:, lanes] * gained
    own_sums[0, pl.ds(i, 1), :] = as_row(square)
    own_sums[1, pl.ds(i, 1), :] = as_row(cross)
    xbuf[0:8] = xbuf[SPAN : SPAN + 8]
    dbuf[0:8] = dbuf[SPAN : SPAN + 8]
    h_out[slot(i)] = nt(gg_ref[slot(1 - core)], wout_ref[...]).astype(BF16)
    h_copy(i).start()
    kept[...] = nt(gg_ref[slot(core)], wout_ref[...])

    @pl.when(i == spans - 1)
    def _():
        def s_copy(k, device):
            return pltpu.make_async_remote_copy(
                src_ref=own_sums, dst_ref=s_in.at[k], send_sem=s_sem.at[0, k],
                recv_sem=s_sem.at[1, k], device_id=device, device_id_type=MESH_IDS,
            )

        sent = [s_copy(0, across), s_copy(1, beyond), s_copy(2, crossed)]
        for copy in sent:
            copy.start()
        join(i)
        mine_put = pltpu.make_async_copy(mine, mine_ref, put_sem.at[0])
        mine_put.start()
        for copy in sent:
            copy.wait_recv()
        near = own_sums[...] + s_in[0]
        sums_ref[...] = near + (s_in[1] + s_in[2])
        for k in range(early):
            y_copy(k).wait_recv()
        far_put = pltpu.make_async_copy(far, far_ref, put_sem.at[1])
        far_put.start()
        for copy in sent:
            copy.wait_send()

        def drain(k, carry):
            h_copy(k).wait_send()
            return carry

        lax.fori_loop(0, spans, drain, 0)
        for k in range(early):
            y_copy(k).wait_send()
        mine_put.wait()
        far_put.wait()


def mixer_forward(docs, normed, cotangent, w_in, w_out, params, ggain, heads, early):
    tokens, model = normed.shape
    inner = w_out.shape[1]
    chan = inner + 2 * LANES
    spans = tokens // SPAN

    def tok(width):
        return pl.BlockSpec((SPAN, width), lambda i: (i, 0))

    def full(shape):
        return pl.BlockSpec(shape, lambda i: (0,) * len(shape))

    anywhere = pl.BlockSpec(memory_space=pl.ANY)
    sums = (2, spans, SPAN)
    outs = (
        jax.ShapeDtypeStruct((tokens, inner), F32),
        jax.ShapeDtypeStruct((tokens, chan), F32),
        jax.ShapeDtypeStruct((tokens, chan), F32),
        jax.ShapeDtypeStruct((tokens, inner), F32),
        jax.ShapeDtypeStruct((tokens, LANES), F32),
        jax.ShapeDtypeStruct((spans, LANES, inner), BF16),
        jax.ShapeDtypeStruct((tokens, inner), F32),
        jax.ShapeDtypeStruct(sums, F32),
        jax.ShapeDtypeStruct((tokens // 2, model), BF16),
        jax.ShapeDtypeStruct((early * SPAN // 2, model), BF16),
    )
    out_specs = (
        tok(inner), tok(chan), tok(chan), tok(inner), tok(LANES),
        pl.BlockSpec((1, LANES, inner), lambda i: (i, 0, 0)),
        tok(inner), full(sums), anywhere, anywhere,
    )
    consts = (w_in, w_out) + params + (ggain,)
    dma, vmem = pltpu.SemaphoreType.DMA, pltpu.VMEM
    return pl.pallas_call(
        lambda *refs: forward_kernel((inner, heads, early), *refs),
        out_shape=outs,
        grid=(spans,),
        in_specs=[full(docs.shape), tok(model), tok(model)] + [full(v.shape) for v in consts],
        out_specs=out_specs,
        scratch_shapes=[
            vmem((SPAN + 8, chan), F32), vmem((SPAN + 8, LANES), F32), vmem((LANES, inner), F32),
            vmem((8, LANES), F32), vmem((8, chan), F32), vmem((8, inner), F32),
            vmem((SPAN, inner), BF16), vmem(sums, F32),
            vmem((tokens // 2, model), BF16), vmem((tokens // 2, model), BF16),
            vmem((SPAN // 2, model), F32), vmem((tokens // 2, model), BF16),
            vmem((early * SPAN // 2, model), BF16),
            dma((2, spans)), dma((2, early)), vmem((3,) + sums, F32), dma((2, 3)), dma((2,)),
        ],
        compiler_params=pltpu.CompilerParams(
            dimension_semantics=("arbitrary",), vmem_limit_bytes=VMEM_MOST,
            collective_id=2, has_side_effects=True,
        ),
        cost_estimate=cost(40.0),
        name="mixer_forward",
    )(docs, normed, cotangent, *consts)


def gating_kernel(
    inner_all, axis, gate_ref, ssd_ref, dn_ref, sums_ref, ggain_ref,
    nout_ref, dgate_ref, dssd_ref, ggrad_ref,
):
    c = pl.program_id(0)
    inner = gate_ref.shape[1]
    gain = ggain_ref[:, pl.ds(pl.multiple_of(lax.axis_index(axis) * inner, LANES), inner)]

    @pl.when(c == 0)
    def _():
        ggrad_ref[...] = jnp.zeros(ggrad_ref.shape, F32)

    inv = lax.rsqrt(as_column(sums_ref[0, pl.ds(c, 1), :]) * (1.0 / inner_all) + EPS)
    pull = as_column(sums_ref[1, pl.ds(c, 1), :]) * (inv * inv * inv) * (1.0 / inner_all)
    for group in range(inner // LANES):
        lanes = slice(group * LANES, (group + 1) * LANES)
        gate = gate_ref[:, lanes]
        sig = jax.nn.sigmoid(gate)
        silu = gate * sig
        ssd = ssd_ref[:, lanes]
        gated = ssd * silu
        dn = dn_ref[:, lanes]
        g_l = gain[:, lanes]
        nout = gated * inv
        nout_ref[:, lanes] = (nout * g_l).astype(BF16)
        ggrad_ref[:, lanes] += fold(dn * nout)
        d_gated = dn * g_l * inv - gated * pull
        dssd_ref[:, lanes] = d_gated * silu
        dgate_ref[:, lanes] = (d_gated * ssd * (sig * (1.0 + gate * (1.0 - sig)))).astype(BF16)


def gating(gate, ssd, dn, sums, ggain):
    tokens, inner = gate.shape

    def full(shape):
        return pl.BlockSpec(shape, lambda i: (0,) * len(shape))

    tok = pl.BlockSpec((SPAN, inner), lambda i: (i, 0))
    return pl.pallas_call(
        lambda *refs: gating_kernel(ggain.shape[1], "tensor", *refs),
        out_shape=(
            jax.ShapeDtypeStruct((tokens, inner), BF16),
            jax.ShapeDtypeStruct((tokens, inner), BF16),
            jax.ShapeDtypeStruct((tokens, inner), F32),
            jax.ShapeDtypeStruct((8, inner), F32),
        ),
        grid=(tokens // SPAN,),
        in_specs=[tok, tok, tok, full(sums.shape), full(ggain.shape)],
        out_specs=(tok, tok, tok, full((8, inner))),
        compiler_params=pltpu.CompilerParams(dimension_semantics=("arbitrary",)),
        cost_estimate=cost(10.0),
        name="gating",
    )(gate, ssd, dn, sums, ggain)


def backward_kernel(
    dims, axis, base, count,
    docs_ref, mixed_ref, pre_ref, ssd_ref, stp_ref, state_ref, dssd_ref, dgate_ref,
    cw_ref, cb_ref, dtb_ref, dec_ref, skip_ref, pin_ref, din_ref, sin_ref,
    dall_ref, gconv_ref, gskip_ref, ghead_ref, pout_ref, dout_ref, sout_ref,
    pbuf, dbuf, dstate, par, cwb,
):
    inner, heads, inner_all = dims
    pairs = heads // 2
    chan = inner + 2 * LANES
    i = pl.program_id(0)
    c = base + count - 1 - i
    rank = lax.axis_index(axis)

    @pl.when(i == 0)
    def _():
        pbuf[SPAN : SPAN + 8] = pin_ref[...]
        dbuf[SPAN : SPAN + 8] = din_ref[...]
        dstate[...] = sin_ref[...]
        own_params(rank, heads, inner, inner_all, dtb_ref, dec_ref, skip_ref, cw_ref, cb_ref, par, cwb)
        gconv_ref[...] = jnp.zeros(gconv_ref.shape, F32)
        gskip_ref[...] = jnp.zeros(gskip_ref.shape, F32)
        ghead_ref[...] = jnp.zeros(ghead_ref.shape, F32)

    dall_ref[:, 0:inner] = dgate_ref[...]
    drow = docs_ref[pl.ds(c, 1), :].astype(F32)
    dcol = as_column(drow)
    before = docs_ref[pl.ds(jnp.maximum(c - 1, 0), 1), :].astype(F32)
    enter = as_column(before)[SPAN - 1 : SPAN]
    enter = jnp.where(c == 0, -1.0, enter)
    dbuf[0:SPAN] = dcol
    keeps = [None] + [dbuf[k : k + SPAN] == dcol for k in range(1, 4)]

    raw = stp_ref[...] + par[0:1]
    step = softplus(raw)
    row_i, col_i = iota((SPAN, SPAN), 0), iota((SPAN, SPAN), 1)
    tril = (row_i >= col_i).astype(BF16)
    log_step = step * par[1:2]
    running = tri_sum(tril, log_step, heads)
    run_rows = jnp.transpose(running)
    ending = running[SPAN - 1 : SPAN]
    tail = jnp.where(dcol == dcol[SPAN - 1 : SPAN], jnp.exp(ending - running), 0.0)
    reach = jnp.where(dcol == enter, jnp.exp(running), 0.0)
    same = jnp.concatenate([dcol, dcol], 1) == drow
    bias = jnp.where(same & (row_i <= col_i), 0.0, FAR)

    def activate(group):
        lanes = slice(group * LANES, (group + 1) * LANES)
        pre = pre_ref[:, lanes]
        sig = jax.nn.sigmoid(pre)
        return pre * sig, sig * (1.0 + pre * (1.0 - sig))

    b_act, b_slope = activate(pairs)
    c_act, c_slope = activate(pairs + 1)
    b_rows, c_rows = b_act.astype(BF16), c_act.astype(BF16)
    c_turned = jnp.transpose(c_act).astype(BF16)
    scores = exact_nt(b_act, c_act)
    low_half = iota((SPAN, LANES), 1) < LANES // 2
    half = SPAN // 2
    d_scores = [jnp.zeros((half, SPAN), F32), jnp.zeros((half, half), F32)]
    d_b = jnp.zeros((SPAN, LANES), F32)
    d_c = jnp.zeros((SPAN, LANES), F32)
    head_up = jnp.zeros((SPAN, LANES), F32)
    head_down = jnp.zeros((SPAN, LANES), F32)
    head_step = jnp.zeros((SPAN, LANES), F32)
    head_hold = jnp.zeros((8, LANES), F32)
    for pair in range(pairs):
        lanes = slice(pair * LANES, (pair + 1) * LANES)
        ones_at = (iota((LANES, LANES), 1) == 2 * pair + iota((LANES, LANES), 0) // (LANES // 2)).astype(BF16)

        def head_sum(v):
            hi = v.astype(BF16)
            low = (v - hi.astype(F32)).astype(BF16)
            return nn(hi, ones_at) + nn(low, ones_at)

        act, slope = activate(pair)
        step_l = pair_lanes(step, pair, low_half)
        tail_l = pair_lanes(tail, pair, low_half)
        reach_l = pair_lanes(reach, pair, low_half)
        skip_l = pair_lanes(par[2:3], pair, low_half[0:1])
        ssd = ssd_ref[:, lanes]
        d_ssd = dssd_ref[:, lanes]
        gskip_ref[:, lanes] += fold(d_ssd * act)
        dyb = d_ssd.astype(BF16)
        scaled = act * step_l
        xb = scaled.astype(BF16)
        held = state_ref[0, :, lanes]
        d_held = dstate[:, lanes]
        d_held_b = d_held.astype(BF16)
        ry = (d_ssd * reach_l).astype(BF16)
        xt = (scaled * tail_l).astype(BF16)
        parts = []
        for sub in range(2):
            head = 2 * pair + sub
            x_own = jnp.where(low_half if sub == 0 else ~low_half, scaled, 0.0).astype(BF16)
            blocks = []
            for blk in range(2):
                rows = slice(blk * half, (blk + 1) * half)
                cols = slice(blk * half, SPAN)
                gap = run_rows[head : head + 1, cols] - running[rows, head : head + 1]
                decay = jnp.exp(gap + bias[rows, cols])
                blocks.append(nn((decay * scores[rows, cols]).astype(BF16), dyb[cols]))
                d_scores[blk] = d_scores[blk] + decay * nt(x_own[rows], dyb[cols])
            parts.append(jnp.concatenate(blocks, 0))
        d_within = jnp.where(low_half, parts[0], parts[1])
        from_state = tail_l * nn(b_rows, d_held_b)
        d_scaled = d_within + from_state
        xf = xb.astype(F32)
        head_up += head_sum(dyb.astype(F32) * (ssd - skip_l * act) - xf * d_within)
        head_down += head_sum(xf * from_state)
        head_step += head_sum(d_scaled * act)
        hold = reach_l[SPAN - 1 : SPAN]
        hold_sum = jnp.sum((d_held * held.astype(F32)).reshape(LANES // 8, 8, LANES), axis=0) * hold
        head_hold += head_sum(hold_sum)
        d_b += nt(xt, d_held_b)
        d_c += nt(ry, held)
        dstate[:, lanes] = hold * d_held + nn(c_turned, ry)
        pbuf[0:SPAN, lanes] = (skip_l * d_ssd + step_l * d_scaled) * slope

    ds_b = jnp.concatenate(
        [
            d_scores[0],
            jnp.concatenate([jnp.zeros((half, half), F32), d_scores[1]], 1),
        ],
        0,
    )
    d_b += nn(ds_b.astype(BF16), c_rows)
    d_c += nn(jnp.transpose(ds_b).astype(BF16), b_rows)
    pbuf[0:SPAN, inner : inner + LANES] = d_b * b_slope
    pbuf[0:SPAN, inner + LANES : chan] = d_c * c_slope

    triu = (row_i <= col_i).astype(BF16)
    below = (row_i > col_i).astype(BF16)
    d_log = (
        tri_sum(triu, head_up, heads)
        + tri_sum(below, head_down, heads)
        + jnp.sum(head_hold, axis=0, keepdims=True)
    )
    d_step = d_log * par[1:2] + head_step
    d_raw = jnp.where(iota((SPAN, LANES), 1) < heads, d_step * jax.nn.sigmoid(raw), 0.0)
    dall_ref[:, inner + chan :] = d_raw.astype(BF16)
    ghead_ref[0] += fold(d_raw)
    ghead_ref[1] += fold(d_log * log_step)

    for group in range(chan // LANES):
        lanes = slice(group * LANES, (group + 1) * LANES)
        mixed = mixed_ref[:, lanes]
        own = pbuf[0:SPAN, lanes]
        acc = cwb[3:4, lanes] * own
        gconv_ref[3, :, lanes] += fold(mixed * own)
        gconv_ref[4, :, lanes] += fold(own)
        for k in range(1, 4):
            later = jnp.where(keeps[k], pbuf[k : k + SPAN, lanes], 0.0)
            acc = acc + cwb[3 - k : 4 - k, lanes] * later
            gconv_ref[3 - k, :, lanes] += fold(mixed * later)
        dall_ref[:, inner + group * LANES : inner + (group + 1) * LANES] = acc.astype(BF16)
    pbuf[SPAN : SPAN + 8] = pbuf[0:8]
    dbuf[SPAN : SPAN + 8] = dbuf[0:8]
    pout_ref[...] = pbuf[0:8]
    dout_ref[...] = dbuf[0:8]
    sout_ref[...] = dstate[...]


def mixer_backward(docs, arrays, params, carry, base, count, heads, inner_all):
    mixed, pre, ssd, stp, states, dssd, dgate = arrays
    tokens, inner = ssd.shape
    chan = inner + 2 * LANES
    width = inner + chan + LANES

    def tok(wide):
        return pl.BlockSpec((SPAN, wide), lambda i: (base + count - 1 - i, 0))

    def full(shape):
        return pl.BlockSpec(shape, lambda i: (0,) * len(shape))

    outs = (
        jax.ShapeDtypeStruct((count * SPAN, width), BF16),
        jax.ShapeDtypeStruct((5, 8, chan), F32),
        jax.ShapeDtypeStruct((8, inner), F32),
        jax.ShapeDtypeStruct((2, 8, LANES), F32),
        jax.ShapeDtypeStruct((8, chan), F32),
        jax.ShapeDtypeStruct((8, LANES), F32),
        jax.ShapeDtypeStruct((LANES, inner), F32),
    )
    consts = params + carry
    return pl.pallas_call(
        lambda *refs: backward_kernel((inner, heads, inner_all), "tensor", base, count, *refs),
        out_shape=outs,
        grid=(count,),
        in_specs=[
            full(docs.shape), tok(chan), tok(chan), tok(inner), tok(LANES),
            pl.BlockSpec((1, LANES, inner), lambda i: (base + count - 1 - i, 0, 0)),
            tok(inner), tok(inner),
        ]
        + [full(v.shape) for v in consts],
        out_specs=(pl.BlockSpec((SPAN, width), lambda i: (count - 1 - i, 0)),)
        + tuple(full(v.shape) for v in outs[1:]),
        scratch_shapes=[
            pltpu.VMEM((SPAN + 8, chan), F32),
            pltpu.VMEM((SPAN + 8, LANES), F32),
            pltpu.VMEM((LANES, inner), F32),
            pltpu.VMEM((8, LANES), F32),
            pltpu.VMEM((8, chan), F32),
        ],
        compiler_params=pltpu.CompilerParams(
            dimension_semantics=("arbitrary",), vmem_limit_bytes=VMEM_MOST
        ),
        cost_estimate=cost(20.0),
        name="mixer_backward",
    )(docs, mixed, pre, ssd, stp, states, dssd, dgate, *consts)


def gather_kernel(
    dims, hid_ref, cot_ref, ngain_ref, w_ref, step_ref, wo_ref,
    win_ref, wout_ref, normed_ref, *refs,
):
    lines, depth, inner, inner_all, aligned = dims
    outs = refs[:4] if aligned else ()
    mine, zsend, zrecv, xsend, xrecv, takes, puts = refs[len(outs):]
    trank, drank = lax.axis_index("tensor"), lax.axis_index("dp")
    line, side = drank // 2, drank % 2
    model = hid_ref.shape[1]
    off = pl.multiple_of(trank * inner, LANES)
    pieces = (
        (w_ref, inner_all + off, win_ref, inner, inner),
        (w_ref, 2 * inner_all, win_ref, 2 * inner, 2 * LANES),
        (step_ref, 0, win_ref, 2 * inner + 2 * LANES, LANES),
        (w_ref, off, win_ref, 0, inner),
        (wo_ref, 0, wout_ref, 0, inner),
    )

    def peer(step):
        return {"dp": lax.rem(line + step, lines) * 2 + side}

    partner = {"dp": line * 2 + 1 - side}
    barrier = pltpu.get_barrier_semaphore()
    for step in range(1, lines):
        pl.semaphore_signal(barrier, inc=1, device_id=peer(step), device_id_type=MESH_IDS)
    pl.semaphore_signal(barrier, inc=1, device_id=partner, device_id_type=MESH_IDS)
    pl.semaphore_wait(barrier, lines)

    def rows(index):
        return pl.ds(pl.multiple_of(index * depth, depth), depth)

    def block(p, index):
        _, _, dst, at, width = pieces[p]
        return dst.at[rows(index), pl.ds(at, width)]

    def own(p):
        src, at, _, _, width = pieces[p]
        return src.at[:, pl.ds(at, width)]

    def z_copy(p, step, src, index):
        return pltpu.make_async_remote_copy(
            src_ref=src, dst_ref=block(p, index), send_sem=zsend.at[p, step - 1],
            recv_sem=zrecv.at[p, step - 1], device_id=peer(step), device_id_type=MESH_IDS,
        )

    def x_copy(p, step, src, index):
        return pltpu.make_async_remote_copy(
            src_ref=src, dst_ref=block(p, index), send_sem=xsend.at[p, step],
            recv_sem=xrecv.at[p, step], device_id=partner, device_id_type=MESH_IDS,
        )

    count = len(pieces)
    for p in range(count):
        for step in range(1, lines):
            z_copy(p, step, own(p), drank).start()
        x_copy(p, 0, own(p), drank).start()
    spots, at = [], 0
    for p in range(count):
        spots.append(mine.at[:, pl.ds(at, pieces[p][4])])
        at += pieces[p][4]
    fetched = [pltpu.make_async_copy(own(p), spots[p], takes.at[p]) for p in range(count)]
    for copy in fetched:
        copy.start()

    gain = ngain_ref[...]

    def normalize(hid, cot, normed, *sorted_refs):
        value = hid[...].astype(F32)
        inv = lax.rsqrt(jnp.mean(value * value, -1, keepdims=True) + EPS)
        normed[...] = (value * inv * gain).astype(BF16)
        if aligned:
            for src, away, here in (
                (normed, sorted_refs[0], sorted_refs[1]), (cot, sorted_refs[2], sorted_refs[3]),
            ):
                for j in range(lines):
                    first = lax.rem(line + j, lines) * 2
                    lanes = slice(j * depth, (j + 1) * depth)
                    away[:, lanes] = src[:, pl.ds(pl.multiple_of((first + 1 - side) * depth, depth), depth)]
                    here[:, lanes] = src[:, pl.ds(pl.multiple_of((first + side) * depth, depth), depth)]

    full = pl.BlockSpec((SPAN, model), lambda i: (i, 0))
    half = pl.BlockSpec((SPAN, lines * depth), lambda i: (i, 0))
    pltpu.emit_pipeline(
        normalize, grid=(hid_ref.shape[0] // SPAN,), in_specs=[full, full],
        out_specs=[full] + [half] * len(outs),
    )(hid_ref, cot_ref, normed_ref, *outs)

    stored = [pltpu.make_async_copy(spots[p], block(p, drank), puts.at[p]) for p in range(count)]
    for p in range(count):
        fetched[p].wait()
        stored[p].start()
    for p in range(count):
        for step in range(1, lines):
            source = lax.rem(line - step + lines, lines) * 2 + side
            got = block(p, source)
            z_copy(p, step, got, source).wait_recv()
            x_copy(p, step, got, source).start()
    for p in range(count):
        for step in range(lines):
            source = lax.rem(line - step + lines, lines) * 2 + 1 - side
            x_copy(p, step, block(p, source), source).wait_recv()
    for p in range(count):
        for step in range(1, lines):
            z_copy(p, step, own(p), drank).wait_send()
        for step in range(lines):
            x_copy(p, step, own(p), drank).wait_send()
        stored[p].wait()


def gather_weights(hidden, cotangent, norm_gain, in_weight, own_step, out_weight, lines, inner_all):
    tokens, model = hidden.shape
    depth, inner = out_weight.shape
    aligned = depth % LANES == 0
    width = 2 * inner + 3 * LANES
    half = jax.ShapeDtypeStruct((tokens, lines * depth), BF16)
    anywhere = pl.BlockSpec(memory_space=pl.ANY)
    outs = (
        jax.ShapeDtypeStruct((model, width), BF16),
        jax.ShapeDtypeStruct((model, inner), BF16),
        jax.ShapeDtypeStruct((tokens, model), BF16),
    ) + (half,) * (4 if aligned else 0)
    dma = pltpu.SemaphoreType.DMA
    return pl.pallas_call(
        lambda *refs: gather_kernel((lines, depth, inner, inner_all, aligned), *refs),
        out_shape=outs,
        in_specs=[anywhere, anywhere, pl.BlockSpec(memory_space=pltpu.VMEM)] + [anywhere] * 3,
        out_specs=(anywhere,) * len(outs),
        scratch_shapes=[
            pltpu.VMEM((depth, width + inner), BF16),
            dma((5, max(1, lines - 1))), dma((5, max(1, lines - 1))), dma((5, lines)), dma((5, lines)),
            dma((5,)), dma((5,)),
        ],
        compiler_params=pltpu.CompilerParams(collective_id=0, has_side_effects=True),
        cost_estimate=cost(45.0),
        name="gather_weights",
    )(hidden, cotangent, norm_gain, in_weight, own_step, out_weight)


def tail_kernel(
    dims, da_ref, db_ref, naway_ref, nhere_ref, w_ref, hid_ref, ngain_ref, ggate_ref, flat_ref,
    delta_ref, gin_ref, flatout_ref,
    da, db, naway, nhere, w, hid, loads,
    x_out, x_in, x_sem, here, low, z_in, z_sem, total,
    h_out, h_in, h_sem, mine, y_in, y_sem, done, d_sem, delta_sem,
    gates, g_sem, values, v_sem, shared, s_sem, put_sem,
    flat, flat_in, f_sem,
):
    lines, depth, inner, heads, inner_all = dims
    trank, drank = lax.axis_index("tensor"), lax.axis_index("dp")
    line, side = drank // 2, drank % 2
    core = trank % 2
    across = {"tensor": trank + 1 - 2 * core}
    beyond = {"tensor": (trank + 2) % 4}
    partner = {"dp": line * 2 + 1 - side}
    half = da_ref.shape[0]
    part = half // 2
    wide = inner + 3 * LANES
    blocks = lines * depth // LANES
    pieces = part // LANES

    def peer(step):
        return {"dp": lax.rem(line + step, lines) * 2 + side}

    barrier = pltpu.get_barrier_semaphore()
    for device in [across, beyond, partner] + [peer(step) for step in range(1, lines)]:
        pl.semaphore_signal(barrier, inc=1, device_id=device, device_id_type=MESH_IDS)
    pl.semaphore_wait(barrier, lines + 2)

    def remote(src, dst, sems, index, device):
        return pltpu.make_async_remote_copy(
            src_ref=src, dst_ref=dst, send_sem=sems.at[0, index], recv_sem=sems.at[1, index],
            device_id=device, device_id_type=MESH_IDS,
        )

    gate_near = remote(ggate_ref, gates.at[1], g_sem, 0, across)
    gate_far = remote(ggate_ref, gates.at[2], g_sem, 1, beyond)
    gate_pass = remote(gates.at[2], gates.at[3], g_sem, 2, across)
    gate_near.start()
    gate_far.start()

    fetch = [
        pltpu.make_async_copy(src, dst, loads.at[k])
        for k, (src, dst) in enumerate(
            (
                (naway_ref, naway), (da_ref, da), (db_ref, db), (w_ref, w), (hid_ref, hid),
                (nhere_ref, nhere), (ggate_ref, gates.at[0]), (flat_ref, flat),
            )
        )
    ]
    for copy in fetch:
        copy.start()

    def block_rows(k):
        return pl.ds(pl.multiple_of(k * LANES, LANES), LANES)

    def weight_grad(source, k):
        cols = block_rows(k)
        return tn(source[0:half, cols], da[:, inner:]) + tn(source[half : 2 * half, cols], db[:, inner:])

    def x_copy(k):
        rows = block_rows(k)
        return remote(x_out.at[rows], x_in.at[rows], x_sem, k, partner)

    for copy in fetch[:3]:
        copy.wait()

    def send_block(k, carry):
        x_out[block_rows(k)] = weight_grad(naway, k).astype(BF16)
        x_copy(k).start()
        return carry

    lax.fori_loop(0, blocks, send_block, 0)

    for copy in fetch[3:5]:
        copy.wait()

    def share(start, k):
        rows = pl.ds(pl.multiple_of(start + k * LANES, LANES), LANES)
        made = nt(da[rows], w[...])
        value = hid[rows].astype(F32)
        inv = lax.rsqrt(jnp.mean(value * value, -1, keepdims=True) + EPS)
        return made, jnp.sum(made * (value * inv), axis=0, keepdims=True)

    def h_copy(k):
        rows = block_rows(k)
        return remote(h_out.at[rows], h_in.at[rows], h_sem, k, across)

    def send_share(k, norm):
        made, part_sum = share((1 - core) * part, k)
        h_out[block_rows(k)] = made.astype(BF16)
        h_copy(k).start()
        return norm + part_sum

    norm = lax.fori_loop(0, pieces, send_share, jnp.zeros((1, w.shape[0]), F32))

    def y_copy(k):
        rows = block_rows(k)
        return remote(mine.at[rows], y_in.at[rows], y_sem, k, beyond)

    def join_share(k, norm):
        made, part_sum = share(core * part, k)
        h_copy(k).wait_recv()
        mine[block_rows(k)] = (made + h_in[block_rows(k)].astype(F32)).astype(BF16)
        y_copy(k).start()
        return norm + part_sum

    norm = lax.fori_loop(0, pieces, join_share, norm)
    gate_far.wait_recv()
    gate_pass.start()

    fetch[7].wait()
    for k in range(w.shape[0] // LANES):
        flat[k : k + 1] = flat[k : k + 1] + norm[:, k * LANES : (k + 1) * LANES]
    hops = [across, beyond, partner]
    bit = 1
    while bit < lines:
        hops.append({"dp": (line + bit * (1 - 2 * ((line // bit) % 2))) * 2 + side})
        bit *= 2

    def flat_copy(k):
        return remote(flat.at[...] if k == 0 else flat_in.at[len(hops) + k], flat_in.at[k], f_sem, k, hops[k])

    flat_copy(0).start()
    fetch[5].wait()

    def keep_block(k, carry):
        here[block_rows(k)] = weight_grad(nhere, k)
        return carry

    lax.fori_loop(0, blocks, keep_block, 0)

    def flat_step(k):
        flat_copy(k).wait_recv()
        held = flat[...] if k == 0 else flat_in[len(hops) + k]
        held = held + flat_in[k]
        if k + 1 < len(hops):
            flat_in[len(hops) + k + 1] = held
            flat_copy(k + 1).start()
        return held

    flat_step(0)

    def z_copy(step):
        rows = pl.ds(step * depth, depth)
        return remote(low.at[rows], z_in.at[step - 1], z_sem, step - 1, peer(step))

    per = LANES // depth
    for k in range(blocks):
        x_copy(k).wait_recv()
        rows = slice(k * LANES, (k + 1) * LANES)
        joined = here[rows] + x_in[rows].astype(F32)
        low[rows] = joined.astype(BF16)
        if k == 0:
            total[...] = joined[0:depth]
        for step in range(max(1, k * per), (k + 1) * per):
            z_copy(step).start()
        if k == 0:
            flat_step(1)

    gain = ngain_ref[...]

    def done_copy(k):
        rows = block_rows(k)
        return remote(done.at[0, rows], done.at[1, rows], d_sem, k, across)

    def own_rows(k):
        return pl.ds(pl.multiple_of(core * part + k * LANES, LANES), LANES)

    def own_put(k):
        return pltpu.make_async_copy(done.at[0, block_rows(k)], delta_ref.at[own_rows(k)], delta_sem.at[0, k])

    def finish(k, carry):
        y_copy(k).wait_recv()
        rows = block_rows(k)
        d_hidden = mine[rows].astype(F32) + y_in[rows].astype(F32)
        value = hid[own_rows(k)].astype(F32)
        inv = lax.rsqrt(jnp.mean(value * value, -1, keepdims=True) + EPS)
        scaled = d_hidden * gain
        pull = jnp.mean(scaled * value, -1, keepdims=True)
        done[0, rows] = (inv * scaled - value * (inv * inv * inv) * pull).astype(BF16)
        done_copy(k).start()
        own_put(k).start()
        return carry

    lax.fori_loop(0, pieces, finish, 0)
    flat_step(2)

    for step in range(1, lines):
        z_copy(step).wait_recv()
        total[...] += z_in[step - 1].astype(F32)
    values[0] = total[:, 0:inner]
    shared[0, :, 0 : 2 * LANES] = total[:, inner : inner + 2 * LANES]
    steps = pltpu.roll(total[:, inner + 2 * LANES :], trank * heads, 1)
    lane = iota(steps.shape, 1) - trank * heads
    shared[0, :, 2 * LANES :] = jnp.where((lane >= 0) & (lane < heads), steps, 0.0)
    shared_near = remote(shared.at[0], shared.at[1], s_sem, 0, across)
    shared_far = remote(shared.at[2], shared.at[3], s_sem, 1, beyond)
    value_near = remote(values.at[0], values.at[1], v_sem, 0, across)
    value_far = remote(values.at[0], values.at[2], v_sem, 1, beyond)
    value_pass = remote(values.at[2], values.at[3], v_sem, 2, across)
    shared_near.start()
    value_far.start()
    value_near.start()

    last = flat_in.shape[0] - 1
    for k in range(3, len(hops)):
        held = flat_step(k)
    flat_in[last] = held
    flat_put = pltpu.make_async_copy(flat_in.at[last], flatout_ref, put_sem.at[9])
    flat_put.start()

    shared_near.wait_recv()
    shared[2] = shared[0] + shared[1]
    shared_far.start()

    def put(source, k, first, column_of, index):
        column = pl.multiple_of(first + column_of * inner, LANES)
        return pltpu.make_async_copy(source.at[k], gin_ref.at[:, pl.ds(column, inner)], put_sem.at[index])

    owners = (trank, trank + 1 - 2 * core, (trank + 2) % 4, (trank + 1 - 2 * core + 2) % 4)
    fetch[6].wait()
    puts = [put(gates, 0, 0, owners[0], 0), put(values, 0, inner_all, owners[0], 4)]
    puts[0].start()
    puts[1].start()

    def other_put(k):
        rows = block_rows(k)
        dst = pl.ds(pl.multiple_of((1 - core) * part + k * LANES, LANES), LANES)
        return pltpu.make_async_copy(done.at[1, rows], delta_ref.at[dst], delta_sem.at[1, k])

    def other_rows(k, carry):
        done_copy(k).wait_recv()
        other_put(k).start()
        return carry

    lax.fori_loop(0, pieces, other_rows, 0)
    for k, (near, far, passed, source, first, at) in enumerate(
        (
            (gate_near, gate_far, gate_pass, gates, 0, 0),
            (value_near, value_far, value_pass, values, inner_all, 4),
        )
    ):
        near.wait_recv()
        if k == 1:
            far.wait_recv()
            passed.start()
        puts += [put(source, 1, first, owners[1], at + 1), put(source, 2, first, owners[2], at + 2)]
        puts[-2].start()
        puts[-1].start()
    shared_far.wait_recv()
    shared[1] = shared[2] + shared[3]
    shared_put = pltpu.make_async_copy(
        shared.at[1], gin_ref.at[:, pl.ds(2 * inner_all, 3 * LANES)], put_sem.at[8]
    )
    shared_put.start()
    for passed, source, first, at in ((gate_pass, gates, 0, 3), (value_pass, values, inner_all, 7)):
        passed.wait_recv()
        puts.append(put(source, 3, first, owners[3], at))
        puts[-1].start()

    def drain(k, carry):
        h_copy(k).wait_send()
        y_copy(k).wait_send()
        done_copy(k).wait_send()
        own_put(k).wait()
        other_put(k).wait()
        return carry

    lax.fori_loop(0, pieces, drain, 0)
    for k in range(blocks):
        x_copy(k).wait_send()
    for step in range(1, lines):
        z_copy(step).wait_send()
    for copy in (
        gate_near, gate_far, gate_pass, value_near, value_far, value_pass, shared_near, shared_far,
    ):
        copy.wait_send()
    for k in range(len(hops)):
        flat_copy(k).wait_send()
    for copy in puts + [shared_put, flat_put]:
        copy.wait()


def tail(da, db, naway, nhere, w, hid, norm_gain, ggate, flat, lines, depth, heads, inner_all):
    half, width = da.shape
    model = w.shape[0]
    inner = ggate.shape[1]
    wide = width - inner
    part = half // 2
    blocks, pieces = lines * depth // LANES, part // LANES
    hops = 3 + (lines - 1).bit_length()
    dma = pltpu.SemaphoreType.DMA
    vmem = pltpu.VMEM
    anywhere = pl.BlockSpec(memory_space=pl.ANY)
    fars = max(1, lines - 1)
    return pl.pallas_call(
        lambda *refs: tail_kernel((lines, depth, inner, heads, inner_all), *refs),
        out_shape=(
            jax.ShapeDtypeStruct((half, model), BF16),
            jax.ShapeDtypeStruct((depth, 2 * inner_all + 3 * LANES), F32),
            jax.ShapeDtypeStruct(flat.shape, F32),
        ),
        in_specs=[anywhere] * 6 + [pl.BlockSpec(memory_space=vmem)] + [anywhere] * 2,
        out_specs=(anywhere,) * 3,
        scratch_shapes=[
            vmem(da.shape, BF16), vmem(db.shape, BF16), vmem(naway.shape, BF16), vmem(nhere.shape, BF16),
            vmem(w.shape, BF16), vmem(hid.shape, BF16), dma((8,)),
            vmem((lines * depth, wide), BF16), vmem((lines * depth, wide), BF16), dma((2, blocks)),
            vmem((lines * depth, wide), F32), vmem((lines * depth, wide), BF16),
            vmem((fars, depth, wide), BF16), dma((2, fars)), vmem((depth, wide), F32),
            vmem((part, model), BF16), vmem((part, model), BF16), dma((2, pieces)),
            vmem((part, model), BF16), vmem((part, model), BF16), dma((2, pieces)),
            vmem((2, part, model), BF16), dma((2, pieces)), dma((2, pieces)),
            vmem((4, depth, inner), F32), dma((2, 3)),
            vmem((4, depth, inner), F32), dma((2, 3)),
            vmem((4, depth, 3 * LANES), F32), dma((2, 2)), dma((10,)),
            vmem(flat.shape, F32), vmem((2 * hops + 1,) + flat.shape, F32), dma((2, hops)),
        ],
        compiler_params=pltpu.CompilerParams(
            collective_id=1, has_side_effects=True, vmem_limit_bytes=VMEM_MOST
        ),
        cost_estimate=cost(45.0),
        name="tail",
    )(da, db, naway, nhere, w, hid, norm_gain, ggate, flat)


def swap(v, axis, to):
    return lax.ppermute(v, axis, [(k, to(k)) for k in range(lax.axis_size(axis))])


def tie(*items):
    return lax.optimization_barrier(items)


def flip(bits):
    return lambda k: k ^ bits


def body(
    hidden_in, doc_ids, cotangent, norm_gain, in_weight, conv_weight, conv_bias,
    dt_bias, log_decay, skip_gain, gate_gain, out_weight,
):
    tcount, dcount = lax.axis_size("tensor"), lax.axis_size("dp")
    trank, drank = lax.axis_index("tensor"), lax.axis_index("dp")
    lines = dcount // 2
    line, side = drank // 2, drank % 2
    core = trank % 2
    inner_all, head_all = gate_gain.shape[0], dt_bias.shape[0]
    inner, heads = inner_all // tcount, head_all // tcount
    tokens, model = hidden_in.shape
    base_bc = 2 * inner_all
    base_dt = base_bc + 2 * LANES
    depth = in_weight.shape[0]
    chan = inner + 2 * LANES

    def line_to(step):
        return lambda k: ((k // 2 + step) % lines) * 2 + k % 2

    own_step = jnp.pad(
        lax.dynamic_slice_in_dim(in_weight, base_dt + trank * heads, heads, 1),
        ((0, 0), (0, LANES - heads)),
    )
    w_in, w_out, normed, *sorted_parts = gather_weights(
        hidden_in, cotangent, norm_gain.reshape(1, -1), in_weight, own_step, out_weight,
        lines, inner_all,
    )
    if not sorted_parts:

        def features(v, which):
            return jnp.concatenate(
                [
                    lax.dynamic_slice_in_dim(v, (((line + j) % lines) * 2 + which) * depth, depth, 1)
                    for j in range(lines)
                ],
                1,
            )

        sorted_parts = [features(v, which) for v in (normed, cotangent) for which in (1 - side, side)]
    n_away, n_here, c_away, c_here = sorted_parts

    def row(v):
        return v.reshape(1, -1)

    docs = doc_ids.reshape(tokens // SPAN, SPAN)
    spans = tokens // SPAN
    count = spans // 2
    span_rows = count * SPAN
    part = span_rows // 2
    params = (conv_weight, row(conv_bias), row(dt_bias), row(log_decay), row(skip_gain))

    def own_share(left, right):
        def make(start):
            return nt(lax.dynamic_slice_in_dim(left, start, part, 0), right)

        got = swap(make((1 - core) * part).astype(BF16), "tensor", flip(1))
        return (make(core * part) + got.astype(F32)).astype(BF16)

    def chips_sum(mine, theirs):
        return mine.astype(F32) + theirs.astype(F32)

    def both(own):
        got = swap(own, "tensor", flip(1))
        return [jnp.where(core == 0, own, got), jnp.where(core == 0, got, own)]

    def my_rows(v, h):
        return lax.dynamic_slice_in_dim(v, h * span_rows + core * part, part, 0)

    def span_halves(v, h):
        own = v[h * span_rows : (h + 1) * span_rows].reshape(count, 2, SPAN // 2, v.shape[1])
        return lax.dynamic_index_in_dim(own, core, 1, keepdims=False).reshape(part, v.shape[1])

    def both_spans(own):
        got = swap(own, "tensor", flip(1)).reshape(count, 1, SPAN // 2, model)
        own = own.reshape(count, 1, SPAN // 2, model)
        low, high = jnp.where(core == 0, own, got), jnp.where(core == 0, got, own)
        return jnp.concatenate([low, high], 1).reshape(span_rows, model)

    *held, sums, mine, far_a = mixer_forward(
        doc_ids, normed, cotangent, w_in, w_out, params, row(gate_gain), heads, count
    )
    out_a, out_b = mine[: span_rows // 2], mine[span_rows // 2 :]
    out_b, sums = tie(out_b, sums)
    far_b = swap(out_b, "tensor", flip(2))
    gate, mixed, pre, ssd, stp, states, dn = held
    nout, d_gate, d_ssd, g_gain = gating(gate, ssd, dn, sums, row(gate_gain))
    inv_gate = lax.rsqrt(sums[0].reshape(tokens, 1) * (1.0 / inner_all) + EPS)

    def to_side(away):
        return swap(away, "dp", flip(1))

    def to_lines(here, got):
        here = here + got.astype(F32)
        return here, [here[j * depth : (j + 1) * depth].astype(BF16) for j in range(1, lines)]

    def lines_sum(here, low):
        total = here[:depth]
        for j in range(1, lines):
            total = total + swap(low[j - 1], "dp", line_to(j)).astype(F32)
        return total

    o_away, g_away = tn(c_away, nout).astype(BF16), tn(n_away, d_gate).astype(BF16)
    o_here, g_here = tn(c_here, nout), tn(n_here, d_gate)
    o_away, g_away, o_here, g_here, d_ssd = tie(o_away, g_away, o_here, g_here, d_ssd)
    o_got, g_got = to_side(o_away), to_side(g_away)

    def backward(h, carry, d_ssd):
        return mixer_backward(
            docs, (mixed, pre, ssd, stp, states, d_ssd, d_gate), params, carry,
            h * count, count, heads, inner_all,
        )

    carry = (
        jnp.zeros((8, chan), F32), jnp.full((8, LANES), -2.0, F32), jnp.zeros((LANES, inner), F32),
    )
    d_b, conv_b, skip_b, head_b, *carry = backward(1, carry, d_ssd)
    d_b, o_got, g_got, far_b = tie(d_b, o_got, g_got, far_b)
    o_here, o_low = to_lines(o_here, o_got)
    g_here, g_low = to_lines(g_here, g_got)
    hid_b = own_share(d_b, w_in)
    o_low, g_low, hid_b, carry = tie(o_low, g_low, hid_b, tuple(carry))
    hid_far_b = swap(hid_b, "tensor", flip(2))
    g_out, g_gate = lines_sum(o_here, o_low), lines_sum(g_here, g_low)
    d_a, conv_a, skip_a, head_a, *_ = backward(0, carry, d_ssd)
    d_a, g_out, g_gate, hid_far_b = tie(d_a, g_out, g_gate, hid_far_b)
    g_conv, g_skip, g_head = conv_a + conv_b, skip_a + skip_b, head_a + head_b

    def input_grad(h, d_hidden):
        hid = my_rows(hidden_in, h).astype(F32)
        inv = lax.rsqrt(jnp.mean(hid * hid, -1, keepdims=True) + EPS)
        scaled = d_hidden * norm_gain
        pull = jnp.mean(scaled * hid, -1, keepdims=True)
        norm = jnp.sum(d_hidden * hid * inv, 0) * (trank < 2).astype(F32)
        return (inv * scaled - hid * inv**3 * pull).astype(BF16), norm

    layer_out = []
    for h, out in ((0, chips_sum(out_a, far_a)), (1, chips_sum(out_b, far_b))):
        hid = span_halves(hidden_in, h).astype(F32)
        layer_out.append(both_spans((hid + out * span_halves(inv_gate, h)).astype(BF16)))
    layer_out = jnp.concatenate(layer_out, 0)
    delta_b, norm_b = input_grad(1, chips_sum(hid_b, hid_far_b))
    delta_b = both(delta_b)

    conv = jnp.sum(g_conv, 1)
    head = jnp.sum(g_head, 1)
    skip = jnp.sum(jnp.sum(g_skip, 0).reshape(heads, -1), 1)
    spot = trank * inner

    def place(v, total, start):
        return lax.dynamic_update_slice_in_dim(
            jnp.zeros(v.shape[:-1] + (total,), F32), v, start, v.ndim - 1
        )

    conv_all = place(conv[:, :inner], inner_all + 2 * LANES, spot).at[:, inner_all:].set(conv[:, inner:])
    heads_all = place(jnp.stack([head[0, :heads], head[1, :heads], skip]), head_all, trank * heads)
    flat = jnp.concatenate(
        [norm_b, conv_all.reshape(-1), heads_all.reshape(-1), place(jnp.sum(g_gain, 0), inner_all, spot)]
    )
    flat = jnp.pad(flat, (0, -flat.shape[0] % 1024)).reshape(-1, LANES)

    delta_a, grad_in, flat = tail(
        d_a, d_b, n_away, n_here, w_in, hidden_in[:span_rows], row(norm_gain), g_gate, flat,
        lines, depth, heads, inner_all,
    )
    grad_input = cotangent.astype(F32) + jnp.concatenate([delta_a] + delta_b, 0).astype(F32)
    grad_in_weight = grad_in[:, : in_weight.shape[1]]

    flat = flat.reshape(-1)
    cuts, at = [], 0
    for size in (model, 5 * conv_all.shape[1], 3 * head_all, inner_all):
        cuts.append(flat[at : at + size])
        at += size
    conv_all = cuts[1].reshape(5, -1)
    heads_all = cuts[2].reshape(3, -1)
    return (
        layer_out, grad_input, cuts[0], grad_in_weight, conv_all[:4], conv_all[4],
        heads_all[0], heads_all[1], heads_all[2], cuts[3], g_out,
    )


def solution(mesh):
    rows, whole = P("dp", None), P()
    return jax.shard_map(
        body,
        mesh=mesh,
        in_specs=(rows, rows, rows, whole, rows, whole, whole, whole, whole, whole, whole, P("dp", "tensor")),
        out_specs=(rows, rows, whole, rows, whole, whole, whole, whole, whole, whole, P("dp", "tensor")),
        check_vma=False,
    )
```

```python
import jax
import jax.numpy as jnp
from jax import lax
from jax.experimental import pallas as pl
from jax.experimental.pallas import tpu as pltpu
from jax.sharding import PartitionSpec as P

SPAN = 256
LANES = 128
EPS = 1e-05
FAR = -1e30
VMEM_MOST = 60 * 2**20
F32 = jnp.float32
BF16 = jnp.bfloat16


def cost(micros):
    return pl.CostEstimate(flops=int(micros * 1.15e9), bytes_accessed=1 << 20, transcendentals=0)


def nn(a, b):
    return lax.dot_general(a, b, (((1,), (0,)), ((), ())), preferred_element_type=F32)


def nt(a, b):
    return lax.dot_general(a, b, (((1,), (1,)), ((), ())), preferred_element_type=F32)


def tn(a, b):
    return lax.dot_general(a, b, (((0,), (0,)), ((), ())), preferred_element_type=F32)


def iota(shape, dim):
    return lax.broadcasted_iota(jnp.int32, shape, dim)


def as_column(row, rows=SPAN):
    return jnp.transpose(jnp.broadcast_to(row, (LANES, rows)))


def as_row(block):
    return jnp.sum(jnp.transpose(block), axis=0, keepdims=True)


def split3(v):
    hi = v.astype(BF16)
    rest = v - hi.astype(F32)
    mid = rest.astype(BF16)
    low = (rest - mid.astype(F32)).astype(BF16)
    return hi, mid, low


def tri_sum(tri, v, heads):
    lane = iota(v.shape, 1)
    v = jnp.where(lane < heads, v, 0.0)
    hi = v.astype(BF16).astype(F32)
    rest = v - hi
    mid = rest.astype(BF16).astype(F32)
    low = rest - mid
    packed = hi + pltpu.roll(mid, heads, 1) + pltpu.roll(low, 2 * heads, 1)
    out = nn(tri, packed.astype(BF16))
    return out + pltpu.roll(out, LANES - heads, 1) + pltpu.roll(out, LANES - 2 * heads, 1)


def pair_lanes(cols, pair, low_half):
    rows = cols.shape[0]
    first = jnp.broadcast_to(cols[:, 2 * pair : 2 * pair + 1], (rows, LANES))
    second = jnp.broadcast_to(cols[:, 2 * pair + 1 : 2 * pair + 2], (rows, LANES))
    return jnp.where(low_half, first, second)


def exact_nt(a, b):
    a_hi, b_hi = a.astype(BF16), b.astype(BF16)
    a_lo = (a - a_hi.astype(F32)).astype(BF16)
    b_lo = (b - b_hi.astype(F32)).astype(BF16)
    return nt(a_hi, b_hi) + (nt(a_hi, b_lo) + nt(a_lo, b_hi))


def softplus(v):
    return jnp.maximum(v, 0.0) + jnp.log1p(jnp.exp(-jnp.abs(v)))


def own_lanes(row, rank, heads):
    total = row.shape[1]
    pick = (iota((total, LANES), 0) == rank * heads + iota((total, LANES), 1)) & (
        iota((total, LANES), 1) < heads
    )
    wide = jnp.broadcast_to(row, (8, total))
    out = lax.dot_general(
        wide, pick.astype(F32), (((1,), (0,)), ((), ())),
        precision=lax.Precision.HIGHEST, preferred_element_type=F32,
    )
    return out[0:1]


def fold(v):
    return jnp.sum(v.reshape(SPAN // 8, 8, v.shape[1]), axis=0)


def own_params(rank, heads, inner, inner_all, dtb_ref, dec_ref, skip_ref, cw_ref, cb_ref, par, cwb):
    chan = inner + 2 * LANES
    off = pl.multiple_of(rank * inner, LANES)
    taps = cw_ref.shape[0]
    par[0:1] = own_lanes(dtb_ref[...], rank, heads)
    par[1:2] = -jnp.exp(own_lanes(dec_ref[...], rank, heads))
    par[2:3] = own_lanes(skip_ref[...], rank, heads)
    cwb[0:taps, 0:inner] = cw_ref[:, pl.ds(off, inner)].astype(F32)
    cwb[0:taps, inner:chan] = cw_ref[:, inner_all:].astype(F32)
    cwb[taps : taps + 1, 0:inner] = cb_ref[:, pl.ds(off, inner)]
    cwb[taps : taps + 1, inner:chan] = cb_ref[:, inner_all:]


MESH_IDS = pl.DeviceIdType.MESH


def forward_kernel(
    dims, docs_ref, normed_ref, cot_ref, win_ref, wout_ref, cw_ref, cb_ref,
    dtb_ref, dec_ref, skip_ref, ggain_ref,
    gate_ref, mixed_ref, pre_ref, ssd_ref, stp_ref, state_ref, dn_ref,
    sums_ref, mine_ref, far_ref,
    xbuf, dbuf, state, par, cwb, gain, gg_ref,
    own_sums, h_out, h_in, kept, mine, far, h_sem, y_sem, s_in, s_sem, put_sem,
):
    inner, heads, early = dims
    pairs = heads // 2
    chan = inner + 2 * LANES
    i = pl.program_id(0)
    spans = pl.num_programs(0)
    rank = lax.axis_index("tensor")
    core = rank % 2
    inner_all = ggain_ref.shape[1]
    half = SPAN // 2
    across = {"tensor": rank + 1 - 2 * core}
    beyond = {"tensor": (rank + 2) % 4}
    crossed = {"tensor": (rank + 3 - 2 * core) % 4}

    @pl.when(i == 0)
    def _():
        barrier = pltpu.get_barrier_semaphore()
        for device in (across, beyond, crossed):
            pl.semaphore_signal(barrier, inc=1, device_id=device, device_id_type=MESH_IDS)
        pl.semaphore_wait(barrier, 3)
        xbuf[0:8] = jnp.zeros((8, chan), F32)
        dbuf[0:8] = jnp.full((8, LANES), -1.0, F32)
        state[...] = jnp.zeros(state.shape, F32)
        own_params(rank, heads, inner, inner_all, dtb_ref, dec_ref, skip_ref, cw_ref, cb_ref, par, cwb)
        gain[0:1] = ggain_ref[:, pl.ds(pl.multiple_of(rank * inner, LANES), inner)]

    def slot(k):
        return pl.ds(pl.multiple_of(k * half, half), half)

    def h_copy(k):
        return pltpu.make_async_remote_copy(
            src_ref=h_out.at[slot(k)], dst_ref=h_in.at[slot(k)], send_sem=h_sem.at[0, k],
            recv_sem=h_sem.at[1, k], device_id=across, device_id_type=MESH_IDS,
        )

    def y_copy(k):
        return pltpu.make_async_remote_copy(
            src_ref=mine.at[slot(k)], dst_ref=far.at[slot(k)], send_sem=y_sem.at[0, k],
            recv_sem=y_sem.at[1, k], device_id=beyond, device_id_type=MESH_IDS,
        )

    def join(k):
        h_copy(k).wait_recv()
        mine[slot(k)] = (kept[...] + h_in[slot(k)].astype(F32)).astype(BF16)

    @pl.when(i > 0)
    def _():
        join(i - 1)

        @pl.when(i - 1 < early)
        def _():
            y_copy(i - 1).start()

    nb = normed_ref[...]
    xbuf[8 : 8 + SPAN] = nn(nb, win_ref[:, inner : inner + chan])
    gate_ref[...] = nn(nb, win_ref[:, 0:inner])
    stp = nn(nb, win_ref[:, inner + chan : inner + chan + LANES])
    stp_ref[...] = stp
    mixed_ref[...] = xbuf[8 : 8 + SPAN]
    dn_ref[...] = nn(cot_ref[...], wout_ref[...])

    drow = docs_ref[:, pl.ds(pl.multiple_of(i * SPAN, SPAN), SPAN)].astype(F32)
    dcol = as_column(drow)
    enter = dbuf[7:8]
    dbuf[8 : 8 + SPAN] = dcol
    keeps = [None] + [dbuf[8 - k : 8 - k + SPAN] == dcol for k in range(1, 4)]

    def conv(group):
        lanes = slice(group * LANES, (group + 1) * LANES)
        acc = cwb[4:5, lanes] + cwb[3:4, lanes] * xbuf[8 : 8 + SPAN, lanes]
        for k in range(1, 4):
            acc = acc + cwb[3 - k : 4 - k, lanes] * jnp.where(
                keeps[k], xbuf[8 - k : 8 - k + SPAN, lanes], 0.0
            )
        pre_ref[:, lanes] = acc
        return acc * jax.nn.sigmoid(acc)

    b_act, c_act = conv(pairs), conv(pairs + 1)
    b_rows, c_rows = b_act.astype(BF16), c_act.astype(BF16)

    step = softplus(stp + par[0:1])
    row_i, col_i = iota((SPAN, SPAN), 0), iota((SPAN, SPAN), 1)
    tril = (row_i >= col_i).astype(BF16)
    running = tri_sum(tril, step * par[1:2], heads)
    run_rows = jnp.transpose(running)
    ending = running[SPAN - 1 : SPAN]
    tail = jnp.where(dcol == dcol[SPAN - 1 : SPAN], jnp.exp(ending - running), 0.0)
    reach = jnp.where(dcol == enter, jnp.exp(running), 0.0)
    same = jnp.concatenate([dcol, dcol], 1) == drow
    bias = jnp.where(same & (row_i >= col_i), 0.0, FAR)
    scores = exact_nt(c_act, b_act)
    b_turned = jnp.transpose(b_act).astype(BF16)
    low_half = iota((SPAN, LANES), 1) < LANES // 2
    square = jnp.zeros((SPAN, LANES), F32)
    cross = jnp.zeros((SPAN, LANES), F32)
    for pair in range(pairs):
        lanes = slice(pair * LANES, (pair + 1) * LANES)
        act = conv(pair)
        scaled = act * pair_lanes(step, pair, low_half)
        xb = scaled.astype(BF16)
        tail_l = pair_lanes(tail, pair, low_half)
        reach_l = pair_lanes(reach, pair, low_half)
        held = state[:, lanes]
        held_b = held.astype(BF16)
        state_ref[0, :, lanes] = held_b
        state[:, lanes] = nn(b_turned, (scaled * tail_l).astype(BF16)) + reach_l[SPAN - 1 : SPAN] * held
        out = reach_l * nn(c_rows, held_b)
        parts = []
        for sub in range(2):
            head = 2 * pair + sub
            blocks = []
            for blk in range(2):
                rows = slice(blk * half, (blk + 1) * half)
                width = (blk + 1) * half
                gap = running[rows, head : head + 1] - run_rows[head : head + 1, 0:width]
                weight = jnp.exp(gap + bias[rows, 0:width]) * scores[rows, 0:width]
                blocks.append(nn(weight.astype(BF16), xb[0:width]))
            parts.append(jnp.concatenate(blocks, 0))
        out = out + jnp.where(low_half, parts[0], parts[1])
        skip_l = pair_lanes(par[2:3], pair, low_half[0:1])
        ssd = out + skip_l * act
        ssd_ref[:, lanes] = ssd
        gate = gate_ref[:, lanes]
        gated = ssd * (gate * jax.nn.sigmoid(gate))
        square = square + gated * gated
        gained = gain[0:1, lanes] * gated
        gg_ref[:, lanes] = gained.astype(BF16)
        cross = cross + dn_ref[:, lanes] * gained
    own_sums[0, pl.ds(i, 1), :] = as_row(square)
    own_sums[1, pl.ds(i, 1), :] = as_row(cross)
    xbuf[0:8] = xbuf[SPAN : SPAN + 8]
    dbuf[0:8] = dbuf[SPAN : SPAN + 8]
    h_out[slot(i)] = nt(gg_ref[slot(1 - core)], wout_ref[...]).astype(BF16)
    h_copy(i).start()
    kept[...] = nt(gg_ref[slot(core)], wout_ref[...])

    @pl.when(i == spans - 1)
    def _():
        def s_copy(k, device):
            return pltpu.make_async_remote_copy(
                src_ref=own_sums, dst_ref=s_in.at[k], send_sem=s_sem.at[0, k],
                recv_sem=s_sem.at[1, k], device_id=device, device_id_type=MESH_IDS,
            )

        sent = [s_copy(0, across), s_copy(1, beyond), s_copy(2, crossed)]
        for copy in sent:
            copy.start()
        join(i)
        mine_put = pltpu.make_async_copy(mine, mine_ref, put_sem.at[0])
        mine_put.start()
        for copy in sent:
            copy.wait_recv()
        near = own_sums[...] + s_in[0]
        sums_ref[...] = near + (s_in[1] + s_in[2])
        for k in range(early):
            y_copy(k).wait_recv()
        far_put = pltpu.make_async_copy(far, far_ref, put_sem.at[1])
        far_put.start()
        for copy in sent:
            copy.wait_send()

        def drain(k, carry):
            h_copy(k).wait_send()
            return carry

        lax.fori_loop(0, spans, drain, 0)
        for k in range(early):
            y_copy(k).wait_send()
        mine_put.wait()
        far_put.wait()


def mixer_forward(docs, normed, cotangent, w_in, w_out, params, ggain, heads, early):
    tokens, model = normed.shape
    inner = w_out.shape[1]
    chan = inner + 2 * LANES
    spans = tokens // SPAN

    def tok(width):
        return pl.BlockSpec((SPAN, width), lambda i: (i, 0))

    def full(shape):
        return pl.BlockSpec(shape, lambda i: (0,) * len(shape))

    anywhere = pl.BlockSpec(memory_space=pl.ANY)
    sums = (2, spans, SPAN)
    outs = (
        jax.ShapeDtypeStruct((tokens, inner), F32),
        jax.ShapeDtypeStruct((tokens, chan), F32),
        jax.ShapeDtypeStruct((tokens, chan), F32),
        jax.ShapeDtypeStruct((tokens, inner), F32),
        jax.ShapeDtypeStruct((tokens, LANES), F32),
        jax.ShapeDtypeStruct((spans, LANES, inner), BF16),
        jax.ShapeDtypeStruct((tokens, inner), F32),
        jax.ShapeDtypeStruct(sums, F32),
        jax.ShapeDtypeStruct((tokens // 2, model), BF16),
        jax.ShapeDtypeStruct((early * SPAN // 2, model), BF16),
    )
    out_specs = (
        tok(inner), tok(chan), tok(chan), tok(inner), tok(LANES),
        pl.BlockSpec((1, LANES, inner), lambda i: (i, 0, 0)),
        tok(inner), full(sums), anywhere, anywhere,
    )
    consts = (w_in, w_out) + params + (ggain,)
    dma, vmem = pltpu.SemaphoreType.DMA, pltpu.VMEM
    return pl.pallas_call(
        lambda *refs: forward_kernel((inner, heads, early), *refs),
        out_shape=outs,
        grid=(spans,),
        in_specs=[full(docs.shape), tok(model), tok(model)] + [full(v.shape) for v in consts],
        out_specs=out_specs,
        scratch_shapes=[
            vmem((SPAN + 8, chan), F32), vmem((SPAN + 8, LANES), F32), vmem((LANES, inner), F32),
            vmem((8, LANES), F32), vmem((8, chan), F32), vmem((8, inner), F32),
            vmem((SPAN, inner), BF16), vmem(sums, F32),
            vmem((tokens // 2, model), BF16), vmem((tokens // 2, model), BF16),
            vmem((SPAN // 2, model), F32), vmem((tokens // 2, model), BF16),
            vmem((early * SPAN // 2, model), BF16),
            dma((2, spans)), dma((2, early)), vmem((3,) + sums, F32), dma((2, 3)), dma((2,)),
        ],
        compiler_params=pltpu.CompilerParams(
            dimension_semantics=("arbitrary",), vmem_limit_bytes=VMEM_MOST,
            collective_id=2, has_side_effects=True,
        ),
        cost_estimate=cost(40.0),
        name="mixer_forward",
    )(docs, normed, cotangent, *consts)


def backward_kernel(
    dims,
    docs_ref, hid_ref, gate_ref, dn_ref, gate_low_ref, ssd_low_ref, dn_low_ref,
    ssd_ref, mixed_ref, pre_ref, stp_ref, state_ref, sums_ref,
    cw_ref, cb_ref, dtb_ref, dec_ref, skip_ref, ggain_ref, ngain_ref,
    naway_ref, nhere_ref, caway_ref, chere_ref, w_ref, mine_ref, far_ref,
    delta_ref, layer_ref, gin_ref, gout_ref, flatout_ref,
    naway, nhere, caway, chere, w, loads,
    pbuf, dbuf, dstate, par, cwb, gain,
    gconv, gskip, ghead, ggain, gnorm,
    nout_all, dgate_all, dall, dssd_low, inv_now, inv_own, hid_own,
    h_out, mine, y_in, kept, h_sem, y_sem, d_sem, d_put,
    omine, ofar, oy_sem, o_sem, o_put,
    ax_out, ax_in, ax_sem, az_in, az_sem, atotal,
    bx_out, bx_in, bx_sem, bz_in, bz_sem, btotal,
    gates, g_sem, values, v_sem, shared, s_sem, put_sem, flat, flat_in, f_sem,
):
    inner, heads, inner_all, lines, depth, early = dims
    pairs = heads // 2
    chan = inner + 2 * LANES
    width = inner + chan + LANES
    i = pl.program_id(0)
    spans = pl.num_programs(0)
    tokens = nout_all.shape[0]
    count = tokens // SPAN
    mid = count // 2
    c = count - 1 - i
    half = SPAN // 2
    model = w.shape[0]
    blocks = lines * depth // LANES
    rank, drank = lax.axis_index("tensor"), lax.axis_index("dp")
    line, side = drank // 2, drank % 2
    core = rank % 2
    off = pl.multiple_of(rank * inner, LANES)
    across = {"tensor": rank + 1 - 2 * core}
    beyond = {"tensor": (rank + 2) % 4}
    partner = {"dp": line * 2 + 1 - side}

    def peer(step):
        return {"dp": lax.rem(line + step, lines) * 2 + side}

    def remote(src, dst, sems, index, device):
        return pltpu.make_async_remote_copy(
            src_ref=src, dst_ref=dst, send_sem=sems.at[0, index], recv_sem=sems.at[1, index],
            device_id=device, device_id_type=MESH_IDS,
        )

    def lot(k, size):
        return pl.ds(pl.multiple_of(k * size, size), size)

    fetch = [
        pltpu.make_async_copy(src, dst, loads.at[k])
        for k, (src, dst) in enumerate(
            (
                (mine_ref, omine), (w_ref, w), (far_ref, ofar.at[pl.ds(0, early * half)]),
                (caway_ref, caway), (naway_ref, naway), (chere_ref, chere), (nhere_ref, nhere),
            )
        )
    ]

    def oy_copy(k):
        return remote(omine.at[lot(k, half)], ofar.at[lot(k, half)], oy_sem, k - early, beyond)

    def my_rows(k):
        return pl.ds(pl.multiple_of(k * SPAN + core * half, half), half)

    def o_copy(k):
        return remote(omine.at[lot(k, half)], layer_ref.at[my_rows(k)], o_sem, k, across)

    def o_local(k):
        return pltpu.make_async_copy(omine.at[lot(k, half)], layer_ref.at[my_rows(k)], o_put.at[k])

    def d_copy(k):
        return remote(mine.at[lot(k, half)], delta_ref.at[my_rows(k)], d_sem, k, across)

    def d_local(k):
        return pltpu.make_async_copy(mine.at[lot(k, half)], delta_ref.at[my_rows(k)], d_put.at[k])

    def h_copy(k):
        return remote(h_out.at[lot(k, half)], mine.at[lot(k, half)], h_sem, k, across)

    def y_copy(k):
        return remote(mine.at[lot(k, half)], y_in.at[lot(k, half)], y_sem, k, beyond)

    def ax_copy(k):
        return remote(ax_out.at[lot(k, LANES)], ax_in.at[lot(k, LANES)], ax_sem, k, partner)

    def bx_copy(k):
        return remote(bx_out.at[lot(k, LANES)], bx_in.at[lot(k, LANES)], bx_sem, k, partner)

    def az_copy(step):
        return remote(ax_out.at[pl.ds(step * depth, depth)], az_in.at[step - 1], az_sem, step - 1, peer(step))

    def bz_copy(step):
        return remote(bx_out.at[pl.ds(step * depth, depth)], bz_in.at[step - 1], bz_sem, step - 1, peer(step))

    @pl.when(i == 0)
    def _():
        barrier = pltpu.get_barrier_semaphore()
        for device in [across, beyond, partner] + [peer(step) for step in range(1, lines)]:
            pl.semaphore_signal(barrier, inc=1, device_id=device, device_id_type=MESH_IDS)
        pl.semaphore_wait(barrier, lines + 2)
        for copy in fetch:
            copy.start()
        pbuf[SPAN : SPAN + 8] = jnp.zeros((8, chan), F32)
        dbuf[SPAN : SPAN + 8] = jnp.full((8, LANES), -2.0, F32)
        dstate[...] = jnp.zeros(dstate.shape, F32)
        own_params(rank, heads, inner, inner_all, dtb_ref, dec_ref, skip_ref, cw_ref, cb_ref, par, cwb)
        gain[0:1] = ggain_ref[:, pl.ds(off, inner)]
        for acc in (gconv, gskip, ghead, ggain, gnorm):
            acc[...] = jnp.zeros(acc.shape, F32)
        fetch[0].wait()
        for k in range(early, count):
            oy_copy(k).start()

    def join(k):
        h_copy(k).wait_recv()
        mine[lot(k, half)] = (kept[...] + mine[lot(k, half)].astype(F32)).astype(BF16)
        y_copy(k).start()

    @pl.when(i > 0)
    def _():
        join(c + 1)

    def out_grads(n_side, c_side, k):
        cols = lot(k, LANES)
        return jnp.concatenate(
            [tn(c_side[:, cols], nout_all[...]), tn(n_side[:, cols], dgate_all[...])], 1
        )

    def scan_grads(n_side, k):
        return tn(n_side[:, lot(k, LANES)], dall[...])

    per = LANES // depth

    def to_lines(k, joined, x_copy_of, x_out, z_copy_of, total):
        x_copy_of(k).wait_send()
        x_out[lot(k, LANES)] = joined.astype(BF16)
        if isinstance(k, int):
            if k == 0:
                total[...] = joined[0:depth]
            for step in range(max(1, k * per), (k + 1) * per):
                z_copy_of(step).start()

    def a_block(k):
        ax_copy(k).wait_recv()
        joined = out_grads(nhere, chere, k) + ax_in[lot(k, LANES)].astype(F32)
        to_lines(k, joined, ax_copy, ax_out, az_copy, atotal)

    def b_block(k):
        bx_copy(k).wait_recv()
        joined = scan_grads(nhere, k) + bx_in[lot(k, LANES)].astype(F32)
        to_lines(k, joined, bx_copy, bx_out, bz_copy, btotal)

    for k in range(blocks - 1):
        @pl.when(i == mid + 1 + k)
        def _():
            a_block(k)

    @pl.when(i == mid)
    def _():
        for copy in fetch[2:]:
            copy.wait()

    hid_own[lot(c, half)] = hid_ref[lot(core, half)]

    def inverse(k):
        inv = lax.rsqrt(as_column(sums_ref[0, pl.ds(k, 1), :]) * (1.0 / inner_all) + EPS)
        pull = as_column(sums_ref[1, pl.ds(k, 1), :]) * (inv * inv * inv) * (1.0 / inner_all)
        inv_now[...] = inv
        inv_own[lot(k, half)] = inv_now[lot(core, half)]
        return inv, pull

    def gating(k, scales, lanes, gate_in, ssd_in, dn_in):
        inv, pull = scales
        gate = gate_in[:, lanes]
        sig = jax.nn.sigmoid(gate)
        silu = gate * sig
        ssd = ssd_in[:, lanes]
        gated = ssd * silu
        dn = dn_in[:, lanes]
        g_l = gain[0:1, lanes]
        nout = gated * inv
        nout_all[lot(k, SPAN), lanes] = (nout * g_l).astype(BF16)
        ggain[:, lanes] += fold(dn * nout)
        d_gated = dn * g_l * inv - gated * pull
        dgate_all[lot(k, SPAN), lanes] = (d_gated * ssd * (sig * (1.0 + gate * (1.0 - sig)))).astype(BF16)
        return d_gated * silu

    def finish_out(k):
        total = omine[lot(k, half)].astype(F32) + ofar[lot(k, half)].astype(F32)
        inv = inv_own[lot(k, half)]
        value = hid_own[lot(k, half)].astype(F32)
        for group in range(model // LANES):
            lanes = slice(group * LANES, (group + 1) * LANES)
            omine[lot(k, half), lanes] = (value[:, lanes] + total[:, lanes] * inv).astype(BF16)
        o_copy(k).start()
        o_local(k).start()

    def scan_step(first):
        if first:
            scales, low_scales = inverse(c), inverse(c - mid)
        drow = docs_ref[:, lot(c, SPAN)].astype(F32)
        dcol = as_column(drow)
        before = docs_ref[:, lot(jnp.maximum(c - 1, 0), SPAN)].astype(F32)
        enter = as_column(before)[SPAN - 1 : SPAN]
        enter = jnp.where(c == 0, -1.0, enter)
        dbuf[0:SPAN] = dcol
        keeps = [None] + [dbuf[k : k + SPAN] == dcol for k in range(1, 4)]
        if not first:
            ax_out[lot(i - mid, LANES)] = out_grads(naway, caway, i - mid).astype(BF16)
        raw = stp_ref[...] + par[0:1]
        step = softplus(raw)
        row_i, col_i = iota((SPAN, SPAN), 0), iota((SPAN, SPAN), 1)
        tril = (row_i >= col_i).astype(BF16)
        log_step = step * par[1:2]
        running = tri_sum(tril, log_step, heads)
        run_rows = jnp.transpose(running)
        ending = running[SPAN - 1 : SPAN]
        tail = jnp.where(dcol == dcol[SPAN - 1 : SPAN], jnp.exp(ending - running), 0.0)
        reach = jnp.where(dcol == enter, jnp.exp(running), 0.0)
        same = jnp.concatenate([dcol, dcol], 1) == drow
        bias = jnp.where(same & (row_i <= col_i), 0.0, FAR)

        def activate(group):
            lanes = slice(group * LANES, (group + 1) * LANES)
            pre = pre_ref[:, lanes]
            sig = jax.nn.sigmoid(pre)
            return pre * sig, sig * (1.0 + pre * (1.0 - sig))

        b_act, b_slope = activate(pairs)
        c_act, c_slope = activate(pairs + 1)
        b_rows, c_rows = b_act.astype(BF16), c_act.astype(BF16)
        c_turned = jnp.transpose(c_act).astype(BF16)
        scores = exact_nt(b_act, c_act)
        low_half = iota((SPAN, LANES), 1) < LANES // 2
        d_scores = [jnp.zeros((half, SPAN), F32), jnp.zeros((half, half), F32)]
        d_b = jnp.zeros((SPAN, LANES), F32)
        d_c = jnp.zeros((SPAN, LANES), F32)
        head_up = jnp.zeros((SPAN, LANES), F32)
        head_down = jnp.zeros((SPAN, LANES), F32)
        head_step = jnp.zeros((SPAN, LANES), F32)
        head_hold = jnp.zeros((8, LANES), F32)
        for pair in range(pairs):
            lanes = slice(pair * LANES, (pair + 1) * LANES)
            ones_at = (iota((LANES, LANES), 1) == 2 * pair + iota((LANES, LANES), 0) // (LANES // 2)).astype(BF16)

            def head_sum(v):
                hi = v.astype(BF16)
                low = (v - hi.astype(F32)).astype(BF16)
                return nn(hi, ones_at) + nn(low, ones_at)

            act, slope = activate(pair)
            step_l = pair_lanes(step, pair, low_half)
            tail_l = pair_lanes(tail, pair, low_half)
            reach_l = pair_lanes(reach, pair, low_half)
            skip_l = pair_lanes(par[2:3], pair, low_half[0:1])
            ssd = ssd_ref[:, lanes]
            if first:
                d_ssd = gating(c, scales, lanes, gate_ref, ssd_ref, dn_ref)
                dssd_low[lot(c - mid, SPAN), lanes] = gating(
                    c - mid, low_scales, lanes, gate_low_ref, ssd_low_ref, dn_low_ref
                )
            else:
                d_ssd = dssd_low[lot(c, SPAN), lanes]
            gskip[:, lanes] += fold(d_ssd * act)
            dyb = d_ssd.astype(BF16)
            scaled = act * step_l
            xb = scaled.astype(BF16)
            held = state_ref[0, :, lanes]
            d_held = dstate[:, lanes]
            d_held_b = d_held.astype(BF16)
            ry = (d_ssd * reach_l).astype(BF16)
            xt = (scaled * tail_l).astype(BF16)
            parts = []
            for sub in range(2):
                head = 2 * pair + sub
                x_own = jnp.where(low_half if sub == 0 else ~low_half, scaled, 0.0).astype(BF16)
                blocks = []
                for blk in range(2):
                    rows = slice(blk * half, (blk + 1) * half)
                    cols = slice(blk * half, SPAN)
                    gap = run_rows[head : head + 1, cols] - running[rows, head : head + 1]
                    decay = jnp.exp(gap + bias[rows, cols])
                    blocks.append(nn((decay * scores[rows, cols]).astype(BF16), dyb[cols]))
                    d_scores[blk] = d_scores[blk] + decay * nt(x_own[rows], dyb[cols])
                parts.append(jnp.concatenate(blocks, 0))
            d_within = jnp.where(low_half, parts[0], parts[1])
            from_state = tail_l * nn(b_rows, d_held_b)
            d_scaled = d_within + from_state
            xf = xb.astype(F32)
            head_up += head_sum(dyb.astype(F32) * (ssd - skip_l * act) - xf * d_within)
            head_down += head_sum(xf * from_state)
            head_step += head_sum(d_scaled * act)
            hold = reach_l[SPAN - 1 : SPAN]
            hold_sum = jnp.sum((d_held * held.astype(F32)).reshape(LANES // 8, 8, LANES), axis=0) * hold
            head_hold += head_sum(hold_sum)
            d_b += nt(xt, d_held_b)
            d_c += nt(ry, held)
            dstate[:, lanes] = hold * d_held + nn(c_turned, ry)
            pbuf[0:SPAN, lanes] = (skip_l * d_ssd + step_l * d_scaled) * slope

        ds_b = jnp.concatenate(
            [
                d_scores[0],
                jnp.concatenate([jnp.zeros((half, half), F32), d_scores[1]], 1),
            ],
            0,
        )
        d_b += nn(ds_b.astype(BF16), c_rows)
        d_c += nn(jnp.transpose(ds_b).astype(BF16), b_rows)
        pbuf[0:SPAN, inner : inner + LANES] = d_b * b_slope
        pbuf[0:SPAN, inner + LANES : chan] = d_c * c_slope

        triu = (row_i <= col_i).astype(BF16)
        below = (row_i > col_i).astype(BF16)
        d_log = (
            tri_sum(triu, head_up, heads)
            + tri_sum(below, head_down, heads)
            + jnp.sum(head_hold, axis=0, keepdims=True)
        )
        d_step = d_log * par[1:2] + head_step
        d_raw = jnp.where(iota((SPAN, LANES), 1) < heads, d_step * jax.nn.sigmoid(raw), 0.0)
        dall[lot(c, SPAN), chan:] = d_raw.astype(BF16)
        ghead[0] += fold(d_raw)
        ghead[1] += fold(d_log * log_step)

        for group in range(chan // LANES):
            lanes = slice(group * LANES, (group + 1) * LANES)
            mixed = mixed_ref[:, lanes]
            own = pbuf[0:SPAN, lanes]
            acc = cwb[3:4, lanes] * own
            gconv[3, :, lanes] += fold(mixed * own)
            gconv[4, :, lanes] += fold(own)
            for k in range(1, 4):
                later = jnp.where(keeps[k], pbuf[k : k + SPAN, lanes], 0.0)
                acc = acc + cwb[3 - k : 4 - k, lanes] * later
                gconv[3 - k, :, lanes] += fold(mixed * later)
            dall[lot(c, SPAN), lanes] = acc.astype(BF16)
        pbuf[SPAN : SPAN + 8] = pbuf[0:8]
        dbuf[SPAN : SPAN + 8] = dbuf[0:8]

    @pl.when(i < mid)
    def _():
        scan_step(True)

    @pl.when(i >= mid)
    def _():
        for k in (c + mid, c):
            if k is not c:
                oy_copy(k).wait_recv()
                oy_copy(k).wait_send()
            finish_out(k)
        scan_step(False)
        ax_copy(i - mid).start()

    @pl.when(i == 0)
    def _():
        fetch[1].wait()

    def share(which):
        rows = pl.ds(pl.multiple_of(c * SPAN + which * half, half), half)
        made = nt(dgate_all[rows], w[:, 0:inner]) + nt(dall[rows], w[:, inner:])
        value = hid_ref[lot(which, half)].astype(F32)
        inv = lax.rsqrt(jnp.mean(value * value, -1, keepdims=True) + EPS)
        gnorm[...] += jnp.sum((made * (value * inv)).reshape(half // 8, 8, model), axis=0)
        return made

    h_out[lot(c, half)] = share(1 - core).astype(BF16)
    h_copy(c).start()
    kept[...] = share(core)

    @pl.when(i == count - 1)
    def _():
        def send_block(k, carry):
            bx_out[lot(k, LANES)] = scan_grads(naway, k).astype(BF16)
            bx_copy(k).start()
            return carry

        lax.fori_loop(0, blocks, send_block, 0)
        join(0)
        a_block(blocks - 1)

        chan_all = inner_all + 2 * LANES
        tap_rows, own_rows = chan_all // LANES, inner // LANES
        flat[...] = jnp.zeros(flat.shape, F32)
        norm = jnp.sum(gnorm[...], axis=0, keepdims=True)
        at = model // LANES
        for k in range(at):
            flat[k : k + 1] = norm[:, k * LANES : (k + 1) * LANES]
        for tap in range(gconv.shape[0]):
            row = jnp.sum(gconv[tap], axis=0, keepdims=True)
            for k in range(chan // LANES):
                place = at + k + (rank * own_rows if k < own_rows else (tap_rows - chan // LANES))
                flat[pl.ds(place, 1), :] = row[:, k * LANES : (k + 1) * LANES]
            at += tap_rows
        lane = iota((1, LANES), 1)
        spread = jnp.zeros((1, LANES), F32)
        for k in range(2):
            row = jnp.where(lane < heads, jnp.sum(ghead[k], axis=0, keepdims=True), 0.0)
            spread = spread + pltpu.roll(row, 4 * heads * k + rank * heads, 1)
        flat[at : at + 1] = spread
        at += 1
        for acc in (ggain, gskip):
            row = jnp.sum(acc[...], axis=0, keepdims=True)
            for k in range(own_rows):
                flat[pl.ds(at + rank * own_rows + k, 1), :] = row[:, k * LANES : (k + 1) * LANES]
            at += inner_all // LANES

        hops = [across, beyond, partner]
        bit = 1
        while bit < lines:
            hops.append({"dp": (line + bit * (1 - 2 * ((line // bit) % 2))) * 2 + side})
            bit *= 2
        last = flat_in.shape[0] - 1

        def flat_copy(k):
            return remote(
                flat.at[...] if k == 0 else flat_in.at[len(hops) + k], flat_in.at[k], f_sem, k, hops[k]
            )

        def flat_step(k):
            flat_copy(k).wait_recv()
            held = (flat[...] if k == 0 else flat_in[len(hops) + k]) + flat_in[k]
            if k + 1 < len(hops):
                flat_in[len(hops) + k + 1] = held
                flat_copy(k + 1).start()
            else:
                flat_in[last] = held

        flat_copy(0).start()

        for step in range(1, lines):
            az_copy(step).wait_recv()
            atotal[...] += az_in[step - 1].astype(F32)
        gates[0] = atotal[:, inner:]
        gout_put = pltpu.make_async_copy(atotal.at[:, pl.ds(0, inner)], gout_ref, put_sem.at[9])
        gout_put.start()
        gate_near = remote(gates.at[0], gates.at[1], g_sem, 0, across)
        gate_far = remote(gates.at[0], gates.at[2], g_sem, 1, beyond)
        gate_pass = remote(gates.at[2], gates.at[3], g_sem, 2, across)
        gate_near.start()
        gate_far.start()
        flat_step(0)

        gain_row = ngain_ref[...]

        def finish_hidden(k, carry):
            y_copy(k).wait_recv()
            y_copy(k).wait_send()
            d_hidden = mine[lot(k, half)].astype(F32) + y_in[lot(k, half)].astype(F32)
            value = hid_own[lot(k, half)].astype(F32)
            inv = lax.rsqrt(jnp.mean(value * value, -1, keepdims=True) + EPS)
            scaled = d_hidden * gain_row
            pull = jnp.mean(scaled * value, -1, keepdims=True)
            mine[lot(k, half)] = (inv * scaled - value * (inv * inv * inv) * pull).astype(BF16)
            d_copy(k).start()
            d_local(k).start()
            return carry

        def down(k, carry):
            return finish_hidden(count - 1 - k, carry)

        b_block(0)
        lax.fori_loop(0, 3, down, 0)
        flat_step(1)
        b_block(1)
        lax.fori_loop(3, 5, down, 0)
        flat_step(2)
        b_block(2)
        gate_far.wait_recv()
        gate_pass.start()
        b_block(3)
        for k in range(3, len(hops)):
            flat_step(k)
        flat_put = pltpu.make_async_copy(flat_in.at[last], flatout_ref, put_sem.at[10])
        flat_put.start()
        lax.fori_loop(5, count - 1, down, 0)

        for step in range(1, lines):
            bz_copy(step).wait_recv()
            btotal[...] += bz_in[step - 1].astype(F32)
        values[0] = btotal[:, 0:inner]
        value_near = remote(values.at[0], values.at[1], v_sem, 0, across)
        value_far = remote(values.at[0], values.at[2], v_sem, 1, beyond)
        value_pass = remote(values.at[2], values.at[3], v_sem, 2, across)
        shared_near = remote(shared.at[0], shared.at[1], s_sem, 0, across)
        shared_far = remote(shared.at[2], shared.at[3], s_sem, 1, beyond)
        shared[0, :, 0 : 2 * LANES] = btotal[:, inner : inner + 2 * LANES]
        steps = pltpu.roll(btotal[:, inner + 2 * LANES :], rank * heads, 1)
        place = iota(steps.shape, 1) - rank * heads
        shared[0, :, 2 * LANES :] = jnp.where((place >= 0) & (place < heads), steps, 0.0)
        shared_near.start()
        value_far.start()
        value_near.start()
        finish_hidden(0, 0)
        shared_near.wait_recv()
        shared[2] = shared[0] + shared[1]
        shared_far.start()

        def put(source, k, first, owner, index):
            column = pl.multiple_of(first + owner * inner, LANES)
            return pltpu.make_async_copy(source.at[k], gin_ref.at[:, pl.ds(column, inner)], put_sem.at[index])

        owners = (rank, rank + 1 - 2 * core, (rank + 2) % 4, (rank + 3 - 2 * core) % 4)
        puts = [put(gates, 0, 0, owners[0], 0), put(values, 0, inner_all, owners[0], 4)]
        gate_near.wait_recv()
        gate_pass.wait_recv()
        puts += [put(gates, k, 0, owners[k], k) for k in range(1, 4)]
        value_near.wait_recv()
        puts.append(put(values, 1, inner_all, owners[1], 5))
        for copy in puts:
            copy.start()
        value_far.wait_recv()
        value_pass.start()
        puts.append(put(values, 2, inner_all, owners[2], 6))
        puts[-1].start()
        shared_far.wait_recv()
        shared[1] = shared[2] + shared[3]
        puts.append(
            pltpu.make_async_copy(
                shared.at[1], gin_ref.at[:, pl.ds(2 * inner_all, 3 * LANES)], put_sem.at[8]
            )
        )
        puts[-1].start()
        value_pass.wait_recv()
        puts.append(put(values, 3, inner_all, owners[3], 7))
        puts[-1].start()

        def drain(k, carry):
            h_copy(k).wait_send()
            d_copy(k).wait()
            d_local(k).wait()
            o_copy(k).wait()
            o_local(k).wait()
            return carry

        lax.fori_loop(0, count, drain, 0)
        for step in range(1, lines):
            az_copy(step).wait_send()
            bz_copy(step).wait_send()
        for copy in (
            gate_near, gate_far, gate_pass, value_near, value_far, value_pass, shared_near, shared_far,
        ):
            copy.wait_send()
        for k in range(len(hops)):
            flat_copy(k).wait_send()
        for copy in puts + [gout_put, flat_put]:
            copy.wait()


def mixer_backward(
    docs, hidden, held, sums, params, ggain, ngain, sorted_parts, w_in, mine, far,
    heads, lines, depth, early,
):
    gate, mixed, pre, ssd, stp, states, dn = held
    tokens, inner = ssd.shape
    model = hidden.shape[1]
    chan = inner + 2 * LANES
    width = inner + chan + LANES
    wide = width - inner
    inner_all = ggain.shape[1]
    count = tokens // SPAN
    mid = count // 2
    half = SPAN // 2
    blocks, fars = lines * depth // LANES, max(1, lines - 1)
    hops = 3 + (lines - 1).bit_length()
    rows = (model + 5 * (inner_all + 2 * LANES) + LANES + 2 * inner_all) // LANES
    rows += -rows % 8

    def tok(size):
        return pl.BlockSpec((SPAN, size), lambda i: (count - 1 - i, 0))

    def early_tok(size, base):
        return pl.BlockSpec((SPAN, size), lambda i: (base + (mid - 1 - i) * (1 - i // mid), 0))

    def full(shape):
        return pl.BlockSpec(shape, lambda i: (0,) * len(shape))

    anywhere = pl.BlockSpec(memory_space=pl.ANY)
    dma, vmem = pltpu.SemaphoreType.DMA, pltpu.VMEM
    consts = params + (ggain, ngain)
    big = tuple(sorted_parts)[0:2] + tuple(sorted_parts)[2:4] + (w_in, mine, far)
    side_shape = (tokens, lines * depth)
    return pl.pallas_call(
        lambda *refs: backward_kernel((inner, heads, inner_all, lines, depth, early), *refs),
        out_shape=(
            jax.ShapeDtypeStruct((tokens, model), BF16),
            jax.ShapeDtypeStruct((tokens, model), BF16),
            jax.ShapeDtypeStruct((depth, 2 * inner_all + 3 * LANES), F32),
            jax.ShapeDtypeStruct((depth, inner), F32),
            jax.ShapeDtypeStruct((rows, LANES), F32),
        ),
        grid=(count,),
        in_specs=[
            full(docs.shape), tok(model), early_tok(inner, mid), early_tok(inner, mid),
            early_tok(inner, 0), early_tok(inner, 0), early_tok(inner, 0),
            tok(inner), tok(chan), tok(chan), tok(LANES),
            pl.BlockSpec((1, LANES, inner), lambda i: (count - 1 - i, 0, 0)),
            full(sums.shape),
        ]
        + [full(v.shape) for v in consts]
        + [anywhere] * len(big),
        out_specs=(anywhere,) * 5,
        scratch_shapes=[
            vmem(side_shape, BF16), vmem(side_shape, BF16), vmem(side_shape, BF16), vmem(side_shape, BF16),
            vmem(w_in.shape, BF16), dma((len(big),)),
            vmem((SPAN + 8, chan), F32), vmem((SPAN + 8, LANES), F32), vmem((LANES, inner), F32),
            vmem((8, LANES), F32), vmem((8, chan), F32), vmem((8, inner), F32),
            vmem((5, 8, chan), F32), vmem((8, inner), F32), vmem((2, 8, LANES), F32),
            vmem((8, inner), F32), vmem((8, model), F32),
            vmem((tokens, inner), BF16), vmem((tokens, inner), BF16), vmem((tokens, wide), BF16),
            vmem((tokens // 2, inner), F32), vmem((SPAN, LANES), F32), vmem((tokens // 2, LANES), F32),
            vmem((tokens // 2, model), BF16),
            vmem((tokens // 2, model), BF16), vmem((tokens // 2, model), BF16),
            vmem((tokens // 2, model), BF16), vmem((half, model), F32),
            dma((2, count)), dma((2, count)), dma((2, count)), dma((count,)),
            vmem((tokens // 2, model), BF16), vmem((tokens // 2, model), BF16),
            dma((2, count - early)), dma((2, count)), dma((count,)),
            vmem((blocks * LANES, 2 * inner), BF16), vmem((blocks * LANES, 2 * inner), BF16),
            dma((2, blocks)), vmem((fars, depth, 2 * inner), BF16), dma((2, fars)),
            vmem((depth, 2 * inner), F32),
            vmem((blocks * LANES, wide), BF16), vmem((blocks * LANES, wide), BF16),
            dma((2, blocks)), vmem((fars, depth, wide), BF16), dma((2, fars)), vmem((depth, wide), F32),
            vmem((4, depth, inner), F32), dma((2, 3)), vmem((4, depth, inner), F32), dma((2, 3)),
            vmem((4, depth, 3 * LANES), F32), dma((2, 2)), dma((11,)),
            vmem((rows, LANES), F32), vmem((2 * hops + 1, rows, LANES), F32), dma((2, hops)),
        ],
        compiler_params=pltpu.CompilerParams(
            dimension_semantics=("arbitrary",), vmem_limit_bytes=67043328,
            collective_id=1, has_side_effects=True,
        ),
        cost_estimate=cost(90.0),
        name="mixer_backward",
    )(
        docs, hidden, gate, dn, gate, ssd, dn, ssd, mixed, pre, stp, states, sums, *consts, *big
    )


def gather_kernel(
    dims, hid_ref, cot_ref, ngain_ref, w_ref, step_ref, wo_ref,
    win_ref, wout_ref, normed_ref, *refs,
):
    lines, depth, inner, inner_all, aligned = dims
    outs = refs[:4] if aligned else ()
    mine, zsend, zrecv, xsend, xrecv, takes, puts = refs[len(outs):]
    trank, drank = lax.axis_index("tensor"), lax.axis_index("dp")
    line, side = drank // 2, drank % 2
    model = hid_ref.shape[1]
    off = pl.multiple_of(trank * inner, LANES)
    pieces = (
        (w_ref, inner_all + off, win_ref, inner, inner),
        (w_ref, 2 * inner_all, win_ref, 2 * inner, 2 * LANES),
        (step_ref, 0, win_ref, 2 * inner + 2 * LANES, LANES),
        (w_ref, off, win_ref, 0, inner),
        (wo_ref, 0, wout_ref, 0, inner),
    )

    def peer(step):
        return {"dp": lax.rem(line + step, lines) * 2 + side}

    partner = {"dp": line * 2 + 1 - side}
    barrier = pltpu.get_barrier_semaphore()
    for step in range(1, lines):
        pl.semaphore_signal(barrier, inc=1, device_id=peer(step), device_id_type=MESH_IDS)
    pl.semaphore_signal(barrier, inc=1, device_id=partner, device_id_type=MESH_IDS)
    pl.semaphore_wait(barrier, lines)

    def rows(index):
        return pl.ds(pl.multiple_of(index * depth, depth), depth)

    def block(p, index):
        _, _, dst, at, width = pieces[p]
        return dst.at[rows(index), pl.ds(at, width)]

    def own(p):
        src, at, _, _, width = pieces[p]
        return src.at[:, pl.ds(at, width)]

    def z_copy(p, step, src, index):
        return pltpu.make_async_remote_copy(
            src_ref=src, dst_ref=block(p, index), send_sem=zsend.at[p, step - 1],
            recv_sem=zrecv.at[p, step - 1], device_id=peer(step), device_id_type=MESH_IDS,
        )

    def x_copy(p, step, src, index):
        return pltpu.make_async_remote_copy(
            src_ref=src, dst_ref=block(p, index), send_sem=xsend.at[p, step],
            recv_sem=xrecv.at[p, step], device_id=partner, device_id_type=MESH_IDS,
        )

    count = len(pieces)
    for p in range(count):
        for step in range(1, lines):
            z_copy(p, step, own(p), drank).start()
        x_copy(p, 0, own(p), drank).start()
    spots, at = [], 0
    for p in range(count):
        spots.append(mine.at[:, pl.ds(at, pieces[p][4])])
        at += pieces[p][4]
    fetched = [pltpu.make_async_copy(own(p), spots[p], takes.at[p]) for p in range(count)]
    for copy in fetched:
        copy.start()

    gain = ngain_ref[...]

    def normalize(hid, cot, normed, *sorted_refs):
        value = hid[...].astype(F32)
        inv = lax.rsqrt(jnp.mean(value * value, -1, keepdims=True) + EPS)
        normed[...] = (value * inv * gain).astype(BF16)
        if aligned:
            for src, away, here in (
                (normed, sorted_refs[0], sorted_refs[1]), (cot, sorted_refs[2], sorted_refs[3]),
            ):
                for j in range(lines):
                    first = lax.rem(line + j, lines) * 2
                    lanes = slice(j * depth, (j + 1) * depth)
                    away[:, lanes] = src[:, pl.ds(pl.multiple_of((first + 1 - side) * depth, depth), depth)]
                    here[:, lanes] = src[:, pl.ds(pl.multiple_of((first + side) * depth, depth), depth)]

    full = pl.BlockSpec((SPAN, model), lambda i: (i, 0))
    half = pl.BlockSpec((SPAN, lines * depth), lambda i: (i, 0))
    pltpu.emit_pipeline(
        normalize, grid=(hid_ref.shape[0] // SPAN,), in_specs=[full, full],
        out_specs=[full] + [half] * len(outs),
    )(hid_ref, cot_ref, normed_ref, *outs)

    stored = [pltpu.make_async_copy(spots[p], block(p, drank), puts.at[p]) for p in range(count)]
    for p in range(count):
        fetched[p].wait()
        stored[p].start()
    for p in range(count):
        for step in range(1, lines):
            source = lax.rem(line - step + lines, lines) * 2 + side
            got = block(p, source)
            z_copy(p, step, got, source).wait_recv()
            x_copy(p, step, got, source).start()
    for p in range(count):
        for step in range(lines):
            source = lax.rem(line - step + lines, lines) * 2 + 1 - side
            x_copy(p, step, block(p, source), source).wait_recv()
    for p in range(count):
        for step in range(1, lines):
            z_copy(p, step, own(p), drank).wait_send()
        for step in range(lines):
            x_copy(p, step, own(p), drank).wait_send()
        stored[p].wait()


def gather_weights(hidden, cotangent, norm_gain, in_weight, own_step, out_weight, lines, inner_all):
    tokens, model = hidden.shape
    depth, inner = out_weight.shape
    aligned = depth % LANES == 0
    width = 2 * inner + 3 * LANES
    half = jax.ShapeDtypeStruct((tokens, lines * depth), BF16)
    anywhere = pl.BlockSpec(memory_space=pl.ANY)
    outs = (
        jax.ShapeDtypeStruct((model, width), BF16),
        jax.ShapeDtypeStruct((model, inner), BF16),
        jax.ShapeDtypeStruct((tokens, model), BF16),
    ) + (half,) * (4 if aligned else 0)
    dma = pltpu.SemaphoreType.DMA
    return pl.pallas_call(
        lambda *refs: gather_kernel((lines, depth, inner, inner_all, aligned), *refs),
        out_shape=outs,
        in_specs=[anywhere, anywhere, pl.BlockSpec(memory_space=pltpu.VMEM)] + [anywhere] * 3,
        out_specs=(anywhere,) * len(outs),
        scratch_shapes=[
            pltpu.VMEM((depth, width + inner), BF16),
            dma((5, max(1, lines - 1))), dma((5, max(1, lines - 1))), dma((5, lines)), dma((5, lines)),
            dma((5,)), dma((5,)),
        ],
        compiler_params=pltpu.CompilerParams(collective_id=0, has_side_effects=True),
        cost_estimate=cost(45.0),
        name="gather_weights",
    )(hidden, cotangent, norm_gain, in_weight, own_step, out_weight)


def body(
    hidden_in, doc_ids, cotangent, norm_gain, in_weight, conv_weight, conv_bias,
    dt_bias, log_decay, skip_gain, gate_gain, out_weight,
):
    tcount, dcount = lax.axis_size("tensor"), lax.axis_size("dp")
    trank, drank = lax.axis_index("tensor"), lax.axis_index("dp")
    lines = dcount // 2
    line, side = drank // 2, drank % 2
    inner_all, head_all = gate_gain.shape[0], dt_bias.shape[0]
    inner, heads = inner_all // tcount, head_all // tcount
    tokens, model = hidden_in.shape
    base_bc = 2 * inner_all
    base_dt = base_bc + 2 * LANES
    depth = in_weight.shape[0]

    def line_to(step):
        return lambda k: ((k // 2 + step) % lines) * 2 + k % 2

    own_step = jnp.pad(
        lax.dynamic_slice_in_dim(in_weight, base_dt + trank * heads, heads, 1),
        ((0, 0), (0, LANES - heads)),
    )
    w_in, w_out, normed, *sorted_parts = gather_weights(
        hidden_in, cotangent, norm_gain.reshape(1, -1), in_weight, own_step, out_weight,
        lines, inner_all,
    )
    if not sorted_parts:

        def features(v, which):
            return jnp.concatenate(
                [
                    lax.dynamic_slice_in_dim(v, (((line + j) % lines) * 2 + which) * depth, depth, 1)
                    for j in range(lines)
                ],
                1,
            )

        sorted_parts = [features(v, which) for v in (normed, cotangent) for which in (1 - side, side)]
    n_away, n_here, c_away, c_here = sorted_parts

    def row(v):
        return v.reshape(1, -1)

    params = (conv_weight, row(conv_bias), row(dt_bias), row(log_decay), row(skip_gain))

    early = 4
    *held, sums, mine, far = mixer_forward(
        doc_ids, normed, cotangent, w_in, w_out, params, row(gate_gain), heads, early
    )
    delta, layer_out, grad_in, g_out, flat = mixer_backward(
        doc_ids, hidden_in, held, sums, params, row(gate_gain), row(norm_gain), sorted_parts, w_in,
        mine, far, heads, lines, depth, early,
    )
    grad_input = cotangent.astype(F32) + delta.astype(F32)
    chan_all = inner_all + 2 * LANES
    flat = flat.reshape(-1)
    cuts, at = [], 0
    for size in (model, 5 * chan_all, LANES, inner_all, inner_all):
        cuts.append(flat[at : at + size])
        at += size
    conv_all = cuts[1].reshape(5, chan_all)
    return (
        layer_out, grad_input, cuts[0], grad_in[:, : in_weight.shape[1]], conv_all[:4], conv_all[4],
        cuts[2][:head_all], cuts[2][head_all : 2 * head_all],
        jnp.sum(cuts[4].reshape(head_all, -1), 1), cuts[3], g_out,
    )


def solution(mesh):
    rows, whole = P("dp", None), P()
    return jax.shard_map(
        body,
        mesh=mesh,
        in_specs=(rows, rows, rows, whole, rows, whole, whole, whole, whole, whole, whole, P("dp", "tensor")),
        out_specs=(rows, rows, whole, rows, whole, whole, whole, whole, whole, whole, P("dp", "tensor")),
        check_vma=False,
    )
```

```python
import jax
import jax.numpy as jnp
from jax import lax
from jax.experimental import pallas as pl
from jax.experimental.pallas import tpu as pltpu
from jax.sharding import PartitionSpec as P

SPAN = 256
LANES = 128
EPS = 1e-05
FAR = -1e30
VMEM_MOST = 60 * 2**20
F32 = jnp.float32
BF16 = jnp.bfloat16


def cost(micros):
    return pl.CostEstimate(flops=int(micros * 1.15e9), bytes_accessed=1 << 20, transcendentals=0)


def nn(a, b):
    return lax.dot_general(a, b, (((1,), (0,)), ((), ())), preferred_element_type=F32)


def nt(a, b):
    return lax.dot_general(a, b, (((1,), (1,)), ((), ())), preferred_element_type=F32)


def tn(a, b):
    return lax.dot_general(a, b, (((0,), (0,)), ((), ())), preferred_element_type=F32)


def iota(shape, dim):
    return lax.broadcasted_iota(jnp.int32, shape, dim)


def as_column(row, rows=SPAN):
    return jnp.transpose(jnp.broadcast_to(row, (LANES, rows)))


def as_row(block):
    return jnp.sum(jnp.transpose(block), axis=0, keepdims=True)


def split3(v):
    hi = v.astype(BF16)
    rest = v - hi.astype(F32)
    mid = rest.astype(BF16)
    low = (rest - mid.astype(F32)).astype(BF16)
    return hi, mid, low


def tri_sum(tri, v, heads):
    lane = iota(v.shape, 1)
    v = jnp.where(lane < heads, v, 0.0)
    hi = v.astype(BF16).astype(F32)
    rest = v - hi
    mid = rest.astype(BF16).astype(F32)
    low = rest - mid
    packed = hi + pltpu.roll(mid, heads, 1) + pltpu.roll(low, 2 * heads, 1)
    out = nn(tri, packed.astype(BF16))
    return out + pltpu.roll(out, LANES - heads, 1) + pltpu.roll(out, LANES - 2 * heads, 1)


def pair_lanes(cols, pair, low_half):
    rows = cols.shape[0]
    first = jnp.broadcast_to(cols[:, 2 * pair : 2 * pair + 1], (rows, LANES))
    second = jnp.broadcast_to(cols[:, 2 * pair + 1 : 2 * pair + 2], (rows, LANES))
    return jnp.where(low_half, first, second)


def exact_nt(a, b):
    a_hi, b_hi = a.astype(BF16), b.astype(BF16)
    a_lo = (a - a_hi.astype(F32)).astype(BF16)
    b_lo = (b - b_hi.astype(F32)).astype(BF16)
    return nt(a_hi, b_hi) + (nt(a_hi, b_lo) + nt(a_lo, b_hi))


def softplus(v):
    return jnp.maximum(v, 0.0) + jnp.log1p(jnp.exp(-jnp.abs(v)))


def own_lanes(row, rank, heads):
    total = row.shape[1]
    pick = (iota((total, LANES), 0) == rank * heads + iota((total, LANES), 1)) & (
        iota((total, LANES), 1) < heads
    )
    wide = jnp.broadcast_to(row, (8, total))
    out = lax.dot_general(
        wide, pick.astype(F32), (((1,), (0,)), ((), ())),
        precision=lax.Precision.HIGHEST, preferred_element_type=F32,
    )
    return out[0:1]


def fold(v):
    return jnp.sum(v.reshape(SPAN // 8, 8, v.shape[1]), axis=0)


def own_params(rank, heads, inner, inner_all, dtb_ref, dec_ref, skip_ref, cw_ref, cb_ref, par, cwb):
    chan = inner + 2 * LANES
    off = pl.multiple_of(rank * inner, LANES)
    taps = cw_ref.shape[0]
    par[0:1] = own_lanes(dtb_ref[...], rank, heads)
    par[1:2] = -jnp.exp(own_lanes(dec_ref[...], rank, heads))
    par[2:3] = own_lanes(skip_ref[...], rank, heads)
    cwb[0:taps, 0:inner] = cw_ref[:, pl.ds(off, inner)].astype(F32)
    cwb[0:taps, inner:chan] = cw_ref[:, inner_all:].astype(F32)
    cwb[taps : taps + 1, 0:inner] = cb_ref[:, pl.ds(off, inner)]
    cwb[taps : taps + 1, inner:chan] = cb_ref[:, inner_all:]


MESH_IDS = pl.DeviceIdType.MESH


def forward_kernel(
    dims, docs_ref, normed_ref, cot_ref, win_ref, wout_ref, cw_ref, cb_ref,
    dtb_ref, dec_ref, skip_ref, ggain_ref,
    gate_ref, mixed_ref, pre_ref, ssd_ref, stp_ref, state_ref, dn_ref,
    sums_ref, mine_ref, far_ref,
    xbuf, dbuf, state, par, cwb, gain, gg_ref,
    own_sums, h_out, h_in, kept, mine, far, h_sem, y_sem, s_in, s_sem, put_sem,
):
    inner, heads, early = dims
    pairs = heads // 2
    chan = inner + 2 * LANES
    i = pl.program_id(0)
    spans = pl.num_programs(0)
    rank = lax.axis_index("tensor")
    core = rank % 2
    inner_all = ggain_ref.shape[1]
    half = SPAN // 2
    across = {"tensor": rank + 1 - 2 * core}
    beyond = {"tensor": (rank + 2) % 4}
    crossed = {"tensor": (rank + 3 - 2 * core) % 4}

    @pl.when(i == 0)
    def _():
        barrier = pltpu.get_barrier_semaphore()
        for device in (across, beyond, crossed):
            pl.semaphore_signal(barrier, inc=1, device_id=device, device_id_type=MESH_IDS)
        pl.semaphore_wait(barrier, 3)
        xbuf[0:8] = jnp.zeros((8, chan), F32)
        dbuf[0:8] = jnp.full((8, LANES), -1.0, F32)
        state[...] = jnp.zeros(state.shape, F32)
        own_params(rank, heads, inner, inner_all, dtb_ref, dec_ref, skip_ref, cw_ref, cb_ref, par, cwb)
        gain[0:1] = ggain_ref[:, pl.ds(pl.multiple_of(rank * inner, LANES), inner)]

    def slot(k):
        return pl.ds(pl.multiple_of(k * half, half), half)

    def h_copy(k):
        return pltpu.make_async_remote_copy(
            src_ref=h_out.at[slot(k)], dst_ref=h_in.at[slot(k)], send_sem=h_sem.at[0, k],
            recv_sem=h_sem.at[1, k], device_id=across, device_id_type=MESH_IDS,
        )

    def y_copy(k):
        return pltpu.make_async_remote_copy(
            src_ref=mine.at[slot(k)], dst_ref=far.at[slot(k)], send_sem=y_sem.at[0, k],
            recv_sem=y_sem.at[1, k], device_id=beyond, device_id_type=MESH_IDS,
        )

    def join(k):
        h_copy(k).wait_recv()
        mine[slot(k)] = (kept[slot(core)] + h_in[slot(k)].astype(F32)).astype(BF16)

    nb = normed_ref[...]
    xbuf[8 : 8 + SPAN] = nn(nb, win_ref[:, inner : inner + chan])
    gate_ref[...] = nn(nb, win_ref[:, 0:inner])
    stp = nn(nb, win_ref[:, inner + chan : inner + chan + LANES])
    stp_ref[...] = stp
    mixed_ref[...] = xbuf[8 : 8 + SPAN]
    dn_ref[...] = nn(cot_ref[...], wout_ref[...])

    drow = docs_ref[:, pl.ds(pl.multiple_of(i * SPAN, SPAN), SPAN)].astype(F32)
    dcol = as_column(drow)
    enter = dbuf[7:8]
    dbuf[8 : 8 + SPAN] = dcol
    keeps = [None] + [dbuf[8 - k : 8 - k + SPAN] == dcol for k in range(1, 4)]

    def conv(group):
        lanes = slice(group * LANES, (group + 1) * LANES)
        acc = cwb[4:5, lanes] + cwb[3:4, lanes] * xbuf[8 : 8 + SPAN, lanes]
        for k in range(1, 4):
            acc = acc + cwb[3 - k : 4 - k, lanes] * jnp.where(
                keeps[k], xbuf[8 - k : 8 - k + SPAN, lanes], 0.0
            )
        pre_ref[:, lanes] = acc
        return acc * jax.nn.sigmoid(acc)

    b_act, c_act = conv(pairs), conv(pairs + 1)
    b_rows, c_rows = b_act.astype(BF16), c_act.astype(BF16)

    step = softplus(stp + par[0:1])
    row_i, col_i = iota((SPAN, SPAN), 0), iota((SPAN, SPAN), 1)
    tril = (row_i >= col_i).astype(BF16)
    running = tri_sum(tril, step * par[1:2], heads)
    run_rows = jnp.transpose(running)
    ending = running[SPAN - 1 : SPAN]
    tail = jnp.where(dcol == dcol[SPAN - 1 : SPAN], jnp.exp(ending - running), 0.0)
    reach = jnp.where(dcol == enter, jnp.exp(running), 0.0)
    same = jnp.concatenate([dcol, dcol], 1) == drow
    bias = jnp.where(same & (row_i >= col_i), 0.0, FAR)
    scores = exact_nt(c_act, b_act)
    b_turned = jnp.transpose(b_act).astype(BF16)
    low_half = iota((SPAN, LANES), 1) < LANES // 2
    square = jnp.zeros((SPAN, LANES), F32)
    cross = jnp.zeros((SPAN, LANES), F32)
    for pair in range(pairs):
        lanes = slice(pair * LANES, (pair + 1) * LANES)
        act = conv(pair)
        scaled = act * pair_lanes(step, pair, low_half)
        xb = scaled.astype(BF16)
        tail_l = pair_lanes(tail, pair, low_half)
        reach_l = pair_lanes(reach, pair, low_half)
        held = state[:, lanes]
        held_b = held.astype(BF16)
        state_ref[0, :, lanes] = held_b
        state[:, lanes] = nn(b_turned, (scaled * tail_l).astype(BF16)) + reach_l[SPAN - 1 : SPAN] * held
        out = reach_l * nn(c_rows, held_b)
        parts = []
        for sub in range(2):
            head = 2 * pair + sub
            blocks = []
            for blk in range(2):
                rows = slice(blk * half, (blk + 1) * half)
                width = (blk + 1) * half
                gap = running[rows, head : head + 1] - run_rows[head : head + 1, 0:width]
                weight = jnp.exp(gap + bias[rows, 0:width]) * scores[rows, 0:width]
                blocks.append(nn(weight.astype(BF16), xb[0:width]))
            parts.append(jnp.concatenate(blocks, 0))
        out = out + jnp.where(low_half, parts[0], parts[1])
        skip_l = pair_lanes(par[2:3], pair, low_half[0:1])
        ssd = out + skip_l * act
        ssd_ref[:, lanes] = ssd
        gate = gate_ref[:, lanes]
        gated = ssd * (gate * jax.nn.sigmoid(gate))
        square = square + gated * gated
        gained = gain[0:1, lanes] * gated
        gg_ref[:, lanes] = gained.astype(BF16)
        cross = cross + dn_ref[:, lanes] * gained
    own_sums[0, pl.ds(i, 1), :] = as_row(square)
    own_sums[1, pl.ds(i, 1), :] = as_row(cross)
    xbuf[0:8] = xbuf[SPAN : SPAN + 8]
    dbuf[0:8] = dbuf[SPAN : SPAN + 8]
    @pl.when(i > 0)
    def _():
        join(i - 1)

        @pl.when(i - 1 < early)
        def _():
            y_copy(i - 1).start()

    kept[...] = nt(gg_ref[...], wout_ref[...])
    h_out[slot(i)] = kept[slot(1 - core)].astype(BF16)
    h_copy(i).start()

    @pl.when(i == spans - 1)
    def _():
        def s_copy(k, device):
            return pltpu.make_async_remote_copy(
                src_ref=own_sums, dst_ref=s_in.at[k], send_sem=s_sem.at[0, k],
                recv_sem=s_sem.at[1, k], device_id=device, device_id_type=MESH_IDS,
            )

        sent = [s_copy(0, across), s_copy(1, beyond), s_copy(2, crossed)]
        for copy in sent:
            copy.start()
        join(i)
        mine_put = pltpu.make_async_copy(mine, mine_ref, put_sem.at[0])
        mine_put.start()
        for copy in sent:
            copy.wait_recv()
        near = own_sums[...] + s_in[0]
        sums_ref[...] = near + (s_in[1] + s_in[2])
        for k in range(early):
            y_copy(k).wait_recv()
        far_put = pltpu.make_async_copy(far, far_ref, put_sem.at[1])
        far_put.start()
        for copy in sent:
            copy.wait_send()

        def drain(k, carry):
            h_copy(k).wait_send()
            return carry

        lax.fori_loop(0, spans, drain, 0)
        for k in range(early):
            y_copy(k).wait_send()
        mine_put.wait()
        far_put.wait()


def mixer_forward(docs, normed, cotangent, w_in, w_out, params, ggain, heads, early):
    tokens, model = normed.shape
    inner = w_out.shape[1]
    chan = inner + 2 * LANES
    spans = tokens // SPAN

    def tok(width):
        return pl.BlockSpec((SPAN, width), lambda i: (i, 0))

    def full(shape):
        return pl.BlockSpec(shape, lambda i: (0,) * len(shape))

    anywhere = pl.BlockSpec(memory_space=pl.ANY)
    sums = (2, spans, SPAN)
    outs = (
        jax.ShapeDtypeStruct((tokens, inner), F32),
        jax.ShapeDtypeStruct((tokens, chan), F32),
        jax.ShapeDtypeStruct((tokens, chan), F32),
        jax.ShapeDtypeStruct((tokens, inner), F32),
        jax.ShapeDtypeStruct((tokens, LANES), F32),
        jax.ShapeDtypeStruct((spans, LANES, inner), BF16),
        jax.ShapeDtypeStruct((tokens, inner), F32),
        jax.ShapeDtypeStruct(sums, F32),
        jax.ShapeDtypeStruct((tokens // 2, model), BF16),
        jax.ShapeDtypeStruct((early * SPAN // 2, model), BF16),
    )
    out_specs = (
        tok(inner), tok(chan), tok(chan), tok(inner), tok(LANES),
        pl.BlockSpec((1, LANES, inner), lambda i: (i, 0, 0)),
        tok(inner), full(sums), anywhere, anywhere,
    )
    consts = (w_in, w_out) + params + (ggain,)
    dma, vmem = pltpu.SemaphoreType.DMA, pltpu.VMEM
    return pl.pallas_call(
        lambda *refs: forward_kernel((inner, heads, early), *refs),
        out_shape=outs,
        grid=(spans,),
        in_specs=[full(docs.shape), tok(model), tok(model)] + [full(v.shape) for v in consts],
        out_specs=out_specs,
        scratch_shapes=[
            vmem((SPAN + 8, chan), F32), vmem((SPAN + 8, LANES), F32), vmem((LANES, inner), F32),
            vmem((8, LANES), F32), vmem((8, chan), F32), vmem((8, inner), F32),
            vmem((SPAN, inner), BF16), vmem(sums, F32),
            vmem((tokens // 2, model), BF16), vmem((tokens // 2, model), BF16),
            vmem((SPAN, model), F32), vmem((tokens // 2, model), BF16),
            vmem((early * SPAN // 2, model), BF16),
            dma((2, spans)), dma((2, early)), vmem((3,) + sums, F32), dma((2, 3)), dma((2,)),
        ],
        compiler_params=pltpu.CompilerParams(
            dimension_semantics=("arbitrary",), vmem_limit_bytes=VMEM_MOST,
            collective_id=2, has_side_effects=True,
        ),
        cost_estimate=cost(40.0),
        name="mixer_forward",
    )(docs, normed, cotangent, *consts)


def backward_kernel(
    dims,
    docs_ref, hid_ref, gate_ref, dn_ref, gate_low_ref, ssd_low_ref, dn_low_ref,
    ssd_ref, mixed_ref, pre_ref, stp_ref, state_ref, sums_ref,
    cw_ref, cb_ref, dtb_ref, dec_ref, skip_ref, ggain_ref, ngain_ref,
    naway_ref, nhere_ref, caway_ref, chere_ref, w_ref, mine_ref, far_ref,
    delta_ref, layer_ref, gin_ref, gout_ref, flatout_ref,
    naway, nhere, caway, chere, w, loads,
    pbuf, dbuf, dstate, par, cwb, gain,
    gconv, gskip, ghead, ggain, gnorm,
    nout_all, dgate_all, dall, dssd_low, inv_now, inv_own, hid_own,
    h_out, mine, y_in, kept, h_sem, y_sem, d_sem, d_put,
    omine, ofar, oy_sem, o_sem, o_put,
    ax_out, ax_in, ax_sem, az_in, az_sem, atotal,
    sx_out, sx_in, sx_sem, sz_in, sz_sem, stotal, shere,
    vx_out, vx_in, vx_sem, vz_in, vz_sem, vtotal, vhere, vbuf,
    gates, g_sem, values, v_sem, shared, s_sem, put_sem, flat, flat_in, f_sem,
):
    inner, heads, inner_all, lines, depth, early = dims
    pairs = heads // 2
    chan = inner + 2 * LANES
    width = inner + chan + LANES
    i = pl.program_id(0)
    spans = pl.num_programs(0)
    tokens = nout_all.shape[0]
    count = tokens // SPAN
    mid = count // 2
    c = count - 1 - i
    half = SPAN // 2
    model = w.shape[0]
    blocks = lines * depth // LANES
    rank, drank = lax.axis_index("tensor"), lax.axis_index("dp")
    line, side = drank // 2, drank % 2
    core = rank % 2
    off = pl.multiple_of(rank * inner, LANES)
    across = {"tensor": rank + 1 - 2 * core}
    beyond = {"tensor": (rank + 2) % 4}
    partner = {"dp": line * 2 + 1 - side}

    def peer(step):
        return {"dp": lax.rem(line + step, lines) * 2 + side}

    def remote(src, dst, sems, index, device):
        return pltpu.make_async_remote_copy(
            src_ref=src, dst_ref=dst, send_sem=sems.at[0, index], recv_sem=sems.at[1, index],
            device_id=device, device_id_type=MESH_IDS,
        )

    def lot(k, size):
        return pl.ds(pl.multiple_of(k * size, size), size)

    fetch = [
        pltpu.make_async_copy(src, dst, loads.at[k])
        for k, (src, dst) in enumerate(
            (
                (mine_ref, omine), (w_ref, w), (far_ref, ofar.at[pl.ds(0, early * half)]),
                (caway_ref, caway), (naway_ref, naway), (chere_ref, chere), (nhere_ref, nhere),
            )
        )
    ]

    def oy_copy(k):
        return remote(omine.at[lot(k, half)], ofar.at[lot(k, half)], oy_sem, k - early, beyond)

    def my_rows(k):
        return pl.ds(pl.multiple_of(k * SPAN + core * half, half), half)

    def o_copy(k):
        return remote(omine.at[lot(k, half)], layer_ref.at[my_rows(k)], o_sem, k, across)

    def o_local(k):
        return pltpu.make_async_copy(omine.at[lot(k, half)], layer_ref.at[my_rows(k)], o_put.at[k])

    def d_copy(k):
        return remote(mine.at[lot(k, half)], delta_ref.at[my_rows(k)], d_sem, k, across)

    def d_local(k):
        return pltpu.make_async_copy(mine.at[lot(k, half)], delta_ref.at[my_rows(k)], d_put.at[k])

    def h_copy(k):
        return remote(h_out.at[lot(k, half)], mine.at[lot(k, half)], h_sem, k, across)

    def y_copy(k):
        return remote(mine.at[lot(k, half)], y_in.at[lot(k, half)], y_sem, k, beyond)

    def ax_copy(k):
        return remote(ax_out.at[lot(k, LANES)], ax_in.at[lot(k, LANES)], ax_sem, k, partner)

    def sx_copy(k):
        return remote(sx_out.at[lot(k, LANES)], sx_in.at[lot(k, LANES)], sx_sem, k, partner)

    def vx_copy(k):
        return remote(vx_out.at[lot(k, LANES)], vx_in.at[lot(k, LANES)], vx_sem, k, partner)

    def az_copy(step):
        return remote(ax_out.at[pl.ds(step * depth, depth)], az_in.at[step - 1], az_sem, step - 1, peer(step))

    def sz_copy(step):
        return remote(sx_out.at[pl.ds(step * depth, depth)], sz_in.at[step - 1], sz_sem, step - 1, peer(step))

    def vz_copy(step):
        return remote(vx_out.at[pl.ds(step * depth, depth)], vz_in.at[step - 1], vz_sem, step - 1, peer(step))

    @pl.when(i == 0)
    def _():
        barrier = pltpu.get_barrier_semaphore()
        for device in [across, beyond, partner] + [peer(step) for step in range(1, lines)]:
            pl.semaphore_signal(barrier, inc=1, device_id=device, device_id_type=MESH_IDS)
        pl.semaphore_wait(barrier, lines + 2)
        for copy in fetch:
            copy.start()
        pbuf[SPAN : SPAN + 8] = jnp.zeros((8, chan), F32)
        dbuf[SPAN : SPAN + 8] = jnp.full((8, LANES), -2.0, F32)
        dstate[...] = jnp.zeros(dstate.shape, F32)
        own_params(rank, heads, inner, inner_all, dtb_ref, dec_ref, skip_ref, cw_ref, cb_ref, par, cwb)
        gain[0:1] = ggain_ref[:, pl.ds(off, inner)]
        for acc in (gconv, gskip, ghead, ggain, gnorm):
            acc[...] = jnp.zeros(acc.shape, F32)
        fetch[0].wait()
        for k in range(early, count):
            oy_copy(k).start()

    def join(k):
        h_copy(k).wait_recv()
        mine[lot(k, half)] = (kept[lot(core, half)] + mine[lot(k, half)].astype(F32)).astype(BF16)
        y_copy(k).start()

    def out_grads(n_side, c_side, k):
        cols = lot(k, LANES)
        return jnp.concatenate(
            [tn(c_side[:, cols], nout_all[...]), tn(n_side[:, cols], dgate_all[...])], 1
        )

    per = LANES // depth

    def to_lines(k, joined, x_copy_of, x_out, z_copy_of, total):
        x_copy_of(k).wait_send()
        x_out[lot(k, LANES)] = joined.astype(BF16)
        if isinstance(k, int):
            if k == 0:
                total[...] = joined[0:depth]
            for step in range(max(1, k * per), (k + 1) * per):
                z_copy_of(step).start()

    def a_block(k):
        ax_copy(k).wait_recv()
        joined = out_grads(nhere, chere, k) + ax_in[lot(k, LANES)].astype(F32)
        to_lines(k, joined, ax_copy, ax_out, az_copy, atotal)

    def s_block(k):
        sx_copy(k).wait_recv()
        joined = shere[lot(k, LANES)] + sx_in[lot(k, LANES)].astype(F32)
        to_lines(k, joined, sx_copy, sx_out, sz_copy, stotal)

    def v_block(k):
        vx_copy(k).wait_recv()
        joined = vhere[lot(k, LANES)] + vx_in[lot(k, LANES)].astype(F32)
        to_lines(k, joined, vx_copy, vx_out, vz_copy, vtotal)

    @pl.when(i == mid)
    def _():
        for copy in fetch[2:]:
            copy.wait()

    hid_own[lot(c, half)] = hid_ref[lot(core, half)]

    def inverse(k):
        inv = lax.rsqrt(as_column(sums_ref[0, pl.ds(k, 1), :]) * (1.0 / inner_all) + EPS)
        pull = as_column(sums_ref[1, pl.ds(k, 1), :]) * (inv * inv * inv) * (1.0 / inner_all)
        inv_now[...] = inv
        inv_own[lot(k, half)] = inv_now[lot(core, half)]
        return inv, pull

    def gating(k, scales, lanes, gate_in, ssd_in, dn_in):
        inv, pull = scales
        gate = gate_in[:, lanes]
        sig = jax.nn.sigmoid(gate)
        silu = gate * sig
        ssd = ssd_in[:, lanes]
        gated = ssd * silu
        dn = dn_in[:, lanes]
        g_l = gain[0:1, lanes]
        nout = gated * inv
        nout_all[lot(k, SPAN), lanes] = (nout * g_l).astype(BF16)
        ggain[:, lanes] += fold(dn * nout)
        d_gated = dn * g_l * inv - gated * pull
        dgate_all[lot(k, SPAN), lanes] = (d_gated * ssd * (sig * (1.0 + gate * (1.0 - sig)))).astype(BF16)
        return d_gated * silu

    def finish_out(k):
        total = omine[lot(k, half)].astype(F32) + ofar[lot(k, half)].astype(F32)
        inv = inv_own[lot(k, half)]
        value = hid_own[lot(k, half)].astype(F32)
        for group in range(model // LANES):
            lanes = slice(group * LANES, (group + 1) * LANES)
            omine[lot(k, half), lanes] = (value[:, lanes] + total[:, lanes] * inv).astype(BF16)
        o_copy(k).start()
        o_local(k).start()

    def scan_step(first):
        if first:
            scales, low_scales = inverse(c), inverse(c - mid)
        drow = docs_ref[:, lot(c, SPAN)].astype(F32)
        dcol = as_column(drow)
        before = docs_ref[:, lot(jnp.maximum(c - 1, 0), SPAN)].astype(F32)
        enter = as_column(before)[SPAN - 1 : SPAN]
        enter = jnp.where(c == 0, -1.0, enter)
        dbuf[0:SPAN] = dcol
        keeps = [None] + [dbuf[k : k + SPAN] == dcol for k in range(1, 4)]
        if not first:
            block = lax.rem(i - mid + 1, blocks)
            ax_out[lot(block, LANES)] = out_grads(naway, caway, block).astype(BF16)
        raw = stp_ref[...] + par[0:1]
        step = softplus(raw)
        row_i, col_i = iota((SPAN, SPAN), 0), iota((SPAN, SPAN), 1)
        tril = (row_i >= col_i).astype(BF16)
        log_step = step * par[1:2]
        running = tri_sum(tril, log_step, heads)
        run_rows = jnp.transpose(running)
        ending = running[SPAN - 1 : SPAN]
        tail = jnp.where(dcol == dcol[SPAN - 1 : SPAN], jnp.exp(ending - running), 0.0)
        reach = jnp.where(dcol == enter, jnp.exp(running), 0.0)
        same = jnp.concatenate([dcol, dcol], 1) == drow
        bias = jnp.where(same & (row_i <= col_i), 0.0, FAR)

        def activate(group):
            lanes = slice(group * LANES, (group + 1) * LANES)
            pre = pre_ref[:, lanes]
            sig = jax.nn.sigmoid(pre)
            return pre * sig, sig * (1.0 + pre * (1.0 - sig))

        b_act, b_slope = activate(pairs)
        c_act, c_slope = activate(pairs + 1)
        b_rows, c_rows = b_act.astype(BF16), c_act.astype(BF16)
        c_turned = jnp.transpose(c_act).astype(BF16)
        scores = exact_nt(b_act, c_act)
        low_half = iota((SPAN, LANES), 1) < LANES // 2
        d_scores = [jnp.zeros((half, SPAN), F32), jnp.zeros((half, half), F32)]
        d_b = jnp.zeros((SPAN, LANES), F32)
        d_c = jnp.zeros((SPAN, LANES), F32)
        head_up = jnp.zeros((SPAN, LANES), F32)
        head_down = jnp.zeros((SPAN, LANES), F32)
        head_step = jnp.zeros((SPAN, LANES), F32)
        head_hold = jnp.zeros((8, LANES), F32)
        for pair in range(pairs):
            lanes = slice(pair * LANES, (pair + 1) * LANES)
            ones_at = (iota((LANES, LANES), 1) == 2 * pair + iota((LANES, LANES), 0) // (LANES // 2)).astype(BF16)

            def head_sum(v):
                hi = v.astype(BF16)
                low = (v - hi.astype(F32)).astype(BF16)
                return nn(hi, ones_at) + nn(low, ones_at)

            act, slope = activate(pair)
            step_l = pair_lanes(step, pair, low_half)
            tail_l = pair_lanes(tail, pair, low_half)
            reach_l = pair_lanes(reach, pair, low_half)
            skip_l = pair_lanes(par[2:3], pair, low_half[0:1])
            ssd = ssd_ref[:, lanes]
            if first:
                d_ssd = gating(c, scales, lanes, gate_ref, ssd_ref, dn_ref)
                dssd_low[lot(c - mid, SPAN), lanes] = gating(
                    c - mid, low_scales, lanes, gate_low_ref, ssd_low_ref, dn_low_ref
                )
            else:
                d_ssd = dssd_low[lot(c, SPAN), lanes]
            gskip[:, lanes] += fold(d_ssd * act)
            dyb = d_ssd.astype(BF16)
            scaled = act * step_l
            xb = scaled.astype(BF16)
            held = state_ref[0, :, lanes]
            d_held = dstate[:, lanes]
            d_held_b = d_held.astype(BF16)
            ry = (d_ssd * reach_l).astype(BF16)
            xt = (scaled * tail_l).astype(BF16)
            parts = []
            for sub in range(2):
                head = 2 * pair + sub
                x_own = jnp.where(low_half if sub == 0 else ~low_half, scaled, 0.0).astype(BF16)
                tiles = []
                for blk in range(2):
                    rows = slice(blk * half, (blk + 1) * half)
                    cols = slice(blk * half, SPAN)
                    gap = run_rows[head : head + 1, cols] - running[rows, head : head + 1]
                    decay = jnp.exp(gap + bias[rows, cols])
                    tiles.append(nn((decay * scores[rows, cols]).astype(BF16), dyb[cols]))
                    d_scores[blk] = d_scores[blk] + decay * nt(x_own[rows], dyb[cols])
                parts.append(jnp.concatenate(tiles, 0))
            d_within = jnp.where(low_half, parts[0], parts[1])
            from_state = tail_l * nn(b_rows, d_held_b)
            d_scaled = d_within + from_state
            xf = xb.astype(F32)
            head_up += head_sum(dyb.astype(F32) * (ssd - skip_l * act) - xf * d_within)
            head_down += head_sum(xf * from_state)
            head_step += head_sum(d_scaled * act)
            hold = reach_l[SPAN - 1 : SPAN]
            hold_sum = jnp.sum((d_held * held.astype(F32)).reshape(LANES // 8, 8, LANES), axis=0) * hold
            head_hold += head_sum(hold_sum)
            d_b += nt(xt, d_held_b)
            d_c += nt(ry, held)
            dstate[:, lanes] = hold * d_held + nn(c_turned, ry)
            pbuf[0:SPAN, lanes] = (skip_l * d_ssd + step_l * d_scaled) * slope

        ds_b = jnp.concatenate(
            [
                d_scores[0],
                jnp.concatenate([jnp.zeros((half, half), F32), d_scores[1]], 1),
            ],
            0,
        )
        d_b += nn(ds_b.astype(BF16), c_rows)
        d_c += nn(jnp.transpose(ds_b).astype(BF16), b_rows)
        pbuf[0:SPAN, inner : inner + LANES] = d_b * b_slope
        pbuf[0:SPAN, inner + LANES : chan] = d_c * c_slope

        triu = (row_i <= col_i).astype(BF16)
        below = (row_i > col_i).astype(BF16)
        d_log = (
            tri_sum(triu, head_up, heads)
            + tri_sum(below, head_down, heads)
            + jnp.sum(head_hold, axis=0, keepdims=True)
        )
        d_step = d_log * par[1:2] + head_step
        d_raw = jnp.where(iota((SPAN, LANES), 1) < heads, d_step * jax.nn.sigmoid(raw), 0.0)
        dall[lot(c, SPAN), chan:] = d_raw.astype(BF16)
        ghead[0] += fold(d_raw)
        ghead[1] += fold(d_log * log_step)

        for group in range(chan // LANES):
            lanes = slice(group * LANES, (group + 1) * LANES)
            mixed = mixed_ref[:, lanes]
            own = pbuf[0:SPAN, lanes]
            acc = cwb[3:4, lanes] * own
            gconv[3, :, lanes] += fold(mixed * own)
            gconv[4, :, lanes] += fold(own)
            for k in range(1, 4):
                later = jnp.where(keeps[k], pbuf[k : k + SPAN, lanes], 0.0)
                acc = acc + cwb[3 - k : 4 - k, lanes] * later
                gconv[3 - k, :, lanes] += fold(mixed * later)
            dall[lot(c, SPAN), lanes] = acc.astype(BF16)
        pbuf[SPAN : SPAN + 8] = pbuf[0:8]
        dbuf[SPAN : SPAN + 8] = dbuf[0:8]

    @pl.when(i < mid)
    def _():
        scan_step(True)

    @pl.when(i >= mid)
    def _():
        for k in (c + mid, c):
            if k is not c:
                oy_copy(k).wait_recv()
                oy_copy(k).wait_send()
            finish_out(k)
        scan_step(False)
        ax_copy(lax.rem(i - mid + 1, blocks)).start()

    @pl.when(i > 0)
    def _():
        join(c + 1)

    order = tuple(range(1, blocks)) + (0,)
    for k in range(blocks - 1):
        @pl.when(i == mid + 1 + k)
        def _():
            a_block(order[k])

    @pl.when(i == 0)
    def _():
        fetch[1].wait()

    rows_now = lot(c, SPAN)
    kept[...] = nt(dgate_all[rows_now], w[:, 0:inner]) + nt(dall[rows_now], w[:, inner:])
    h_out[lot(c, half)] = kept[lot(1 - core, half)].astype(BF16)
    h_copy(c).start()
    value = hid_ref[...].astype(F32)
    unit = value * lax.rsqrt(jnp.mean(value * value, -1, keepdims=True) + EPS)
    gnorm[...] += fold(kept[...] * unit)

    @pl.when(i == count - 1)
    def _():
        sx_out[...] = tn(naway[...], dall[:, inner:]).astype(BF16)
        for k in order:
            sx_copy(k).start()
        vx_out[LANES:] = tn(naway[:, LANES:], dall[:, 0:inner]).astype(BF16)
        for k in order[:-1]:
            vx_copy(k).start()
        vx_out[0:LANES] = tn(naway[:, 0:LANES], dall[:, 0:inner]).astype(BF16)
        vx_copy(0).start()
        join(0)

        chan_all = inner_all + 2 * LANES
        tap_rows, own_rows = chan_all // LANES, inner // LANES
        flat[...] = jnp.zeros(flat.shape, F32)
        norm = jnp.sum(gnorm[...], axis=0, keepdims=True)
        at = model // LANES
        for k in range(at):
            flat[k : k + 1] = norm[:, k * LANES : (k + 1) * LANES]
        for tap in range(gconv.shape[0]):
            row = jnp.sum(gconv[tap], axis=0, keepdims=True)
            for k in range(chan // LANES):
                place = at + k + (rank * own_rows if k < own_rows else (tap_rows - chan // LANES))
                flat[pl.ds(place, 1), :] = row[:, k * LANES : (k + 1) * LANES]
            at += tap_rows
        lane = iota((1, LANES), 1)
        spread = jnp.zeros((1, LANES), F32)
        for k in range(2):
            row = jnp.where(lane < heads, jnp.sum(ghead[k], axis=0, keepdims=True), 0.0)
            spread = spread + pltpu.roll(row, 4 * heads * k + rank * heads, 1)
        flat[at : at + 1] = spread
        at += 1
        for acc in (ggain, gskip):
            row = jnp.sum(acc[...], axis=0, keepdims=True)
            for k in range(own_rows):
                flat[pl.ds(at + rank * own_rows + k, 1), :] = row[:, k * LANES : (k + 1) * LANES]
            at += inner_all // LANES

        hops = [across, beyond, partner]
        bit = 1
        while bit < lines:
            hops.append({"dp": (line + bit * (1 - 2 * ((line // bit) % 2))) * 2 + side})
            bit *= 2
        last = flat_in.shape[0] - 1

        def flat_copy(k):
            return remote(
                flat.at[...] if k == 0 else flat_in.at[len(hops) + k], flat_in.at[k], f_sem, k, hops[k]
            )

        def flat_step(k):
            flat_copy(k).wait_recv()
            held = (flat[...] if k == 0 else flat_in[len(hops) + k]) + flat_in[k]
            if k + 1 < len(hops):
                flat_in[len(hops) + k + 1] = held
                flat_copy(k + 1).start()
            else:
                flat_in[last] = held

        flat_copy(0).start()

        a_block(order[-1])
        gain_row = ngain_ref[...]

        def finish_hidden(k, carry):
            y_copy(k).wait_recv()
            y_copy(k).wait_send()
            d_hidden = mine[lot(k, half)].astype(F32) + y_in[lot(k, half)].astype(F32)
            value = hid_own[lot(k, half)].astype(F32)
            inv = lax.rsqrt(jnp.mean(value * value, -1, keepdims=True) + EPS)
            scaled = d_hidden * gain_row
            pull = jnp.mean(scaled * value, -1, keepdims=True)
            mine[lot(k, half)] = (inv * scaled - value * (inv * inv * inv) * pull).astype(BF16)
            d_copy(k).start()
            d_local(k).start()
            return carry

        def down(k, carry):
            return finish_hidden(count - 1 - k, carry)

        shere[...] = tn(nhere[...], dall[:, inner:])
        for k in order:
            s_block(k)
        vhere[...] = tn(nhere[...], dall[:, 0:inner])
        flat_step(0)
        lax.fori_loop(0, 3, down, 0)
        for k in order[:-1]:
            v_block(k)
        flat_step(1)
        for step in range(1, lines):
            az_copy(step).wait_recv()
            atotal[...] += az_in[step - 1].astype(F32)
        gates[0] = atotal[:, inner:]
        gout_put = pltpu.make_async_copy(atotal.at[:, pl.ds(0, inner)], gout_ref, put_sem.at[9])
        gout_put.start()
        gate_near = remote(gates.at[0], gates.at[1], g_sem, 0, across)
        gate_far = remote(gates.at[0], gates.at[2], g_sem, 1, beyond)
        gate_pass = remote(gates.at[2], gates.at[3], g_sem, 2, across)
        gate_near.start()
        gate_far.start()
        for step in range(1, lines):
            sz_copy(step).wait_recv()
            stotal[...] += sz_in[step - 1].astype(F32)
        shared_near = remote(shared.at[0], shared.at[1], s_sem, 0, across)
        shared_far = remote(shared.at[2], shared.at[3], s_sem, 1, beyond)
        shared[0, :, 0 : 2 * LANES] = stotal[:, 0 : 2 * LANES]
        steps = pltpu.roll(stotal[:, 2 * LANES :], rank * heads, 1)
        place = iota(steps.shape, 1) - rank * heads
        shared[0, :, 2 * LANES :] = jnp.where((place >= 0) & (place < heads), steps, 0.0)
        shared_near.start()
        flat_step(2)
        v_block(order[-1])
        lax.fori_loop(3, 6, down, 0)
        shared_near.wait_recv()
        shared[2] = shared[0] + shared[1]
        shared_far.start()
        gate_far.wait_recv()
        gate_pass.start()
        for k in range(3, len(hops)):
            flat_step(k)
        flat_put = pltpu.make_async_copy(flat_in.at[last], flatout_ref, put_sem.at[10])
        flat_put.start()
        lax.fori_loop(6, count, down, 0)

        for step in range(1, lines):
            vz_copy(step).wait_recv()
            vtotal[...] += vz_in[step - 1].astype(F32)
        values[0] = vtotal[...].astype(BF16)
        value_near = remote(values.at[0], values.at[1], v_sem, 0, across)
        value_far = remote(values.at[0], values.at[2], v_sem, 1, beyond)
        value_pass = remote(values.at[2], values.at[3], v_sem, 2, across)
        value_far.start()
        value_near.start()

        def put(source, k, first, owner, index):
            column = pl.multiple_of(first + owner * inner, LANES)
            return pltpu.make_async_copy(source.at[k], gin_ref.at[:, pl.ds(column, inner)], put_sem.at[index])

        owners = (rank, rank + 1 - 2 * core, (rank + 2) % 4, (rank + 3 - 2 * core) % 4)
        gate_near.wait_recv()
        gate_pass.wait_recv()
        puts = [put(gates, k, 0, owners[k], k) for k in range(4)]
        shared_far.wait_recv()
        shared[1] = shared[2] + shared[3]
        puts.append(
            pltpu.make_async_copy(
                shared.at[1], gin_ref.at[:, pl.ds(2 * inner_all, 3 * LANES)], put_sem.at[8]
            )
        )
        for copy in puts:
            copy.start()

        def put_values(k):
            vbuf[k] = values[k].astype(F32)
            puts.append(put(vbuf, k, inner_all, owners[k], 4 + k))
            puts[-1].start()

        put_values(0)
        value_near.wait_recv()
        put_values(1)
        value_far.wait_recv()
        value_pass.start()
        put_values(2)
        value_pass.wait_recv()
        put_values(3)

        def drain(k, carry):
            h_copy(k).wait_send()
            d_copy(k).wait()
            d_local(k).wait()
            o_copy(k).wait()
            o_local(k).wait()
            return carry

        lax.fori_loop(0, count, drain, 0)
        for step in range(1, lines):
            az_copy(step).wait_send()
            sz_copy(step).wait_send()
            vz_copy(step).wait_send()
        for copy in (
            gate_near, gate_far, gate_pass, value_near, value_far, value_pass, shared_near, shared_far,
        ):
            copy.wait_send()
        for k in range(len(hops)):
            flat_copy(k).wait_send()
        for copy in puts + [gout_put, flat_put]:
            copy.wait()


def mixer_backward(
    docs, hidden, held, sums, params, ggain, ngain, sorted_parts, w_in, mine, far,
    heads, lines, depth, early,
):
    gate, mixed, pre, ssd, stp, states, dn = held
    tokens, inner = ssd.shape
    model = hidden.shape[1]
    chan = inner + 2 * LANES
    width = inner + chan + LANES
    wide = width - inner
    inner_all = ggain.shape[1]
    count = tokens // SPAN
    mid = count // 2
    half = SPAN // 2
    blocks, fars = lines * depth // LANES, max(1, lines - 1)
    hops = 3 + (lines - 1).bit_length()
    rows = (model + 5 * (inner_all + 2 * LANES) + LANES + 2 * inner_all) // LANES
    rows += -rows % 8

    def tok(size):
        return pl.BlockSpec((SPAN, size), lambda i: (count - 1 - i, 0))

    def early_tok(size, base):
        return pl.BlockSpec((SPAN, size), lambda i: (base + (mid - 1 - i) * (1 - i // mid), 0))

    def full(shape):
        return pl.BlockSpec(shape, lambda i: (0,) * len(shape))

    anywhere = pl.BlockSpec(memory_space=pl.ANY)
    dma, vmem = pltpu.SemaphoreType.DMA, pltpu.VMEM
    consts = params + (ggain, ngain)
    big = tuple(sorted_parts)[0:2] + tuple(sorted_parts)[2:4] + (w_in, mine, far)
    side_shape = (tokens, lines * depth)
    return pl.pallas_call(
        lambda *refs: backward_kernel((inner, heads, inner_all, lines, depth, early), *refs),
        out_shape=(
            jax.ShapeDtypeStruct((tokens, model), BF16),
            jax.ShapeDtypeStruct((tokens, model), BF16),
            jax.ShapeDtypeStruct((depth, 2 * inner_all + 3 * LANES), F32),
            jax.ShapeDtypeStruct((depth, inner), F32),
            jax.ShapeDtypeStruct((rows, LANES), F32),
        ),
        grid=(count,),
        in_specs=[
            full(docs.shape), tok(model), early_tok(inner, mid), early_tok(inner, mid),
            early_tok(inner, 0), early_tok(inner, 0), early_tok(inner, 0),
            tok(inner), tok(chan), tok(chan), tok(LANES),
            pl.BlockSpec((1, LANES, inner), lambda i: (count - 1 - i, 0, 0)),
            full(sums.shape),
        ]
        + [full(v.shape) for v in consts]
        + [anywhere] * len(big),
        out_specs=(anywhere,) * 5,
        scratch_shapes=[
            vmem(side_shape, BF16), vmem(side_shape, BF16), vmem(side_shape, BF16), vmem(side_shape, BF16),
            vmem(w_in.shape, BF16), dma((len(big),)),
            vmem((SPAN + 8, chan), F32), vmem((SPAN + 8, LANES), F32), vmem((LANES, inner), F32),
            vmem((8, LANES), F32), vmem((8, chan), F32), vmem((8, inner), F32),
            vmem((5, 8, chan), F32), vmem((8, inner), F32), vmem((2, 8, LANES), F32),
            vmem((8, inner), F32), vmem((8, model), F32),
            vmem((tokens, inner), BF16), vmem((tokens, inner), BF16), vmem((tokens, wide), BF16),
            vmem((tokens // 2, inner), F32), vmem((SPAN, LANES), F32), vmem((tokens // 2, LANES), F32),
            vmem((tokens // 2, model), BF16),
            vmem((tokens // 2, model), BF16), vmem((tokens // 2, model), BF16),
            vmem((tokens // 2, model), BF16), vmem((SPAN, model), F32),
            dma((2, count)), dma((2, count)), dma((2, count)), dma((count,)),
            vmem((tokens // 2, model), BF16), vmem((tokens // 2, model), BF16),
            dma((2, count - early)), dma((2, count)), dma((count,)),
            vmem((blocks * LANES, 2 * inner), BF16), vmem((blocks * LANES, 2 * inner), BF16),
            dma((2, blocks)), vmem((fars, depth, 2 * inner), BF16), dma((2, fars)),
            vmem((depth, 2 * inner), F32),
            vmem((blocks * LANES, 3 * LANES), BF16), vmem((blocks * LANES, 3 * LANES), BF16),
            dma((2, blocks)), vmem((fars, depth, 3 * LANES), BF16), dma((2, fars)),
            vmem((depth, 3 * LANES), F32), vmem((blocks * LANES, 3 * LANES), F32),
            vmem((blocks * LANES, inner), BF16), vmem((blocks * LANES, inner), BF16),
            dma((2, blocks)), vmem((fars, depth, inner), BF16), dma((2, fars)), vmem((depth, inner), F32),
            vmem((blocks * LANES, inner), F32), vmem((4, depth, inner), F32),
            vmem((4, depth, inner), F32), dma((2, 3)), vmem((4, depth, inner), BF16), dma((2, 3)),
            vmem((4, depth, 3 * LANES), F32), dma((2, 2)), dma((11,)),
            vmem((rows, LANES), F32), vmem((2 * hops + 1, rows, LANES), F32), dma((2, hops)),
        ],
        compiler_params=pltpu.CompilerParams(
            dimension_semantics=("arbitrary",), vmem_limit_bytes=67043328,
            collective_id=1, has_side_effects=True,
        ),
        cost_estimate=cost(90.0),
        name="mixer_backward",
    )(
        docs, hidden, gate, dn, gate, ssd, dn, ssd, mixed, pre, stp, states, sums, *consts, *big
    )


def finish_kernel(
    dims, cot_ref, delta_ref, layer_ref, gin_ref, flat_ref,
    out_ref, grad_ref, norm_ref, win_ref, taps_ref, bias_ref, dt_ref, decay_ref, skip_ref, gain_ref,
):
    inner_all, heads = dims
    grad_ref[...] = cot_ref[...].astype(F32) + delta_ref[...].astype(F32)
    out_ref[...] = layer_ref[...]
    win_ref[...] = gin_ref[:, 0 : win_ref.shape[1]]

    @pl.when(pl.program_id(0) == 0)
    def _():
        at = norm_ref.shape[1] // LANES

        def spread(dst, row, first, count):
            for k in range(count):
                dst[row : row + 1, k * LANES : (k + 1) * LANES] = flat_ref[first + k : first + k + 1]

        spread(norm_ref, 0, 0, at)
        wide = taps_ref.shape[1] // LANES
        for tap in range(taps_ref.shape[0]):
            spread(taps_ref, tap, at + tap * wide, wide)
        at += taps_ref.shape[0] * wide
        spread(bias_ref, 0, at, wide)
        at += wide
        dt_ref[...] = flat_ref[at : at + 1, 0:heads]
        decay_ref[...] = flat_ref[at : at + 1, heads : 2 * heads]
        at += 1
        spread(gain_ref, 0, at, inner_all // LANES)
        at += inner_all // LANES
        per = inner_all // heads
        lane = iota((1, LANES), 1)
        found = jnp.zeros((1, LANES), F32)
        for k in range(inner_all // LANES):
            row = flat_ref[at + k : at + k + 1]
            for part in range(LANES // per):
                inside = (lane >= part * per) & (lane < (part + 1) * per)
                total = jnp.sum(jnp.where(inside, row, 0.0), axis=1, keepdims=True)
                found = jnp.where(lane == k * (LANES // per) + part, total, found)
        skip_ref[...] = found[:, 0:heads]


def finish(cotangent, delta, layer_out, grad_in, flat, columns, inner_all, heads):
    tokens, model = cotangent.shape
    depth = grad_in.shape[0]
    steps = 8
    chan_all = inner_all + 2 * LANES

    def tok(v, size):
        return pl.BlockSpec((v // steps, size), lambda i: (i, 0))

    def full(shape):
        return pl.BlockSpec(shape, lambda i: (0,) * len(shape))

    small = [(1, model), (4, chan_all), (1, chan_all), (1, heads), (1, heads), (1, heads), (1, inner_all)]
    if depth % (8 * steps) == 0:
        rows, shown = tok(depth, grad_in.shape[1]), tok(depth, columns)
    else:
        rows, shown = full(grad_in.shape), full((depth, columns))
    return pl.pallas_call(
        lambda *refs: finish_kernel((inner_all, heads), *refs),
        out_shape=[
            jax.ShapeDtypeStruct((tokens, model), BF16),
            jax.ShapeDtypeStruct((tokens, model), F32),
            jax.ShapeDtypeStruct(small[0], F32),
            jax.ShapeDtypeStruct((depth, columns), F32),
        ]
        + [jax.ShapeDtypeStruct(v, F32) for v in small[1:]],
        grid=(steps,),
        in_specs=[tok(tokens, model)] * 3 + [rows, full(flat.shape)],
        out_specs=[tok(tokens, model)] * 2 + [full(small[0]), shown] + [full(v) for v in small[1:]],
        compiler_params=pltpu.CompilerParams(dimension_semantics=("arbitrary",)),
        cost_estimate=cost(9.0),
        name="finish",
    )(cotangent, delta, layer_out, grad_in, flat)


def gather_kernel(
    dims, hid_ref, cot_ref, ngain_ref, w_ref, step_ref, wo_ref,
    win_ref, wout_ref, normed_ref, *refs,
):
    lines, depth, inner, inner_all, aligned = dims
    outs = refs[:4] if aligned else ()
    mine, zsend, zrecv, xsend, xrecv, takes, puts = refs[len(outs):]
    trank, drank = lax.axis_index("tensor"), lax.axis_index("dp")
    line, side = drank // 2, drank % 2
    model = hid_ref.shape[1]
    off = pl.multiple_of(trank * inner, LANES)
    pieces = (
        (w_ref, inner_all + off, win_ref, inner, inner),
        (w_ref, 2 * inner_all, win_ref, 2 * inner, 2 * LANES),
        (step_ref, 0, win_ref, 2 * inner + 2 * LANES, LANES),
        (w_ref, off, win_ref, 0, inner),
        (wo_ref, 0, wout_ref, 0, inner),
    )

    def peer(step):
        return {"dp": lax.rem(line + step, lines) * 2 + side}

    partner = {"dp": line * 2 + 1 - side}
    barrier = pltpu.get_barrier_semaphore()
    for step in range(1, lines):
        pl.semaphore_signal(barrier, inc=1, device_id=peer(step), device_id_type=MESH_IDS)
    pl.semaphore_signal(barrier, inc=1, device_id=partner, device_id_type=MESH_IDS)
    pl.semaphore_wait(barrier, lines)

    def rows(index):
        return pl.ds(pl.multiple_of(index * depth, depth), depth)

    def block(p, index):
        _, _, dst, at, width = pieces[p]
        return dst.at[rows(index), pl.ds(at, width)]

    def own(p):
        src, at, _, _, width = pieces[p]
        return src.at[:, pl.ds(at, width)]

    def z_copy(p, step, src, index):
        return pltpu.make_async_remote_copy(
            src_ref=src, dst_ref=block(p, index), send_sem=zsend.at[p, step - 1],
            recv_sem=zrecv.at[p, step - 1], device_id=peer(step), device_id_type=MESH_IDS,
        )

    def x_copy(p, step, src, index):
        return pltpu.make_async_remote_copy(
            src_ref=src, dst_ref=block(p, index), send_sem=xsend.at[p, step],
            recv_sem=xrecv.at[p, step], device_id=partner, device_id_type=MESH_IDS,
        )

    count = len(pieces)
    for p in range(count):
        for step in range(1, lines):
            z_copy(p, step, own(p), drank).start()
        x_copy(p, 0, own(p), drank).start()
    spots, at = [], 0
    for p in range(count):
        spots.append(mine.at[:, pl.ds(at, pieces[p][4])])
        at += pieces[p][4]
    fetched = [pltpu.make_async_copy(own(p), spots[p], takes.at[p]) for p in range(count)]
    for copy in fetched:
        copy.start()

    gain = ngain_ref[...]

    def normalize(hid, cot, normed, *sorted_refs):
        value = hid[...].astype(F32)
        inv = lax.rsqrt(jnp.mean(value * value, -1, keepdims=True) + EPS)
        normed[...] = (value * inv * gain).astype(BF16)
        if aligned:
            for src, away, here in (
                (normed, sorted_refs[0], sorted_refs[1]), (cot, sorted_refs[2], sorted_refs[3]),
            ):
                for j in range(lines):
                    first = lax.rem(line + j, lines) * 2
                    lanes = slice(j * depth, (j + 1) * depth)
                    away[:, lanes] = src[:, pl.ds(pl.multiple_of((first + 1 - side) * depth, depth), depth)]
                    here[:, lanes] = src[:, pl.ds(pl.multiple_of((first + side) * depth, depth), depth)]

    full = pl.BlockSpec((SPAN, model), lambda i: (i, 0))
    half = pl.BlockSpec((SPAN, lines * depth), lambda i: (i, 0))
    pltpu.emit_pipeline(
        normalize, grid=(hid_ref.shape[0] // SPAN,), in_specs=[full, full],
        out_specs=[full] + [half] * len(outs),
    )(hid_ref, cot_ref, normed_ref, *outs)

    stored = [pltpu.make_async_copy(spots[p], block(p, drank), puts.at[p]) for p in range(count)]
    for p in range(count):
        fetched[p].wait()
        stored[p].start()
    for p in range(count):
        for step in range(1, lines):
            source = lax.rem(line - step + lines, lines) * 2 + side
            got = block(p, source)
            z_copy(p, step, got, source).wait_recv()
            x_copy(p, step, got, source).start()
    for p in range(count):
        for step in range(lines):
            source = lax.rem(line - step + lines, lines) * 2 + 1 - side
            x_copy(p, step, block(p, source), source).wait_recv()
    for p in range(count):
        for step in range(1, lines):
            z_copy(p, step, own(p), drank).wait_send()
        for step in range(lines):
            x_copy(p, step, own(p), drank).wait_send()
        stored[p].wait()


def gather_weights(hidden, cotangent, norm_gain, in_weight, own_step, out_weight, lines, inner_all):
    tokens, model = hidden.shape
    depth, inner = out_weight.shape
    aligned = depth % LANES == 0
    width = 2 * inner + 3 * LANES
    half = jax.ShapeDtypeStruct((tokens, lines * depth), BF16)
    anywhere = pl.BlockSpec(memory_space=pl.ANY)
    outs = (
        jax.ShapeDtypeStruct((model, width), BF16),
        jax.ShapeDtypeStruct((model, inner), BF16),
        jax.ShapeDtypeStruct((tokens, model), BF16),
    ) + (half,) * (4 if aligned else 0)
    dma = pltpu.SemaphoreType.DMA
    return pl.pallas_call(
        lambda *refs: gather_kernel((lines, depth, inner, inner_all, aligned), *refs),
        out_shape=outs,
        in_specs=[anywhere, anywhere, pl.BlockSpec(memory_space=pltpu.VMEM)] + [anywhere] * 3,
        out_specs=(anywhere,) * len(outs),
        scratch_shapes=[
            pltpu.VMEM((depth, width + inner), BF16),
            dma((5, max(1, lines - 1))), dma((5, max(1, lines - 1))), dma((5, lines)), dma((5, lines)),
            dma((5,)), dma((5,)),
        ],
        compiler_params=pltpu.CompilerParams(collective_id=0, has_side_effects=True),
        cost_estimate=cost(45.0),
        name="gather_weights",
    )(hidden, cotangent, norm_gain, in_weight, own_step, out_weight)


def body(
    hidden_in, doc_ids, cotangent, norm_gain, in_weight, conv_weight, conv_bias,
    dt_bias, log_decay, skip_gain, gate_gain, out_weight,
):
    tcount, dcount = lax.axis_size("tensor"), lax.axis_size("dp")
    trank, drank = lax.axis_index("tensor"), lax.axis_index("dp")
    lines = dcount // 2
    line, side = drank // 2, drank % 2
    inner_all, head_all = gate_gain.shape[0], dt_bias.shape[0]
    inner, heads = inner_all // tcount, head_all // tcount
    tokens, model = hidden_in.shape
    base_bc = 2 * inner_all
    base_dt = base_bc + 2 * LANES
    depth = in_weight.shape[0]

    def line_to(step):
        return lambda k: ((k // 2 + step) % lines) * 2 + k % 2

    own_step = jnp.pad(
        lax.dynamic_slice_in_dim(in_weight, base_dt + trank * heads, heads, 1),
        ((0, 0), (0, LANES - heads)),
    )
    w_in, w_out, normed, *sorted_parts = gather_weights(
        hidden_in, cotangent, norm_gain.reshape(1, -1), in_weight, own_step, out_weight,
        lines, inner_all,
    )
    if not sorted_parts:

        def features(v, which):
            return jnp.concatenate(
                [
                    lax.dynamic_slice_in_dim(v, (((line + j) % lines) * 2 + which) * depth, depth, 1)
                    for j in range(lines)
                ],
                1,
            )

        sorted_parts = [features(v, which) for v in (normed, cotangent) for which in (1 - side, side)]
    n_away, n_here, c_away, c_here = sorted_parts

    def row(v):
        return v.reshape(1, -1)

    params = (conv_weight, row(conv_bias), row(dt_bias), row(log_decay), row(skip_gain))

    early = 4
    *held, sums, mine, far = mixer_forward(
        doc_ids, normed, cotangent, w_in, w_out, params, row(gate_gain), heads, early
    )
    delta, layer_out, grad_in, g_out, flat = mixer_backward(
        doc_ids, hidden_in, held, sums, params, row(gate_gain), row(norm_gain), sorted_parts, w_in,
        mine, far, heads, lines, depth, early,
    )
    layer_out, grad_input, g_norm, grad_in_weight, taps, bias, dt, decay, skip, gain = finish(
        cotangent, delta, layer_out, grad_in, flat, in_weight.shape[1], inner_all, head_all
    )
    return (
        layer_out, grad_input, g_norm.reshape(-1), grad_in_weight, taps, bias.reshape(-1),
        dt.reshape(-1), decay.reshape(-1), skip.reshape(-1), gain.reshape(-1), g_out,
    )


def solution(mesh):
    rows, whole = P("dp", None), P()
    return jax.shard_map(
        body,
        mesh=mesh,
        in_specs=(rows, rows, rows, whole, rows, whole, whole, whole, whole, whole, whole, P("dp", "tensor")),
        out_specs=(rows, rows, whole, rows, whole, whole, whole, whole, whole, whole, P("dp", "tensor")),
        check_vma=False,
    )
```

```python
import jax
import jax.numpy as jnp
from jax import lax
from jax.experimental import pallas as pl
from jax.experimental.pallas import tpu as pltpu
from jax.sharding import PartitionSpec as P

SPAN = 256
LANES = 128
EPS = 1e-05
FAR = -1e30
LOG2_E = 1.4426950408889634
VMEM_MOST = 60 * 2**20
F32 = jnp.float32
BF16 = jnp.bfloat16


def cost(micros):
    return pl.CostEstimate(flops=int(micros * 1.15e9), bytes_accessed=1 << 20, transcendentals=0)


def nn(a, b):
    return lax.dot_general(a, b, (((1,), (0,)), ((), ())), preferred_element_type=F32)


def nt(a, b):
    return lax.dot_general(a, b, (((1,), (1,)), ((), ())), preferred_element_type=F32)


def tn(a, b):
    return lax.dot_general(a, b, (((0,), (0,)), ((), ())), preferred_element_type=F32)


def iota(shape, dim):
    return lax.broadcasted_iota(jnp.int32, shape, dim)


def as_column(row, rows=SPAN):
    return jnp.transpose(jnp.broadcast_to(row, (LANES, rows)))


def as_row(block):
    ones = jnp.ones((16, LANES), BF16)
    hi = block.astype(BF16)
    low = (block - hi.astype(F32)).astype(BF16)
    return (nt(ones, hi) + nt(ones, low))[0:1]


def sigmoid(v):
    return 0.5 * jnp.tanh(0.5 * v) + 0.5


def row_sum(v, tri):
    hi = v.astype(BF16).astype(F32)
    rest = v - hi
    mid = rest.astype(BF16).astype(F32)
    count = v.shape[0]
    out = nn(jnp.concatenate([hi, mid, rest - mid], 0).astype(BF16), tri)
    return out[0:count] + out[count : 2 * count] + out[2 * count :]


def pair_lanes(cols, first, low_half):
    rows = cols.shape[0]
    left = jnp.broadcast_to(cols[:, first : first + 1], (rows, LANES))
    right = jnp.broadcast_to(cols[:, first + 1 : first + 2], (rows, LANES))
    return jnp.where(low_half, left, right)


def exact_nt(a, b):
    a_hi, b_hi = a.astype(BF16), b.astype(BF16)
    a_lo = (a - a_hi.astype(F32)).astype(BF16)
    b_lo = (b - b_hi.astype(F32)).astype(BF16)
    return nt(a_hi, b_hi) + (nt(a_hi, b_lo) + nt(a_lo, b_hi))


def softplus(v):
    return jnp.maximum(v, 0.0) + jnp.log1p(jnp.exp(-jnp.abs(v)))


def own_lanes(row, rank, heads):
    total = row.shape[1]
    pick = (iota((total, LANES), 0) == rank * heads + iota((total, LANES), 1)) & (
        iota((total, LANES), 1) < heads
    )
    wide = jnp.broadcast_to(row, (8, total))
    out = lax.dot_general(
        wide, pick.astype(F32), (((1,), (0,)), ((), ())),
        precision=lax.Precision.HIGHEST, preferred_element_type=F32,
    )
    return out[0:1]


def own_rows_of(row, rank, heads):
    total = row.shape[1]
    place = iota((heads, total), 1) == rank * heads + iota((heads, total), 0)
    picked = jnp.where(place, jnp.broadcast_to(row, (heads, total)), 0.0)
    return jnp.broadcast_to(jnp.sum(picked, axis=1, keepdims=True), (heads, SPAN))


def head_scales(raw, rate, doc, enter, extra):
    step = softplus(raw)
    log_step = step * rate
    row_i, col_i = iota((SPAN, SPAN), 0), iota((SPAN, SPAN), 1)
    running = row_sum(log_step, (row_i <= col_i).astype(BF16))
    ending = jnp.broadcast_to(running[:, SPAN - 1 :], running.shape)
    last = jnp.broadcast_to(doc[:, SPAN - 1 :], doc.shape)
    tail = jnp.where(doc == last, jnp.exp(ending - running), 0.0)
    reach = jnp.where(doc == enter, jnp.exp(running), 0.0)
    scaled = running * LOG2_E
    rows = [scaled, step, tail, reach, doc] + extra
    used = sum(v.shape[0] for v in rows)
    packed = jnp.concatenate(rows + [jnp.zeros((LANES - used, SPAN), F32)], 0)
    return log_step, scaled, jnp.transpose(packed)


def fold(v):
    return jnp.sum(v.reshape(SPAN // 8, 8, v.shape[1]), axis=0)


def own_params(rank, heads, inner, inner_all, dtb_ref, dec_ref, skip_ref, cw_ref, cb_ref, par, skips, cwb):
    chan = inner + 2 * LANES
    off = pl.multiple_of(rank * inner, LANES)
    taps = cw_ref.shape[0]
    par[0] = own_rows_of(dtb_ref[...], rank, heads)
    par[1] = -jnp.exp(own_rows_of(dec_ref[...], rank, heads))
    skips[0:1] = own_lanes(skip_ref[...], rank, heads)
    cwb[0:taps, 0:inner] = cw_ref[:, pl.ds(off, inner)].astype(F32)
    cwb[0:taps, inner:chan] = cw_ref[:, inner_all:].astype(F32)
    for k in range(chan // LANES):
        row = rank * (inner // LANES) + k if k < inner // LANES else (inner_all - inner) // LANES + k
        cwb[taps : taps + 1, k * LANES : (k + 1) * LANES] = cb_ref[pl.ds(row, 1), :]


MESH_IDS = pl.DeviceIdType.MESH


def forward_kernel(
    dims, docs_ref, normed_ref, cot_ref, win_ref, wout_ref, cw_ref, cb_ref,
    dtb_ref, dec_ref, skip_ref, ggain_ref,
    gate_ref, mixed_ref, pre_ref, ssd_ref, stp_ref, state_ref, dn_ref,
    sums_ref, mine_ref, far_ref,
    xbuf, dbuf, state, par, skips, cwb, gain, gg_ref,
    own_sums, h_out, h_in, kept, mine, far, h_sem, y_sem, s_in, s_sem, put_sem,
):
    inner, heads, early = dims
    pairs = heads // 2
    chan = inner + 2 * LANES
    i = pl.program_id(0)
    spans = pl.num_programs(0)
    rank = lax.axis_index("tensor")
    core = rank % 2
    inner_all = ggain_ref.shape[1]
    half = SPAN // 2
    across = {"tensor": rank + 1 - 2 * core}
    beyond = {"tensor": (rank + 2) % 4}
    crossed = {"tensor": (rank + 3 - 2 * core) % 4}

    @pl.when(i == 0)
    def _():
        barrier = pltpu.get_barrier_semaphore()
        for device in (across, beyond, crossed):
            pl.semaphore_signal(barrier, inc=1, device_id=device, device_id_type=MESH_IDS)
        pl.semaphore_wait(barrier, 3)
        xbuf[0:8] = jnp.zeros((8, chan), F32)
        dbuf[0:8] = jnp.full((8, LANES), -1.0, F32)
        state[...] = jnp.zeros(state.shape, F32)
        own_params(rank, heads, inner, inner_all, dtb_ref, dec_ref, skip_ref, cw_ref, cb_ref, par, skips, cwb)
        gain[0:1] = ggain_ref[:, pl.ds(pl.multiple_of(rank * inner, LANES), inner)]

    def slot(k):
        return pl.ds(pl.multiple_of(k * half, half), half)

    def h_copy(k):
        return pltpu.make_async_remote_copy(
            src_ref=h_out.at[slot(k)], dst_ref=h_in.at[slot(k)], send_sem=h_sem.at[0, k],
            recv_sem=h_sem.at[1, k], device_id=across, device_id_type=MESH_IDS,
        )

    def y_copy(k):
        return pltpu.make_async_remote_copy(
            src_ref=mine.at[slot(k)], dst_ref=far.at[slot(k)], send_sem=y_sem.at[0, k],
            recv_sem=y_sem.at[1, k], device_id=beyond, device_id_type=MESH_IDS,
        )

    def join(k):
        h_copy(k).wait_recv()
        mine[slot(k)] = (kept[slot(core)] + h_in[slot(k)].astype(F32)).astype(BF16)

    nb = normed_ref[...]
    xbuf[8 : 8 + SPAN] = nt(nb, win_ref[inner : inner + chan])
    gate_ref[...] = nt(nb, win_ref[0:inner])
    both_cores = nt(win_ref[inner + chan : inner + chan + 2 * heads], nb)
    stp = jnp.where(core == 0, both_cores[0:heads], both_cores[heads:])
    stp_ref[...] = stp
    mixed_ref[...] = xbuf[8 : 8 + SPAN]
    dn_ref[...] = nn(cot_ref[...], wout_ref[...])

    drow = docs_ref[:, pl.ds(pl.multiple_of(i * SPAN, SPAN), SPAN)].astype(F32)
    doc = jnp.broadcast_to(drow, (heads, SPAN))
    enter = jnp.broadcast_to(dbuf[7:8, 0:1], (heads, SPAN))
    _, run_rows, cols = head_scales(stp + par[0], par[1], doc, enter, [])
    dcol = jnp.broadcast_to(cols[:, 4 * heads : 4 * heads + 1], (SPAN, LANES))
    dbuf[8 : 8 + SPAN] = dcol
    keeps = [None] + [dbuf[8 - k : 8 - k + SPAN] == dcol for k in range(1, 4)]

    def conv(group):
        lanes = slice(group * LANES, (group + 1) * LANES)
        acc = cwb[4:5, lanes] + cwb[3:4, lanes] * xbuf[8 : 8 + SPAN, lanes]
        for k in range(1, 4):
            acc = acc + cwb[3 - k : 4 - k, lanes] * jnp.where(
                keeps[k], xbuf[8 - k : 8 - k + SPAN, lanes], 0.0
            )
        pre_ref[:, lanes] = acc
        return acc * sigmoid(acc)

    b_act, c_act = conv(pairs), conv(pairs + 1)
    b_rows, c_rows = b_act.astype(BF16), c_act.astype(BF16)

    row_i, col_i = iota((SPAN, SPAN), 0), iota((SPAN, SPAN), 1)
    same = jnp.concatenate([dcol, dcol], 1) == drow
    bias = jnp.where(same & (row_i >= col_i), 0.0, FAR)
    scores = exact_nt(c_act, b_act)
    b_turned = jnp.transpose(b_act).astype(BF16)
    low_half = iota((SPAN, LANES), 1) < LANES // 2
    square = jnp.zeros((SPAN, LANES), F32)
    cross = jnp.zeros((SPAN, LANES), F32)
    for pair in range(pairs):
        lanes = slice(pair * LANES, (pair + 1) * LANES)
        act = conv(pair)
        scaled = act * pair_lanes(cols, heads + 2 * pair, low_half)
        xb = scaled.astype(BF16)
        tail_l = pair_lanes(cols, 2 * heads + 2 * pair, low_half)
        reach_l = pair_lanes(cols, 3 * heads + 2 * pair, low_half)
        held = state[:, lanes]
        held_b = held.astype(BF16)
        state_ref[0, :, lanes] = held_b
        state[:, lanes] = nn(b_turned, (scaled * tail_l).astype(BF16)) + reach_l[SPAN - 1 : SPAN] * held
        out = reach_l * nn(c_rows, held_b)
        parts = []
        for sub in range(2):
            head = 2 * pair + sub
            blocks = []
            for blk in range(2):
                rows = slice(blk * half, (blk + 1) * half)
                width = (blk + 1) * half
                gap = cols[rows, head : head + 1] - run_rows[head : head + 1, 0:width]
                weight = jnp.exp2(gap + bias[rows, 0:width]) * scores[rows, 0:width]
                blocks.append(nn(weight.astype(BF16), xb[0:width]))
            parts.append(jnp.concatenate(blocks, 0))
        out = out + jnp.where(low_half, parts[0], parts[1])
        skip_l = pair_lanes(skips[0:1], 2 * pair, low_half[0:1])
        ssd = out + skip_l * act
        ssd_ref[:, lanes] = ssd
        gate = gate_ref[:, lanes]
        gated = ssd * (gate * sigmoid(gate))
        square = square + gated * gated
        gained = gain[0:1, lanes] * gated
        gg_ref[:, lanes] = gained.astype(BF16)
        cross = cross + dn_ref[:, lanes] * gained
    own_sums[0, pl.ds(i, 1), :] = as_row(square)
    own_sums[1, pl.ds(i, 1), :] = as_row(cross)
    xbuf[0:8] = xbuf[SPAN : SPAN + 8]
    dbuf[0:8] = dbuf[SPAN : SPAN + 8]
    @pl.when(i > 0)
    def _():
        join(i - 1)

        @pl.when(i - 1 < early)
        def _():
            y_copy(i - 1).start()

    kept[...] = nt(gg_ref[...], wout_ref[...])
    h_out[slot(i)] = kept[slot(1 - core)].astype(BF16)
    h_copy(i).start()

    @pl.when(i == spans - 1)
    def _():
        def s_copy(k, device):
            return pltpu.make_async_remote_copy(
                src_ref=own_sums, dst_ref=s_in.at[k], send_sem=s_sem.at[0, k],
                recv_sem=s_sem.at[1, k], device_id=device, device_id_type=MESH_IDS,
            )

        sent = [s_copy(0, across), s_copy(1, beyond), s_copy(2, crossed)]
        for copy in sent:
            copy.start()
        join(i)
        mine_put = pltpu.make_async_copy(mine, mine_ref, put_sem.at[0])
        mine_put.start()
        for copy in sent:
            copy.wait_recv()
        near = own_sums[...] + s_in[0]
        sums_ref[...] = near + (s_in[1] + s_in[2])
        for k in range(early):
            y_copy(k).wait_recv()
        far_put = pltpu.make_async_copy(far, far_ref, put_sem.at[1])
        far_put.start()
        for copy in sent:
            copy.wait_send()

        def drain(k, carry):
            h_copy(k).wait_send()
            return carry

        lax.fori_loop(0, spans, drain, 0)
        for k in range(early):
            y_copy(k).wait_send()
        mine_put.wait()
        far_put.wait()


def mixer_forward(docs, normed, cotangent, w_in, w_out, params, ggain, heads, early):
    tokens, model = normed.shape
    inner = w_out.shape[1]
    chan = inner + 2 * LANES
    spans = tokens // SPAN

    def tok(width):
        return pl.BlockSpec((SPAN, width), lambda i: (i, 0))

    def full(shape):
        return pl.BlockSpec(shape, lambda i: (0,) * len(shape))

    anywhere = pl.BlockSpec(memory_space=pl.ANY)
    sums = (2, spans, SPAN)
    outs = (
        jax.ShapeDtypeStruct((tokens, inner), F32),
        jax.ShapeDtypeStruct((tokens, chan), F32),
        jax.ShapeDtypeStruct((tokens, chan), F32),
        jax.ShapeDtypeStruct((tokens, inner), F32),
        jax.ShapeDtypeStruct((heads, tokens), F32),
        jax.ShapeDtypeStruct((spans, LANES, inner), BF16),
        jax.ShapeDtypeStruct((tokens, inner), F32),
        jax.ShapeDtypeStruct(sums, F32),
        jax.ShapeDtypeStruct((tokens // 2, model), BF16),
        jax.ShapeDtypeStruct((early * SPAN // 2, model), BF16),
    )
    out_specs = (
        tok(inner), tok(chan), tok(chan), tok(inner), pl.BlockSpec((heads, SPAN), lambda i: (0, i)),
        pl.BlockSpec((1, LANES, inner), lambda i: (i, 0, 0)),
        tok(inner), full(sums), anywhere, anywhere,
    )
    consts = (w_in, w_out) + params + (ggain,)
    dma, vmem = pltpu.SemaphoreType.DMA, pltpu.VMEM
    return pl.pallas_call(
        lambda *refs: forward_kernel((inner, heads, early), *refs),
        out_shape=outs,
        grid=(spans,),
        in_specs=[full(docs.shape), tok(model), tok(model)] + [full(v.shape) for v in consts],
        out_specs=out_specs,
        scratch_shapes=[
            vmem((SPAN + 8, chan), F32), vmem((SPAN + 8, LANES), F32), vmem((LANES, inner), F32),
            vmem((2, heads, SPAN), F32), vmem((8, LANES), F32), vmem((8, chan), F32), vmem((8, inner), F32),
            vmem((SPAN, inner), BF16), vmem(sums, F32),
            vmem((tokens // 2, model), BF16), vmem((tokens // 2, model), BF16),
            vmem((SPAN, model), F32), vmem((tokens // 2, model), BF16),
            vmem((early * SPAN // 2, model), BF16),
            dma((2, spans)), dma((2, early)), vmem((3,) + sums, F32), dma((2, 3)), dma((2,)),
        ],
        compiler_params=pltpu.CompilerParams(
            dimension_semantics=("arbitrary",), vmem_limit_bytes=VMEM_MOST,
            collective_id=2, has_side_effects=True,
        ),
        cost_estimate=cost(40.0),
        name="mixer_forward",
    )(docs, normed, cotangent, *consts)


def backward_kernel(
    dims,
    docs_ref, hid_ref, gate_ref, dn_ref, gate_low_ref, ssd_low_ref, dn_low_ref,
    ssd_ref, mixed_ref, pre_ref, stp_ref, state_ref, sums_ref,
    cw_ref, cb_ref, dtb_ref, dec_ref, skip_ref, ggain_ref, ngain_ref,
    naway_ref, nhere_ref, caway_ref, chere_ref, w_ref, mine_ref, far_ref,
    delta_ref, layer_ref, gin_ref, gout_ref, flatout_ref,
    naway, nhere, caway, chere, w, loads,
    pbuf, dbuf, dstate, par, skips, cwb, gain, w_step, sumv,
    gconv, gskip, ghead, ggain, gnorm,
    nout_all, dgate_all, dall, dssd_low, inv_now, inv_own, hid_own,
    h_out, mine, y_in, kept, h_sem, y_sem, d_sem, d_put,
    omine, ofar, oy_sem, o_sem, o_put,
    ax_out, ax_in, ax_sem, az_in, az_sem, atotal,
    sx_out, sx_in, sx_sem, sz_in, sz_sem, stotal, shere,
    vx_out, vx_in, vx_sem, vz_in, vz_sem, vtotal, vhere, vbuf,
    gates, g_sem, values, v_sem, shared, s_sem, put_sem, flat, flat_in, f_sem,
):
    inner, heads, inner_all, lines, depth, early = dims
    pairs = heads // 2
    chan = inner + 2 * LANES
    width = inner + chan + LANES
    i = pl.program_id(0)
    spans = pl.num_programs(0)
    tokens = nout_all.shape[0]
    count = tokens // SPAN
    mid = count // 2
    c = count - 1 - i
    half = SPAN // 2
    model = w.shape[1]
    blocks = lines * depth // LANES
    rank, drank = lax.axis_index("tensor"), lax.axis_index("dp")
    line, side = drank // 2, drank % 2
    core = rank % 2
    off = pl.multiple_of(rank * inner, LANES)
    across = {"tensor": rank + 1 - 2 * core}
    beyond = {"tensor": (rank + 2) % 4}
    partner = {"dp": line * 2 + 1 - side}

    def peer(step):
        return {"dp": lax.rem(line + step, lines) * 2 + side}

    def remote(src, dst, sems, index, device):
        return pltpu.make_async_remote_copy(
            src_ref=src, dst_ref=dst, send_sem=sems.at[0, index], recv_sem=sems.at[1, index],
            device_id=device, device_id_type=MESH_IDS,
        )

    def lot(k, size):
        return pl.ds(pl.multiple_of(k * size, size), size)

    fetch = [
        pltpu.make_async_copy(src, dst, loads.at[k])
        for k, (src, dst) in enumerate(
            (
                (mine_ref, omine), (w_ref, w), (far_ref, ofar.at[pl.ds(0, early * half)]),
                (caway_ref, caway), (naway_ref, naway), (chere_ref, chere), (nhere_ref, nhere),
            )
        )
    ]

    def oy_copy(k):
        return remote(omine.at[lot(k, half)], ofar.at[lot(k, half)], oy_sem, k - early, beyond)

    def my_rows(k):
        return pl.ds(pl.multiple_of(k * SPAN + core * half, half), half)

    def o_copy(k):
        return remote(omine.at[lot(k, half)], layer_ref.at[my_rows(k)], o_sem, k, across)

    def o_local(k):
        return pltpu.make_async_copy(omine.at[lot(k, half)], layer_ref.at[my_rows(k)], o_put.at[k])

    def d_copy(k):
        return remote(mine.at[lot(k, half)], delta_ref.at[my_rows(k)], d_sem, k, across)

    def d_local(k):
        return pltpu.make_async_copy(mine.at[lot(k, half)], delta_ref.at[my_rows(k)], d_put.at[k])

    def h_copy(k):
        return remote(h_out.at[lot(k, half)], mine.at[lot(k, half)], h_sem, k, across)

    def y_copy(k):
        return remote(mine.at[lot(k, half)], y_in.at[lot(k, half)], y_sem, k, beyond)

    def ax_copy(k):
        return remote(ax_out.at[lot(k, LANES)], ax_in.at[lot(k, LANES)], ax_sem, k, partner)

    def sx_copy(k):
        return remote(sx_out.at[lot(k, LANES)], sx_in.at[lot(k, LANES)], sx_sem, k, partner)

    def vx_copy(k):
        return remote(vx_out.at[lot(k, LANES)], vx_in.at[lot(k, LANES)], vx_sem, k, partner)

    def az_copy(step):
        return remote(ax_out.at[pl.ds(step * depth, depth)], az_in.at[step - 1], az_sem, step - 1, peer(step))

    def sz_copy(step):
        return remote(sx_out.at[pl.ds(step * depth, depth)], sz_in.at[step - 1], sz_sem, step - 1, peer(step))

    def vz_copy(step):
        return remote(vx_out.at[pl.ds(step * depth, depth)], vz_in.at[step - 1], vz_sem, step - 1, peer(step))

    @pl.when(i == 0)
    def _():
        barrier = pltpu.get_barrier_semaphore()
        for device in [across, beyond, partner] + [peer(step) for step in range(1, lines)]:
            pl.semaphore_signal(barrier, inc=1, device_id=device, device_id_type=MESH_IDS)
        pl.semaphore_wait(barrier, lines + 2)
        for copy in fetch:
            copy.start()
        pbuf[SPAN : SPAN + 8] = jnp.zeros((8, chan), F32)
        dbuf[SPAN : SPAN + 8] = jnp.full((8, LANES), -2.0, F32)
        dstate[...] = jnp.zeros(dstate.shape, F32)
        own_params(rank, heads, inner, inner_all, dtb_ref, dec_ref, skip_ref, cw_ref, cb_ref, par, skips, cwb)
        gain[0:1] = ggain_ref[:, pl.ds(off, inner)]
        for acc in (gconv, gskip, ghead, ggain, gnorm):
            acc[...] = jnp.zeros(acc.shape, F32)
        fetch[0].wait()
        for k in range(early, count):
            oy_copy(k).start()

    def join(k):
        h_copy(k).wait_recv()
        mine[lot(k, half)] = (kept[lot(core, half)] + mine[lot(k, half)].astype(F32)).astype(BF16)
        y_copy(k).start()

    def out_grads(n_side, c_side, k):
        cols = lot(k, LANES)
        return jnp.concatenate(
            [tn(c_side[:, cols], nout_all[...]), tn(n_side[:, cols], dgate_all[...])], 1
        )

    per = LANES // depth

    def to_lines(k, joined, x_copy_of, x_out, z_copy_of, total):
        x_copy_of(k).wait_send()
        x_out[lot(k, LANES)] = joined.astype(BF16)
        if isinstance(k, int):
            if k == 0:
                total[...] = joined[0:depth]
            for step in range(max(1, k * per), (k + 1) * per):
                z_copy_of(step).start()

    def a_block(k):
        ax_copy(k).wait_recv()
        joined = out_grads(nhere, chere, k) + ax_in[lot(k, LANES)].astype(F32)
        to_lines(k, joined, ax_copy, ax_out, az_copy, atotal)

    def s_block(k):
        sx_copy(k).wait_recv()
        joined = shere[lot(k, LANES)] + sx_in[lot(k, LANES)].astype(F32)
        to_lines(k, joined, sx_copy, sx_out, sz_copy, stotal)

    def v_block(k):
        vx_copy(k).wait_recv()
        joined = vhere[lot(k, LANES)] + vx_in[lot(k, LANES)].astype(F32)
        to_lines(k, joined, vx_copy, vx_out, vz_copy, vtotal)

    @pl.when(i == mid)
    def _():
        for copy in fetch[2:]:
            copy.wait()

    hid_own[lot(c, half)] = hid_ref[lot(core, half)]

    def inverse(k):
        inv = lax.rsqrt(sums_ref[0, pl.ds(k, 1), :] * (1.0 / inner_all) + EPS)
        pull = sums_ref[1, pl.ds(k, 1), :] * (inv * inv * inv) * (1.0 / inner_all)
        return inv, pull

    def spread_inverse(k, cols, first):
        inv = jnp.broadcast_to(cols[:, first : first + 1], (SPAN, LANES))
        inv_now[...] = inv
        inv_own[lot(k, half)] = inv_now[lot(core, half)]
        return inv, jnp.broadcast_to(cols[:, first + 1 : first + 2], (SPAN, LANES))

    def gating(k, scales, lanes, gate_in, ssd_in, dn_in):
        inv, pull = scales
        gate = gate_in[:, lanes]
        sig = sigmoid(gate)
        silu = gate * sig
        ssd = ssd_in[:, lanes]
        gated = ssd * silu
        dn = dn_in[:, lanes]
        g_l = gain[0:1, lanes]
        nout = gated * inv
        nout_all[lot(k, SPAN), lanes] = (nout * g_l).astype(BF16)
        ggain[:, lanes] += fold(dn * nout)
        d_gated = dn * g_l * inv - gated * pull
        dgate_all[lot(k, SPAN), lanes] = (d_gated * ssd * (sig * (1.0 + gate * (1.0 - sig)))).astype(BF16)
        return d_gated * silu

    def finish_out(k):
        total = omine[lot(k, half)].astype(F32) + ofar[lot(k, half)].astype(F32)
        inv = inv_own[lot(k, half)]
        value = hid_own[lot(k, half)].astype(F32)
        for group in range(model // LANES):
            lanes = slice(group * LANES, (group + 1) * LANES)
            omine[lot(k, half), lanes] = (value[:, lanes] + total[:, lanes] * inv).astype(BF16)
        o_copy(k).start()
        o_local(k).start()

    def scan_step(first):
        drow = docs_ref[:, lot(c, SPAN)].astype(F32)
        before = docs_ref[:, lot(jnp.maximum(c - 1, 0), SPAN)].astype(F32)
        doc = jnp.broadcast_to(drow, (heads, SPAN))
        enter = jnp.broadcast_to(before[:, SPAN - 1 :], (heads, SPAN))
        enter = jnp.where(c == 0, -1.0, enter)
        extra = []
        if first:
            row = iota((8, SPAN), 0)
            block = jnp.zeros((8, SPAN), F32)
            for k, v in enumerate(inverse(c) + inverse(c - mid)):
                block = jnp.where(row == k, jnp.broadcast_to(v, (8, SPAN)), block)
            extra = [block]
        raw = stp_ref[...] + par[0]
        log_step, run_rows, cols = head_scales(raw, par[1], doc, enter, extra)
        dcol = jnp.broadcast_to(cols[:, 4 * heads : 4 * heads + 1], (SPAN, LANES))
        if first:
            scales = spread_inverse(c, cols, 5 * heads)
            low_scales = spread_inverse(c - mid, cols, 5 * heads + 2)
        dbuf[0:SPAN] = dcol
        keeps = [None] + [dbuf[k : k + SPAN] == dcol for k in range(1, 4)]
        if not first:
            block = lax.rem(i - mid + 1, blocks)
            ax_out[lot(block, LANES)] = out_grads(naway, caway, block).astype(BF16)
        row_i, col_i = iota((SPAN, SPAN), 0), iota((SPAN, SPAN), 1)
        same = jnp.concatenate([dcol, dcol], 1) == drow
        bias = jnp.where(same & (row_i <= col_i), 0.0, FAR)

        def activate(group):
            lanes = slice(group * LANES, (group + 1) * LANES)
            pre = pre_ref[:, lanes]
            sig = sigmoid(pre)
            return pre * sig, sig * (1.0 + pre * (1.0 - sig))

        b_act, b_slope = activate(pairs)
        c_act, c_slope = activate(pairs + 1)
        b_rows, c_rows = b_act.astype(BF16), c_act.astype(BF16)
        c_turned = jnp.transpose(c_act).astype(BF16)
        scores = exact_nt(b_act, c_act)
        low_half = iota((SPAN, LANES), 1) < LANES // 2
        d_scores = [jnp.zeros((half, SPAN), F32), jnp.zeros((half, half), F32)]
        d_b = jnp.zeros((SPAN, LANES), F32)
        d_c = jnp.zeros((SPAN, LANES), F32)
        holds = []
        for pair in range(pairs):
            lanes = slice(pair * LANES, (pair + 1) * LANES)
            act, slope = activate(pair)
            step_l = pair_lanes(cols, heads + 2 * pair, low_half)
            tail_l = pair_lanes(cols, 2 * heads + 2 * pair, low_half)
            reach_l = pair_lanes(cols, 3 * heads + 2 * pair, low_half)
            skip_l = pair_lanes(skips[0:1], 2 * pair, low_half[0:1])
            ssd = ssd_ref[:, lanes]
            if first:
                d_ssd = gating(c, scales, lanes, gate_ref, ssd_ref, dn_ref)
                dssd_low[lot(c - mid, SPAN), lanes] = gating(
                    c - mid, low_scales, lanes, gate_low_ref, ssd_low_ref, dn_low_ref
                )
            else:
                d_ssd = dssd_low[lot(c, SPAN), lanes]
            gskip[:, lanes] += fold(d_ssd * act)
            dyb = d_ssd.astype(BF16)
            scaled = act * step_l
            xb = scaled.astype(BF16)
            held = state_ref[0, :, lanes]
            d_held = dstate[:, lanes]
            d_held_b = d_held.astype(BF16)
            ry = (d_ssd * reach_l).astype(BF16)
            xt = (scaled * tail_l).astype(BF16)
            parts = []
            for sub in range(2):
                head = 2 * pair + sub
                x_own = jnp.where(low_half if sub == 0 else ~low_half, scaled, 0.0).astype(BF16)
                tiles = []
                for blk in range(2):
                    rows = slice(blk * half, (blk + 1) * half)
                    span = slice(blk * half, SPAN)
                    gap = run_rows[head : head + 1, span] - cols[rows, head : head + 1]
                    decay = jnp.exp2(gap + bias[rows, span])
                    tiles.append(nn((decay * scores[rows, span]).astype(BF16), dyb[span]))
                    d_scores[blk] = d_scores[blk] + decay * nt(x_own[rows], dyb[span])
                parts.append(jnp.concatenate(tiles, 0))
            d_within = jnp.where(low_half, parts[0], parts[1])
            from_state = tail_l * nn(b_rows, d_held_b)
            d_scaled = d_within + from_state
            xf = xb.astype(F32)
            up = dyb.astype(F32) * (ssd - skip_l * act) - xf * d_within
            up_hi = up.astype(BF16)
            sumv[0, :, lanes] = up_hi
            sumv[1, :, lanes] = (up - up_hi.astype(F32)).astype(BF16)
            sumv[2, :, lanes] = (xf * from_state).astype(BF16)
            sumv[3, :, lanes] = (d_scaled * act).astype(BF16)
            hold = reach_l[SPAN - 1 : SPAN]
            held_sum = jnp.sum((d_held * held.astype(F32)).reshape(LANES // 8, 8, LANES), axis=0)
            holds.append(jnp.sum(held_sum, axis=0, keepdims=True) * hold)
            d_b += nt(xt, d_held_b)
            d_c += nt(ry, held)
            dstate[:, lanes] = hold * d_held + nn(c_turned, ry)
            pbuf[0:SPAN, lanes] = (skip_l * d_ssd + step_l * d_scaled) * slope

        ds_b = jnp.concatenate(
            [
                d_scores[0],
                jnp.concatenate([jnp.zeros((half, half), F32), d_scores[1]], 1),
            ],
            0,
        )
        d_b += nn(ds_b.astype(BF16), c_rows)
        d_c += nn(jnp.transpose(ds_b).astype(BF16), b_rows)
        pbuf[0:SPAN, inner : inner + LANES] = d_b * b_slope
        pbuf[0:SPAN, inner + LANES : chan] = d_c * c_slope

        per_head = inner // heads
        owner = (iota((2 * heads, inner), 0) == iota((2 * heads, inner), 1) // per_head).astype(BF16)
        up = (nt(owner, sumv[0]) + nt(owner, sumv[1]))[0:heads]
        down = nt(owner, sumv[2])[0:heads]
        direct = nt(owner, sumv[3])[0:heads]
        hold_row = jnp.broadcast_to(jnp.concatenate(holds, 1), (heads, inner))
        inside = iota((heads, inner), 0) == iota((heads, inner), 1) // per_head
        hold_sum = jnp.sum(jnp.where(inside, hold_row, 0.0), axis=1, keepdims=True)
        d_log = (
            row_sum(up, (row_i >= col_i).astype(BF16))
            + row_sum(down, (row_i < col_i).astype(BF16))
            + jnp.broadcast_to(hold_sum, (heads, SPAN))
        )
        d_raw = (d_log * par[1] + direct) * sigmoid(raw)
        turned = jnp.transpose(jnp.concatenate([d_raw, jnp.zeros((LANES - heads, SPAN), F32)], 0))
        dall[lot(c, SPAN), chan:] = turned.astype(BF16)
        ghead[0] += d_raw
        ghead[1] += d_log * log_step

        for group in range(chan // LANES):
            lanes = slice(group * LANES, (group + 1) * LANES)
            mixed = mixed_ref[:, lanes]
            own = pbuf[0:SPAN, lanes]
            acc = cwb[3:4, lanes] * own
            gconv[3, :, lanes] += fold(mixed * own)
            gconv[4, :, lanes] += fold(own)
            for k in range(1, 4):
                later = jnp.where(keeps[k], pbuf[k : k + SPAN, lanes], 0.0)
                acc = acc + cwb[3 - k : 4 - k, lanes] * later
                gconv[3 - k, :, lanes] += fold(mixed * later)
            dall[lot(c, SPAN), lanes] = acc.astype(BF16)
        pbuf[SPAN : SPAN + 8] = pbuf[0:8]
        dbuf[SPAN : SPAN + 8] = dbuf[0:8]

    @pl.when(i < mid)
    def _():
        scan_step(True)

    @pl.when(i >= mid)
    def _():
        for k in (c + mid, c):
            if k is not c:
                oy_copy(k).wait_recv()
                oy_copy(k).wait_send()
            finish_out(k)
        scan_step(False)
        ax_copy(lax.rem(i - mid + 1, blocks)).start()

    @pl.when(i > 0)
    def _():
        join(c + 1)

    order = tuple(range(1, blocks)) + (0,)
    for k in range(blocks - 1):
        @pl.when(i == mid + 1 + k)
        def _():
            a_block(order[k])

    @pl.when(i == 0)
    def _():
        fetch[1].wait()
        both_cores = w[inner + chan : inner + chan + 2 * heads].astype(F32)
        own = jnp.where(core == 0, both_cores[0:heads], both_cores[heads:])
        w_step[...] = jnp.concatenate([own, jnp.zeros((LANES - heads, model), F32)], 0).astype(BF16)

    rows_now = lot(c, SPAN)
    kept[...] = (
        nn(dgate_all[rows_now], w[0:inner])
        + nn(dall[rows_now, 0:chan], w[inner : inner + chan])
        + nn(dall[rows_now, chan:], w_step[...])
    )
    h_out[lot(c, half)] = kept[lot(1 - core, half)].astype(BF16)
    h_copy(c).start()
    value = hid_ref[...].astype(F32)
    unit = value * lax.rsqrt(jnp.mean(value * value, -1, keepdims=True) + EPS)
    gnorm[...] += fold(kept[...] * unit)

    @pl.when(i == count - 1)
    def _():
        sx_out[...] = tn(naway[...], dall[:, inner:]).astype(BF16)
        for k in order:
            sx_copy(k).start()
        vx_out[LANES:] = tn(naway[:, LANES:], dall[:, 0:inner]).astype(BF16)
        for k in order[:-1]:
            vx_copy(k).start()
        vx_out[0:LANES] = tn(naway[:, 0:LANES], dall[:, 0:inner]).astype(BF16)
        vx_copy(0).start()
        join(0)

        chan_all = inner_all + 2 * LANES
        tap_rows, own_rows = chan_all // LANES, inner // LANES
        flat[...] = jnp.zeros(flat.shape, F32)
        norm = jnp.sum(gnorm[...], axis=0, keepdims=True)
        at = model // LANES
        for k in range(at):
            flat[k : k + 1] = norm[:, k * LANES : (k + 1) * LANES]
        for tap in range(gconv.shape[0]):
            row = jnp.sum(gconv[tap], axis=0, keepdims=True)
            for k in range(chan // LANES):
                place = at + k + (rank * own_rows if k < own_rows else (tap_rows - chan // LANES))
                flat[pl.ds(place, 1), :] = row[:, k * LANES : (k + 1) * LANES]
            at += tap_rows
        spread = jnp.zeros((1, LANES), F32)
        for k in range(2):
            total = jnp.broadcast_to(jnp.sum(ghead[k], axis=1, keepdims=True), (heads, LANES))
            place = iota((heads, LANES), 1) == 4 * heads * k + rank * heads + iota((heads, LANES), 0)
            spread = spread + jnp.sum(jnp.where(place, total, 0.0), axis=0, keepdims=True)
        flat[at : at + 1] = spread
        at += 1
        for acc in (ggain, gskip):
            row = jnp.sum(acc[...], axis=0, keepdims=True)
            for k in range(own_rows):
                flat[pl.ds(at + rank * own_rows + k, 1), :] = row[:, k * LANES : (k + 1) * LANES]
            at += inner_all // LANES

        hops = [across, beyond, partner]
        bit = 1
        while bit < lines:
            hops.append({"dp": (line + bit * (1 - 2 * ((line // bit) % 2))) * 2 + side})
            bit *= 2
        last = flat_in.shape[0] - 1

        def flat_copy(k):
            return remote(
                flat.at[...] if k == 0 else flat_in.at[len(hops) + k], flat_in.at[k], f_sem, k, hops[k]
            )

        def flat_step(k):
            flat_copy(k).wait_recv()
            held = (flat[...] if k == 0 else flat_in[len(hops) + k]) + flat_in[k]
            if k + 1 < len(hops):
                flat_in[len(hops) + k + 1] = held
                flat_copy(k + 1).start()
            else:
                flat_in[last] = held

        flat_copy(0).start()

        a_block(order[-1])
        gain_row = ngain_ref[...]

        def finish_hidden(k, carry):
            y_copy(k).wait_recv()
            y_copy(k).wait_send()
            d_hidden = mine[lot(k, half)].astype(F32) + y_in[lot(k, half)].astype(F32)
            value = hid_own[lot(k, half)].astype(F32)
            inv = lax.rsqrt(jnp.mean(value * value, -1, keepdims=True) + EPS)
            scaled = d_hidden * gain_row
            pull = jnp.mean(scaled * value, -1, keepdims=True)
            mine[lot(k, half)] = (inv * scaled - value * (inv * inv * inv) * pull).astype(BF16)
            d_copy(k).start()
            d_local(k).start()
            return carry

        def down(k, carry):
            return finish_hidden(count - 1 - k, carry)

        shere[...] = tn(nhere[...], dall[:, inner:])
        for k in order:
            s_block(k)
        vhere[...] = tn(nhere[...], dall[:, 0:inner])
        flat_step(0)
        lax.fori_loop(0, 3, down, 0)
        for k in order[:-1]:
            v_block(k)
        flat_step(1)
        for step in range(1, lines):
            az_copy(step).wait_recv()
            atotal[...] += az_in[step - 1].astype(F32)
        gates[0] = atotal[:, inner:]
        gout_put = pltpu.make_async_copy(atotal.at[:, pl.ds(0, inner)], gout_ref, put_sem.at[9])
        gout_put.start()
        gate_near = remote(gates.at[0], gates.at[1], g_sem, 0, across)
        gate_far = remote(gates.at[0], gates.at[2], g_sem, 1, beyond)
        gate_pass = remote(gates.at[2], gates.at[3], g_sem, 2, across)
        gate_near.start()
        gate_far.start()
        for step in range(1, lines):
            sz_copy(step).wait_recv()
            stotal[...] += sz_in[step - 1].astype(F32)
        shared_near = remote(shared.at[0], shared.at[1], s_sem, 0, across)
        shared_far = remote(shared.at[2], shared.at[3], s_sem, 1, beyond)
        shared[0, :, 0 : 2 * LANES] = stotal[:, 0 : 2 * LANES]
        steps = pltpu.roll(stotal[:, 2 * LANES :], rank * heads, 1)
        place = iota(steps.shape, 1) - rank * heads
        shared[0, :, 2 * LANES :] = jnp.where((place >= 0) & (place < heads), steps, 0.0)
        shared_near.start()
        flat_step(2)
        v_block(order[-1])
        lax.fori_loop(3, 6, down, 0)
        shared_near.wait_recv()
        shared[2] = shared[0] + shared[1]
        shared_far.start()
        gate_far.wait_recv()
        gate_pass.start()
        for k in range(3, len(hops)):
            flat_step(k)
        flat_put = pltpu.make_async_copy(flat_in.at[last], flatout_ref, put_sem.at[10])
        flat_put.start()
        lax.fori_loop(6, count, down, 0)

        for step in range(1, lines):
            vz_copy(step).wait_recv()
            vtotal[...] += vz_in[step - 1].astype(F32)
        values[0] = vtotal[...].astype(BF16)
        value_near = remote(values.at[0], values.at[1], v_sem, 0, across)
        value_far = remote(values.at[0], values.at[2], v_sem, 1, beyond)
        value_pass = remote(values.at[2], values.at[3], v_sem, 2, across)
        value_far.start()
        value_near.start()

        def put(source, k, first, owner, index):
            column = pl.multiple_of(first + owner * inner, LANES)
            return pltpu.make_async_copy(source.at[k], gin_ref.at[:, pl.ds(column, inner)], put_sem.at[index])

        owners = (rank, rank + 1 - 2 * core, (rank + 2) % 4, (rank + 3 - 2 * core) % 4)
        gate_near.wait_recv()
        gate_pass.wait_recv()
        puts = [put(gates, k, 0, owners[k], k) for k in range(4)]
        shared_far.wait_recv()
        shared[1] = shared[2] + shared[3]
        puts.append(
            pltpu.make_async_copy(
                shared.at[1], gin_ref.at[:, pl.ds(2 * inner_all, 3 * LANES)], put_sem.at[8]
            )
        )
        for copy in puts:
            copy.start()

        def put_values(k):
            vbuf[k] = values[k].astype(F32)
            puts.append(put(vbuf, k, inner_all, owners[k], 4 + k))
            puts[-1].start()

        put_values(0)
        value_near.wait_recv()
        put_values(1)
        value_far.wait_recv()
        value_pass.start()
        put_values(2)
        value_pass.wait_recv()
        put_values(3)

        def drain(k, carry):
            h_copy(k).wait_send()
            d_copy(k).wait()
            d_local(k).wait()
            o_copy(k).wait()
            o_local(k).wait()
            return carry

        lax.fori_loop(0, count, drain, 0)
        for step in range(1, lines):
            az_copy(step).wait_send()
            sz_copy(step).wait_send()
            vz_copy(step).wait_send()
        for copy in (
            gate_near, gate_far, gate_pass, value_near, value_far, value_pass, shared_near, shared_far,
        ):
            copy.wait_send()
        for k in range(len(hops)):
            flat_copy(k).wait_send()
        for copy in puts + [gout_put, flat_put]:
            copy.wait()


def mixer_backward(
    docs, hidden, held, sums, params, ggain, ngain, sorted_parts, w_in, mine, far,
    heads, lines, depth, early,
):
    gate, mixed, pre, ssd, stp, states, dn = held
    tokens, inner = ssd.shape
    model = hidden.shape[1]
    chan = inner + 2 * LANES
    width = inner + chan + LANES
    wide = width - inner
    inner_all = ggain.shape[1]
    count = tokens // SPAN
    mid = count // 2
    half = SPAN // 2
    blocks, fars = lines * depth // LANES, max(1, lines - 1)
    hops = 3 + (lines - 1).bit_length()
    rows = (model + 5 * (inner_all + 2 * LANES) + LANES + 2 * inner_all) // LANES
    rows += -rows % 8

    def tok(size):
        return pl.BlockSpec((SPAN, size), lambda i: (count - 1 - i, 0))

    def early_tok(size, base):
        return pl.BlockSpec((SPAN, size), lambda i: (base + (mid - 1 - i) * (1 - i // mid), 0))

    def full(shape):
        return pl.BlockSpec(shape, lambda i: (0,) * len(shape))

    anywhere = pl.BlockSpec(memory_space=pl.ANY)
    dma, vmem = pltpu.SemaphoreType.DMA, pltpu.VMEM
    consts = params + (ggain, ngain)
    big = tuple(sorted_parts)[0:2] + tuple(sorted_parts)[2:4] + (w_in, mine, far)
    side_shape = (tokens, lines * depth)
    return pl.pallas_call(
        lambda *refs: backward_kernel((inner, heads, inner_all, lines, depth, early), *refs),
        out_shape=(
            jax.ShapeDtypeStruct((tokens, model), BF16),
            jax.ShapeDtypeStruct((tokens, model), BF16),
            jax.ShapeDtypeStruct((depth, 2 * inner_all + 3 * LANES), F32),
            jax.ShapeDtypeStruct((depth, inner), F32),
            jax.ShapeDtypeStruct((rows, LANES), F32),
        ),
        grid=(count,),
        in_specs=[
            full(docs.shape), tok(model), early_tok(inner, mid), early_tok(inner, mid),
            early_tok(inner, 0), early_tok(inner, 0), early_tok(inner, 0),
            tok(inner), tok(chan), tok(chan), pl.BlockSpec((heads, SPAN), lambda i: (0, count - 1 - i)),
            pl.BlockSpec((1, LANES, inner), lambda i: (count - 1 - i, 0, 0)),
            full(sums.shape),
        ]
        + [full(v.shape) for v in consts]
        + [anywhere] * len(big),
        out_specs=(anywhere,) * 5,
        scratch_shapes=[
            vmem(side_shape, BF16), vmem(side_shape, BF16), vmem(side_shape, BF16), vmem(side_shape, BF16),
            vmem(w_in.shape, BF16), dma((len(big),)),
            vmem((SPAN + 8, chan), F32), vmem((SPAN + 8, LANES), F32), vmem((LANES, inner), F32),
            vmem((2, heads, SPAN), F32), vmem((8, LANES), F32), vmem((8, chan), F32), vmem((8, inner), F32),
            vmem((LANES, model), BF16), vmem((4, SPAN, inner), BF16),
            vmem((5, 8, chan), F32), vmem((8, inner), F32), vmem((2, heads, SPAN), F32),
            vmem((8, inner), F32), vmem((8, model), F32),
            vmem((tokens, inner), BF16), vmem((tokens, inner), BF16), vmem((tokens, wide), BF16),
            vmem((tokens // 2, inner), F32), vmem((SPAN, LANES), F32), vmem((tokens // 2, LANES), F32),
            vmem((tokens // 2, model), BF16),
            vmem((tokens // 2, model), BF16), vmem((tokens // 2, model), BF16),
            vmem((tokens // 2, model), BF16), vmem((SPAN, model), F32),
            dma((2, count)), dma((2, count)), dma((2, count)), dma((count,)),
            vmem((tokens // 2, model), BF16), vmem((tokens // 2, model), BF16),
            dma((2, count - early)), dma((2, count)), dma((count,)),
            vmem((blocks * LANES, 2 * inner), BF16), vmem((blocks * LANES, 2 * inner), BF16),
            dma((2, blocks)), vmem((fars, depth, 2 * inner), BF16), dma((2, fars)),
            vmem((depth, 2 * inner), F32),
            vmem((blocks * LANES, 3 * LANES), BF16), vmem((blocks * LANES, 3 * LANES), BF16),
            dma((2, blocks)), vmem((fars, depth, 3 * LANES), BF16), dma((2, fars)),
            vmem((depth, 3 * LANES), F32), vmem((blocks * LANES, 3 * LANES), F32),
            vmem((blocks * LANES, inner), BF16), vmem((blocks * LANES, inner), BF16),
            dma((2, blocks)), vmem((fars, depth, inner), BF16), dma((2, fars)), vmem((depth, inner), F32),
            vmem((blocks * LANES, inner), F32), vmem((4, depth, inner), F32),
            vmem((4, depth, inner), F32), dma((2, 3)), vmem((4, depth, inner), BF16), dma((2, 3)),
            vmem((4, depth, 3 * LANES), F32), dma((2, 2)), dma((11,)),
            vmem((rows, LANES), F32), vmem((2 * hops + 1, rows, LANES), F32), dma((2, hops)),
        ],
        compiler_params=pltpu.CompilerParams(
            dimension_semantics=("arbitrary",), vmem_limit_bytes=67043328,
            collective_id=1, has_side_effects=True,
        ),
        cost_estimate=cost(90.0),
        name="mixer_backward",
    )(
        docs, hidden, gate, dn, gate, ssd, dn, ssd, mixed, pre, stp, states, sums, *consts, *big
    )


def finish_kernel(
    dims, cot_ref, delta_ref, layer_ref, gin_ref, flat_ref,
    out_ref, grad_ref, norm_ref, win_ref, taps_ref, bias_ref, dt_ref, decay_ref, skip_ref, gain_ref,
):
    inner_all, heads, turned = dims
    grad_ref[...] = cot_ref[...].astype(F32) + delta_ref[...].astype(F32)
    out_ref[...] = layer_ref[...]
    if turned:
        win_ref[...] = jnp.transpose(gin_ref[...])
    else:
        win_ref[...] = gin_ref[:, 0 : win_ref.shape[1]]

    @pl.when(pl.program_id(0) == 0)
    def _():
        at = norm_ref.shape[1] // LANES

        def spread(dst, row, first, count):
            for k in range(count):
                dst[row : row + 1, k * LANES : (k + 1) * LANES] = flat_ref[first + k : first + k + 1]

        spread(norm_ref, 0, 0, at)
        wide = taps_ref.shape[1] // LANES
        for tap in range(taps_ref.shape[0]):
            spread(taps_ref, tap, at + tap * wide, wide)
        at += taps_ref.shape[0] * wide
        bias_ref[...] = flat_ref[at : at + wide]
        at += wide
        dt_ref[...] = flat_ref[at : at + 1, 0:heads]
        decay_ref[...] = flat_ref[at : at + 1, heads : 2 * heads]
        at += 1
        spread(gain_ref, 0, at, inner_all // LANES)
        at += inner_all // LANES
        per = inner_all // heads
        lane = iota((1, LANES), 1)
        found = jnp.zeros((1, LANES), F32)
        for k in range(inner_all // LANES):
            row = flat_ref[at + k : at + k + 1]
            for part in range(LANES // per):
                inside = (lane >= part * per) & (lane < (part + 1) * per)
                total = jnp.sum(jnp.where(inside, row, 0.0), axis=1, keepdims=True)
                found = jnp.where(lane == k * (LANES // per) + part, total, found)
        skip_ref[...] = found[:, 0:heads]


def finish(cotangent, delta, layer_out, grad_in, flat, columns, inner_all, heads, turned):
    tokens, model = cotangent.shape
    depth = grad_in.shape[0]
    steps = 8
    chan_all = inner_all + 2 * LANES

    def tok(v, size):
        return pl.BlockSpec((v // steps, size), lambda i: (i, 0))

    def full(shape):
        return pl.BlockSpec(shape, lambda i: (0,) * len(shape))

    small = [(1, model), (4, chan_all), (chan_all // LANES, LANES), (1, heads), (1, heads), (1, heads), (1, inner_all)]
    if turned:
        cut = grad_in.shape[1] // (steps - 1)
        rows = pl.BlockSpec((depth, cut), lambda i: (0, i - i // (steps - 1)))
        shown = pl.BlockSpec((cut, depth), lambda i: (i - i // (steps - 1), 0))
    else:
        rows, shown = full(grad_in.shape), full((depth, columns))
    return pl.pallas_call(
        lambda *refs: finish_kernel((inner_all, heads, turned), *refs),
        out_shape=[
            jax.ShapeDtypeStruct((tokens, model), BF16),
            jax.ShapeDtypeStruct((tokens, model), F32),
            jax.ShapeDtypeStruct(small[0], F32),
            jax.ShapeDtypeStruct((columns, depth) if turned else (depth, columns), F32),
        ]
        + [jax.ShapeDtypeStruct(v, F32) for v in small[1:]],
        grid=(steps,),
        in_specs=[tok(tokens, model)] * 3 + [rows, full(flat.shape)],
        out_specs=[tok(tokens, model)] * 2 + [full(small[0]), shown] + [full(v) for v in small[1:]],
        compiler_params=pltpu.CompilerParams(dimension_semantics=("arbitrary",)),
        cost_estimate=cost(9.0),
        name="finish",
    )(cotangent, delta, layer_out, grad_in, flat)


def gather_kernel(
    dims, hid_ref, cot_ref, ngain_ref, w_ref, step_ref, wo_ref,
    win_ref, wout_ref, normed_ref, *refs,
):
    lines, depth, inner, inner_all, heads, turned = dims
    outs = refs[:4] if turned else ()
    mine, zsend, zrecv, xsend, xrecv, takes, puts, qsend, qrecv = refs[len(outs):]
    trank, drank = lax.axis_index("tensor"), lax.axis_index("dp")
    line, side = drank // 2, drank % 2
    core = trank % 2
    model = hid_ref.shape[1]
    off = pl.multiple_of(trank * inner, LANES)
    base = 2 * inner_all
    if turned:
        quarter = 2 * LANES // 4
        own_quarter = pl.multiple_of(trank * quarter, quarter)
        chip = 2 * heads
        steps = pl.multiple_of(base + 2 * LANES + (trank // 2) * chip, chip)
        cut = inner // 2
        pieces = [
            (w_ref, base + own_quarter, win_ref, 2 * inner + own_quarter, quarter),
            (w_ref, steps, win_ref, 2 * inner + 2 * LANES, chip),
        ]
        pieces += [(w_ref, inner_all + off + k * cut, win_ref, inner + k * cut, cut) for k in range(2)]
        pieces += [(w_ref, off + k * cut, win_ref, k * cut, cut) for k in range(2)]
        pieces += [(wo_ref, k * LANES, wout_ref, k * LANES, LANES) for k in range(inner // LANES)]
    else:
        pieces = [
            (w_ref, inner_all + off, win_ref, inner, inner),
            (w_ref, base, win_ref, 2 * inner, 2 * LANES),
            (step_ref, 0, win_ref, 2 * inner + 2 * LANES, LANES),
            (w_ref, off, win_ref, 0, inner),
            (wo_ref, 0, wout_ref, 0, inner),
        ]

    def peer(step):
        return {"dp": lax.rem(line + step, lines) * 2 + side}

    partner = {"dp": line * 2 + 1 - side}
    family = (
        {"tensor": trank + 1 - 2 * core}, {"tensor": (trank + 2) % 4},
        {"tensor": (trank + 3 - 2 * core) % 4},
    )
    others = [partner] + [peer(step) for step in range(1, lines)] + (list(family) if turned else [])
    barrier = pltpu.get_barrier_semaphore()
    for device in others:
        pl.semaphore_signal(barrier, inc=1, device_id=device, device_id_type=MESH_IDS)
    pl.semaphore_wait(barrier, len(others))

    def lanes_of(index):
        return pl.ds(pl.multiple_of(index * depth, depth), depth)

    def in_rows(p):
        return turned and pieces[p][0] is w_ref

    def block(p, index):
        _, _, dst, at, width = pieces[p]
        if in_rows(p):
            return dst.at[pl.ds(at, width), lanes_of(index)]
        return dst.at[lanes_of(index), pl.ds(at, width)]

    def own(p):
        src, at, _, _, width = pieces[p]
        return src.at[pl.ds(at, width)] if in_rows(p) else src.at[:, pl.ds(at, width)]

    def z_copy(p, step, src, index):
        return pltpu.make_async_remote_copy(
            src_ref=src, dst_ref=block(p, index), send_sem=zsend.at[p, step - 1],
            recv_sem=zrecv.at[p, step - 1], device_id=peer(step), device_id_type=MESH_IDS,
        )

    def x_copy(p, step, src, index):
        return pltpu.make_async_remote_copy(
            src_ref=src, dst_ref=block(p, index), send_sem=xsend.at[p, step],
            recv_sem=xrecv.at[p, step], device_id=partner, device_id_type=MESH_IDS,
        )

    count = len(pieces)
    for p in range(count):
        for step in range(1, lines):
            z_copy(p, step, own(p), drank).start()
        x_copy(p, 0, own(p), drank).start()
    spots, at = [], 0
    for p in range(count):
        width = pieces[p][4]
        if in_rows(p):
            spots.append(mine.at[pl.ds(at, width), pl.ds(0, depth)])
            at += width
        elif turned:
            spots.append(mine.at[pl.ds(at, depth), pl.ds(0, width)])
            at += depth
        else:
            spots.append(mine.at[:, pl.ds(at, width)])
            at += width
    fetched = [pltpu.make_async_copy(own(p), spots[p], takes.at[p]) for p in range(count)]
    for copy in fetched:
        copy.start()

    gain = ngain_ref[...]

    def normalize(hid, cot, normed, *sorted_refs):
        value = hid[...].astype(F32)
        inv = lax.rsqrt(jnp.mean(value * value, -1, keepdims=True) + EPS)
        normed[...] = (value * inv * gain).astype(BF16)
        if turned:
            for src, away, here in (
                (normed, sorted_refs[0], sorted_refs[1]), (cot, sorted_refs[2], sorted_refs[3]),
            ):
                for j in range(lines):
                    first = lax.rem(line + j, lines) * 2
                    lanes = slice(j * depth, (j + 1) * depth)
                    away[:, lanes] = src[:, lanes_of(first + 1 - side)]
                    here[:, lanes] = src[:, lanes_of(first + side)]

    full = pl.BlockSpec((SPAN, model), lambda i: (i, 0))
    half = pl.BlockSpec((SPAN, lines * depth), lambda i: (i, 0))
    pltpu.emit_pipeline(
        normalize, grid=(hid_ref.shape[0] // SPAN,), in_specs=[full, full],
        out_specs=[full] + [half] * len(outs),
    )(hid_ref, cot_ref, normed_ref, *outs)

    stored = [pltpu.make_async_copy(spots[p], block(p, drank), puts.at[p]) for p in range(count)]
    for p in range(count):
        fetched[p].wait()
        stored[p].start()

    def source_line(step):
        return lax.rem(line - step + lines, lines) * 2

    def x_arrived(p):
        for step in range(lines):
            source = source_line(step) + 1 - side
            x_copy(p, step, block(p, source), source).wait_recv()

    def quarter_copy(k, device):
        rows = win_ref.at[pl.ds(2 * inner + own_quarter, quarter)]
        return pltpu.make_async_remote_copy(
            src_ref=rows, dst_ref=rows, send_sem=qsend.at[k], recv_sem=qrecv.at[k],
            device_id=device, device_id_type=MESH_IDS,
        )

    def quarter_from(k, owner):
        rows = win_ref.at[pl.ds(pl.multiple_of(2 * inner + owner * quarter, quarter), quarter)]
        return pltpu.make_async_remote_copy(
            src_ref=rows, dst_ref=rows, send_sem=qsend.at[k], recv_sem=qrecv.at[k],
            device_id=family[k], device_id_type=MESH_IDS,
        )

    for p in range(count):
        for step in range(1, lines):
            source = source_line(step) + side
            got = block(p, source)
            z_copy(p, step, got, source).wait_recv()
            x_copy(p, step, got, source).start()
        if turned and p == 3:
            stored[0].wait()
            x_arrived(0)
            for k in range(3):
                quarter_copy(k, family[k]).start()
    for p in range(1 if turned else 0, count):
        x_arrived(p)
    if turned:
        owners = (trank + 1 - 2 * core, (trank + 2) % 4, (trank + 3 - 2 * core) % 4)
        for k in range(3):
            quarter_from(k, owners[k]).wait_recv()
            quarter_copy(k, family[k]).wait_send()
    for p in range(count):
        for step in range(1, lines):
            z_copy(p, step, own(p), drank).wait_send()
        for step in range(lines):
            x_copy(p, step, own(p), drank).wait_send()
        if not (turned and p == 0):
            stored[p].wait()


def gather_weights(
    hidden, cotangent, norm_gain, in_weight, own_step, out_weight, lines, inner_all, heads, turned
):
    tokens, model = hidden.shape
    depth, inner = out_weight.shape
    half = jax.ShapeDtypeStruct((tokens, lines * depth), BF16)
    anywhere = pl.BlockSpec(memory_space=pl.ANY)
    rows = 2 * inner + 2 * LANES + 2 * heads
    width = 2 * inner + 3 * LANES
    count = 6 + inner // LANES if turned else 5
    outs = (
        jax.ShapeDtypeStruct((rows, model) if turned else (model, width), BF16),
        jax.ShapeDtypeStruct((model, inner), BF16),
        jax.ShapeDtypeStruct((tokens, model), BF16),
    ) + (half,) * (4 if turned else 0)
    dma = pltpu.SemaphoreType.DMA
    held = (rows + depth * (inner // LANES), LANES) if turned else (depth, width + inner)
    fars = max(1, lines - 1)
    return pl.pallas_call(
        lambda *refs: gather_kernel((lines, depth, inner, inner_all, heads, turned), *refs),
        out_shape=outs,
        in_specs=[anywhere, anywhere, pl.BlockSpec(memory_space=pltpu.VMEM)] + [anywhere] * 3,
        out_specs=(anywhere,) * len(outs),
        scratch_shapes=[
            pltpu.VMEM(held, BF16),
            dma((count, fars)), dma((count, fars)), dma((count, lines)), dma((count, lines)),
            dma((count,)), dma((count,)), dma((3,)), dma((3,)),
        ],
        compiler_params=pltpu.CompilerParams(collective_id=0, has_side_effects=True),
        cost_estimate=cost(45.0),
        name="gather_weights",
    )(hidden, cotangent, norm_gain, in_weight, own_step, out_weight)


def body(
    hidden_in, doc_ids, cotangent, norm_gain, in_weight, conv_weight, conv_bias,
    dt_bias, log_decay, skip_gain, gate_gain, out_weight,
):
    tcount, dcount = lax.axis_size("tensor"), lax.axis_size("dp")
    trank, drank = lax.axis_index("tensor"), lax.axis_index("dp")
    lines = dcount // 2
    line, side = drank // 2, drank % 2
    inner_all, head_all = gate_gain.shape[0], dt_bias.shape[0]
    inner, heads = inner_all // tcount, head_all // tcount
    tokens, model = hidden_in.shape
    base_bc = 2 * inner_all
    base_dt = base_bc + 2 * LANES
    depth = in_weight.shape[0]

    def line_to(step):
        return lambda k: ((k // 2 + step) % lines) * 2 + k % 2

    turned = depth % LANES == 0
    if turned:
        weight_in = own_step = in_weight.T
    else:
        weight_in = in_weight
        own_step = jnp.pad(
            lax.dynamic_slice_in_dim(in_weight, base_dt + trank * heads, heads, 1),
            ((0, 0), (0, LANES - heads)),
        )
    w_in, w_out, normed, *sorted_parts = gather_weights(
        hidden_in, cotangent, norm_gain.reshape(1, -1), weight_in, own_step,
        out_weight, lines, inner_all, heads, turned,
    )
    if not turned:
        pair = lax.dynamic_update_slice_in_dim(
            jnp.zeros((2 * heads, model), BF16),
            w_in[:, 2 * inner + 2 * LANES :][:, :heads].T, trank % 2 * heads, 0,
        )
        w_in = jnp.concatenate([w_in[:, : 2 * inner + 2 * LANES].T, pair], 0)
    if not sorted_parts:

        def features(v, which):
            return jnp.concatenate(
                [
                    lax.dynamic_slice_in_dim(v, (((line + j) % lines) * 2 + which) * depth, depth, 1)
                    for j in range(lines)
                ],
                1,
            )

        sorted_parts = [features(v, which) for v in (normed, cotangent) for which in (1 - side, side)]
    n_away, n_here, c_away, c_here = sorted_parts

    def row(v):
        return v.reshape(1, -1)

    params = (conv_weight, conv_bias.reshape(-1, LANES), row(dt_bias), row(log_decay), row(skip_gain))

    early = 4
    *held, sums, mine, far = mixer_forward(
        doc_ids, normed, cotangent, w_in, w_out, params, row(gate_gain), heads, early
    )
    delta, layer_out, grad_in, g_out, flat = mixer_backward(
        doc_ids, hidden_in, held, sums, params, row(gate_gain), row(norm_gain), sorted_parts, w_in,
        mine, far, heads, lines, depth, early,
    )
    layer_out, grad_input, g_norm, grad_in_weight, taps, bias, dt, decay, skip, gain = finish(
        cotangent, delta, layer_out, grad_in, flat, in_weight.shape[1], inner_all, head_all, turned
    )
    return (
        layer_out, grad_input, g_norm.reshape(-1), grad_in_weight.T if turned else grad_in_weight, taps, bias.reshape(-1),
        dt.reshape(-1), decay.reshape(-1), skip.reshape(-1), gain.reshape(-1), g_out,
    )


def solution(mesh):
    rows, whole = P("dp", None), P()
    return jax.shard_map(
        body,
        mesh=mesh,
        in_specs=(rows, rows, rows, whole, rows, whole, whole, whole, whole, whole, whole, P("dp", "tensor")),
        out_specs=(rows, rows, whole, rows, whole, whole, whole, whole, whole, whole, P("dp", "tensor")),
        check_vma=False,
    )
```

```python
import jax
import jax.numpy as jnp
from jax import lax
from jax.experimental import pallas as pl
from jax.experimental.pallas import tpu as pltpu
from jax.sharding import PartitionSpec as P

SPAN = 256
LANES = 128
EPS = 1e-05
FAR = -1e30
LOG2_E = 1.4426950408889634
VMEM_MOST = 60 * 2**20
F32 = jnp.float32
BF16 = jnp.bfloat16


def cost(micros):
    return pl.CostEstimate(flops=int(micros * 1.15e9), bytes_accessed=1 << 20, transcendentals=0)


def nn(a, b):
    return lax.dot_general(a, b, (((1,), (0,)), ((), ())), preferred_element_type=F32)


def nt(a, b):
    return lax.dot_general(a, b, (((1,), (1,)), ((), ())), preferred_element_type=F32)


def tn(a, b):
    return lax.dot_general(a, b, (((0,), (0,)), ((), ())), preferred_element_type=F32)


def iota(shape, dim):
    return lax.broadcasted_iota(jnp.int32, shape, dim)


def as_column(row, rows=SPAN):
    return jnp.transpose(jnp.broadcast_to(row, (LANES, rows)))


def as_row(block):
    ones = jnp.ones((16, LANES), BF16)
    hi = block.astype(BF16)
    low = (block - hi.astype(F32)).astype(BF16)
    return (nt(ones, hi) + nt(ones, low))[0:1]


def sigmoid(v):
    return 0.5 * jnp.tanh(0.5 * v) + 0.5


def row_sum(v, tri):
    hi = v.astype(BF16).astype(F32)
    rest = v - hi
    mid = rest.astype(BF16).astype(F32)
    count = v.shape[0]
    out = nn(jnp.concatenate([hi, mid, rest - mid], 0).astype(BF16), tri)
    return out[0:count] + out[count : 2 * count] + out[2 * count :]


def pair_lanes(cols, first, low_half):
    rows = cols.shape[0]
    left = jnp.broadcast_to(cols[:, first : first + 1], (rows, LANES))
    right = jnp.broadcast_to(cols[:, first + 1 : first + 2], (rows, LANES))
    return jnp.where(low_half, left, right)


def exact_nt(a, b):
    a_hi, b_hi = a.astype(BF16), b.astype(BF16)
    a_lo = (a - a_hi.astype(F32)).astype(BF16)
    b_lo = (b - b_hi.astype(F32)).astype(BF16)
    return nt(a_hi, b_hi) + (nt(a_hi, b_lo) + nt(a_lo, b_hi))


def softplus(v):
    return jnp.maximum(v, 0.0) + jnp.log1p(jnp.exp(-jnp.abs(v)))


def own_lanes(row, rank, heads):
    total = row.shape[1]
    pick = (iota((total, LANES), 0) == rank * heads + iota((total, LANES), 1)) & (
        iota((total, LANES), 1) < heads
    )
    wide = jnp.broadcast_to(row, (8, total))
    out = lax.dot_general(
        wide, pick.astype(F32), (((1,), (0,)), ((), ())),
        precision=lax.Precision.HIGHEST, preferred_element_type=F32,
    )
    return out[0:1]


def own_rows_of(row, rank, heads):
    total = row.shape[1]
    place = iota((heads, total), 1) == rank * heads + iota((heads, total), 0)
    picked = jnp.where(place, jnp.broadcast_to(row, (heads, total)), 0.0)
    return jnp.broadcast_to(jnp.sum(picked, axis=1, keepdims=True), (heads, SPAN))


def head_scales(raw, rate, doc, enter, extra):
    step = softplus(raw)
    log_step = step * rate
    row_i, col_i = iota((SPAN, SPAN), 0), iota((SPAN, SPAN), 1)
    running = row_sum(log_step, (row_i <= col_i).astype(BF16))
    ending = jnp.broadcast_to(running[:, SPAN - 1 :], running.shape)
    last = jnp.broadcast_to(doc[:, SPAN - 1 :], doc.shape)
    tail = jnp.where(doc == last, jnp.exp(ending - running), 0.0)
    reach = jnp.where(doc == enter, jnp.exp(running), 0.0)
    scaled = running * LOG2_E
    rows = [scaled, step, tail, reach, doc] + extra
    used = sum(v.shape[0] for v in rows)
    packed = jnp.concatenate(rows + [jnp.zeros((LANES - used, SPAN), F32)], 0)
    return log_step, scaled, jnp.transpose(packed)


def fold(v):
    return jnp.sum(v.reshape(SPAN // 8, 8, v.shape[1]), axis=0)


def own_params(rank, heads, inner, inner_all, dtb_ref, dec_ref, skip_ref, cw_ref, cb_ref, par, skips, cwb):
    chan = inner + 2 * LANES
    off = pl.multiple_of(rank * inner, LANES)
    taps = cw_ref.shape[0]
    par[0] = own_rows_of(dtb_ref[...], rank, heads)
    par[1] = -jnp.exp(own_rows_of(dec_ref[...], rank, heads))
    skips[0:1] = own_lanes(skip_ref[...], rank, heads)
    cwb[0:taps, 0:inner] = cw_ref[:, pl.ds(off, inner)].astype(F32)
    cwb[0:taps, inner:chan] = cw_ref[:, inner_all:].astype(F32)
    for k in range(chan // LANES):
        row = rank * (inner // LANES) + k if k < inner // LANES else (inner_all - inner) // LANES + k
        cwb[taps : taps + 1, k * LANES : (k + 1) * LANES] = cb_ref[pl.ds(row, 1), :]


MESH_IDS = pl.DeviceIdType.MESH


def forward_kernel(
    dims, docs_ref, normed_ref, cot_low_ref, cot_high_ref, win_ref, wo_ref, cw_ref, cb_ref,
    dtb_ref, dec_ref, skip_ref, ggain_ref,
    gate_ref, mixed_ref, pre_ref, ssd_ref, stp_ref, state_ref,
    sums_ref, mine_ref, far_ref, wfull_ref,
    xbuf, dbuf, state, par, skips, cwb, gain, gg_all,
    own_sums, h_out, h_in, kept, mine, far, h_sem, y_sem, s_in, s_sem, put_sem,
    wout, oz_sem, ox_sem, own_sem,
):
    inner, heads, lines, depth, turned = dims
    pairs = heads // 2
    chan = inner + 2 * LANES
    i = pl.program_id(0)
    spans = gg_all.shape[0] // SPAN
    mid = spans // 2
    rank = lax.axis_index("tensor")
    core = rank % 2
    inner_all = ggain_ref.shape[1]
    half = SPAN // 2
    across = {"tensor": rank + 1 - 2 * core}
    beyond = {"tensor": (rank + 2) % 4}
    crossed = {"tensor": (rank + 3 - 2 * core) % 4}
    drank = lax.axis_index("dp")
    line, side = drank // 2, drank % 2
    partner = {"dp": line * 2 + 1 - side}
    portions = 2 if turned else 0
    cut = inner // 2

    def peer(step):
        return {"dp": lax.rem(line + step, lines) * 2 + side}

    def o_block(p, index):
        return wout.at[pl.ds(pl.multiple_of(index * depth, depth), depth), pl.ds(p * cut, cut)]

    def own_block(p):
        return wo_ref.at[:, pl.ds(p * cut, cut)]

    def oz_copy(p, step, src, index):
        return pltpu.make_async_remote_copy(
            src_ref=src, dst_ref=o_block(p, index), send_sem=oz_sem.at[0, p, step - 1],
            recv_sem=oz_sem.at[1, p, step - 1], device_id=peer(step), device_id_type=MESH_IDS,
        )

    def ox_copy(p, step, src, index):
        return pltpu.make_async_remote_copy(
            src_ref=src, dst_ref=o_block(p, index), send_sem=ox_sem.at[0, p, step],
            recv_sem=ox_sem.at[1, p, step], device_id=partner, device_id_type=MESH_IDS,
        )

    def source(step):
        return lax.rem(line - step + lines, lines) * 2

    if turned:
        own_copies = [
            pltpu.make_async_copy(own_block(p), o_block(p, drank), own_sem.at[p]) for p in range(portions)
        ]
    else:
        own_copies = [pltpu.make_async_copy(wo_ref, wout, own_sem.at[0])]

    @pl.when(i == 0)
    def _():
        others = [across, beyond, crossed]
        if turned:
            others += [partner] + [peer(step) for step in range(1, lines)]
        barrier = pltpu.get_barrier_semaphore()
        for device in others:
            pl.semaphore_signal(barrier, inc=1, device_id=device, device_id_type=MESH_IDS)
        pl.semaphore_wait(barrier, len(others))
        for p in range(portions):
            for step in range(1, lines):
                oz_copy(p, step, own_block(p), drank).start()
            ox_copy(p, 0, own_block(p), drank).start()
        for copy in own_copies:
            copy.start()
        xbuf[0:8] = jnp.zeros((8, chan), F32)
        dbuf[0:8] = jnp.full((8, LANES), -1.0, F32)
        state[...] = jnp.zeros(state.shape, F32)
        own_params(rank, heads, inner, inner_all, dtb_ref, dec_ref, skip_ref, cw_ref, cb_ref, par, skips, cwb)
        gain[0:1] = ggain_ref[:, pl.ds(pl.multiple_of(rank * inner, LANES), inner)]

    def slot(k):
        return pl.ds(pl.multiple_of(k * half, half), half)

    def h_copy(k):
        return pltpu.make_async_remote_copy(
            src_ref=h_out.at[slot(k)], dst_ref=h_in.at[slot(k)], send_sem=h_sem.at[0, k],
            recv_sem=h_sem.at[1, k], device_id=across, device_id_type=MESH_IDS,
        )

    def y_copy(k):
        return pltpu.make_async_remote_copy(
            src_ref=mine.at[slot(k)], dst_ref=far.at[slot(k // mid)], send_sem=y_sem.at[0, k // mid],
            recv_sem=y_sem.at[1, k // mid], device_id=beyond, device_id_type=MESH_IDS,
        )

    full_copy = pltpu.make_async_copy(wout, wfull_ref, put_sem.at[2])

    def join(k):
        h_copy(k).wait_recv()
        mine[slot(k)] = (kept[k // mid, slot(core)] + h_in[slot(k)].astype(F32)).astype(BF16)

    nb = normed_ref[...]
    xbuf[8 : 8 + SPAN] = nt(nb, win_ref[inner : inner + chan])
    gate_ref[...] = nt(nb, win_ref[0:inner])
    both_cores = nt(win_ref[inner + chan : inner + chan + 2 * heads], nb)
    stp = jnp.where(core == 0, both_cores[0:heads], both_cores[heads:])
    stp_ref[...] = stp
    mixed_ref[...] = xbuf[8 : 8 + SPAN]

    drow = docs_ref[:, pl.ds(pl.multiple_of(i * SPAN, SPAN), SPAN)].astype(F32)
    doc = jnp.broadcast_to(drow, (heads, SPAN))
    enter = jnp.broadcast_to(dbuf[7:8, 0:1], (heads, SPAN))
    _, run_rows, cols = head_scales(stp + par[0], par[1], doc, enter, [])
    dcol = jnp.broadcast_to(cols[:, 4 * heads : 4 * heads + 1], (SPAN, LANES))
    dbuf[8 : 8 + SPAN] = dcol
    keeps = [None] + [dbuf[8 - k : 8 - k + SPAN] == dcol for k in range(1, 4)]

    def conv(group):
        lanes = slice(group * LANES, (group + 1) * LANES)
        acc = cwb[4:5, lanes] + cwb[3:4, lanes] * xbuf[8 : 8 + SPAN, lanes]
        for k in range(1, 4):
            acc = acc + cwb[3 - k : 4 - k, lanes] * jnp.where(
                keeps[k], xbuf[8 - k : 8 - k + SPAN, lanes], 0.0
            )
        pre_ref[:, lanes] = acc
        return acc * sigmoid(acc)

    b_act, c_act = conv(pairs), conv(pairs + 1)
    b_rows, c_rows = b_act.astype(BF16), c_act.astype(BF16)

    row_i, col_i = iota((SPAN, SPAN), 0), iota((SPAN, SPAN), 1)
    same = jnp.concatenate([dcol, dcol], 1) == drow
    bias = jnp.where(same & (row_i >= col_i), 0.0, FAR)
    scores = exact_nt(c_act, b_act)
    b_turned = jnp.transpose(b_act).astype(BF16)
    low_half = iota((SPAN, LANES), 1) < LANES // 2
    square = jnp.zeros((SPAN, LANES), F32)
    for pair in range(pairs):
        lanes = slice(pair * LANES, (pair + 1) * LANES)
        act = conv(pair)
        scaled = act * pair_lanes(cols, heads + 2 * pair, low_half)
        xb = scaled.astype(BF16)
        tail_l = pair_lanes(cols, 2 * heads + 2 * pair, low_half)
        reach_l = pair_lanes(cols, 3 * heads + 2 * pair, low_half)
        held = state[:, lanes]
        held_b = held.astype(BF16)
        state_ref[0, :, lanes] = held_b
        state[:, lanes] = nn(b_turned, (scaled * tail_l).astype(BF16)) + reach_l[SPAN - 1 : SPAN] * held
        out = reach_l * nn(c_rows, held_b)
        parts = []
        for sub in range(2):
            head = 2 * pair + sub
            blocks = []
            for blk in range(2):
                rows = slice(blk * half, (blk + 1) * half)
                width = (blk + 1) * half
                gap = cols[rows, head : head + 1] - run_rows[head : head + 1, 0:width]
                weight = jnp.exp2(gap + bias[rows, 0:width]) * scores[rows, 0:width]
                blocks.append(nn(weight.astype(BF16), xb[0:width]))
            parts.append(jnp.concatenate(blocks, 0))
        out = out + jnp.where(low_half, parts[0], parts[1])
        skip_l = pair_lanes(skips[0:1], 2 * pair, low_half[0:1])
        ssd = out + skip_l * act
        ssd_ref[:, lanes] = ssd
        gate = gate_ref[:, lanes]
        gated = ssd * (gate * sigmoid(gate))
        square = square + gated * gated
        gained = gain[0:1, lanes] * gated
        gg_all[pl.ds(pl.multiple_of(i * SPAN, SPAN), SPAN), lanes] = gained.astype(BF16)
    own_sums[0, pl.ds(i, 1), :] = as_row(square)
    xbuf[0:8] = xbuf[SPAN : SPAN + 8]
    dbuf[0:8] = dbuf[SPAN : SPAN + 8]

    for p in range(portions):
        @pl.when(i == p + 1)
        def _():
            for step in range(1, lines):
                got = o_block(p, source(step) + side)
                oz_copy(p, step, got, source(step) + side).wait_recv()
                ox_copy(p, step, got, source(step) + side).start()

    @pl.when(i == mid)
    def _():
        for copy in own_copies:
            copy.wait()
        for p in range(portions):
            for step in range(lines):
                index = source(step) + 1 - side
                ox_copy(p, step, o_block(p, index), index).wait_recv()
        full_copy.start()

    @pl.when(i > mid)
    def _():
        join(i - 1 - mid)
        join(i - 1)

    @pl.when(i == mid + 1)
    def _():
        y_copy(0).start()
        y_copy(mid).start()

    @pl.when(i >= mid)
    def _():
        for which, (k, cot_ref) in enumerate(((i - mid, cot_low_ref), (i, cot_high_ref))):
            rows = gg_all[pl.ds(pl.multiple_of(k * SPAN, SPAN), SPAN)]
            kept[which] = nt(rows, wout[...])
            cross = jnp.zeros((SPAN, LANES), F32)
            for group in range(wout.shape[0] // LANES):
                lanes = slice(group * LANES, (group + 1) * LANES)
                cross = cross + kept[which, :, lanes] * cot_ref[:, lanes].astype(F32)
            own_sums[1, pl.ds(k, 1), :] = as_row(cross)
            h_out[slot(k)] = kept[which, slot(1 - core)].astype(BF16)
            h_copy(k).start()

    @pl.when(i == spans - 1)
    def _():
        def s_copy(k, device):
            return pltpu.make_async_remote_copy(
                src_ref=own_sums, dst_ref=s_in.at[k], send_sem=s_sem.at[0, k],
                recv_sem=s_sem.at[1, k], device_id=device, device_id_type=MESH_IDS,
            )

        sent = [s_copy(0, across), s_copy(1, beyond), s_copy(2, crossed)]
        for copy in sent:
            copy.start()
        join(i - mid)
        join(i)
        mine_put = pltpu.make_async_copy(mine, mine_ref, put_sem.at[0])
        mine_put.start()
        for copy in sent:
            copy.wait_recv()
        near = own_sums[...] + s_in[0]
        sums_ref[...] = near + (s_in[1] + s_in[2])
        for k in (0, mid):
            y_copy(k).wait_recv()
        far_put = pltpu.make_async_copy(far, far_ref, put_sem.at[1])
        far_put.start()
        for copy in sent:
            copy.wait_send()

        def drain(k, carry):
            h_copy(k).wait_send()
            return carry

        lax.fori_loop(0, spans, drain, 0)
        for k in (0, mid):
            y_copy(k).wait_send()
        for p in range(portions):
            for step in range(1, lines):
                oz_copy(p, step, own_block(p), drank).wait_send()
            for step in range(lines):
                ox_copy(p, step, own_block(p), drank).wait_send()
        mine_put.wait()
        far_put.wait()
        full_copy.wait()


def mixer_forward(docs, normed, cotangent, w_in, w_out, params, ggain, heads, lines, turned):
    tokens, model = normed.shape
    depth, inner = w_out.shape
    half = tokens // 2
    mid = tokens // SPAN // 2
    chan = inner + 2 * LANES
    spans = tokens // SPAN

    def tok(width):
        return pl.BlockSpec((SPAN, width), lambda i: (i, 0))

    def late(width, base):
        return pl.BlockSpec((SPAN, width), lambda i: (base + (i - mid) * (i // mid), 0))

    def full(shape):
        return pl.BlockSpec(shape, lambda i: (0,) * len(shape))

    anywhere = pl.BlockSpec(memory_space=pl.ANY)
    sums = (2, spans, SPAN)
    outs = (
        jax.ShapeDtypeStruct((tokens, inner), F32),
        jax.ShapeDtypeStruct((tokens, chan), F32),
        jax.ShapeDtypeStruct((tokens, chan), F32),
        jax.ShapeDtypeStruct((tokens, inner), F32),
        jax.ShapeDtypeStruct((heads, tokens), F32),
        jax.ShapeDtypeStruct((spans, LANES, inner), BF16),
        jax.ShapeDtypeStruct(sums, F32),
        jax.ShapeDtypeStruct((tokens // 2, model), BF16),
        jax.ShapeDtypeStruct((SPAN, model), BF16),
        jax.ShapeDtypeStruct((model, inner), BF16),
    )
    out_specs = (
        tok(inner), tok(chan), tok(chan), tok(inner), pl.BlockSpec((heads, SPAN), lambda i: (0, i)),
        pl.BlockSpec((1, LANES, inner), lambda i: (i, 0, 0)),
        full(sums), anywhere, anywhere, anywhere,
    )
    consts = params + (ggain,)
    dma, vmem = pltpu.SemaphoreType.DMA, pltpu.VMEM
    return pl.pallas_call(
        lambda *refs: forward_kernel((inner, heads, lines, depth, turned), *refs),
        out_shape=outs,
        grid=(spans,),
        in_specs=[
            full(docs.shape), tok(model), late(model, 0), late(model, mid), full(w_in.shape), anywhere,
        ]
        + [full(v.shape) for v in consts],
        out_specs=out_specs,
        scratch_shapes=[
            vmem((SPAN + 8, chan), F32), vmem((SPAN + 8, LANES), F32), vmem((LANES, inner), F32),
            vmem((2, heads, SPAN), F32), vmem((8, LANES), F32), vmem((8, chan), F32), vmem((8, inner), F32),
            vmem((tokens, inner), BF16), vmem(sums, F32),
            vmem((tokens // 2, model), BF16), vmem((tokens // 2, model), BF16),
            vmem((2, SPAN, model), F32), vmem((tokens // 2, model), BF16),
            vmem((SPAN, model), BF16),
            dma((2, spans)), dma((2, 2)), vmem((3,) + sums, F32), dma((2, 3)), dma((3,)),
            vmem((model, inner), BF16), dma((2, 2, max(1, lines - 1))), dma((2, 2, lines)), dma((2,)),
        ],
        compiler_params=pltpu.CompilerParams(
            dimension_semantics=("arbitrary",), vmem_limit_bytes=VMEM_MOST,
            collective_id=2, has_side_effects=True,
        ),
        cost_estimate=cost(40.0),
        name="mixer_forward",
    )(docs, normed, cotangent, cotangent, w_in, w_out, *consts)


def backward_kernel(
    dims,
    docs_ref, hid_ref, gate_ref, cot_ref, gate_low_ref, ssd_low_ref, cot_low_ref,
    ssd_ref, mixed_ref, pre_ref, stp_ref, state_ref, sums_ref,
    cw_ref, cb_ref, dtb_ref, dec_ref, skip_ref, ggain_ref, ngain_ref,
    naway_ref, nhere_ref, caway_ref, chere_ref, w_ref, mine_ref, far_ref, wout_ref,
    delta_ref, layer_ref, gin_ref, gout_ref, flatout_ref,
    naway, nhere, caway, chere, w, wout, loads,
    pbuf, dbuf, dstate, par, skips, cwb, gain, w_step, sumv,
    gconv, gskip, ghead, ggain, gnorm,
    nout_all, dgate_all, dall, dssd_low, inv_own, hid_own,
    h_out, mine, y_in, kept, h_sem, y_sem, d_sem, d_put,
    omine, ofar, oy_sem, o_sem, o_put,
    ax_out, ax_in, ax_sem, az_in, az_sem, atotal,
    sx_out, sx_in, sx_sem, sz_in, sz_sem, stotal, shere,
    vx_out, vx_in, vx_sem, vz_in, vz_sem, vtotal, vhere, vbuf,
    gates, g_sem, values, v_sem, shared, shared_low, s_sem, put_sem, flat, flat_in, f_sem,
):
    inner, heads, inner_all, lines, depth = dims
    pairs = heads // 2
    chan = inner + 2 * LANES
    width = inner + chan + LANES
    i = pl.program_id(0)
    spans = pl.num_programs(0)
    tokens = nout_all.shape[0]
    count = tokens // SPAN
    mid = count // 2
    c = count - 1 - i
    half = SPAN // 2
    model = w.shape[1]
    blocks = lines * depth // LANES
    rank, drank = lax.axis_index("tensor"), lax.axis_index("dp")
    line, side = drank // 2, drank % 2
    core = rank % 2
    off = pl.multiple_of(rank * inner, LANES)
    across = {"tensor": rank + 1 - 2 * core}
    beyond = {"tensor": (rank + 2) % 4}
    partner = {"dp": line * 2 + 1 - side}

    def peer(step):
        return {"dp": lax.rem(line + step, lines) * 2 + side}

    def remote(src, dst, sems, index, device):
        return pltpu.make_async_remote_copy(
            src_ref=src, dst_ref=dst, send_sem=sems.at[0, index], recv_sem=sems.at[1, index],
            device_id=device, device_id_type=MESH_IDS,
        )

    def lot(k, size):
        return pl.ds(pl.multiple_of(k * size, size), size)

    fetch = [
        pltpu.make_async_copy(src, dst, loads.at[k])
        for k, (src, dst) in enumerate(
            (
                (mine_ref, omine), (w_ref, w), (far_ref.at[pl.ds(0, half)], ofar.at[pl.ds(0, half)]),
                (far_ref.at[pl.ds(half, half)], ofar.at[pl.ds(mid * half, half)]),
                (caway_ref, caway), (naway_ref, naway), (chere_ref, chere), (nhere_ref, nhere),
                (wout_ref, wout),
            )
        )
    ]

    def oy_copy(k):
        return remote(omine.at[lot(k, half)], ofar.at[lot(k, half)], oy_sem, k, beyond)

    def my_rows(k):
        return pl.ds(pl.multiple_of(k * SPAN + core * half, half), half)

    def o_copy(k):
        return remote(omine.at[lot(k, half)], layer_ref.at[my_rows(k)], o_sem, k, across)

    def o_local(k):
        return pltpu.make_async_copy(omine.at[lot(k, half)], layer_ref.at[my_rows(k)], o_put.at[k])

    def d_copy(k):
        return remote(mine.at[lot(k, half)], delta_ref.at[my_rows(k)], d_sem, k, across)

    def d_local(k):
        return pltpu.make_async_copy(mine.at[lot(k, half)], delta_ref.at[my_rows(k)], d_put.at[k])

    def h_copy(k):
        return remote(h_out.at[lot(k % 2, half)], mine.at[lot(k, half)], h_sem, k, across)

    def y_copy(k):
        return remote(mine.at[lot(k, half)], y_in.at[lot(k, half)], y_sem, k, beyond)

    def ax_copy(k):
        return remote(ax_out.at[lot(k, LANES)], ax_in.at[lot(k, LANES)], ax_sem, k, partner)

    def sx_copy(k):
        return remote(sx_out.at[lot(k, LANES)], sx_in.at[lot(k, LANES)], sx_sem, k, partner)

    def vx_copy(k):
        return remote(vx_out.at[lot(k, LANES)], vx_in.at[lot(k, LANES)], vx_sem, k, partner)

    def az_copy(step):
        return remote(ax_out.at[pl.ds(step * depth, depth)], az_in.at[step - 1], az_sem, step - 1, peer(step))

    def sz_copy(step):
        return remote(sx_out.at[pl.ds(step * depth, depth)], sz_in.at[step - 1], sz_sem, step - 1, peer(step))

    def vz_copy(step):
        return remote(vx_out.at[pl.ds(step * depth, depth)], vz_in.at[step - 1], vz_sem, step - 1, peer(step))

    @pl.when(i == 0)
    def _():
        for copy in [fetch[-1]] + fetch[:-1]:
            copy.start()
        barrier = pltpu.get_barrier_semaphore()
        for device in [across, beyond, partner] + [peer(step) for step in range(1, lines)]:
            pl.semaphore_signal(barrier, inc=1, device_id=device, device_id_type=MESH_IDS)
        pl.semaphore_wait(barrier, lines + 2)
        fetch[-1].wait()
        pbuf[SPAN : SPAN + 8] = jnp.zeros((8, chan), F32)
        dbuf[SPAN : SPAN + 8] = jnp.full((8, LANES), -2.0, F32)
        dstate[...] = jnp.zeros(dstate.shape, F32)
        own_params(rank, heads, inner, inner_all, dtb_ref, dec_ref, skip_ref, cw_ref, cb_ref, par, skips, cwb)
        gain[0:1] = ggain_ref[:, pl.ds(off, inner)]
        for acc in (gconv, gskip, ghead, ggain, gnorm):
            acc[...] = jnp.zeros(acc.shape, F32)
        fetch[0].wait()
        for k in range(1, mid):
            oy_copy(count - k).start()
            oy_copy(mid - k).start()

    def join(k):
        h_copy(k).wait()
        mine[lot(k, half)] = (kept[lot(core, half)] + mine[lot(k, half)].astype(F32)).astype(BF16)
        y_copy(k).start()

    def out_grads(n_side, c_side, k):
        cols = lot(k, LANES)
        return jnp.concatenate(
            [tn(c_side[:, cols], nout_all[...]), tn(n_side[:, cols], dgate_all[...])], 1
        )

    per = LANES // depth

    def to_lines(k, joined, x_copy_of, x_out, z_copy_of, total):
        x_copy_of(k).wait_send()
        x_out[lot(k, LANES)] = joined.astype(BF16)
        if isinstance(k, int):
            if k == 0:
                total[...] = joined[0:depth]
            for step in range(max(1, k * per), (k + 1) * per):
                z_copy_of(step).start()

    def a_block(k):
        ax_copy(k).wait_recv()
        joined = out_grads(nhere, chere, k) + ax_in[lot(k, LANES)].astype(F32)
        to_lines(k, joined, ax_copy, ax_out, az_copy, atotal)

    def s_block(k):
        sx_copy(k).wait_recv()
        joined = shere[lot(k, LANES)] + sx_in[lot(k, LANES)].astype(F32)
        to_lines(k, joined, sx_copy, sx_out, sz_copy, stotal)

    def v_block(k):
        vx_copy(k).wait_recv()
        joined = vhere[lot(k, LANES)] + vx_in[lot(k, LANES)].astype(F32)
        to_lines(k, joined, vx_copy, vx_out, vz_copy, vtotal)

    @pl.when(i == mid)
    def _():
        for copy in fetch[2:-1]:
            copy.wait()

    hid_own[lot(c, half)] = hid_ref[lot(core, half)]

    def inverse(k):
        inv = lax.rsqrt(sums_ref[0, pl.ds(k, 1), :] * (1.0 / inner_all) + EPS)
        pull = sums_ref[1, pl.ds(k, 1), :] * (inv * inv * inv) * (1.0 / inner_all)
        inv_own[pl.ds(k, 1), :] = jnp.where(core == 0, inv[:, 0:half], inv[:, half:])
        return inv, pull

    def spread_inverse(cols, first):
        inv = jnp.broadcast_to(cols[:, first : first + 1], (SPAN, LANES))
        return inv, jnp.broadcast_to(cols[:, first + 1 : first + 2], (SPAN, LANES))

    def gating(k, scales, lanes, gate_in, ssd_in, dn_in):
        inv, pull = scales
        gate = gate_in[:, lanes]
        sig = sigmoid(gate)
        silu = gate * sig
        ssd = ssd_in[:, lanes]
        gated = ssd * silu
        dn = dn_in
        g_l = gain[0:1, lanes]
        nout = gated * inv
        nout_all[lot(k, SPAN), lanes] = (nout * g_l).astype(BF16)
        ggain[:, lanes] += fold(dn * nout)
        d_gated = dn * g_l * inv - gated * pull
        dgate_all[lot(k, SPAN), lanes] = (d_gated * ssd * (sig * (1.0 + gate * (1.0 - sig)))).astype(BF16)
        return d_gated * silu

    def finish_out(k):
        total = omine[lot(k, half)].astype(F32) + ofar[lot(k, half)].astype(F32)
        inv = as_column(inv_own[pl.ds(k, 1), :], half)
        value = hid_own[lot(k, half)].astype(F32)
        for group in range(model // LANES):
            lanes = slice(group * LANES, (group + 1) * LANES)
            omine[lot(k, half), lanes] = (value[:, lanes] + total[:, lanes] * inv).astype(BF16)
        o_copy(k).start()
        o_local(k).start()

    def scan_step(first):
        drow = docs_ref[:, lot(c, SPAN)].astype(F32)
        before = docs_ref[:, lot(jnp.maximum(c - 1, 0), SPAN)].astype(F32)
        doc = jnp.broadcast_to(drow, (heads, SPAN))
        enter = jnp.broadcast_to(before[:, SPAN - 1 :], (heads, SPAN))
        enter = jnp.where(c == 0, -1.0, enter)
        extra = []
        if first:
            row = iota((8, SPAN), 0)
            block = jnp.zeros((8, SPAN), F32)
            for k, v in enumerate(inverse(c) + inverse(c - mid)):
                block = jnp.where(row == k, jnp.broadcast_to(v, (8, SPAN)), block)
            extra = [block]
        raw = stp_ref[...] + par[0]
        log_step, run_rows, cols = head_scales(raw, par[1], doc, enter, extra)
        dcol = jnp.broadcast_to(cols[:, 4 * heads : 4 * heads + 1], (SPAN, LANES))
        if first:
            scales = spread_inverse(cols, 5 * heads)
            low_scales = spread_inverse(cols, 5 * heads + 2)
        dbuf[0:SPAN] = dcol
        keeps = [None] + [dbuf[k : k + SPAN] == dcol for k in range(1, 4)]
        row_i, col_i = iota((SPAN, SPAN), 0), iota((SPAN, SPAN), 1)
        same = jnp.concatenate([dcol, dcol], 1) == drow
        bias = jnp.where(same & (row_i <= col_i), 0.0, FAR)

        def activate(group):
            lanes = slice(group * LANES, (group + 1) * LANES)
            pre = pre_ref[:, lanes]
            sig = sigmoid(pre)
            return pre * sig, sig * (1.0 + pre * (1.0 - sig))

        b_act, b_slope = activate(pairs)
        c_act, c_slope = activate(pairs + 1)
        b_rows, c_rows = b_act.astype(BF16), c_act.astype(BF16)
        c_turned = jnp.transpose(c_act).astype(BF16)
        scores = exact_nt(b_act, c_act)
        low_half = iota((SPAN, LANES), 1) < LANES // 2
        d_scores = [jnp.zeros((half, SPAN), F32), jnp.zeros((half, half), F32)]
        d_b = jnp.zeros((SPAN, LANES), F32)
        d_c = jnp.zeros((SPAN, LANES), F32)
        holds = []
        for pair in range(pairs):
            lanes = slice(pair * LANES, (pair + 1) * LANES)
            act, slope = activate(pair)
            step_l = pair_lanes(cols, heads + 2 * pair, low_half)
            tail_l = pair_lanes(cols, 2 * heads + 2 * pair, low_half)
            reach_l = pair_lanes(cols, 3 * heads + 2 * pair, low_half)
            skip_l = pair_lanes(skips[0:1], 2 * pair, low_half[0:1])
            ssd = ssd_ref[:, lanes]
            if first:
                if pair % 2 == 0:
                    both = slice(pair * LANES, (pair + 2) * LANES)
                    dn_both, dn_low_both = nn(cot_ref[...], wout[:, both]), nn(cot_low_ref[...], wout[:, both])
                side_lanes = slice(pair % 2 * LANES, (pair % 2 + 1) * LANES)
                d_ssd = gating(c, scales, lanes, gate_ref, ssd_ref, dn_both[:, side_lanes])
                dssd_low[lot(c - mid, SPAN), lanes] = gating(
                    c - mid, low_scales, lanes, gate_low_ref, ssd_low_ref, dn_low_both[:, side_lanes]
                )
            else:
                d_ssd = dssd_low[lot(c, SPAN), lanes]
            gskip[:, lanes] += fold(d_ssd * act)
            dyb = d_ssd.astype(BF16)
            scaled = act * step_l
            xb = scaled.astype(BF16)
            held = state_ref[0, :, lanes]
            d_held = dstate[:, lanes]
            d_held_b = d_held.astype(BF16)
            ry = (d_ssd * reach_l).astype(BF16)
            xt = (scaled * tail_l).astype(BF16)
            parts = []
            for sub in range(2):
                head = 2 * pair + sub
                x_own = jnp.where(low_half if sub == 0 else ~low_half, scaled, 0.0).astype(BF16)
                tiles = []
                for blk in range(2):
                    rows = slice(blk * half, (blk + 1) * half)
                    span = slice(blk * half, SPAN)
                    gap = run_rows[head : head + 1, span] - cols[rows, head : head + 1]
                    decay = jnp.exp2(gap + bias[rows, span])
                    tiles.append(nn((decay * scores[rows, span]).astype(BF16), dyb[span]))
                    d_scores[blk] = d_scores[blk] + decay * nt(x_own[rows], dyb[span])
                parts.append(jnp.concatenate(tiles, 0))
            d_within = jnp.where(low_half, parts[0], parts[1])
            from_state = tail_l * nn(b_rows, d_held_b)
            d_scaled = d_within + from_state
            xf = xb.astype(F32)
            up = dyb.astype(F32) * (ssd - skip_l * act) - xf * d_within
            up_hi = up.astype(BF16)
            sumv[0, :, lanes] = up_hi
            sumv[1, :, lanes] = (up - up_hi.astype(F32)).astype(BF16)
            sumv[2, :, lanes] = (xf * from_state).astype(BF16)
            sumv[3, :, lanes] = (d_scaled * act).astype(BF16)
            hold = reach_l[SPAN - 1 : SPAN]
            held_sum = jnp.sum((d_held * held.astype(F32)).reshape(LANES // 8, 8, LANES), axis=0)
            holds.append(jnp.sum(held_sum, axis=0, keepdims=True) * hold)
            d_b += nt(xt, d_held_b)
            d_c += nt(ry, held)
            dstate[:, lanes] = hold * d_held + nn(c_turned, ry)
            pbuf[0:SPAN, lanes] = (skip_l * d_ssd + step_l * d_scaled) * slope

        ds_b = jnp.concatenate(
            [
                d_scores[0],
                jnp.concatenate([jnp.zeros((half, half), F32), d_scores[1]], 1),
            ],
            0,
        )
        d_b += nn(ds_b.astype(BF16), c_rows)
        d_c += nn(jnp.transpose(ds_b).astype(BF16), b_rows)
        pbuf[0:SPAN, inner : inner + LANES] = d_b * b_slope
        pbuf[0:SPAN, inner + LANES : chan] = d_c * c_slope

        per_head = inner // heads
        owner = (iota((2 * heads, inner), 0) == iota((2 * heads, inner), 1) // per_head).astype(BF16)
        up = (nt(owner, sumv[0]) + nt(owner, sumv[1]))[0:heads]
        down = nt(owner, sumv[2])[0:heads]
        direct = nt(owner, sumv[3])[0:heads]
        hold_row = jnp.broadcast_to(jnp.concatenate(holds, 1), (heads, inner))
        inside = iota((heads, inner), 0) == iota((heads, inner), 1) // per_head
        hold_sum = jnp.sum(jnp.where(inside, hold_row, 0.0), axis=1, keepdims=True)
        d_log = (
            row_sum(up, (row_i >= col_i).astype(BF16))
            + row_sum(down, (row_i < col_i).astype(BF16))
            + jnp.broadcast_to(hold_sum, (heads, SPAN))
        )
        d_raw = (d_log * par[1] + direct) * sigmoid(raw)
        turned = jnp.transpose(jnp.concatenate([d_raw, jnp.zeros((LANES - heads, SPAN), F32)], 0))
        dall[lot(c, SPAN), chan:] = turned.astype(BF16)
        ghead[0] += d_raw
        ghead[1] += d_log * log_step

        for group in range(chan // LANES):
            lanes = slice(group * LANES, (group + 1) * LANES)
            mixed = mixed_ref[:, lanes]
            own = pbuf[0:SPAN, lanes]
            acc = cwb[3:4, lanes] * own
            gconv[3, :, lanes] += fold(mixed * own)
            gconv[4, :, lanes] += fold(own)
            for k in range(1, 4):
                later = jnp.where(keeps[k], pbuf[k : k + SPAN, lanes], 0.0)
                acc = acc + cwb[3 - k : 4 - k, lanes] * later
                gconv[3 - k, :, lanes] += fold(mixed * later)
            dall[lot(c, SPAN), lanes] = acc.astype(BF16)
        pbuf[SPAN : SPAN + 8] = pbuf[0:8]
        dbuf[SPAN : SPAN + 8] = dbuf[0:8]

    @pl.when(i < mid)
    def _():
        scan_step(True)

    @pl.when(i >= mid)
    def _():
        block = lax.rem(i - mid + 1, blocks)
        ax_out[lot(block, LANES)] = out_grads(naway, caway, block).astype(BF16)
        ax_copy(block).start()
        @pl.when(i < count - 1)
        def _():
            for k in (c + mid, c):
                oy_copy(k).wait()

        finish_out(c + mid)
        finish_out(c)
        scan_step(False)

    @pl.when(i > 0)
    def _():
        join(c + 1)

    order = tuple(range(1, blocks)) + (0,)
    for k in range(blocks - 1):
        @pl.when(i == mid + 1 + k)
        def _():
            a_block(order[k])

    @pl.when(i == 0)
    def _():
        fetch[1].wait()
        both_cores = w[inner + chan : inner + chan + 2 * heads].astype(F32)
        own = jnp.where(core == 0, both_cores[0:heads], both_cores[heads:])
        w_step[...] = jnp.concatenate([own, jnp.zeros((LANES - heads, model), F32)], 0).astype(BF16)

    rows_now = lot(c, SPAN)
    kept[...] = (
        nn(dgate_all[rows_now], w[0:inner])
        + nn(dall[rows_now, 0:chan], w[inner : inner + chan])
        + nn(dall[rows_now, chan:], w_step[...])
    )
    h_out[lot(c % 2, half)] = kept[lot(1 - core, half)].astype(BF16)
    h_copy(c).start()
    value = hid_ref[...].astype(F32)
    unit = value * lax.rsqrt(jnp.mean(value * value, -1, keepdims=True) + EPS)
    gnorm[...] += fold(kept[...] * unit)

    @pl.when(i == count - 1)
    def _():
        chan_all = inner_all + 2 * LANES
        tap_rows, own_rows = chan_all // LANES, inner // LANES
        flat[...] = jnp.zeros(flat.shape, F32)
        norm = jnp.sum(gnorm[...], axis=0, keepdims=True)
        at = model // LANES
        for k in range(at):
            flat[k : k + 1] = norm[:, k * LANES : (k + 1) * LANES]
        for tap in range(gconv.shape[0]):
            row = jnp.sum(gconv[tap], axis=0, keepdims=True)
            for k in range(chan // LANES):
                place = at + k + (rank * own_rows if k < own_rows else (tap_rows - chan // LANES))
                flat[pl.ds(place, 1), :] = row[:, k * LANES : (k + 1) * LANES]
            at += tap_rows
        spread = jnp.zeros((1, LANES), F32)
        for k in range(2):
            total = jnp.broadcast_to(jnp.sum(ghead[k], axis=1, keepdims=True), (heads, LANES))
            place = iota((heads, LANES), 1) == 4 * heads * k + rank * heads + iota((heads, LANES), 0)
            spread = spread + jnp.sum(jnp.where(place, total, 0.0), axis=0, keepdims=True)
        flat[at : at + 1] = spread
        at += 1
        for acc in (ggain, gskip):
            row = jnp.sum(acc[...], axis=0, keepdims=True)
            for k in range(own_rows):
                flat[pl.ds(at + rank * own_rows + k, 1), :] = row[:, k * LANES : (k + 1) * LANES]
            at += inner_all // LANES

        hops = [partner]
        bit = 1
        while bit < lines:
            hops.append({"dp": (line + bit * (1 - 2 * ((line // bit) % 2))) * 2 + side})
            bit *= 2
        hops += [across, beyond]
        last = flat_in.shape[0] - 1

        def flat_copy(k):
            return remote(
                flat.at[...] if k == 0 else flat_in.at[len(hops) + k], flat_in.at[k], f_sem, k, hops[k]
            )

        def flat_step(k):
            flat_copy(k).wait_recv()
            held = (flat[...] if k == 0 else flat_in[len(hops) + k]) + flat_in[k]
            if k + 1 < len(hops):
                flat_in[len(hops) + k + 1] = held
                flat_copy(k + 1).start()
            else:
                flat_in[last] = held

        flat_copy(0).start()
        sx_out[...] = tn(naway[...], dall[:, inner:]).astype(BF16)
        for k in order:
            sx_copy(k).start()
        flat_step(0)
        vx_out[LANES:] = tn(naway[:, LANES:], dall[:, 0:inner]).astype(BF16)
        for k in order[:-1]:
            vx_copy(k).start()
        vx_out[0:LANES] = tn(naway[:, 0:LANES], dall[:, 0:inner]).astype(BF16)
        vx_copy(0).start()
        flat_step(1)
        join(0)

        a_block(order[-1])
        for k in range(2, len(hops) - 2):
            flat_step(k)
        gain_row = ngain_ref[...]

        def finish_hidden(k, carry):
            y_copy(k).wait_recv()
            y_copy(k).wait_send()
            d_hidden = mine[lot(k, half)].astype(F32) + y_in[lot(k, half)].astype(F32)
            value = hid_own[lot(k, half)].astype(F32)
            inv = lax.rsqrt(jnp.mean(value * value, -1, keepdims=True) + EPS)
            scaled = d_hidden * gain_row
            pull = jnp.mean(scaled * value, -1, keepdims=True)
            mine[lot(k, half)] = (inv * scaled - value * (inv * inv * inv) * pull).astype(BF16)
            d_copy(k).start()
            d_local(k).start()
            return carry

        def down(k, carry):
            return finish_hidden(count - 1 - k, carry)

        shere[...] = tn(nhere[...], dall[:, inner:])
        for k in order:
            s_block(k)
        vhere[...] = tn(nhere[...], dall[:, 0:inner])
        lax.fori_loop(0, 3, down, 0)
        for k in order[:-1]:
            v_block(k)
        flat_step(len(hops) - 2)
        for step in range(1, lines):
            az_copy(step).wait_recv()
            atotal[...] += az_in[step - 1].astype(F32)
        gates[0] = atotal[:, inner:].astype(BF16)
        gout_put = pltpu.make_async_copy(atotal.at[:, pl.ds(0, inner)], gout_ref, put_sem.at[9])
        gout_put.start()
        gate_near = remote(gates.at[0], gates.at[1], g_sem, 0, across)
        gate_far = remote(gates.at[0], gates.at[2], g_sem, 1, beyond)
        gate_pass = remote(gates.at[2], gates.at[3], g_sem, 2, across)
        gate_near.start()
        gate_far.start()
        for step in range(1, lines):
            sz_copy(step).wait_recv()
            stotal[...] += sz_in[step - 1].astype(F32)
        shared_near = remote(shared.at[0], shared.at[1], s_sem, 0, across)
        shared_far = remote(shared_low.at[0], shared_low.at[1], s_sem, 1, beyond)
        shared[0, :, 0 : 2 * LANES] = stotal[:, 0 : 2 * LANES]
        steps = pltpu.roll(stotal[:, 2 * LANES :], rank * heads, 1)
        place = iota(steps.shape, 1) - rank * heads
        shared[0, :, 2 * LANES :] = jnp.where((place >= 0) & (place < heads), steps, 0.0)
        shared_near.start()
        v_block(order[-1])
        lax.fori_loop(3, 6, down, 0)
        shared_near.wait_recv()
        shared_low[0] = (shared[0] + shared[1]).astype(BF16)
        shared_far.start()
        gate_far.wait_recv()
        gate_pass.start()
        flat_step(len(hops) - 1)
        flat_put = pltpu.make_async_copy(flat_in.at[last], flatout_ref, put_sem.at[10])
        flat_put.start()
        lax.fori_loop(6, count, down, 0)

        for step in range(1, lines):
            vz_copy(step).wait_recv()
            vtotal[...] += vz_in[step - 1].astype(F32)
        values[0] = vtotal[...].astype(BF16)
        value_near = remote(values.at[0], values.at[1], v_sem, 0, across)
        value_far = remote(values.at[0], values.at[2], v_sem, 1, beyond)
        value_pass = remote(values.at[2], values.at[3], v_sem, 2, across)
        value_far.start()
        value_near.start()

        def put(source, k, first, owner, index):
            column = pl.multiple_of(first + owner * inner, LANES)
            return pltpu.make_async_copy(source.at[k], gin_ref.at[:, pl.ds(column, inner)], put_sem.at[index])

        owners = (rank, rank + 1 - 2 * core, (rank + 2) % 4, (rank + 3 - 2 * core) % 4)
        gate_near.wait_recv()
        gate_pass.wait_recv()
        gate_puts = [put(vbuf, k, 0, owners[k], k) for k in range(4)]
        for k in range(4):
            vbuf[k] = gates[k].astype(F32)
            gate_puts[k].start()
        shared_far.wait_recv()
        shared[1] = shared_low[0].astype(F32) + shared_low[1].astype(F32)
        puts = [
            pltpu.make_async_copy(
                shared.at[1], gin_ref.at[:, pl.ds(2 * inner_all, 3 * LANES)], put_sem.at[8]
            )
        ]
        puts[0].start()
        for copy in gate_puts:
            copy.wait()

        def put_values(k):
            vbuf[k] = values[k].astype(F32)
            puts.append(put(vbuf, k, inner_all, owners[k], 4 + k))
            puts[-1].start()

        put_values(0)
        value_near.wait_recv()
        put_values(1)
        value_far.wait_recv()
        value_pass.start()
        put_values(2)
        value_pass.wait_recv()
        put_values(3)

        def drain(k, carry):
            d_copy(k).wait()
            d_local(k).wait()
            o_copy(k).wait()
            o_local(k).wait()
            return carry

        lax.fori_loop(0, count, drain, 0)
        for step in range(1, lines):
            az_copy(step).wait_send()
            sz_copy(step).wait_send()
            vz_copy(step).wait_send()
        for copy in (
            gate_near, gate_far, gate_pass, value_near, value_far, value_pass, shared_near, shared_far,
        ):
            copy.wait_send()
        for k in range(len(hops)):
            flat_copy(k).wait_send()
        for copy in puts + [gout_put, flat_put]:
            copy.wait()


def mixer_backward(
    docs, hidden, cotangent, held, sums, params, ggain, ngain, sorted_parts, w_in, mine, far, w_out,
    heads, lines, depth,
):
    gate, mixed, pre, ssd, stp, states = held
    tokens, inner = ssd.shape
    model = hidden.shape[1]
    chan = inner + 2 * LANES
    width = inner + chan + LANES
    wide = width - inner
    inner_all = ggain.shape[1]
    count = tokens // SPAN
    mid = count // 2
    half = SPAN // 2
    blocks, fars = lines * depth // LANES, max(1, lines - 1)
    hops = 3 + (lines - 1).bit_length()
    rows = (model + 5 * (inner_all + 2 * LANES) + LANES + 2 * inner_all) // LANES
    rows += -rows % 8

    def tok(size):
        return pl.BlockSpec((SPAN, size), lambda i: (count - 1 - i, 0))

    def early_tok(size, base):
        return pl.BlockSpec((SPAN, size), lambda i: (base + (mid - 1 - i) * (1 - i // mid), 0))

    def full(shape):
        return pl.BlockSpec(shape, lambda i: (0,) * len(shape))

    anywhere = pl.BlockSpec(memory_space=pl.ANY)
    dma, vmem = pltpu.SemaphoreType.DMA, pltpu.VMEM
    consts = params + (ggain, ngain)
    big = tuple(sorted_parts)[0:2] + tuple(sorted_parts)[2:4] + (w_in, mine, far, w_out)
    side_shape = (tokens, lines * depth)
    return pl.pallas_call(
        lambda *refs: backward_kernel((inner, heads, inner_all, lines, depth), *refs),
        out_shape=(
            jax.ShapeDtypeStruct((tokens, model), BF16),
            jax.ShapeDtypeStruct((tokens, model), BF16),
            jax.ShapeDtypeStruct((depth, 2 * inner_all + 3 * LANES), F32),
            jax.ShapeDtypeStruct((depth, inner), F32),
            jax.ShapeDtypeStruct((rows, LANES), F32),
        ),
        grid=(count,),
        in_specs=[
            full(docs.shape), tok(model), early_tok(inner, mid), early_tok(model, mid),
            early_tok(inner, 0), early_tok(inner, 0), early_tok(model, 0),
            tok(inner), tok(chan), tok(chan), pl.BlockSpec((heads, SPAN), lambda i: (0, count - 1 - i)),
            pl.BlockSpec((1, LANES, inner), lambda i: (count - 1 - i, 0, 0)),
            full(sums.shape),
        ]
        + [full(v.shape) for v in consts]
        + [anywhere] * len(big),
        out_specs=(anywhere,) * 5,
        scratch_shapes=[
            vmem(side_shape, BF16), vmem(side_shape, BF16), vmem(side_shape, BF16), vmem(side_shape, BF16),
            vmem(w_in.shape, BF16), vmem(w_out.shape, BF16), dma((len(big) + 1,)),
            vmem((SPAN + 8, chan), F32), vmem((SPAN + 8, LANES), F32), vmem((LANES, inner), F32),
            vmem((2, heads, SPAN), F32), vmem((8, LANES), F32), vmem((8, chan), F32), vmem((8, inner), F32),
            vmem((LANES, model), BF16), vmem((4, SPAN, inner), BF16),
            vmem((5, 8, chan), F32), vmem((8, inner), F32), vmem((2, heads, SPAN), F32),
            vmem((8, inner), F32), vmem((8, model), F32),
            vmem((tokens, inner), BF16), vmem((tokens, inner), BF16), vmem((tokens, wide), BF16),
            vmem((tokens // 2, inner), F32), vmem((count, LANES), F32),
            vmem((tokens // 2, model), BF16),
            vmem((SPAN, model), BF16), vmem((tokens // 2, model), BF16),
            vmem((tokens // 2, model), BF16), vmem((SPAN, model), F32),
            dma((2, count)), dma((2, count)), dma((2, count)), dma((count,)),
            vmem((tokens // 2, model), BF16), vmem((tokens // 2, model), BF16),
            dma((2, count)), dma((2, count)), dma((count,)),
            vmem((blocks * LANES, 2 * inner), BF16), vmem((blocks * LANES, 2 * inner), BF16),
            dma((2, blocks)), vmem((fars, depth, 2 * inner), BF16), dma((2, fars)),
            vmem((depth, 2 * inner), F32),
            vmem((blocks * LANES, 3 * LANES), BF16), vmem((blocks * LANES, 3 * LANES), BF16),
            dma((2, blocks)), vmem((fars, depth, 3 * LANES), BF16), dma((2, fars)),
            vmem((depth, 3 * LANES), F32), vmem((blocks * LANES, 3 * LANES), F32),
            vmem((blocks * LANES, inner), BF16), vmem((blocks * LANES, inner), BF16),
            dma((2, blocks)), vmem((fars, depth, inner), BF16), dma((2, fars)), vmem((depth, inner), F32),
            vmem((blocks * LANES, inner), F32), vmem((4, depth, inner), F32),
            vmem((4, depth, inner), BF16), dma((2, 3)), vmem((4, depth, inner), BF16), dma((2, 3)),
            vmem((2, depth, 3 * LANES), F32), vmem((2, depth, 3 * LANES), BF16), dma((2, 2)), dma((11,)),
            vmem((rows, LANES), F32), vmem((2 * hops + 1, rows, LANES), F32), dma((2, hops)),
        ],
        compiler_params=pltpu.CompilerParams(
            dimension_semantics=("arbitrary",), vmem_limit_bytes=67043328,
            collective_id=1, has_side_effects=True,
        ),
        cost_estimate=cost(90.0),
        name="mixer_backward",
    )(
        docs, hidden, gate, cotangent, gate, ssd, cotangent, ssd, mixed, pre, stp, states, sums, *consts, *big
    )


def finish_kernel(
    dims, cot_ref, delta_ref, layer_ref, gin_ref, flat_ref,
    out_ref, grad_ref, norm_ref, win_ref, taps_ref, bias_ref, dt_ref, decay_ref, skip_ref, gain_ref,
):
    inner_all, heads, turned = dims
    grad_ref[...] = cot_ref[...].astype(F32) + delta_ref[...].astype(F32)
    out_ref[...] = layer_ref[...]
    if turned:
        win_ref[...] = jnp.transpose(gin_ref[...])
    else:
        win_ref[...] = gin_ref[:, 0 : win_ref.shape[1]]

    @pl.when(pl.program_id(0) == 0)
    def _():
        at = norm_ref.shape[1] // LANES

        def spread(dst, row, first, count):
            for k in range(count):
                dst[row : row + 1, k * LANES : (k + 1) * LANES] = flat_ref[first + k : first + k + 1]

        spread(norm_ref, 0, 0, at)
        wide = taps_ref.shape[1] // LANES
        for tap in range(taps_ref.shape[0]):
            spread(taps_ref, tap, at + tap * wide, wide)
        at += taps_ref.shape[0] * wide
        bias_ref[...] = flat_ref[at : at + wide]
        at += wide
        dt_ref[...] = flat_ref[at : at + 1, 0:heads]
        decay_ref[...] = flat_ref[at : at + 1, heads : 2 * heads]
        at += 1
        spread(gain_ref, 0, at, inner_all // LANES)
        at += inner_all // LANES
        per = inner_all // heads
        lane = iota((1, LANES), 1)
        found = jnp.zeros((1, LANES), F32)
        for k in range(inner_all // LANES):
            row = flat_ref[at + k : at + k + 1]
            for part in range(LANES // per):
                inside = (lane >= part * per) & (lane < (part + 1) * per)
                total = jnp.sum(jnp.where(inside, row, 0.0), axis=1, keepdims=True)
                found = jnp.where(lane == k * (LANES // per) + part, total, found)
        skip_ref[...] = found[:, 0:heads]


def finish(cotangent, delta, layer_out, grad_in, flat, columns, inner_all, heads, turned):
    tokens, model = cotangent.shape
    depth = grad_in.shape[0]
    steps = 8
    chan_all = inner_all + 2 * LANES

    def tok(v, size):
        return pl.BlockSpec((v // steps, size), lambda i: (i, 0))

    def full(shape):
        return pl.BlockSpec(shape, lambda i: (0,) * len(shape))

    small = [(1, model), (4, chan_all), (chan_all // LANES, LANES), (1, heads), (1, heads), (1, heads), (1, inner_all)]
    if turned:
        cut = grad_in.shape[1] // (steps - 1)
        rows = pl.BlockSpec((depth, cut), lambda i: (0, i - i // (steps - 1)))
        shown = pl.BlockSpec((cut, depth), lambda i: (i - i // (steps - 1), 0))
    else:
        rows, shown = full(grad_in.shape), full((depth, columns))
    return pl.pallas_call(
        lambda *refs: finish_kernel((inner_all, heads, turned), *refs),
        out_shape=[
            jax.ShapeDtypeStruct((tokens, model), BF16),
            jax.ShapeDtypeStruct((tokens, model), F32),
            jax.ShapeDtypeStruct(small[0], F32),
            jax.ShapeDtypeStruct((columns, depth) if turned else (depth, columns), F32),
        ]
        + [jax.ShapeDtypeStruct(v, F32) for v in small[1:]],
        grid=(steps,),
        in_specs=[tok(tokens, model)] * 3 + [rows, full(flat.shape)],
        out_specs=[tok(tokens, model)] * 2 + [full(small[0]), shown] + [full(v) for v in small[1:]],
        compiler_params=pltpu.CompilerParams(dimension_semantics=("arbitrary",)),
        cost_estimate=cost(9.0),
        name="finish",
    )(cotangent, delta, layer_out, grad_in, flat)


def gather_kernel(
    dims, hid_ref, cot_ref, ngain_ref, w_ref, step_ref, wo_ref,
    win_ref, *refs,
):
    lines, depth, inner, inner_all, heads, turned = dims
    wout_ref = None if turned else refs[0]
    refs = refs[0 if turned else 1 :]
    normed_ref, refs = refs[0], refs[1:]
    outs = refs[:4] if turned else ()
    mine, zsend, zrecv, xsend, xrecv, takes, puts, qsend, qrecv = refs[len(outs):]
    trank, drank = lax.axis_index("tensor"), lax.axis_index("dp")
    line, side = drank // 2, drank % 2
    core = trank % 2
    model = hid_ref.shape[1]
    off = pl.multiple_of(trank * inner, LANES)
    base = 2 * inner_all
    if turned:
        quarter = 2 * LANES // 4
        own_quarter = pl.multiple_of(trank * quarter, quarter)
        chip = 2 * heads
        steps = pl.multiple_of(base + 2 * LANES + (trank // 2) * chip, chip)
        cut = inner // 2
        pieces = [
            (w_ref, base + own_quarter, win_ref, 2 * inner + own_quarter, quarter),
            (w_ref, steps, win_ref, 2 * inner + 2 * LANES, chip),
        ]
        pieces += [(w_ref, inner_all + off + k * cut, win_ref, inner + k * cut, cut) for k in range(2)]
        pieces += [(w_ref, off + k * cut, win_ref, k * cut, cut) for k in range(2)]
    else:
        pieces = [
            (w_ref, inner_all + off, win_ref, inner, inner),
            (w_ref, base, win_ref, 2 * inner, 2 * LANES),
            (step_ref, 0, win_ref, 2 * inner + 2 * LANES, LANES),
            (w_ref, off, win_ref, 0, inner),
            (wo_ref, 0, wout_ref, 0, inner),
        ]

    def peer(step):
        return {"dp": lax.rem(line + step, lines) * 2 + side}

    partner = {"dp": line * 2 + 1 - side}
    family = (
        {"tensor": trank + 1 - 2 * core}, {"tensor": (trank + 2) % 4},
        {"tensor": (trank + 3 - 2 * core) % 4},
    )
    others = [partner] + [peer(step) for step in range(1, lines)] + (list(family) if turned else [])
    barrier = pltpu.get_barrier_semaphore()
    for device in others:
        pl.semaphore_signal(barrier, inc=1, device_id=device, device_id_type=MESH_IDS)
    pl.semaphore_wait(barrier, len(others))

    def lanes_of(index):
        return pl.ds(pl.multiple_of(index * depth, depth), depth)

    def in_rows(p):
        return turned and pieces[p][0] is w_ref

    def block(p, index):
        _, _, dst, at, width = pieces[p]
        if in_rows(p):
            return dst.at[pl.ds(at, width), lanes_of(index)]
        return dst.at[lanes_of(index), pl.ds(at, width)]

    def own(p):
        src, at, _, _, width = pieces[p]
        return src.at[pl.ds(at, width)] if in_rows(p) else src.at[:, pl.ds(at, width)]

    def z_copy(p, step, src, index):
        return pltpu.make_async_remote_copy(
            src_ref=src, dst_ref=block(p, index), send_sem=zsend.at[p, step - 1],
            recv_sem=zrecv.at[p, step - 1], device_id=peer(step), device_id_type=MESH_IDS,
        )

    def x_copy(p, step, src, index):
        return pltpu.make_async_remote_copy(
            src_ref=src, dst_ref=block(p, index), send_sem=xsend.at[p, step],
            recv_sem=xrecv.at[p, step], device_id=partner, device_id_type=MESH_IDS,
        )

    count = len(pieces)
    for p in range(count):
        for step in range(1, lines):
            z_copy(p, step, own(p), drank).start()
        x_copy(p, 0, own(p), drank).start()
    spots, at = [], 0
    for p in range(count):
        width = pieces[p][4]
        if in_rows(p):
            spots.append(mine.at[pl.ds(at, width), pl.ds(0, depth)])
            at += width
        elif turned:
            spots.append(mine.at[pl.ds(at, depth), pl.ds(0, width)])
            at += depth
        else:
            spots.append(mine.at[:, pl.ds(at, width)])
            at += width
    fetched = [pltpu.make_async_copy(own(p), spots[p], takes.at[p]) for p in range(count)]
    for copy in fetched:
        copy.start()

    gain = ngain_ref[...]

    def normalize(hid, cot, normed, *sorted_refs):
        value = hid[...].astype(F32)
        inv = lax.rsqrt(jnp.mean(value * value, -1, keepdims=True) + EPS)
        normed[...] = (value * inv * gain).astype(BF16)
        if turned:
            for src, away, here in (
                (normed, sorted_refs[0], sorted_refs[1]), (cot, sorted_refs[2], sorted_refs[3]),
            ):
                for j in range(lines):
                    first = lax.rem(line + j, lines) * 2
                    lanes = slice(j * depth, (j + 1) * depth)
                    away[:, lanes] = src[:, lanes_of(first + 1 - side)]
                    here[:, lanes] = src[:, lanes_of(first + side)]

    full = pl.BlockSpec((SPAN, model), lambda i: (i, 0))
    half = pl.BlockSpec((SPAN, lines * depth), lambda i: (i, 0))
    pltpu.emit_pipeline(
        normalize, grid=(hid_ref.shape[0] // SPAN,), in_specs=[full, full],
        out_specs=[full] + [half] * len(outs),
    )(hid_ref, cot_ref, normed_ref, *outs)

    stored = [pltpu.make_async_copy(spots[p], block(p, drank), puts.at[p]) for p in range(count)]
    for p in range(count):
        fetched[p].wait()
        stored[p].start()

    def source_line(step):
        return lax.rem(line - step + lines, lines) * 2

    def x_arrived(p):
        for step in range(lines):
            source = source_line(step) + 1 - side
            x_copy(p, step, block(p, source), source).wait_recv()

    def quarter_copy(k, device):
        rows = win_ref.at[pl.ds(2 * inner + own_quarter, quarter)]
        return pltpu.make_async_remote_copy(
            src_ref=rows, dst_ref=rows, send_sem=qsend.at[k], recv_sem=qrecv.at[k],
            device_id=device, device_id_type=MESH_IDS,
        )

    def quarter_from(k, owner):
        rows = win_ref.at[pl.ds(pl.multiple_of(2 * inner + owner * quarter, quarter), quarter)]
        return pltpu.make_async_remote_copy(
            src_ref=rows, dst_ref=rows, send_sem=qsend.at[k], recv_sem=qrecv.at[k],
            device_id=family[k], device_id_type=MESH_IDS,
        )

    for p in range(count):
        for step in range(1, lines):
            source = source_line(step) + side
            got = block(p, source)
            z_copy(p, step, got, source).wait_recv()
            x_copy(p, step, got, source).start()
        if turned and p == 3:
            stored[0].wait()
            x_arrived(0)
            for k in range(3):
                quarter_copy(k, family[k]).start()
    for p in range(1 if turned else 0, count):
        x_arrived(p)
    if turned:
        owners = (trank + 1 - 2 * core, (trank + 2) % 4, (trank + 3 - 2 * core) % 4)
        for k in range(3):
            quarter_from(k, owners[k]).wait_recv()
            quarter_copy(k, family[k]).wait_send()
    for p in range(count):
        for step in range(1, lines):
            z_copy(p, step, own(p), drank).wait_send()
        for step in range(lines):
            x_copy(p, step, own(p), drank).wait_send()
        if not (turned and p == 0):
            stored[p].wait()


def gather_weights(
    hidden, cotangent, norm_gain, in_weight, own_step, out_weight, lines, inner_all, heads, turned
):
    tokens, model = hidden.shape
    depth, inner = out_weight.shape
    half = jax.ShapeDtypeStruct((tokens, lines * depth), BF16)
    anywhere = pl.BlockSpec(memory_space=pl.ANY)
    rows = 2 * inner + 2 * LANES + 2 * heads
    width = 2 * inner + 3 * LANES
    count = 6 if turned else 5
    outs = (
        (jax.ShapeDtypeStruct((rows, model) if turned else (model, width), BF16),)
        + (() if turned else (jax.ShapeDtypeStruct((model, inner), BF16),))
        + (jax.ShapeDtypeStruct((tokens, model), BF16),)
        + (half,) * (4 if turned else 0)
    )
    dma = pltpu.SemaphoreType.DMA
    held = (rows, LANES) if turned else (depth, width + inner)
    fars = max(1, lines - 1)
    return pl.pallas_call(
        lambda *refs: gather_kernel((lines, depth, inner, inner_all, heads, turned), *refs),
        out_shape=outs,
        in_specs=[anywhere, anywhere, pl.BlockSpec(memory_space=pltpu.VMEM)] + [anywhere] * 3,
        out_specs=(anywhere,) * len(outs),
        scratch_shapes=[
            pltpu.VMEM(held, BF16),
            dma((count, fars)), dma((count, fars)), dma((count, lines)), dma((count, lines)),
            dma((count,)), dma((count,)), dma((3,)), dma((3,)),
        ],
        compiler_params=pltpu.CompilerParams(collective_id=0, has_side_effects=True),
        cost_estimate=cost(45.0),
        name="gather_weights",
    )(hidden, cotangent, norm_gain, in_weight, own_step, out_weight)


def body(
    hidden_in, doc_ids, cotangent, norm_gain, in_weight, conv_weight, conv_bias,
    dt_bias, log_decay, skip_gain, gate_gain, out_weight,
):
    tcount, dcount = lax.axis_size("tensor"), lax.axis_size("dp")
    trank, drank = lax.axis_index("tensor"), lax.axis_index("dp")
    lines = dcount // 2
    line, side = drank // 2, drank % 2
    inner_all, head_all = gate_gain.shape[0], dt_bias.shape[0]
    inner, heads = inner_all // tcount, head_all // tcount
    tokens, model = hidden_in.shape
    base_bc = 2 * inner_all
    base_dt = base_bc + 2 * LANES
    depth = in_weight.shape[0]

    def line_to(step):
        return lambda k: ((k // 2 + step) % lines) * 2 + k % 2

    turned = depth % LANES == 0
    if turned:
        weight_in = own_step = in_weight.T
    else:
        weight_in = in_weight
        own_step = jnp.pad(
            lax.dynamic_slice_in_dim(in_weight, base_dt + trank * heads, heads, 1),
            ((0, 0), (0, LANES - heads)),
        )
    w_in, *rest = gather_weights(
        hidden_in, cotangent, norm_gain.reshape(1, -1), weight_in, own_step,
        out_weight, lines, inner_all, heads, turned,
    )
    w_out, rest = (out_weight, rest) if turned else (rest[0], rest[1:])
    normed, *sorted_parts = rest
    if not turned:
        pair = lax.dynamic_update_slice_in_dim(
            jnp.zeros((2 * heads, model), BF16),
            w_in[:, 2 * inner + 2 * LANES :][:, :heads].T, trank % 2 * heads, 0,
        )
        w_in = jnp.concatenate([w_in[:, : 2 * inner + 2 * LANES].T, pair], 0)
    if not sorted_parts:

        def features(v, which):
            return jnp.concatenate(
                [
                    lax.dynamic_slice_in_dim(v, (((line + j) % lines) * 2 + which) * depth, depth, 1)
                    for j in range(lines)
                ],
                1,
            )

        sorted_parts = [features(v, which) for v in (normed, cotangent) for which in (1 - side, side)]
    n_away, n_here, c_away, c_here = sorted_parts

    def row(v):
        return v.reshape(1, -1)

    params = (conv_weight, conv_bias.reshape(-1, LANES), row(dt_bias), row(log_decay), row(skip_gain))

    *held, sums, mine, far, w_full = mixer_forward(
        doc_ids, normed, cotangent, w_in, w_out, params, row(gate_gain), heads, lines, turned
    )
    delta, layer_out, grad_in, g_out, flat = mixer_backward(
        doc_ids, hidden_in, cotangent, held, sums, params, row(gate_gain), row(norm_gain), sorted_parts, w_in,
        mine, far, w_full, heads, lines, depth,
    )
    layer_out, grad_input, g_norm, grad_in_weight, taps, bias, dt, decay, skip, gain = finish(
        cotangent, delta, layer_out, grad_in, flat, in_weight.shape[1], inner_all, head_all, turned
    )
    return (
        layer_out, grad_input, g_norm.reshape(-1), grad_in_weight.T if turned else grad_in_weight, taps, bias.reshape(-1),
        dt.reshape(-1), decay.reshape(-1), skip.reshape(-1), gain.reshape(-1), g_out,
    )


def solution(mesh):
    rows, whole = P("dp", None), P()
    return jax.shard_map(
        body,
        mesh=mesh,
        in_specs=(rows, rows, rows, whole, rows, whole, whole, whole, whole, whole, whole, P("dp", "tensor")),
        out_specs=(rows, rows, whole, rows, whole, whole, whole, whole, whole, whole, P("dp", "tensor")),
        check_vma=False,
    )
```

```python
import jax
import jax.numpy as jnp
from jax import lax
from jax.experimental import pallas as pl
from jax.experimental.pallas import tpu as pltpu
from jax.sharding import PartitionSpec as P

SPAN = 256
LANES = 128
EPS = 1e-05
FAR = -1e30
LOG2_E = 1.4426950408889634
VMEM_MOST = 60 * 2**20
F32 = jnp.float32
BF16 = jnp.bfloat16


def cost(micros):
    return pl.CostEstimate(flops=int(micros * 1.15e9), bytes_accessed=1 << 20, transcendentals=0)


def nn(a, b):
    return lax.dot_general(a, b, (((1,), (0,)), ((), ())), preferred_element_type=F32)


def nt(a, b):
    return lax.dot_general(a, b, (((1,), (1,)), ((), ())), preferred_element_type=F32)


def tn(a, b):
    return lax.dot_general(a, b, (((0,), (0,)), ((), ())), preferred_element_type=F32)


def iota(shape, dim):
    return lax.broadcasted_iota(jnp.int32, shape, dim)


def as_column(row, rows=SPAN):
    return jnp.transpose(jnp.broadcast_to(row, (LANES, rows)))


def as_row(block):
    ones = jnp.ones((16, LANES), BF16)
    hi = block.astype(BF16)
    low = (block - hi.astype(F32)).astype(BF16)
    return (nt(ones, hi) + nt(ones, low))[0:1]


def sigmoid(v):
    return 0.5 * jnp.tanh(0.5 * v) + 0.5


def row_sum(v, tri):
    hi = v.astype(BF16).astype(F32)
    rest = v - hi
    mid = rest.astype(BF16).astype(F32)
    count = v.shape[0]
    out = nn(jnp.concatenate([hi, mid, rest - mid], 0).astype(BF16), tri)
    return out[0:count] + out[count : 2 * count] + out[2 * count :]


def pair_lanes(cols, first, low_half):
    rows = cols.shape[0]
    left = jnp.broadcast_to(cols[:, first : first + 1], (rows, LANES))
    right = jnp.broadcast_to(cols[:, first + 1 : first + 2], (rows, LANES))
    return jnp.where(low_half, left, right)


def exact_nt(a, b):
    a_hi, b_hi = a.astype(BF16), b.astype(BF16)
    a_lo = (a - a_hi.astype(F32)).astype(BF16)
    b_lo = (b - b_hi.astype(F32)).astype(BF16)
    return nt(a_hi, b_hi) + (nt(a_hi, b_lo) + nt(a_lo, b_hi))


def softplus(v):
    return jnp.maximum(v, 0.0) + jnp.log1p(jnp.exp(-jnp.abs(v)))


def own_lanes(row, rank, heads):
    total = row.shape[1]
    pick = (iota((total, LANES), 0) == rank * heads + iota((total, LANES), 1)) & (
        iota((total, LANES), 1) < heads
    )
    wide = jnp.broadcast_to(row, (8, total))
    out = lax.dot_general(
        wide, pick.astype(F32), (((1,), (0,)), ((), ())),
        precision=lax.Precision.HIGHEST, preferred_element_type=F32,
    )
    return out[0:1]


def own_rows_of(row, rank, heads):
    total = row.shape[1]
    place = iota((heads, total), 1) == rank * heads + iota((heads, total), 0)
    picked = jnp.where(place, jnp.broadcast_to(row, (heads, total)), 0.0)
    return jnp.broadcast_to(jnp.sum(picked, axis=1, keepdims=True), (heads, SPAN))


def head_scales(raw, rate, doc, enter, extra):
    step = softplus(raw)
    log_step = step * rate
    row_i, col_i = iota((SPAN, SPAN), 0), iota((SPAN, SPAN), 1)
    running = row_sum(log_step, (row_i <= col_i).astype(BF16))
    ending = jnp.broadcast_to(running[:, SPAN - 1 :], running.shape)
    last = jnp.broadcast_to(doc[:, SPAN - 1 :], doc.shape)
    tail = jnp.where(doc == last, jnp.exp(ending - running), 0.0)
    reach = jnp.where(doc == enter, jnp.exp(running), 0.0)
    scaled = running * LOG2_E
    rows = [scaled, step, tail, reach, doc] + extra
    used = sum(v.shape[0] for v in rows)
    packed = jnp.concatenate(rows + [jnp.zeros((LANES - used, SPAN), F32)], 0)
    return log_step, scaled, jnp.transpose(packed)


def fold(v):
    return jnp.sum(v.reshape(SPAN // 8, 8, v.shape[1]), axis=0)


def own_params(rank, heads, inner, inner_all, dtb_ref, dec_ref, skip_ref, cw_ref, cb_ref, par, skips, cwb):
    chan = inner + 2 * LANES
    off = pl.multiple_of(rank * inner, LANES)
    taps = cw_ref.shape[0]
    par[0] = own_rows_of(dtb_ref[...], rank, heads)
    par[1] = -jnp.exp(own_rows_of(dec_ref[...], rank, heads))
    skips[0:1] = own_lanes(skip_ref[...], rank, heads)
    cwb[0:taps, 0:inner] = cw_ref[:, pl.ds(off, inner)].astype(F32)
    cwb[0:taps, inner:chan] = cw_ref[:, inner_all:].astype(F32)
    for k in range(chan // LANES):
        row = rank * (inner // LANES) + k if k < inner // LANES else (inner_all - inner) // LANES + k
        cwb[taps : taps + 1, k * LANES : (k + 1) * LANES] = cb_ref[pl.ds(row, 1), :]


MESH_IDS = pl.DeviceIdType.MESH


def forward_kernel(
    dims, docs_ref, normed_ref, cot_low_ref, cot_high_ref, win_ref, wo_ref, cw_ref, cb_ref,
    dtb_ref, dec_ref, skip_ref, ggain_ref,
    gate_ref, mixed_ref, pre_ref, ssd_ref, stp_ref, state_ref,
    sums_ref, mine_ref, far_ref, wfull_ref,
    xbuf, dbuf, state, par, skips, cwb, gain, gg_all,
    own_sums, h_out, h_in, kept, mine, far, h_sem, y_sem, s_in, s_sem, put_sem,
    wout, oz_sem, ox_sem, own_sem,
):
    inner, heads, lines, depth, turned = dims
    pairs = heads // 2
    chan = inner + 2 * LANES
    i = pl.program_id(0)
    spans = gg_all.shape[0] // SPAN
    mid = spans // 2
    rank = lax.axis_index("tensor")
    core = rank % 2
    inner_all = ggain_ref.shape[1]
    half = SPAN // 2
    across = {"tensor": rank + 1 - 2 * core}
    beyond = {"tensor": (rank + 2) % 4}
    crossed = {"tensor": (rank + 3 - 2 * core) % 4}
    drank = lax.axis_index("dp")
    line, side = drank // 2, drank % 2
    partner = {"dp": line * 2 + 1 - side}
    portions = 2 if turned else 0
    cut = inner // 2

    def peer(step):
        return {"dp": lax.rem(line + step, lines) * 2 + side}

    def o_block(p, index):
        return wout.at[pl.ds(pl.multiple_of(index * depth, depth), depth), pl.ds(p * cut, cut)]

    def own_block(p):
        return wo_ref.at[:, pl.ds(p * cut, cut)]

    def oz_copy(p, step, src, index):
        return pltpu.make_async_remote_copy(
            src_ref=src, dst_ref=o_block(p, index), send_sem=oz_sem.at[0, p, step - 1],
            recv_sem=oz_sem.at[1, p, step - 1], device_id=peer(step), device_id_type=MESH_IDS,
        )

    def ox_copy(p, step, src, index):
        return pltpu.make_async_remote_copy(
            src_ref=src, dst_ref=o_block(p, index), send_sem=ox_sem.at[0, p, step],
            recv_sem=ox_sem.at[1, p, step], device_id=partner, device_id_type=MESH_IDS,
        )

    def source(step):
        return lax.rem(line - step + lines, lines) * 2

    if turned:
        own_copies = [
            pltpu.make_async_copy(own_block(p), o_block(p, drank), own_sem.at[p]) for p in range(portions)
        ]
    else:
        own_copies = [pltpu.make_async_copy(wo_ref, wout, own_sem.at[0])]

    @pl.when(i == 0)
    def _():
        others = [across, beyond, crossed]
        if turned:
            others += [partner] + [peer(step) for step in range(1, lines)]
        barrier = pltpu.get_barrier_semaphore()
        for device in others:
            pl.semaphore_signal(barrier, inc=1, device_id=device, device_id_type=MESH_IDS)
        pl.semaphore_wait(barrier, len(others))
        for p in range(portions):
            for step in range(1, lines):
                oz_copy(p, step, own_block(p), drank).start()
            ox_copy(p, 0, own_block(p), drank).start()
        for copy in own_copies:
            copy.start()
        xbuf[0:8] = jnp.zeros((8, chan), F32)
        dbuf[0:8] = jnp.full((8, LANES), -1.0, F32)
        state[...] = jnp.zeros(state.shape, F32)
        own_params(rank, heads, inner, inner_all, dtb_ref, dec_ref, skip_ref, cw_ref, cb_ref, par, skips, cwb)
        gain[0:1] = ggain_ref[:, pl.ds(pl.multiple_of(rank * inner, LANES), inner)]

    def slot(k):
        return pl.ds(pl.multiple_of(k * half, half), half)

    def h_copy(k):
        return pltpu.make_async_remote_copy(
            src_ref=h_out.at[slot(k)], dst_ref=h_in.at[slot(k)], send_sem=h_sem.at[0, k],
            recv_sem=h_sem.at[1, k], device_id=across, device_id_type=MESH_IDS,
        )

    def y_copy(k):
        return pltpu.make_async_remote_copy(
            src_ref=mine.at[slot(k)], dst_ref=far.at[slot(k // mid)], send_sem=y_sem.at[0, k // mid],
            recv_sem=y_sem.at[1, k // mid], device_id=beyond, device_id_type=MESH_IDS,
        )

    full_copy = pltpu.make_async_copy(wout, wfull_ref, put_sem.at[2])

    def join(k):
        h_copy(k).wait_recv()
        mine[slot(k)] = (kept[k // mid, slot(core)] + h_in[slot(k)].astype(F32)).astype(BF16)

    nb = normed_ref[...]
    xbuf[8 : 8 + SPAN] = nt(nb, win_ref[inner : inner + chan])
    gate_ref[...] = nt(nb, win_ref[0:inner])
    both_cores = nt(win_ref[inner + chan : inner + chan + 2 * heads], nb)
    stp = jnp.where(core == 0, both_cores[0:heads], both_cores[heads:])
    stp_ref[...] = stp
    mixed_ref[...] = xbuf[8 : 8 + SPAN]

    drow = docs_ref[:, pl.ds(pl.multiple_of(i * SPAN, SPAN), SPAN)].astype(F32)
    doc = jnp.broadcast_to(drow, (heads, SPAN))
    enter = jnp.broadcast_to(dbuf[7:8, 0:1], (heads, SPAN))
    _, run_rows, cols = head_scales(stp + par[0], par[1], doc, enter, [])
    dcol = jnp.broadcast_to(cols[:, 4 * heads : 4 * heads + 1], (SPAN, LANES))
    dbuf[8 : 8 + SPAN] = dcol
    keeps = [None] + [dbuf[8 - k : 8 - k + SPAN] == dcol for k in range(1, 4)]

    def conv(group):
        lanes = slice(group * LANES, (group + 1) * LANES)
        acc = cwb[4:5, lanes] + cwb[3:4, lanes] * xbuf[8 : 8 + SPAN, lanes]
        for k in range(1, 4):
            acc = acc + cwb[3 - k : 4 - k, lanes] * jnp.where(
                keeps[k], xbuf[8 - k : 8 - k + SPAN, lanes], 0.0
            )
        pre_ref[:, lanes] = acc
        return acc * sigmoid(acc)

    b_act, c_act = conv(pairs), conv(pairs + 1)
    b_rows, c_rows = b_act.astype(BF16), c_act.astype(BF16)

    row_i, col_i = iota((SPAN, SPAN), 0), iota((SPAN, SPAN), 1)
    same = jnp.concatenate([dcol, dcol], 1) == drow
    bias = jnp.where(same & (row_i >= col_i), 0.0, FAR)
    scores = exact_nt(c_act, b_act)
    b_turned = jnp.transpose(b_act).astype(BF16)
    low_half = iota((SPAN, LANES), 1) < LANES // 2
    square = jnp.zeros((SPAN, LANES), F32)
    for pair in range(pairs):
        lanes = slice(pair * LANES, (pair + 1) * LANES)
        act = conv(pair)
        scaled = act * pair_lanes(cols, heads + 2 * pair, low_half)
        xb = scaled.astype(BF16)
        tail_l = pair_lanes(cols, 2 * heads + 2 * pair, low_half)
        reach_l = pair_lanes(cols, 3 * heads + 2 * pair, low_half)
        held = state[:, lanes]
        held_b = held.astype(BF16)
        state_ref[0, :, lanes] = held_b
        state[:, lanes] = nn(b_turned, (scaled * tail_l).astype(BF16)) + reach_l[SPAN - 1 : SPAN] * held
        out = reach_l * nn(c_rows, held_b)
        parts = []
        for sub in range(2):
            head = 2 * pair + sub
            blocks = []
            for blk in range(2):
                rows = slice(blk * half, (blk + 1) * half)
                width = (blk + 1) * half
                gap = cols[rows, head : head + 1] - run_rows[head : head + 1, 0:width]
                weight = jnp.exp2(gap + bias[rows, 0:width]) * scores[rows, 0:width]
                blocks.append(nn(weight.astype(BF16), xb[0:width]))
            parts.append(jnp.concatenate(blocks, 0))
        out = out + jnp.where(low_half, parts[0], parts[1])
        skip_l = pair_lanes(skips[0:1], 2 * pair, low_half[0:1])
        ssd = out + skip_l * act
        ssd_ref[:, lanes] = ssd
        gate = gate_ref[:, lanes]
        gated = ssd * (gate * sigmoid(gate))
        square = square + gated * gated
        gained = gain[0:1, lanes] * gated
        gg_all[pl.ds(pl.multiple_of(i * SPAN, SPAN), SPAN), lanes] = gained.astype(BF16)
    own_sums[0, pl.ds(i, 1), :] = as_row(square)
    xbuf[0:8] = xbuf[SPAN : SPAN + 8]
    dbuf[0:8] = dbuf[SPAN : SPAN + 8]

    for p in range(portions):
        @pl.when(i == p + 1)
        def _():
            for step in range(1, lines):
                got = o_block(p, source(step) + side)
                oz_copy(p, step, got, source(step) + side).wait_recv()
                ox_copy(p, step, got, source(step) + side).start()

    @pl.when(i == mid)
    def _():
        for copy in own_copies:
            copy.wait()
        for p in range(portions):
            for step in range(lines):
                index = source(step) + 1 - side
                ox_copy(p, step, o_block(p, index), index).wait_recv()
        full_copy.start()

    @pl.when(i > mid)
    def _():
        join(i - 1 - mid)
        join(i - 1)

    @pl.when(i == mid + 1)
    def _():
        y_copy(0).start()
        y_copy(mid).start()

    @pl.when(i >= mid)
    def _():
        for which, (k, cot_ref) in enumerate(((i - mid, cot_low_ref), (i, cot_high_ref))):
            rows = gg_all[pl.ds(pl.multiple_of(k * SPAN, SPAN), SPAN)]
            kept[which] = nt(rows, wout[...])
            cross = jnp.zeros((SPAN, LANES), F32)
            for group in range(wout.shape[0] // LANES):
                lanes = slice(group * LANES, (group + 1) * LANES)
                cross = cross + kept[which, :, lanes] * cot_ref[:, lanes].astype(F32)
            own_sums[1, pl.ds(k, 1), :] = as_row(cross)
            h_out[slot(k)] = kept[which, slot(1 - core)].astype(BF16)
            h_copy(k).start()

    @pl.when(i == spans - 1)
    def _():
        def s_copy(k, device):
            return pltpu.make_async_remote_copy(
                src_ref=own_sums, dst_ref=s_in.at[k], send_sem=s_sem.at[0, k],
                recv_sem=s_sem.at[1, k], device_id=device, device_id_type=MESH_IDS,
            )

        sent = [s_copy(0, across), s_copy(1, beyond), s_copy(2, crossed)]
        for copy in sent:
            copy.start()
        join(i - mid)
        join(i)
        mine_put = pltpu.make_async_copy(mine, mine_ref, put_sem.at[0])
        mine_put.start()
        for copy in sent:
            copy.wait_recv()
        near = own_sums[...] + s_in[0]
        sums_ref[...] = near + (s_in[1] + s_in[2])
        for k in (0, mid):
            y_copy(k).wait_recv()
        far_put = pltpu.make_async_copy(far, far_ref, put_sem.at[1])
        far_put.start()
        for copy in sent:
            copy.wait_send()

        def drain(k, carry):
            h_copy(k).wait_send()
            return carry

        lax.fori_loop(0, spans, drain, 0)
        for k in (0, mid):
            y_copy(k).wait_send()
        for p in range(portions):
            for step in range(1, lines):
                oz_copy(p, step, own_block(p), drank).wait_send()
            for step in range(lines):
                ox_copy(p, step, own_block(p), drank).wait_send()
        mine_put.wait()
        far_put.wait()
        full_copy.wait()


def mixer_forward(docs, normed, cotangent, w_in, w_out, params, ggain, heads, lines, turned):
    tokens, model = normed.shape
    depth, inner = w_out.shape
    half = tokens // 2
    mid = tokens // SPAN // 2
    chan = inner + 2 * LANES
    spans = tokens // SPAN

    def tok(width):
        return pl.BlockSpec((SPAN, width), lambda i: (i, 0))

    def late(width, base):
        return pl.BlockSpec((SPAN, width), lambda i: (base + (i - mid) * (i // mid), 0))

    def full(shape):
        return pl.BlockSpec(shape, lambda i: (0,) * len(shape))

    anywhere = pl.BlockSpec(memory_space=pl.ANY)
    sums = (2, spans, SPAN)
    outs = (
        jax.ShapeDtypeStruct((tokens, inner), F32),
        jax.ShapeDtypeStruct((tokens, chan), F32),
        jax.ShapeDtypeStruct((tokens, chan), F32),
        jax.ShapeDtypeStruct((tokens, inner), F32),
        jax.ShapeDtypeStruct((heads, tokens), F32),
        jax.ShapeDtypeStruct((spans, LANES, inner), BF16),
        jax.ShapeDtypeStruct(sums, F32),
        jax.ShapeDtypeStruct((tokens // 2, model), BF16),
        jax.ShapeDtypeStruct((SPAN, model), BF16),
        jax.ShapeDtypeStruct((model, inner), BF16),
    )
    out_specs = (
        tok(inner), tok(chan), tok(chan), tok(inner), pl.BlockSpec((heads, SPAN), lambda i: (0, i)),
        pl.BlockSpec((1, LANES, inner), lambda i: (i, 0, 0)),
        full(sums), anywhere, anywhere, anywhere,
    )
    consts = params + (ggain,)
    dma, vmem = pltpu.SemaphoreType.DMA, pltpu.VMEM
    return pl.pallas_call(
        lambda *refs: forward_kernel((inner, heads, lines, depth, turned), *refs),
        out_shape=outs,
        grid=(spans,),
        in_specs=[
            full(docs.shape), tok(model), late(model, 0), late(model, mid), full(w_in.shape), anywhere,
        ]
        + [full(v.shape) for v in consts],
        out_specs=out_specs,
        scratch_shapes=[
            vmem((SPAN + 8, chan), F32), vmem((SPAN + 8, LANES), F32), vmem((LANES, inner), F32),
            vmem((2, heads, SPAN), F32), vmem((8, LANES), F32), vmem((8, chan), F32), vmem((8, inner), F32),
            vmem((tokens, inner), BF16), vmem(sums, F32),
            vmem((tokens // 2, model), BF16), vmem((tokens // 2, model), BF16),
            vmem((2, SPAN, model), F32), vmem((tokens // 2, model), BF16),
            vmem((SPAN, model), BF16),
            dma((2, spans)), dma((2, 2)), vmem((3,) + sums, F32), dma((2, 3)), dma((3,)),
            vmem((model, inner), BF16), dma((2, 2, max(1, lines - 1))), dma((2, 2, lines)), dma((2,)),
        ],
        compiler_params=pltpu.CompilerParams(
            dimension_semantics=("arbitrary",), vmem_limit_bytes=VMEM_MOST,
            collective_id=2, has_side_effects=True,
        ),
        cost_estimate=cost(40.0),
        name="mixer_forward",
    )(docs, normed, cotangent, cotangent, w_in, w_out, *consts)


def backward_kernel(
    dims,
    docs_ref, hid_ref, gate_ref, cot_ref, gate_low_ref, ssd_low_ref, cot_low_ref,
    ssd_ref, mixed_ref, pre_ref, stp_ref, state_ref, sums_ref,
    cw_ref, cb_ref, dtb_ref, dec_ref, skip_ref, ggain_ref, ngain_ref,
    naway_ref, nhere_ref, caway_ref, chere_ref, w_ref, mine_ref, far_ref, wout_ref,
    delta_ref, layer_ref, gin_ref, gout_ref, flatout_ref,
    naway, nhere, caway, chere, w, wout, loads,
    pbuf, dbuf, dstate, par, skips, cwb, gain, w_step, sumv,
    gconv, gskip, ghead, ggain, gnorm,
    nout_all, dgate_all, dall, dssd_low, inv_own, hid_own,
    h_out, mine, y_in, kept, h_sem, y_sem, d_sem, d_put,
    omine, ofar, oy_sem, o_sem, o_put,
    ax_out, ax_in, ax_sem, az_in, az_sem, atotal,
    sx_out, sx_in, sx_sem, sz_in, sz_sem, stotal, shere,
    vx_out, vx_in, vx_sem, vz_in, vz_sem, vtotal, vhere, vbuf,
    gates, g_sem, values, v_sem, shared, shared_low, shared_all, s_sem, put_sem, flat, flat_in, f_sem,
):
    inner, heads, inner_all, lines, depth = dims
    pairs = heads // 2
    chan = inner + 2 * LANES
    width = inner + chan + LANES
    i = pl.program_id(0)
    spans = pl.num_programs(0)
    tokens = nout_all.shape[0]
    count = tokens // SPAN
    mid = count // 2
    c = count - 1 - i
    half = SPAN // 2
    model = w.shape[1]
    blocks = lines * depth // LANES
    turned = depth % LANES == 0
    rank, drank = lax.axis_index("tensor"), lax.axis_index("dp")
    line, side = drank // 2, drank % 2
    core = rank % 2
    off = pl.multiple_of(rank * inner, LANES)
    across = {"tensor": rank + 1 - 2 * core}
    beyond = {"tensor": (rank + 2) % 4}
    partner = {"dp": line * 2 + 1 - side}

    def peer(step):
        return {"dp": lax.rem(line + step, lines) * 2 + side}

    def remote(src, dst, sems, index, device):
        return pltpu.make_async_remote_copy(
            src_ref=src, dst_ref=dst, send_sem=sems.at[0, index], recv_sem=sems.at[1, index],
            device_id=device, device_id_type=MESH_IDS,
        )

    def lot(k, size):
        return pl.ds(pl.multiple_of(k * size, size), size)

    fetch = [
        pltpu.make_async_copy(src, dst, loads.at[k])
        for k, (src, dst) in enumerate(
            (
                (mine_ref, omine), (w_ref, w), (far_ref.at[pl.ds(0, half)], ofar.at[pl.ds(0, half)]),
                (far_ref.at[pl.ds(half, half)], ofar.at[pl.ds(mid * half, half)]),
                (caway_ref, caway), (naway_ref, naway), (chere_ref, chere), (nhere_ref, nhere),
                (wout_ref, wout),
            )
        )
    ]

    def oy_copy(k):
        return remote(omine.at[lot(k, half)], ofar.at[lot(k, half)], oy_sem, k, beyond)

    def my_rows(k):
        return pl.ds(pl.multiple_of(k * SPAN + core * half, half), half)

    def o_copy(k):
        return remote(omine.at[lot(k, half)], layer_ref.at[my_rows(k)], o_sem, k, across)

    def o_local(k):
        return pltpu.make_async_copy(omine.at[lot(k, half)], layer_ref.at[my_rows(k)], o_put.at[k])

    def d_copy(k):
        return remote(mine.at[lot(k, half)], delta_ref.at[my_rows(k)], d_sem, k, across)

    def d_local(k):
        return pltpu.make_async_copy(mine.at[lot(k, half)], delta_ref.at[my_rows(k)], d_put.at[k])

    def h_copy(k):
        return remote(h_out.at[lot(k % 2, half)], mine.at[lot(k, half)], h_sem, k, across)

    def y_copy(k):
        return remote(mine.at[lot(k, half)], y_in.at[lot(k, half)], y_sem, k, beyond)

    def ax_copy(k):
        return remote(ax_out.at[lot(k, LANES)], ax_in.at[lot(k, LANES)], ax_sem, k, partner)

    def sx_copy(k):
        return remote(sx_out.at[lot(k, LANES)], sx_in.at[lot(k, LANES)], sx_sem, k, partner)

    def vx_copy(k):
        return remote(vx_out.at[lot(k, LANES)], vx_in.at[lot(k, LANES)], vx_sem, k, partner)

    def az_copy(step):
        return remote(ax_out.at[pl.ds(step * depth, depth)], az_in.at[step - 1], az_sem, step - 1, peer(step))

    def sz_copy(step):
        return remote(sx_out.at[pl.ds(step * depth, depth)], sz_in.at[step - 1], sz_sem, step - 1, peer(step))

    def vz_copy(step):
        return remote(vx_out.at[pl.ds(step * depth, depth)], vz_in.at[step - 1], vz_sem, step - 1, peer(step))

    @pl.when(i == 0)
    def _():
        for copy in [fetch[-1]] + fetch[:-1]:
            copy.start()
        barrier = pltpu.get_barrier_semaphore()
        for device in [across, beyond, partner] + [peer(step) for step in range(1, lines)]:
            pl.semaphore_signal(barrier, inc=1, device_id=device, device_id_type=MESH_IDS)
        pl.semaphore_wait(barrier, lines + 2)
        fetch[-1].wait()
        pbuf[SPAN : SPAN + 8] = jnp.zeros((8, chan), F32)
        dbuf[SPAN : SPAN + 8] = jnp.full((8, LANES), -2.0, F32)
        dstate[...] = jnp.zeros(dstate.shape, F32)
        own_params(rank, heads, inner, inner_all, dtb_ref, dec_ref, skip_ref, cw_ref, cb_ref, par, skips, cwb)
        gain[0:1] = ggain_ref[:, pl.ds(off, inner)]
        for acc in (gconv, gskip, ghead, ggain, gnorm):
            acc[...] = jnp.zeros(acc.shape, F32)
        fetch[0].wait()
        for k in range(1, mid):
            oy_copy(count - k).start()
            oy_copy(mid - k).start()

    def join(k):
        h_copy(k).wait()
        mine[lot(k, half)] = (kept[lot(core, half)] + mine[lot(k, half)].astype(F32)).astype(BF16)
        y_copy(k).start()

    def out_grads(n_side, c_side, k):
        cols = lot(k, LANES)
        return jnp.concatenate(
            [tn(c_side[:, cols], nout_all[...]), tn(n_side[:, cols], dgate_all[...])], 1
        )

    per = LANES // depth

    def to_lines(k, joined, x_copy_of, x_out, z_copy_of, total):
        x_copy_of(k).wait_send()
        x_out[lot(k, LANES)] = joined.astype(BF16)
        if isinstance(k, int):
            if k == 0:
                total[...] = joined[0:depth]
            for step in range(max(1, k * per), (k + 1) * per):
                z_copy_of(step).start()

    def a_block(k):
        ax_copy(k).wait_recv()
        joined = out_grads(nhere, chere, k) + ax_in[lot(k, LANES)].astype(F32)
        to_lines(k, joined, ax_copy, ax_out, az_copy, atotal)

    def s_block(k):
        sx_copy(k).wait_recv()
        joined = shere[lot(k, LANES)] + sx_in[lot(k, LANES)].astype(F32)
        to_lines(k, joined, sx_copy, sx_out, sz_copy, stotal)

    def v_block(k):
        vx_copy(k).wait_recv()
        joined = vhere[lot(k, LANES)] + vx_in[lot(k, LANES)].astype(F32)
        to_lines(k, joined, vx_copy, vx_out, vz_copy, vtotal)

    @pl.when(i == mid)
    def _():
        for copy in fetch[2:-1]:
            copy.wait()

    hid_own[lot(c, half)] = hid_ref[lot(core, half)]

    def inverse(k):
        inv = lax.rsqrt(sums_ref[0, pl.ds(k, 1), :] * (1.0 / inner_all) + EPS)
        pull = sums_ref[1, pl.ds(k, 1), :] * (inv * inv * inv) * (1.0 / inner_all)
        inv_own[pl.ds(k, 1), :] = jnp.where(core == 0, inv[:, 0:half], inv[:, half:])
        return inv, pull

    def spread_inverse(cols, first):
        inv = jnp.broadcast_to(cols[:, first : first + 1], (SPAN, LANES))
        return inv, jnp.broadcast_to(cols[:, first + 1 : first + 2], (SPAN, LANES))

    def gating(k, scales, lanes, gate_in, ssd_in, dn_in):
        inv, pull = scales
        gate = gate_in[:, lanes]
        sig = sigmoid(gate)
        silu = gate * sig
        ssd = ssd_in[:, lanes]
        gated = ssd * silu
        dn = dn_in
        g_l = gain[0:1, lanes]
        nout = gated * inv
        nout_all[lot(k, SPAN), lanes] = (nout * g_l).astype(BF16)
        ggain[:, lanes] += fold(dn * nout)
        d_gated = dn * g_l * inv - gated * pull
        dgate_all[lot(k, SPAN), lanes] = (d_gated * ssd * (sig * (1.0 + gate * (1.0 - sig)))).astype(BF16)
        return d_gated * silu

    def finish_out(k):
        total = omine[lot(k, half)].astype(F32) + ofar[lot(k, half)].astype(F32)
        inv = as_column(inv_own[pl.ds(k, 1), :], half)
        value = hid_own[lot(k, half)].astype(F32)
        for group in range(model // LANES):
            lanes = slice(group * LANES, (group + 1) * LANES)
            omine[lot(k, half), lanes] = (value[:, lanes] + total[:, lanes] * inv).astype(BF16)
        o_copy(k).start()
        o_local(k).start()

    def scan_step(first):
        drow = docs_ref[:, lot(c, SPAN)].astype(F32)
        before = docs_ref[:, lot(jnp.maximum(c - 1, 0), SPAN)].astype(F32)
        doc = jnp.broadcast_to(drow, (heads, SPAN))
        enter = jnp.broadcast_to(before[:, SPAN - 1 :], (heads, SPAN))
        enter = jnp.where(c == 0, -1.0, enter)
        extra = []
        if first:
            row = iota((8, SPAN), 0)
            block = jnp.zeros((8, SPAN), F32)
            for k, v in enumerate(inverse(c) + inverse(c - mid)):
                block = jnp.where(row == k, jnp.broadcast_to(v, (8, SPAN)), block)
            extra = [block]
        raw = stp_ref[...] + par[0]
        log_step, run_rows, cols = head_scales(raw, par[1], doc, enter, extra)
        dcol = jnp.broadcast_to(cols[:, 4 * heads : 4 * heads + 1], (SPAN, LANES))
        if first:
            scales = spread_inverse(cols, 5 * heads)
            low_scales = spread_inverse(cols, 5 * heads + 2)
        dbuf[0:SPAN] = dcol
        keeps = [None] + [dbuf[k : k + SPAN] == dcol for k in range(1, 4)]
        row_i, col_i = iota((SPAN, SPAN), 0), iota((SPAN, SPAN), 1)
        same = jnp.concatenate([dcol, dcol], 1) == drow
        bias = jnp.where(same & (row_i <= col_i), 0.0, FAR)

        def activate(group):
            lanes = slice(group * LANES, (group + 1) * LANES)
            pre = pre_ref[:, lanes]
            sig = sigmoid(pre)
            return pre * sig, sig * (1.0 + pre * (1.0 - sig))

        b_act, b_slope = activate(pairs)
        c_act, c_slope = activate(pairs + 1)
        b_rows, c_rows = b_act.astype(BF16), c_act.astype(BF16)
        c_turned = jnp.transpose(c_act).astype(BF16)
        scores = exact_nt(b_act, c_act)
        low_half = iota((SPAN, LANES), 1) < LANES // 2
        d_scores = [jnp.zeros((half, SPAN), F32), jnp.zeros((half, half), F32)]
        d_b = jnp.zeros((SPAN, LANES), F32)
        d_c = jnp.zeros((SPAN, LANES), F32)
        holds = []
        for pair in range(pairs):
            lanes = slice(pair * LANES, (pair + 1) * LANES)
            act, slope = activate(pair)
            step_l = pair_lanes(cols, heads + 2 * pair, low_half)
            tail_l = pair_lanes(cols, 2 * heads + 2 * pair, low_half)
            reach_l = pair_lanes(cols, 3 * heads + 2 * pair, low_half)
            skip_l = pair_lanes(skips[0:1], 2 * pair, low_half[0:1])
            ssd = ssd_ref[:, lanes]
            if first:
                if pair % 2 == 0:
                    both = slice(pair * LANES, (pair + 2) * LANES)
                    dn_both, dn_low_both = nn(cot_ref[...], wout[:, both]), nn(cot_low_ref[...], wout[:, both])
                side_lanes = slice(pair % 2 * LANES, (pair % 2 + 1) * LANES)
                d_ssd = gating(c, scales, lanes, gate_ref, ssd_ref, dn_both[:, side_lanes])
                dssd_low[lot(c - mid, SPAN), lanes] = gating(
                    c - mid, low_scales, lanes, gate_low_ref, ssd_low_ref, dn_low_both[:, side_lanes]
                )
            else:
                d_ssd = dssd_low[lot(c, SPAN), lanes]
            gskip[:, lanes] += fold(d_ssd * act)
            dyb = d_ssd.astype(BF16)
            scaled = act * step_l
            xb = scaled.astype(BF16)
            held = state_ref[0, :, lanes]
            d_held = dstate[:, lanes]
            d_held_b = d_held.astype(BF16)
            ry = (d_ssd * reach_l).astype(BF16)
            xt = (scaled * tail_l).astype(BF16)
            parts = []
            for sub in range(2):
                head = 2 * pair + sub
                x_own = jnp.where(low_half if sub == 0 else ~low_half, scaled, 0.0).astype(BF16)
                tiles = []
                for blk in range(2):
                    rows = slice(blk * half, (blk + 1) * half)
                    span = slice(blk * half, SPAN)
                    gap = run_rows[head : head + 1, span] - cols[rows, head : head + 1]
                    decay = jnp.exp2(gap + bias[rows, span])
                    tiles.append(nn((decay * scores[rows, span]).astype(BF16), dyb[span]))
                    d_scores[blk] = d_scores[blk] + decay * nt(x_own[rows], dyb[span])
                parts.append(jnp.concatenate(tiles, 0))
            d_within = jnp.where(low_half, parts[0], parts[1])
            from_state = tail_l * nn(b_rows, d_held_b)
            d_scaled = d_within + from_state
            xf = xb.astype(F32)
            up = dyb.astype(F32) * (ssd - skip_l * act) - xf * d_within
            up_hi = up.astype(BF16)
            sumv[0, :, lanes] = up_hi
            sumv[1, :, lanes] = (up - up_hi.astype(F32)).astype(BF16)
            sumv[2, :, lanes] = (xf * from_state).astype(BF16)
            sumv[3, :, lanes] = (d_scaled * act).astype(BF16)
            hold = reach_l[SPAN - 1 : SPAN]
            held_sum = jnp.sum((d_held * held.astype(F32)).reshape(LANES // 8, 8, LANES), axis=0)
            holds.append(jnp.sum(held_sum, axis=0, keepdims=True) * hold)
            d_b += nt(xt, d_held_b)
            d_c += nt(ry, held)
            dstate[:, lanes] = hold * d_held + nn(c_turned, ry)
            pbuf[0:SPAN, lanes] = (skip_l * d_ssd + step_l * d_scaled) * slope

        ds_b = jnp.concatenate(
            [
                d_scores[0],
                jnp.concatenate([jnp.zeros((half, half), F32), d_scores[1]], 1),
            ],
            0,
        )
        d_b += nn(ds_b.astype(BF16), c_rows)
        d_c += nn(jnp.transpose(ds_b).astype(BF16), b_rows)
        pbuf[0:SPAN, inner : inner + LANES] = d_b * b_slope
        pbuf[0:SPAN, inner + LANES : chan] = d_c * c_slope

        per_head = inner // heads
        owner = (iota((2 * heads, inner), 0) == iota((2 * heads, inner), 1) // per_head).astype(BF16)
        up = (nt(owner, sumv[0]) + nt(owner, sumv[1]))[0:heads]
        down = nt(owner, sumv[2])[0:heads]
        direct = nt(owner, sumv[3])[0:heads]
        hold_row = jnp.broadcast_to(jnp.concatenate(holds, 1), (heads, inner))
        inside = iota((heads, inner), 0) == iota((heads, inner), 1) // per_head
        hold_sum = jnp.sum(jnp.where(inside, hold_row, 0.0), axis=1, keepdims=True)
        d_log = (
            row_sum(up, (row_i >= col_i).astype(BF16))
            + row_sum(down, (row_i < col_i).astype(BF16))
            + jnp.broadcast_to(hold_sum, (heads, SPAN))
        )
        d_raw = (d_log * par[1] + direct) * sigmoid(raw)
        turned = jnp.transpose(jnp.concatenate([d_raw, jnp.zeros((LANES - heads, SPAN), F32)], 0))
        dall[lot(c, SPAN), chan:] = turned.astype(BF16)
        ghead[0] += d_raw
        ghead[1] += d_log * log_step

        for group in range(chan // LANES):
            lanes = slice(group * LANES, (group + 1) * LANES)
            mixed = mixed_ref[:, lanes]
            own = pbuf[0:SPAN, lanes]
            acc = cwb[3:4, lanes] * own
            gconv[3, :, lanes] += fold(mixed * own)
            gconv[4, :, lanes] += fold(own)
            for k in range(1, 4):
                later = jnp.where(keeps[k], pbuf[k : k + SPAN, lanes], 0.0)
                acc = acc + cwb[3 - k : 4 - k, lanes] * later
                gconv[3 - k, :, lanes] += fold(mixed * later)
            dall[lot(c, SPAN), lanes] = acc.astype(BF16)
        pbuf[SPAN : SPAN + 8] = pbuf[0:8]
        dbuf[SPAN : SPAN + 8] = dbuf[0:8]

    @pl.when(i < mid)
    def _():
        scan_step(True)

    @pl.when(i >= mid)
    def _():
        block = lax.rem(i - mid + 1, blocks)
        ax_out[lot(block, LANES)] = out_grads(naway, caway, block).astype(BF16)
        ax_copy(block).start()
        scan_step(False)

    @pl.when(i > 0)
    def _():
        join(c + 1)

    order = tuple(range(1, blocks)) + (0,)
    for k in range(blocks - 2):
        @pl.when(i == mid + 1 + k)
        def _():
            a_block(order[k])

    @pl.when(i == 0)
    def _():
        fetch[1].wait()
        both_cores = w[inner + chan : inner + chan + 2 * heads].astype(F32)
        own = jnp.where(core == 0, both_cores[0:heads], both_cores[heads:])
        w_step[...] = jnp.concatenate([own, jnp.zeros((LANES - heads, model), F32)], 0).astype(BF16)

    def share_span():
        rows_now = lot(c, SPAN)
        kept[...] = (
            nn(dgate_all[rows_now], w[0:inner])
            + nn(dall[rows_now, 0:chan], w[inner : inner + chan])
            + nn(dall[rows_now, chan:], w_step[...])
        )
        h_out[lot(c % 2, half)] = kept[lot(1 - core, half)].astype(BF16)
        h_copy(c).start()
        value = hid_ref[...].astype(F32)
        unit = value * lax.rsqrt(jnp.mean(value * value, -1, keepdims=True) + EPS)
        gnorm[...] += fold(kept[...] * unit)

    @pl.when(i < count - 1)
    def _():
        share_span()

    @pl.when(i == count - 1)
    def _():
        sx_out[...] = tn(naway[...], dall[:, inner:]).astype(BF16)
        for k in order:
            sx_copy(k).start()
        share_span()
        chan_all = inner_all + 2 * LANES
        tap_rows, own_rows = chan_all // LANES, inner // LANES
        flat[...] = jnp.zeros(flat.shape, F32)
        norm = jnp.sum(gnorm[...], axis=0, keepdims=True)
        at = model // LANES
        for k in range(at):
            flat[k : k + 1] = norm[:, k * LANES : (k + 1) * LANES]
        for tap in range(gconv.shape[0]):
            row = jnp.sum(gconv[tap], axis=0, keepdims=True)
            for k in range(chan // LANES):
                place = at + k + (rank * own_rows if k < own_rows else (tap_rows - chan // LANES))
                flat[pl.ds(place, 1), :] = row[:, k * LANES : (k + 1) * LANES]
            at += tap_rows
        spread = jnp.zeros((1, LANES), F32)
        for k in range(2):
            total = jnp.broadcast_to(jnp.sum(ghead[k], axis=1, keepdims=True), (heads, LANES))
            place = iota((heads, LANES), 1) == 4 * heads * k + rank * heads + iota((heads, LANES), 0)
            spread = spread + jnp.sum(jnp.where(place, total, 0.0), axis=0, keepdims=True)
        flat[at : at + 1] = spread
        at += 1
        for acc in (ggain, gskip):
            row = jnp.sum(acc[...], axis=0, keepdims=True)
            for k in range(own_rows):
                flat[pl.ds(at + rank * own_rows + k, 1), :] = row[:, k * LANES : (k + 1) * LANES]
            at += inner_all // LANES

        hops = [partner]
        bit = 1
        while bit < lines:
            hops.append({"dp": (line + bit * (1 - 2 * ((line // bit) % 2))) * 2 + side})
            bit *= 2
        hops += [across, beyond]
        last = flat_in.shape[0] - 1

        def flat_copy(k):
            return remote(
                flat.at[...] if k == 0 else flat_in.at[len(hops) + k], flat_in.at[k], f_sem, k, hops[k]
            )

        def flat_step(k):
            flat_copy(k).wait_recv()
            held = (flat[...] if k == 0 else flat_in[len(hops) + k]) + flat_in[k]
            if k + 1 < len(hops):
                flat_in[len(hops) + k + 1] = held
                flat_copy(k + 1).start()
            else:
                flat_in[last] = held

        flat_copy(0).start()
        vx_out[LANES:] = tn(naway[:, LANES:], dall[:, 0:inner]).astype(BF16)
        for k in order[:-1]:
            vx_copy(k).start()
        vx_out[0:LANES] = tn(naway[:, 0:LANES], dall[:, 0:inner]).astype(BF16)
        vx_copy(0).start()
        a_block(order[-2])
        flat_step(0)
        join(0)
        for k in range(count):
            if k % mid:
                oy_copy(k).wait()

        def out_rows(k, carry):
            finish_out(k)
            return carry

        lax.fori_loop(0, count, out_rows, 0)

        a_block(order[-1])
        for k in range(1, len(hops) - 2):
            flat_step(k)
        gain_row = ngain_ref[...]

        def finish_hidden(k, carry):
            y_copy(k).wait_recv()
            y_copy(k).wait_send()
            d_hidden = mine[lot(k, half)].astype(F32) + y_in[lot(k, half)].astype(F32)
            value = hid_own[lot(k, half)].astype(F32)
            inv = lax.rsqrt(jnp.mean(value * value, -1, keepdims=True) + EPS)
            scaled = d_hidden * gain_row
            pull = jnp.mean(scaled * value, -1, keepdims=True)
            mine[lot(k, half)] = (inv * scaled - value * (inv * inv * inv) * pull).astype(BF16)
            d_copy(k).start()
            d_local(k).start()
            return carry

        def down(k, carry):
            return finish_hidden(count - 1 - k, carry)

        shere[...] = tn(nhere[...], dall[:, inner:])
        for k in order:
            s_block(k)
        vhere[...] = tn(nhere[...], dall[:, 0:inner])
        lax.fori_loop(0, 3, down, 0)
        for k in order[:-1]:
            v_block(k)
        flat_step(len(hops) - 2)
        for step in range(1, lines):
            az_copy(step).wait_recv()
            atotal[...] += az_in[step - 1].astype(F32)
        gates[0] = atotal[:, inner:].astype(BF16)
        gout_put = pltpu.make_async_copy(atotal.at[:, pl.ds(0, inner)], gout_ref, put_sem.at[9])
        gout_put.start()
        gate_near = remote(gates.at[0], gates.at[1], g_sem, 0, across)
        gate_far = remote(gates.at[0], gates.at[2], g_sem, 1, beyond)
        gate_pass = remote(gates.at[2], gates.at[3], g_sem, 2, across)
        gate_near.start()
        gate_far.start()
        for step in range(1, lines):
            sz_copy(step).wait_recv()
            stotal[...] += sz_in[step - 1].astype(F32)
        shared_near = remote(shared.at[0], shared.at[1], s_sem, 0, across)
        shared_far = remote(shared_low.at[0], shared_low.at[1], s_sem, 1, beyond)
        shared[0, :, 0 : 2 * LANES] = stotal[:, 0 : 2 * LANES]
        steps = pltpu.roll(stotal[:, 2 * LANES :], rank * heads, 1)
        place = iota(steps.shape, 1) - rank * heads
        shared[0, :, 2 * LANES :] = jnp.where((place >= 0) & (place < heads), steps, 0.0)
        shared_near.start()
        v_block(order[-1])
        lax.fori_loop(3, 6, down, 0)
        shared_near.wait_recv()
        shared_low[0] = (shared[0] + shared[1]).astype(BF16)
        shared_far.start()
        gate_far.wait_recv()
        gate_pass.start()
        flat_step(len(hops) - 1)
        flat_put = pltpu.make_async_copy(flat_in.at[last], flatout_ref, put_sem.at[10])
        flat_put.start()
        lax.fori_loop(6, count, down, 0)

        for step in range(1, lines):
            vz_copy(step).wait_recv()
            vtotal[...] += vz_in[step - 1].astype(F32)
        values[0] = vtotal[...].astype(BF16)
        value_near = remote(values.at[0], values.at[1], v_sem, 0, across)
        value_far = remote(values.at[0], values.at[2], v_sem, 1, beyond)
        value_pass = remote(values.at[2], values.at[3], v_sem, 2, across)
        value_far.start()
        value_near.start()

        def put(source, k, first, owner, index):
            column = pl.multiple_of(first + owner * inner, LANES)
            columns = pl.ds(column, inner)
            dst = gin_ref.at[columns] if turned else gin_ref.at[:, columns]
            return pltpu.make_async_copy(source.at[k], dst, put_sem.at[index])

        def shown(v):
            return jnp.transpose(v) if turned else v

        owners = (rank, rank + 1 - 2 * core, (rank + 2) % 4, (rank + 3 - 2 * core) % 4)
        gate_near.wait_recv()
        gate_pass.wait_recv()
        gate_puts = [put(vbuf, k, 0, owners[k], k) for k in range(4)]
        for k in range(4):
            vbuf[k] = shown(gates[k].astype(F32))
            gate_puts[k].start()
        shared_far.wait_recv()
        shared_all[...] = shown(shared_low[0].astype(F32) + shared_low[1].astype(F32))
        shared_columns = pl.ds(2 * inner_all, 3 * LANES)
        puts = [
            pltpu.make_async_copy(
                shared_all, gin_ref.at[shared_columns] if turned else gin_ref.at[:, shared_columns], put_sem.at[8]
            )
        ]
        puts[0].start()
        for copy in gate_puts:
            copy.wait()

        def put_values(k):
            vbuf[k] = shown(values[k].astype(F32))
            puts.append(put(vbuf, k, inner_all, owners[k], 4 + k))
            puts[-1].start()

        put_values(0)
        value_near.wait_recv()
        put_values(1)
        value_far.wait_recv()
        value_pass.start()
        put_values(2)
        value_pass.wait_recv()
        put_values(3)

        def drain(k, carry):
            d_copy(k).wait()
            d_local(k).wait()
            o_copy(k).wait()
            o_local(k).wait()
            return carry

        lax.fori_loop(0, count, drain, 0)
        for step in range(1, lines):
            az_copy(step).wait_send()
            sz_copy(step).wait_send()
            vz_copy(step).wait_send()
        for copy in (
            gate_near, gate_far, gate_pass, value_near, value_far, value_pass, shared_near, shared_far,
        ):
            copy.wait_send()
        for k in range(len(hops)):
            flat_copy(k).wait_send()
        for copy in puts + [gout_put, flat_put]:
            copy.wait()


def mixer_backward(
    docs, hidden, cotangent, held, sums, params, ggain, ngain, sorted_parts, w_in, mine, far, w_out,
    heads, lines, depth,
):
    gate, mixed, pre, ssd, stp, states = held
    tokens, inner = ssd.shape
    model = hidden.shape[1]
    chan = inner + 2 * LANES
    width = inner + chan + LANES
    wide = width - inner
    inner_all = ggain.shape[1]
    turned = depth % LANES == 0
    columns = 2 * inner_all + 3 * LANES
    count = tokens // SPAN
    mid = count // 2
    half = SPAN // 2
    blocks, fars = lines * depth // LANES, max(1, lines - 1)
    hops = 3 + (lines - 1).bit_length()
    rows = (model + 5 * (inner_all + 2 * LANES) + LANES + 2 * inner_all) // LANES
    rows += -rows % 8

    def tok(size):
        return pl.BlockSpec((SPAN, size), lambda i: (count - 1 - i, 0))

    def early_tok(size, base):
        return pl.BlockSpec((SPAN, size), lambda i: (base + (mid - 1 - i) * (1 - i // mid), 0))

    def full(shape):
        return pl.BlockSpec(shape, lambda i: (0,) * len(shape))

    anywhere = pl.BlockSpec(memory_space=pl.ANY)
    dma, vmem = pltpu.SemaphoreType.DMA, pltpu.VMEM
    consts = params + (ggain, ngain)
    big = tuple(sorted_parts)[0:2] + tuple(sorted_parts)[2:4] + (w_in, mine, far, w_out)
    side_shape = (tokens, lines * depth)
    return pl.pallas_call(
        lambda *refs: backward_kernel((inner, heads, inner_all, lines, depth), *refs),
        out_shape=(
            jax.ShapeDtypeStruct((tokens, model), BF16),
            jax.ShapeDtypeStruct((tokens, model), BF16),
                jax.ShapeDtypeStruct((columns, depth) if turned else (depth, columns), F32),
            jax.ShapeDtypeStruct((depth, inner), F32),
            jax.ShapeDtypeStruct((rows, LANES), F32),
        ),
        grid=(count,),
        in_specs=[
            full(docs.shape), tok(model), early_tok(inner, mid), early_tok(model, mid),
            early_tok(inner, 0), early_tok(inner, 0), early_tok(model, 0),
            tok(inner), tok(chan), tok(chan), pl.BlockSpec((heads, SPAN), lambda i: (0, count - 1 - i)),
            pl.BlockSpec((1, LANES, inner), lambda i: (count - 1 - i, 0, 0)),
            full(sums.shape),
        ]
        + [full(v.shape) for v in consts]
        + [anywhere] * len(big),
        out_specs=(anywhere,) * 5,
        scratch_shapes=[
            vmem(side_shape, BF16), vmem(side_shape, BF16), vmem(side_shape, BF16), vmem(side_shape, BF16),
            vmem(w_in.shape, BF16), vmem(w_out.shape, BF16), dma((len(big) + 1,)),
            vmem((SPAN + 8, chan), F32), vmem((SPAN + 8, LANES), F32), vmem((LANES, inner), F32),
            vmem((2, heads, SPAN), F32), vmem((8, LANES), F32), vmem((8, chan), F32), vmem((8, inner), F32),
            vmem((LANES, model), BF16), vmem((4, SPAN, inner), BF16),
            vmem((5, 8, chan), F32), vmem((8, inner), F32), vmem((2, heads, SPAN), F32),
            vmem((8, inner), F32), vmem((8, model), F32),
            vmem((tokens, inner), BF16), vmem((tokens, inner), BF16), vmem((tokens, wide), BF16),
            vmem((tokens // 2, inner), F32), vmem((count, LANES), F32),
            vmem((tokens // 2, model), BF16),
            vmem((SPAN, model), BF16), vmem((tokens // 2, model), BF16),
            vmem((tokens // 2, model), BF16), vmem((SPAN, model), F32),
            dma((2, count)), dma((2, count)), dma((2, count)), dma((count,)),
            vmem((tokens // 2, model), BF16), vmem((tokens // 2, model), BF16),
            dma((2, count)), dma((2, count)), dma((count,)),
            vmem((blocks * LANES, 2 * inner), BF16), vmem((blocks * LANES, 2 * inner), BF16),
            dma((2, blocks)), vmem((fars, depth, 2 * inner), BF16), dma((2, fars)),
            vmem((depth, 2 * inner), F32),
            vmem((blocks * LANES, 3 * LANES), BF16), vmem((blocks * LANES, 3 * LANES), BF16),
            dma((2, blocks)), vmem((fars, depth, 3 * LANES), BF16), dma((2, fars)),
            vmem((depth, 3 * LANES), F32), vmem((blocks * LANES, 3 * LANES), F32),
            vmem((blocks * LANES, inner), BF16), vmem((blocks * LANES, inner), BF16),
            dma((2, blocks)), vmem((fars, depth, inner), BF16), dma((2, fars)), vmem((depth, inner), F32),
            vmem((blocks * LANES, inner), F32), vmem((4, inner, depth) if turned else (4, depth, inner), F32),
            vmem((4, depth, inner), BF16), dma((2, 3)), vmem((4, depth, inner), BF16), dma((2, 3)),
            vmem((2, depth, 3 * LANES), F32), vmem((2, depth, 3 * LANES), BF16),
            vmem((3 * LANES, depth) if turned else (depth, 3 * LANES), F32), dma((2, 2)), dma((11,)),
            vmem((rows, LANES), F32), vmem((2 * hops + 1, rows, LANES), F32), dma((2, hops)),
        ],
        compiler_params=pltpu.CompilerParams(
            dimension_semantics=("arbitrary",), vmem_limit_bytes=67043328,
            collective_id=1, has_side_effects=True,
        ),
        cost_estimate=cost(90.0),
        name="mixer_backward",
    )(
        docs, hidden, gate, cotangent, gate, ssd, cotangent, ssd, mixed, pre, stp, states, sums, *consts, *big
    )


def finish_kernel(
    dims, cot_ref, delta_ref, layer_ref, gin_ref, flat_ref,
    out_ref, grad_ref, norm_ref, win_ref, taps_ref, bias_ref, dt_ref, decay_ref, skip_ref, gain_ref,
):
    inner_all, heads, turned = dims
    grad_ref[...] = cot_ref[...].astype(F32) + delta_ref[...].astype(F32)
    out_ref[...] = layer_ref[...]
    win_ref[...] = gin_ref[...] if turned else gin_ref[:, 0 : win_ref.shape[1]]

    @pl.when(pl.program_id(0) == 0)
    def _():
        at = norm_ref.shape[1] // LANES

        def spread(dst, row, first, count):
            for k in range(count):
                dst[row : row + 1, k * LANES : (k + 1) * LANES] = flat_ref[first + k : first + k + 1]

        spread(norm_ref, 0, 0, at)
        wide = taps_ref.shape[1] // LANES
        for tap in range(taps_ref.shape[0]):
            spread(taps_ref, tap, at + tap * wide, wide)
        at += taps_ref.shape[0] * wide
        bias_ref[...] = flat_ref[at : at + wide]
        at += wide
        dt_ref[...] = flat_ref[at : at + 1, 0:heads]
        decay_ref[...] = flat_ref[at : at + 1, heads : 2 * heads]
        at += 1
        spread(gain_ref, 0, at, inner_all // LANES)
        at += inner_all // LANES
        per = inner_all // heads
        lane = iota((1, LANES), 1)
        found = jnp.zeros((1, LANES), F32)
        for k in range(inner_all // LANES):
            row = flat_ref[at + k : at + k + 1]
            for part in range(LANES // per):
                inside = (lane >= part * per) & (lane < (part + 1) * per)
                total = jnp.sum(jnp.where(inside, row, 0.0), axis=1, keepdims=True)
                found = jnp.where(lane == k * (LANES // per) + part, total, found)
        skip_ref[...] = found[:, 0:heads]


def finish(cotangent, delta, layer_out, grad_in, flat, columns, inner_all, heads, turned):
    tokens, model = cotangent.shape
    depth = grad_in.shape[1] if turned else grad_in.shape[0]
    steps = 2
    chan_all = inner_all + 2 * LANES

    def tok(v, size):
        return pl.BlockSpec((v // steps, size), lambda i: (i, 0))

    def full(shape):
        return pl.BlockSpec(shape, lambda i: (0,) * len(shape))

    small = [(1, model), (4, chan_all), (chan_all // LANES, LANES), (1, heads), (1, heads), (1, heads), (1, inner_all)]
    if turned:
        cut = grad_in.shape[0] // steps
        rows = shown = pl.BlockSpec((cut, grad_in.shape[1]), lambda i: (i, 0))
    else:
        rows, shown = full(grad_in.shape), full((depth, columns))
    return pl.pallas_call(
        lambda *refs: finish_kernel((inner_all, heads, turned), *refs),
        out_shape=[
            jax.ShapeDtypeStruct((tokens, model), BF16),
            jax.ShapeDtypeStruct((tokens, model), F32),
            jax.ShapeDtypeStruct(small[0], F32),
            jax.ShapeDtypeStruct((columns, depth) if turned else (depth, columns), F32),
        ]
        + [jax.ShapeDtypeStruct(v, F32) for v in small[1:]],
        grid=(steps,),
        in_specs=[tok(tokens, model)] * 3 + [rows, full(flat.shape)],
        out_specs=[tok(tokens, model)] * 2 + [full(small[0]), shown] + [full(v) for v in small[1:]],
        compiler_params=pltpu.CompilerParams(dimension_semantics=("arbitrary",)),
        cost_estimate=cost(9.0),
        name="finish",
    )(cotangent, delta, layer_out, grad_in, flat)


def gather_kernel(
    dims, hid_ref, cot_ref, ngain_ref, w_ref, step_ref, wo_ref,
    win_ref, *refs,
):
    lines, depth, inner, inner_all, heads, turned = dims
    wout_ref = None if turned else refs[0]
    refs = refs[0 if turned else 1 :]
    normed_ref, refs = refs[0], refs[1:]
    outs = refs[:4] if turned else ()
    mine, zsend, zrecv, xsend, xrecv, takes, puts, qsend, qrecv = refs[len(outs):]
    trank, drank = lax.axis_index("tensor"), lax.axis_index("dp")
    line, side = drank // 2, drank % 2
    core = trank % 2
    model = hid_ref.shape[1]
    off = pl.multiple_of(trank * inner, LANES)
    base = 2 * inner_all
    if turned:
        quarter = 2 * LANES // 4
        own_quarter = pl.multiple_of(trank * quarter, quarter)
        chip = 2 * heads
        steps = pl.multiple_of(base + 2 * LANES + (trank // 2) * chip, chip)
        cut = inner // 2
        pieces = [
            (w_ref, base + own_quarter, win_ref, 2 * inner + own_quarter, quarter),
            (w_ref, steps, win_ref, 2 * inner + 2 * LANES, chip),
        ]
        pieces += [(w_ref, inner_all + off + k * cut, win_ref, inner + k * cut, cut) for k in range(2)]
        pieces += [(w_ref, off + k * LANES, win_ref, k * LANES, LANES) for k in range(inner // LANES)]
    else:
        pieces = [
            (w_ref, inner_all + off, win_ref, inner, inner),
            (w_ref, base, win_ref, 2 * inner, 2 * LANES),
            (step_ref, 0, win_ref, 2 * inner + 2 * LANES, LANES),
            (w_ref, off, win_ref, 0, inner),
            (wo_ref, 0, wout_ref, 0, inner),
        ]

    def peer(step):
        return {"dp": lax.rem(line + step, lines) * 2 + side}

    partner = {"dp": line * 2 + 1 - side}
    family = (
        {"tensor": trank + 1 - 2 * core}, {"tensor": (trank + 2) % 4},
        {"tensor": (trank + 3 - 2 * core) % 4},
    )
    others = [partner] + [peer(step) for step in range(1, lines)] + (list(family) if turned else [])
    barrier = pltpu.get_barrier_semaphore()
    for device in others:
        pl.semaphore_signal(barrier, inc=1, device_id=device, device_id_type=MESH_IDS)
    pl.semaphore_wait(barrier, len(others))

    def lanes_of(index):
        return pl.ds(pl.multiple_of(index * depth, depth), depth)

    def in_rows(p):
        return turned and pieces[p][0] is w_ref

    def block(p, index):
        _, _, dst, at, width = pieces[p]
        if in_rows(p):
            return dst.at[pl.ds(at, width), lanes_of(index)]
        return dst.at[lanes_of(index), pl.ds(at, width)]

    def own(p):
        src, at, _, _, width = pieces[p]
        return src.at[pl.ds(at, width)] if in_rows(p) else src.at[:, pl.ds(at, width)]

    def z_copy(p, step, src, index):
        return pltpu.make_async_remote_copy(
            src_ref=src, dst_ref=block(p, index), send_sem=zsend.at[p, step - 1],
            recv_sem=zrecv.at[p, step - 1], device_id=peer(step), device_id_type=MESH_IDS,
        )

    def x_copy(p, step, src, index):
        return pltpu.make_async_remote_copy(
            src_ref=src, dst_ref=block(p, index), send_sem=xsend.at[p, step],
            recv_sem=xrecv.at[p, step], device_id=partner, device_id_type=MESH_IDS,
        )

    count = len(pieces)
    for p in range(count):
        for step in range(1, lines):
            z_copy(p, step, own(p), drank).start()
        x_copy(p, 0, own(p), drank).start()
    spots, at = [], 0
    for p in range(count):
        width = pieces[p][4]
        if in_rows(p):
            spots.append(mine.at[pl.ds(at, width), pl.ds(0, depth)])
            at += width
        elif turned:
            spots.append(mine.at[pl.ds(at, depth), pl.ds(0, width)])
            at += depth
        else:
            spots.append(mine.at[:, pl.ds(at, width)])
            at += width
    fetched = [pltpu.make_async_copy(own(p), spots[p], takes.at[p]) for p in range(count)]
    for copy in fetched:
        copy.start()

    gain = ngain_ref[...]

    def normalize(hid, cot, normed, *sorted_refs):
        value = hid[...].astype(F32)
        inv = lax.rsqrt(jnp.mean(value * value, -1, keepdims=True) + EPS)
        normed[...] = (value * inv * gain).astype(BF16)
        if turned:
            for src, away, here in (
                (normed, sorted_refs[0], sorted_refs[1]), (cot, sorted_refs[2], sorted_refs[3]),
            ):
                for j in range(lines):
                    first = lax.rem(line + j, lines) * 2
                    lanes = slice(j * depth, (j + 1) * depth)
                    away[:, lanes] = src[:, lanes_of(first + 1 - side)]
                    here[:, lanes] = src[:, lanes_of(first + side)]

    full = pl.BlockSpec((SPAN, model), lambda i: (i, 0))
    half = pl.BlockSpec((SPAN, lines * depth), lambda i: (i, 0))
    pltpu.emit_pipeline(
        normalize, grid=(hid_ref.shape[0] // SPAN,), in_specs=[full, full],
        out_specs=[full] + [half] * len(outs),
    )(hid_ref, cot_ref, normed_ref, *outs)

    stored = [pltpu.make_async_copy(spots[p], block(p, drank), puts.at[p]) for p in range(count)]
    for p in range(count):
        fetched[p].wait()
        stored[p].start()

    def source_line(step):
        return lax.rem(line - step + lines, lines) * 2

    def x_arrived(p):
        for step in range(lines):
            source = source_line(step) + 1 - side
            x_copy(p, step, block(p, source), source).wait_recv()

    def quarter_copy(k, device):
        rows = win_ref.at[pl.ds(2 * inner + own_quarter, quarter)]
        return pltpu.make_async_remote_copy(
            src_ref=rows, dst_ref=rows, send_sem=qsend.at[k], recv_sem=qrecv.at[k],
            device_id=device, device_id_type=MESH_IDS,
        )

    def quarter_from(k, owner):
        rows = win_ref.at[pl.ds(pl.multiple_of(2 * inner + owner * quarter, quarter), quarter)]
        return pltpu.make_async_remote_copy(
            src_ref=rows, dst_ref=rows, send_sem=qsend.at[k], recv_sem=qrecv.at[k],
            device_id=family[k], device_id_type=MESH_IDS,
        )

    for p in range(count):
        for step in range(1, lines):
            source = source_line(step) + side
            got = block(p, source)
            z_copy(p, step, got, source).wait_recv()
            x_copy(p, step, got, source).start()
        if turned and p == 3:
            stored[0].wait()
            x_arrived(0)
            for k in range(3):
                quarter_copy(k, family[k]).start()
    for p in range(1 if turned else 0, count):
        x_arrived(p)
    if turned:
        owners = (trank + 1 - 2 * core, (trank + 2) % 4, (trank + 3 - 2 * core) % 4)
        for k in range(3):
            quarter_from(k, owners[k]).wait_recv()
            quarter_copy(k, family[k]).wait_send()
    for p in range(count):
        for step in range(1, lines):
            z_copy(p, step, own(p), drank).wait_send()
        for step in range(lines):
            x_copy(p, step, own(p), drank).wait_send()
        if not (turned and p == 0):
            stored[p].wait()


def gather_weights(
    hidden, cotangent, norm_gain, in_weight, own_step, out_weight, lines, inner_all, heads, turned
):
    tokens, model = hidden.shape
    depth, inner = out_weight.shape
    half = jax.ShapeDtypeStruct((tokens, lines * depth), BF16)
    anywhere = pl.BlockSpec(memory_space=pl.ANY)
    rows = 2 * inner + 2 * LANES + 2 * heads
    width = 2 * inner + 3 * LANES
    count = 4 + inner // LANES if turned else 5
    outs = (
        (jax.ShapeDtypeStruct((rows, model) if turned else (model, width), BF16),)
        + (() if turned else (jax.ShapeDtypeStruct((model, inner), BF16),))
        + (jax.ShapeDtypeStruct((tokens, model), BF16),)
        + (half,) * (4 if turned else 0)
    )
    dma = pltpu.SemaphoreType.DMA
    held = (rows, LANES) if turned else (depth, width + inner)
    fars = max(1, lines - 1)
    return pl.pallas_call(
        lambda *refs: gather_kernel((lines, depth, inner, inner_all, heads, turned), *refs),
        out_shape=outs,
        in_specs=[anywhere, anywhere, pl.BlockSpec(memory_space=pltpu.VMEM)] + [anywhere] * 3,
        out_specs=(anywhere,) * len(outs),
        scratch_shapes=[
            pltpu.VMEM(held, BF16),
            dma((count, fars)), dma((count, fars)), dma((count, lines)), dma((count, lines)),
            dma((count,)), dma((count,)), dma((3,)), dma((3,)),
        ],
        compiler_params=pltpu.CompilerParams(collective_id=0, has_side_effects=True),
        cost_estimate=cost(45.0),
        name="gather_weights",
    )(hidden, cotangent, norm_gain, in_weight, own_step, out_weight)


def body(
    hidden_in, doc_ids, cotangent, norm_gain, in_weight, conv_weight, conv_bias,
    dt_bias, log_decay, skip_gain, gate_gain, out_weight,
):
    tcount, dcount = lax.axis_size("tensor"), lax.axis_size("dp")
    trank, drank = lax.axis_index("tensor"), lax.axis_index("dp")
    lines = dcount // 2
    line, side = drank // 2, drank % 2
    inner_all, head_all = gate_gain.shape[0], dt_bias.shape[0]
    inner, heads = inner_all // tcount, head_all // tcount
    tokens, model = hidden_in.shape
    base_bc = 2 * inner_all
    base_dt = base_bc + 2 * LANES
    depth = in_weight.shape[0]

    def line_to(step):
        return lambda k: ((k // 2 + step) % lines) * 2 + k % 2

    turned = depth % LANES == 0
    if turned:
        weight_in = own_step = in_weight.T
    else:
        weight_in = in_weight
        own_step = jnp.pad(
            lax.dynamic_slice_in_dim(in_weight, base_dt + trank * heads, heads, 1),
            ((0, 0), (0, LANES - heads)),
        )
    w_in, *rest = gather_weights(
        hidden_in, cotangent, norm_gain.reshape(1, -1), weight_in, own_step,
        out_weight, lines, inner_all, heads, turned,
    )
    w_out, rest = (out_weight, rest) if turned else (rest[0], rest[1:])
    normed, *sorted_parts = rest
    if not turned:
        pair = lax.dynamic_update_slice_in_dim(
            jnp.zeros((2 * heads, model), BF16),
            w_in[:, 2 * inner + 2 * LANES :][:, :heads].T, trank % 2 * heads, 0,
        )
        w_in = jnp.concatenate([w_in[:, : 2 * inner + 2 * LANES].T, pair], 0)
    if not sorted_parts:

        def features(v, which):
            return jnp.concatenate(
                [
                    lax.dynamic_slice_in_dim(v, (((line + j) % lines) * 2 + which) * depth, depth, 1)
                    for j in range(lines)
                ],
                1,
            )

        sorted_parts = [features(v, which) for v in (normed, cotangent) for which in (1 - side, side)]
    n_away, n_here, c_away, c_here = sorted_parts

    def row(v):
        return v.reshape(1, -1)

    params = (conv_weight, conv_bias.reshape(-1, LANES), row(dt_bias), row(log_decay), row(skip_gain))

    *held, sums, mine, far, w_full = mixer_forward(
        doc_ids, normed, cotangent, w_in, w_out, params, row(gate_gain), heads, lines, turned
    )
    delta, layer_out, grad_in, g_out, flat = mixer_backward(
        doc_ids, hidden_in, cotangent, held, sums, params, row(gate_gain), row(norm_gain), sorted_parts, w_in,
        mine, far, w_full, heads, lines, depth,
    )
    layer_out, grad_input, g_norm, grad_in_weight, taps, bias, dt, decay, skip, gain = finish(
        cotangent, delta, layer_out, grad_in, flat, in_weight.shape[1], inner_all, head_all, turned
    )
    return (
        layer_out, grad_input, g_norm.reshape(-1), grad_in_weight.T if turned else grad_in_weight, taps, bias.reshape(-1),
        dt.reshape(-1), decay.reshape(-1), skip.reshape(-1), gain.reshape(-1), g_out,
    )


def solution(mesh):
    rows, whole = P("dp", None), P()
    return jax.shard_map(
        body,
        mesh=mesh,
        in_specs=(rows, rows, rows, whole, rows, whole, whole, whole, whole, whole, whole, P("dp", "tensor")),
        out_specs=(rows, rows, whole, rows, whole, whole, whole, whole, whole, whole, P("dp", "tensor")),
        check_vma=False,
    )
```
